32 devices in a mesh: batch: 8 (over z, x), shard: 4 (over y, core).
Axes of the slice: x: 2, y: 2, z: 4, core: 2. Of those that a mesh axis runs over, the one named last changes fastest.
Arguments:
- tokens: float32 [32, 256, 1024], P(('batch', 'shard')), may hold values from -6 to 6
- cotangent: float32 [32, 256, 1024], P(('batch', 'shard')), may hold values from -6 to 6
- lengths: int32 [32], P(('batch', 'shard')), may hold values from 50 to 256, as said below
- ffn_in: bfloat16 [2, 1024, 4096], P(None, None, 'shard'), may hold values from -0.1875 to 0.1875
- ffn_out: bfloat16 [2, 4096, 1024], P(None, None, 'shard'), may hold values from -0.09375 to 0.09375
- ffn_bias: bfloat16 [2, 4096], P(None, 'shard'), may hold values from -2 to 2
- qkv_proj: bfloat16 [3, 1024, 1024], P(None, None, 'shard'), may hold values from -0.1875 to 0.1875
- pos_proj: bfloat16 [1024, 1024], P(None, 'shard'), may hold values from -0.1875 to 0.1875
- out_proj: bfloat16 [1024, 1024], P(None, 'shard'), may hold values from -0.75 to 0.75
- conv_in: bfloat16 [1024, 2048], P(None, 'shard'), may hold values from -0.1875 to 0.1875
- conv_out: bfloat16 [1024, 1024], P(None, 'shard'), may hold values from -0.1875 to 0.1875
- depthwise: bfloat16 [5, 1024], P(None, 'shard'), may hold values from -2.5 to 2.5
- norm_gains: bfloat16 [6, 1024], P(None, 'shard'), may hold values from 0.5 to 1.5
- biases: bfloat16 [16, 1024], P(None, 'shard'), may hold values from -2 to 2
Outputs:
- layer_out: float32 [32, 256, 1024], P(('batch', 'shard'))
- grad_tokens: float32 [32, 256, 1024], P(('batch', 'shard'))
- grad_ffn_in: float32 [2, 1024, 4096], P(None, None, 'shard')
- grad_ffn_out: float32 [2, 4096, 1024], P(None, None, 'shard')
- grad_ffn_bias: float32 [2, 4096], P(None, 'shard')
- grad_qkv_proj: float32 [3, 1024, 1024], P(None, None, 'shard')
- grad_pos_proj: float32 [1024, 1024], P(None, 'shard')
- grad_out_proj: float32 [1024, 1024], P(None, 'shard')
- grad_conv_in: float32 [1024, 2048], P(None, 'shard')
- grad_conv_out: float32 [1024, 1024], P(None, 'shard')
- grad_depthwise: float32 [5, 1024], P(None, 'shard')
- grad_norm_gains: float32 [6, 1024], P(None, 'shard')
- grad_biases: float32 [16, 1024], P(None, 'shard')
The draws below stay inside these ranges and needn't reach their ends.
Inputs may be any that keep to these rules, and one draw needn't show every extreme that they name: `lengths`: each utterance has between 50 and 256 live frames at the start of its 256 slots, the rest padding; some utterance has exactly 256 and some exactly 50.
All inputs are finite; a program needn't handle non-finite values.
Results may differ from the reference program's by a relative error of at most 0.025.
Values may be sent and summed in bfloat16 or wider, within the bound.
A program may use at most 256 MiB of HBM per device.

```python
import math
import jax
import jax.numpy as jnp
from jax import lax

D = 1024
FF = 4096
HEADS = 8
KER = 5
LEN = 256
MIN_LEN = 50
ITEMS = 32


def draw_lengths(key, part):
    first_key, second_key, third_key = jax.random.split(key, 3)
    values = jax.random.randint(first_key, (ITEMS,), MIN_LEN, LEN + 1)
    longest = jax.random.randint(second_key, (), 0, ITEMS)
    values = values.at[longest].set(LEN)
    shortest = (longest + 1 + jax.random.randint(third_key, (), 0, ITEMS - 1)) % ITEMS
    values = values.at[shortest].set(MIN_LEN)
    return values.astype(jnp.int32)


def levels(rng, shape, pieces, smallest, high):
    level, own = 1.0, jax.random.fold_in(rng, 6)
    for axis_at, shards_of in pieces:
        draws = jnp.exp(jax.random.uniform(jax.random.fold_in(own, axis_at), (shards_of,), jnp.float32, smallest / len(pieces), high / len(pieces)))
        level = level * jnp.repeat(draws, shape[axis_at] // shards_of).reshape([-1 if axis == axis_at else 1 for axis in range(len(shape))])
    return level


def noise(stream_key, dims, scale, bound, pieces=(), held_as=jnp.bfloat16):
    values = jax.random.normal(stream_key, dims, jnp.float32) * scale
    if len(pieces) > 0:
        values = levels(stream_key, dims, pieces, -0.22, 0.18) * values
    return jnp.clip(values, min=-bound, max=bound).astype(held_as)


def setup_inputs(seed: int = 0) -> dict:
    splits = jax.random.split(jax.random.key(seed), 15)
    return {
        "tokens": noise(splits[0], (ITEMS, LEN, D), 1.0, 6.0, ((0, 32),), jnp.float32),
        "cotangent": noise(splits[1], (ITEMS, LEN, D), 1.0, 6.0, ((0, 32),), jnp.float32),
        "lengths": draw_lengths(jax.random.fold_in(splits[14], 71), 0),
        "ffn_in": noise(splits[3], (2, D, FF), D ** -0.5, 0.1875, ((2, 4),)),
        "ffn_out": noise(splits[4], (2, FF, D), FF ** -0.5, 0.09375, ((2, 4),)),
        "ffn_bias": noise(splits[5], (2, FF), 0.3, 2.0, ((1, 4),)),
        "qkv_proj": noise(splits[6], (3, D, D), D ** -0.5, 0.1875, ((2, 4),)),
        "pos_proj": noise(splits[7], (D, D), D ** -0.5, 0.1875, ((1, 4),)),
        "out_proj": noise(splits[8], (D, D), (D // 16) ** -0.5, 0.75, ((1, 4),)),
        "conv_in": noise(splits[9], (D, 2 * D), D ** -0.5, 0.1875, ((1, 4),)),
        "conv_out": noise(splits[10], (D, D), D ** -0.5, 0.1875, ((1, 4),)),
        "depthwise": noise(splits[11], (KER, D), KER ** -0.5, 2.5, ((1, 4),)),
        "norm_gains": jnp.clip(1.0 + 0.1 * jax.random.normal(splits[12], (6, D), jnp.float32), 0.5, 1.5).astype(jnp.bfloat16),
        "biases": noise(splits[13], (16, D), 0.3, 2.0, ((1, 4),)),
    }


epsilon = 1e-05
highest = lax.Precision.HIGHEST

@jax.custom_vjp
def low(v):
    return lax.optimization_barrier(v.astype(jnp.bfloat16)).astype(jnp.float32)

@jax.custom_vjp
def low_back(v):
    return v

def low_keep(v):
    return (low(v), None)

def low_pass(kept, grad):
    return (grad,)

def back_keep(v):
    return (v, None)

def back_low(kept, grad):
    return (low(grad),)
low.defvjp(low_keep, low_pass)
low_back.defvjp(back_keep, back_low)

def norm_rows(values_in, gain_row, bias_row):
    row_mean = lax.optimization_barrier(jnp.mean(values_in, axis=-1, keepdims=True))
    centered = values_in - row_mean
    spread = lax.optimization_barrier(jnp.mean(centered * centered, axis=-1, keepdims=True))
    return centered * lax.rsqrt(spread + epsilon) * gain_row + bias_row

def matmul(left_side, right_side):
    return jnp.dot(left_side, right_side, precision=highest)

def position_table(length, features):
    columns = jnp.arange(2 * length - 1, dtype=jnp.float32)
    offsets = length - 1.0 - columns
    freq_rates = jnp.exp(jnp.arange(features // 2, dtype=jnp.float32) * (-2.0 * math.log(10000.0) / features))
    angles = offsets[:, None] * freq_rates[None, :]
    return jnp.concatenate([jnp.sin(angles), jnp.cos(angles)], axis=1)

def depth_conv(gated_rows, kernel):
    length = gated_rows.shape[-2]
    half_width = (kernel.shape[0] - 1) // 2
    padding = [(0, 0)] * (gated_rows.ndim - 2) + [(half_width, half_width), (0, 0)]
    padded = jnp.pad(gated_rows, padding)
    summed = padded[..., 0:length, :] * kernel[0]
    for tap_index in range(1, kernel.shape[0]):
        summed = summed + padded[..., tap_index:tap_index + length, :] * kernel[tap_index]
    return summed

def split_heads(matrix):
    return matrix.reshape(matrix.shape[0], HEADS, matrix.shape[1] // HEADS)

def feed_forward(values_in, params, which_ffn):
    gain_rows, biases = (params[9], params[10])
    gain_index, norm_index, out_index = (0, 0, 1) if which_ffn == 0 else (4, 13, 14)
    hidden = low(norm_rows(values_in, gain_rows[gain_index], biases[norm_index]))
    pre_act = low_back(matmul(hidden, params[0][which_ffn]) + params[2][which_ffn])
    active = low(jax.nn.silu(pre_act))
    return low_back(matmul(active, params[1][which_ffn]) + biases[out_index])

def self_attention(values_in, valid_keys, params):
    gain_rows, biases = (params[9], params[10])
    length, features = values_in.shape
    head_size = features // HEADS
    hidden = low(norm_rows(values_in, gain_rows[1], biases[2]))
    query_rows = low_back(matmul(hidden, params[3][0]) + biases[3])
    key_rows = low(low_back(matmul(hidden, params[3][1])))
    value_rows = low(low_back(matmul(hidden, params[3][2]) + biases[4]))
    with_u = low(query_rows + biases[6])
    with_v = low(query_rows + biases[7])
    table_rows = low(position_table(length, features))
    proj_rows = low(low_back(matmul(table_rows, params[4])))
    content = jnp.einsum('ihd,jhd->hij', split_heads(with_u), split_heads(key_rows), precision=highest)
    wide_scores = jnp.einsum('ihd,chd->hic', split_heads(with_v), split_heads(proj_rows), precision=highest)
    row_ids = jnp.arange(length)[:, None]
    col_ids = jnp.arange(length)[None, :]
    index_map = jnp.broadcast_to((length - 1 - row_ids + col_ids).astype(jnp.int32)[None], (HEADS, length, length))
    shifted = jnp.take_along_axis(wide_scores, index_map, axis=2)
    raw_scores = low_back(content + shifted)
    scores = jnp.where(valid_keys[None, None, :], raw_scores * (1.0 / math.sqrt(head_size)), -1e+30)
    softmax_rows = low(jax.nn.softmax(scores, axis=-1))
    mixed_rows = jnp.einsum('hij,jhd->ihd', softmax_rows, split_heads(value_rows), precision=highest)
    mixed_rows = low(low_back(mixed_rows.reshape(length, features)))
    return low_back(matmul(mixed_rows, params[5]) + biases[5])

def conv_front(values_in, mask_row, params):
    gain_rows, biases = (params[9], params[10])
    features = values_in.shape[1]
    hidden = low(norm_rows(values_in, gain_rows[2], biases[8]))
    pre_act = low_back(matmul(hidden, params[6]) + jnp.concatenate([biases[9], biases[10]]))
    gated_rows = pre_act[:, :features] * jax.nn.sigmoid(pre_act[:, features:]) * mask_row[:, None]
    return depth_conv(gated_rows, params[8])

def conv_rear(conv_rows, row_mean, inverse, params):
    normed = (conv_rows - row_mean) * inverse * params[9][3] + params[10][11]
    active = low(jax.nn.silu(normed))
    return low_back(matmul(active, params[7]) + params[10][12])

def forward(tokens, params, lengths):
    item_count = tokens.shape[0]
    group_size = math.gcd(item_count, max(1, 4096 // LEN))
    blocks = item_count // group_size
    mask_rows = (jnp.arange(LEN)[None, :] < lengths[:, None]).astype(jnp.float32)
    shaped = (tokens.reshape(blocks, group_size, LEN, D), mask_rows.reshape(blocks, group_size, LEN))

    def per_item_front(values_in, mask_row):
        first_rows = values_in + 0.5 * feed_forward(values_in, params, 0)
        second_rows = first_rows + self_attention(first_rows, mask_row > 0.5, params)
        return (second_rows, conv_front(second_rows, mask_row, params))

    def front(pair_in):
        return jax.vmap(per_item_front)(pair_in[0], pair_in[1])
    second_rows, conv_rows = lax.map(jax.checkpoint(front), shaped)
    mask_full = shaped[1][..., None]
    frames = jnp.sum(mask_rows)
    row_mean = lax.optimization_barrier(jnp.sum(conv_rows * mask_full, axis=(0, 1, 2))) / frames
    square = lax.optimization_barrier(jnp.sum(conv_rows * conv_rows * mask_full, axis=(0, 1, 2))) / frames - row_mean * row_mean
    inverse = lax.rsqrt(square + epsilon)

    def per_item_rear(values_in, conv_item, mask_row):
        third_rows = values_in + conv_rear(conv_item, row_mean, inverse, params)
        fourth = third_rows + 0.5 * feed_forward(third_rows, params, 1)
        return norm_rows(fourth, params[9][5], params[10][15]) * mask_row[:, None]

    def rear(triple):
        return jax.vmap(per_item_rear)(triple[0], triple[1], triple[2])
    outputs = lax.map(jax.checkpoint(rear), (second_rows, conv_rows, shaped[1]))
    return outputs.reshape(item_count, LEN, D)

def reference(tokens, cotangent, lengths, ffn_in, ffn_out, ffn_bias, qkv_proj, pos_proj, out_proj, conv_in, conv_out, depthwise, norm_gains, biases):
    params = (ffn_in.astype(jnp.float32), ffn_out.astype(jnp.float32), ffn_bias.astype(jnp.float32), qkv_proj.astype(jnp.float32), pos_proj.astype(jnp.float32), out_proj.astype(jnp.float32), conv_in.astype(jnp.float32), conv_out.astype(jnp.float32), depthwise.astype(jnp.float32), norm_gains.astype(jnp.float32), biases.astype(jnp.float32))

    def run_layer(tokens_in, params_in):
        return forward(tokens_in, params_in, lengths)
    outputs, pull_back = jax.vjp(run_layer, tokens, params)
    grad_tokens, grad_params = pull_back(cotangent)
    return (outputs, grad_tokens, grad_params[0], grad_params[1], grad_params[2], grad_params[3], grad_params[4], grad_params[5], grad_params[6], grad_params[7], grad_params[8], grad_params[9], grad_params[10])
```

```python
import functools
import math

import jax
import jax.numpy as jnp
from jax import lax
from jax.experimental import pallas as pl
from jax.experimental.pallas import tpu as pltpu
from jax.sharding import PartitionSpec as P

HEADS = 8
MESH = pl.DeviceIdType.MESH
epsilon = 1e-05


def f32(a):
    return a.astype(jnp.float32)


def b16(a):
    return a.astype(jnp.bfloat16)


def norm_rows(values_in, gain_row, bias_row):
    row_mean = jnp.mean(values_in, axis=-1, keepdims=True)
    centered = values_in - row_mean
    spread = jnp.mean(centered * centered, axis=-1, keepdims=True)
    return centered * lax.rsqrt(spread + epsilon) * gain_row + bias_row


def dot_rows(a, b):
    return jnp.dot(a, b, preferred_element_type=jnp.float32)


def dot_back(a, b):
    return lax.dot_general(a, b, (((1,), (1,)), ((), ())), preferred_element_type=jnp.float32)


def dot_over(a, b):
    return lax.dot_general(a, b, (((0,), (0,)), ((), ())), preferred_element_type=jnp.float32)


def row_total(a):
    return jnp.sum(f32(a), axis=0)


def position_table(length, features):
    columns = jnp.arange(2 * length - 1, dtype=jnp.float32)
    offsets = length - 1.0 - columns
    freq_rates = jnp.exp(
        jnp.arange(features // 2, dtype=jnp.float32) * (-2.0 * math.log(10000.0) / features)
    )
    angles = offsets[:, None] * freq_rates[None, :]
    return jnp.concatenate([jnp.sin(angles), jnp.cos(angles)], axis=1)


def depth_conv(gated_rows, kernel):
    length = gated_rows.shape[0]
    half_width = (kernel.shape[0] - 1) // 2
    padded = jnp.pad(gated_rows, [(half_width, half_width), (0, 0)])
    summed = padded[0:length] * kernel[0]
    for tap_index in range(1, kernel.shape[0]):
        summed = summed + padded[tap_index : tap_index + length] * kernel[tap_index]
    return summed


def gated_conv(pre_act, mask_col, kernel):
    features = pre_act.shape[1] // 2
    gated_rows = pre_act[:, :features] * jax.nn.sigmoid(pre_act[:, features:]) * mask_col
    return depth_conv(gated_rows, kernel)


def swap(x, axis, mask):
    n = lax.axis_size(axis)
    return lax.ppermute(x, axis, [(i, i ^ mask) for i in range(n)])


def gather_slots(own):
    far = swap(own, "shard", 2)
    near = swap(own, "shard", 1)
    diag = swap(far, "shard", 1)
    return (jnp.concatenate([own, near], 0), jnp.concatenate([far, diag], 0))


def scatter_slots(near_half, far_half):
    rows = near_half.shape[0] // 2
    got_far = swap(b16(far_half[rows:]), "shard", 1)
    sent = b16(far_half[:rows] + f32(got_far))
    got_near = swap(b16(near_half[rows:]), "shard", 1)
    crossed = swap(sent, "shard", 2)
    return near_half[:rows] + f32(got_near) + f32(crossed)


def true_order(pieces, me, axis):
    stacked = jnp.stack(pieces, 0)
    return jnp.concatenate(
        [lax.dynamic_index_in_dim(stacked, me ^ t, 0, keepdims=False) for t in range(len(pieces))],
        axis,
    )


def to_rows(cols, me):
    n = lax.axis_size("shard")
    rows = cols.shape[0] // n
    pieces = []
    for j in range(n):
        part = lax.dynamic_slice_in_dim(cols, (me ^ j) * rows, rows, 0)
        pieces.append(part if j == 0 else swap(part, "shard", j))
    return true_order(pieces, me, 1)


def to_cols(rows_block, me):
    n = lax.axis_size("shard")
    cols = rows_block.shape[1] // n
    pieces = []
    for j in range(n):
        part = lax.dynamic_slice_in_dim(rows_block, (me ^ j) * cols, cols, 1)
        pieces.append(part if j == 0 else swap(part, "shard", j))
    stacked = jnp.stack(pieces, 0)
    return jnp.stack(
        [lax.dynamic_index_in_dim(stacked, me ^ t, 0, keepdims=False) for t in range(n)], 0
    )


def halve_batch(total, order, place):
    for bit in order:
        half = total.shape[0] // 2
        mine = (place >> bit) & 1
        kept = lax.dynamic_slice_in_dim(total, mine * half, half, 0)
        sent = b16(lax.dynamic_slice_in_dim(total, (1 - mine) * half, half, 0))
        total = kept + f32(swap(sent, "batch", 1 << bit))
    return b16(total)


def double_batch(block, order, place, axis=0):
    for bit in reversed(order):
        other = swap(block, "batch", 1 << bit)
        mine = ((place >> bit) & 1) == 0
        block = jnp.concatenate(
            [jnp.where(mine, block, other), jnp.where(mine, other, block)], axis
        )
    return block


def peers_of(axis, index, count):
    return [{axis: lax.rem(index + j, count)} for j in range(1, count)]


def exchange(axis, index, count, source, landing, send_sem, recv_sem):
    copies = []
    for j in range(1, count):
        peer = lax.rem(index + j, count)
        copies.append(
            pltpu.make_async_remote_copy(
                src_ref=source,
                dst_ref=landing.at[index],
                send_sem=send_sem.at[j],
                recv_sem=recv_sem.at[j],
                device_id={axis: peer},
                device_id_type=MESH,
            )
        )
    return copies


def greet(sizes, places):
    barrier = pltpu.get_barrier_semaphore()
    total = 0
    for axis in ("shard", "batch"):
        for device in peers_of(axis, places[axis], sizes[axis]):
            pl.semaphore_signal(barrier, inc=1, device_id=device, device_id_type=MESH)
            total += 1
    pl.semaphore_wait(barrier, total)


def sum_slots(ref, count):
    total = ref[0]
    for j in range(1, count):
        total = total + ref[j]
    return total


def stats_body(ns, nb, x_ref, o_ref, land_s, mid, land_b, ss, rs, sb, rb):
    s, b = lax.axis_index("shard"), lax.axis_index("batch")
    greet({"shard": ns, "batch": nb}, {"shard": s, "batch": b})
    first = exchange("shard", s, ns, x_ref, land_s, ss, rs)
    for copy in first:
        copy.start()
    land_s[s] = x_ref[...]
    for copy in first:
        copy.wait()
    mid[...] = sum_slots(land_s, ns)
    second = exchange("batch", b, nb, mid, land_b, sb, rb)
    for copy in second:
        copy.start()
    land_b[b] = mid[...]
    for copy in second:
        copy.wait()
    o_ref[...] = sum_slots(land_b, nb)


def stats_sum(x, ident):
    ns, nb = lax.axis_size("shard"), lax.axis_size("batch")
    shape = x.shape
    return pl.pallas_call(
        functools.partial(stats_body, ns, nb),
        out_shape=jax.ShapeDtypeStruct(shape, jnp.float32),
        in_specs=[pl.BlockSpec(memory_space=pltpu.VMEM)],
        out_specs=pl.BlockSpec(memory_space=pltpu.VMEM),
        scratch_shapes=[
            pltpu.VMEM((ns,) + shape, jnp.float32),
            pltpu.VMEM(shape, jnp.float32),
            pltpu.VMEM((nb,) + shape, jnp.float32),
            pltpu.SemaphoreType.DMA((ns,)),
            pltpu.SemaphoreType.DMA((ns,)),
            pltpu.SemaphoreType.DMA((nb,)),
            pltpu.SemaphoreType.DMA((nb,)),
        ],
        compiler_params=pltpu.CompilerParams(collective_id=ident, has_side_effects=True),
        name="stats_sum_%d" % ident,
    )(x)


def vector_body(ns, nb, w_ref, l_ref, o_ref, land_s, mid, land_b, ss, rs, sb, rb):
    s, b = lax.axis_index("shard"), lax.axis_index("batch")
    greet({"shard": ns, "batch": nb}, {"shard": s, "batch": b})
    rows = w_ref.shape[1]
    copies = []
    for j in range(1, ns):
        peer = lax.rem(s + j, ns)
        copies.append(
            pltpu.make_async_remote_copy(
                src_ref=w_ref.at[peer],
                dst_ref=land_s.at[s],
                send_sem=ss.at[j],
                recv_sem=rs.at[j],
                device_id={"shard": peer},
                device_id_type=MESH,
            )
        )
    for copy in copies:
        copy.start()
    land_s[s] = w_ref[s]
    for copy in copies:
        copy.wait()
    mid[0:rows] = sum_slots(land_s, ns)
    mid[rows:] = l_ref[...]
    second = exchange("batch", b, nb, mid, land_b, sb, rb)
    for copy in second:
        copy.start()
    land_b[b] = mid[...]
    for copy in second:
        copy.wait()
    o_ref[...] = sum_slots(land_b, nb)


def vector_sum(wide, local, ident):
    ns, nb = lax.axis_size("shard"), lax.axis_size("batch")
    _, r, c = wide.shape
    rows = r + local.shape[0]
    return pl.pallas_call(
        functools.partial(vector_body, ns, nb),
        out_shape=jax.ShapeDtypeStruct((rows, c), jnp.float32),
        in_specs=[pl.BlockSpec(memory_space=pltpu.VMEM)] * 2,
        out_specs=pl.BlockSpec(memory_space=pltpu.VMEM),
        scratch_shapes=[
            pltpu.VMEM((ns, r, c), jnp.float32),
            pltpu.VMEM((rows, c), jnp.float32),
            pltpu.VMEM((nb, rows, c), jnp.float32),
            pltpu.SemaphoreType.DMA((ns,)),
            pltpu.SemaphoreType.DMA((ns,)),
            pltpu.SemaphoreType.DMA((nb,)),
            pltpu.SemaphoreType.DMA((nb,)),
        ],
        compiler_params=pltpu.CompilerParams(collective_id=ident, has_side_effects=True),
        name="vector_sum",
    )(wide, local)


def attend_body(heads, size, scale, len_ref, u_ref, v_ref, k_ref, x_ref, p_ref, mix_ref, soft_ref):
    live = len_ref[pl.program_id(0)]
    length = u_ref.shape[0]
    for h in range(heads):
        cols = slice(h * size, (h + 1) * size)
        wide = dot_back(v_ref[:, cols], p_ref[:, cols])
        moved = pltpu.roll(wide, length + 1, 1, stride=1, stride_axis=0)[:, :length]
        raw = dot_back(u_ref[:, cols], k_ref[:, cols]) + moved
        keys = lax.broadcasted_iota(jnp.int32, (length, length), 1)
        scores = jnp.where(keys < live, raw * scale, -1e30)
        top = jnp.max(scores, axis=-1, keepdims=True)
        grown = jnp.exp(scores - top)
        soft = grown / jnp.sum(grown, axis=-1, keepdims=True)
        soft_ref[:, h * length : (h + 1) * length] = soft
        mix_ref[:, cols] = b16(dot_rows(b16(soft), x_ref[:, cols]))


def attend(lens, with_u, with_v, key, value, proj, length, heads):
    rows, width = with_u.shape
    size = width // heads
    items = rows // length
    block = pl.BlockSpec((length, width), lambda i, n: (i, 0))
    return pl.pallas_call(
        functools.partial(attend_body, heads, size, 1.0 / math.sqrt(size)),
        grid_spec=pltpu.PrefetchScalarGridSpec(
            num_scalar_prefetch=1,
            grid=(items,),
            in_specs=[block, block, block, block, pl.BlockSpec(proj.shape, lambda i, n: (0, 0))],
            out_specs=[block, pl.BlockSpec((length, heads * length), lambda i, n: (i, 0))],
        ),
        out_shape=[
            jax.ShapeDtypeStruct((rows, width), jnp.bfloat16),
            jax.ShapeDtypeStruct((rows, heads * length), jnp.float32),
        ],
        compiler_params=pltpu.CompilerParams(vmem_limit_bytes=32 << 20),
        name="attend",
        cost_estimate=pl.CostEstimate(
            flops=8 * rows * length * width, transcendentals=rows * length * heads, bytes_accessed=rows * width * 10
        ),
    )(lens, with_u, with_v, key, value, proj)


def attend_back_body(
    heads, size, scale, len_ref, g_ref, soft_ref, u_ref, v_ref, k_ref, x_ref, p_ref,
    dq_ref, dk_ref, dx_ref, dp_ref, sum_ref,
):
    item = pl.program_id(0)
    live = len_ref[item]
    length = u_ref.shape[0]
    at_row = lax.broadcasted_iota(jnp.int32, (length, length), 0)
    at_col = lax.broadcasted_iota(jnp.int32, (length, length), 1)
    flip = b16(f32(at_row + at_col == length - 1))
    for h in range(heads):
        cols = slice(h * size, (h + 1) * size)
        soft = soft_ref[:, h * length : (h + 1) * length]
        grad = g_ref[:, cols]
        grad_soft = dot_back(grad, x_ref[:, cols])
        dx_ref[:, cols] = b16(dot_over(b16(soft), grad))
        grad_scores = soft * (grad_soft - jnp.sum(grad_soft * soft, axis=-1, keepdims=True))
        raw = b16(jnp.where(at_col < live, grad_scores, 0.0) * scale)
        grad_u = dot_rows(raw, k_ref[:, cols])
        dk_ref[:, cols] = b16(dot_over(raw, u_ref[:, cols]))
        turned = dot_rows(flip, raw)
        wide = jnp.concatenate([turned, jnp.zeros_like(turned)], 1)
        wide = b16(pltpu.roll(wide, 0, 1, stride=1, stride_axis=0))
        grad_v_turned = dot_rows(wide, p_ref[:, cols])
        v_turned = b16(dot_rows(flip, v_ref[:, cols]))
        dp_ref[0, :, cols] = b16(dot_over(wide, v_turned))
        high = b16(grad_v_turned)
        low = b16(grad_v_turned - f32(high))
        grad_v = dot_rows(flip, high) + dot_rows(flip, low)
        dq_ref[:, cols] = b16(grad_u + grad_v)
        total = jnp.concatenate(
            [
                jnp.sum(grad_u, axis=0, keepdims=True),
                jnp.sum(grad_v_turned, axis=0, keepdims=True),
                jnp.zeros((6, size), jnp.float32),
            ],
            0,
        )
        sum_ref[0, :, cols] = total


def attend_back(lens, grad, soft, with_u, with_v, key, value, proj, length, heads):
    rows, width = with_u.shape
    size = width // heads
    items = rows // length
    block = pl.BlockSpec((length, width), lambda i, n: (i, 0))
    return pl.pallas_call(
        functools.partial(attend_back_body, heads, size, 1.0 / math.sqrt(size)),
        grid_spec=pltpu.PrefetchScalarGridSpec(
            num_scalar_prefetch=1,
            grid=(items,),
            in_specs=[
                block,
                pl.BlockSpec((length, heads * length), lambda i, n: (i, 0)),
                block, block, block, block,
                pl.BlockSpec(proj.shape, lambda i, n: (0, 0)),
            ],
            out_specs=[
                block, block, block,
                pl.BlockSpec((1,) + proj.shape, lambda i, n: (i, 0, 0)),
                pl.BlockSpec((1, 8, width), lambda i, n: (i, 0, 0)),
            ],
        ),
        out_shape=[
            jax.ShapeDtypeStruct((rows, width), jnp.bfloat16),
            jax.ShapeDtypeStruct((rows, width), jnp.bfloat16),
            jax.ShapeDtypeStruct((rows, width), jnp.bfloat16),
            jax.ShapeDtypeStruct((items,) + proj.shape, jnp.bfloat16),
            jax.ShapeDtypeStruct((items, 8, width), jnp.float32),
        ],
        compiler_params=pltpu.CompilerParams(vmem_limit_bytes=32 << 20),
        name="attend_back",
        cost_estimate=pl.CostEstimate(
            flops=26 * rows * length * width, transcendentals=0, bytes_accessed=rows * width * 30
        ),
    )(lens, grad, soft, with_u, with_v, key, value, proj)


def ffn_forward(rows_in, w_in, w_rows, b_in, gain_row, norm_bias):
    halves = gather_slots(b16(norm_rows(rows_in, gain_row, norm_bias)))
    saved, sums = [], []
    for hidden in halves:
        pre = dot_rows(hidden, w_in) + b_in
        active = b16(jax.nn.silu(pre))
        sums.append(dot_rows(active, w_rows))
        saved.append((hidden, pre, active))
    return scatter_slots(*sums), saved


def ffn_back(grad_own, rows_in, saved, w_in, w_rows, gain_row, norm_bias):
    halves = gather_slots(grad_own)
    grad_in = grad_out = grad_b = 0.0
    sums = []
    for grad, (hidden, pre, active) in zip(halves, saved):
        silu_back = jax.vjp(jax.nn.silu, pre)[1]
        grad_pre = b16(silu_back(dot_back(grad, w_rows))[0])
        sums.append(dot_back(grad_pre, w_in))
        grad_out = grad_out + dot_over(active, grad)
        grad_in = grad_in + dot_over(hidden, grad_pre)
        grad_b = grad_b + row_total(grad_pre)
    norm_back = jax.vjp(norm_rows, rows_in, gain_row, norm_bias)[1]
    grad_rows, grad_gain, grad_bias = norm_back(scatter_slots(*sums))
    return grad_rows, grad_gain, grad_bias, grad_in, grad_out, grad_b, row_total(grad_own)


def body(
    tokens, cotangent, lengths, ffn_in, ffn_out, ffn_bias, qkv_proj, pos_proj, out_proj,
    conv_in, conv_out, depthwise, norm_gains, biases,
):
    _, length, features = tokens.shape
    shard, batch = lax.axis_index("shard"), lax.axis_index("batch")
    ns, nb = lax.axis_size("shard"), lax.axis_size("batch")
    width = features // ns
    bits = nb.bit_length() - 1
    order_a = list(range(bits))
    order_b = [1, 0] + list(range(2, bits)) if bits > 1 else order_a
    heads = HEADS // ns
    rows_in = tokens[0]
    grads_in = cotangent[0]

    own_length = jnp.broadcast_to(b16(f32(lengths))[:, None], (1, width))
    packed = jnp.concatenate([norm_gains, biases, depthwise, own_length], 0)
    packed = f32(lax.all_gather(packed, "shard", axis=1, tiled=True))
    gain_rows, bias_rows = packed[0:6], packed[6:22]
    kernel = packed[22:27]
    group_lengths = packed[27].reshape(ns, width)[:, 0].astype(jnp.int32)
    slot_lengths = jnp.stack(
        [lax.dynamic_index_in_dim(group_lengths, shard ^ j, 0, keepdims=False) for j in range(ns)]
    )
    own_biases = f32(biases)
    mask_col = f32(lax.broadcasted_iota(jnp.int32, (length, 1), 0) < lengths[0])
    w_rows = [to_rows(ffn_out[0], shard), to_rows(ffn_out[1], shard)]
    w_in = [ffn_in[0], ffn_in[1]]
    b_in = f32(ffn_bias)

    branch, saved_one = ffn_forward(rows_in, w_in[0], w_rows[0], b_in[0], gain_rows[0], bias_rows[0])
    rows_one = rows_in + 0.5 * (branch + bias_rows[1])

    table_b = b16(position_table(length, features))
    table_b = jnp.pad(table_b, [(0, 1), (0, 0)])
    proj_b = b16(dot_rows(table_b, pos_proj))
    w_out = lax.all_gather(out_proj, "shard", axis=1, tiled=True)
    wc_in = lax.all_gather(conv_in, "shard", axis=1, tiled=True)
    wc_out = lax.all_gather(conv_out, "shard", axis=1, tiled=True)

    halves = gather_slots(b16(norm_rows(rows_one, gain_rows[1], bias_rows[2])))
    saved_mix = []
    mixed = []
    for half, hidden in enumerate(halves):
        query = dot_rows(hidden, qkv_proj[0]) + own_biases[3]
        key = b16(dot_rows(hidden, qkv_proj[1]))
        value = b16(dot_rows(hidden, qkv_proj[2]) + own_biases[4])
        with_u = b16(query + own_biases[6])
        with_v = b16(query + own_biases[7])
        lens = slot_lengths[2 * half : 2 * half + 2]
        mix, soft = attend(lens, with_u, with_v, key, value, proj_b, length, heads)
        mixed += [mix[:length], mix[length:]]
        saved_mix.append((hidden, lens, soft, with_u, with_v, key, value))
    pieces = [mixed[0]] + [swap(mixed[j], "shard", j) for j in range(1, ns)]
    mixed_own = true_order(pieces, shard, 1)
    rows_two = rows_one + (dot_rows(mixed_own, w_out) + bias_rows[5])

    hidden_conv = b16(norm_rows(rows_two, gain_rows[2], bias_rows[8]))
    pre_conv = dot_rows(hidden_conv, wc_in) + jnp.concatenate([bias_rows[9], bias_rows[10]])
    conv_rows = gated_conv(pre_conv, mask_col, kernel)
    sums = jnp.concatenate(
        [
            jnp.sum(conv_rows * mask_col, axis=0).reshape(-1, 128),
            jnp.sum(conv_rows * conv_rows * mask_col, axis=0).reshape(-1, 128),
            jnp.broadcast_to(f32(lengths)[:, None], (8, 128)),
        ],
        0,
    )
    sums = stats_sum(sums, 1)
    lanes = features // 128
    frames = sums[2 * lanes, 0]
    row_mean = sums[:lanes].reshape(features) / frames
    inverse = lax.rsqrt(
        sums[lanes : 2 * lanes].reshape(features) / frames - row_mean * row_mean + epsilon
    )
    normed = (conv_rows - row_mean) * inverse * gain_rows[3] + bias_rows[11]
    active_conv = b16(jax.nn.silu(normed))
    rows_three = rows_two + (dot_rows(active_conv, wc_out) + bias_rows[12])

    branch, saved_two = ffn_forward(
        rows_three, w_in[1], w_rows[1], b_in[1], gain_rows[4], bias_rows[13]
    )
    rows_four = rows_three + 0.5 * (branch + bias_rows[14])
    result = norm_rows(rows_four, gain_rows[5], bias_rows[15]) * mask_col

    final_back = jax.vjp(norm_rows, rows_four, gain_rows[5], bias_rows[15])[1]
    stream, grad_gain_last, grad_bias_last = final_back(grads_in * mask_col)
    two = ffn_back(
        b16(0.5 * stream), rows_three, saved_two, w_in[1], w_rows[1], gain_rows[4], bias_rows[13]
    )
    stream = stream + two[0]

    def reduced(total, order):
        return double_batch(halve_batch(total, order, batch), order, batch)

    def reduced_rows(total, order):
        block = to_cols(halve_batch(total, order, batch), shard)
        block = double_batch(block, order, batch, axis=1)
        return block.reshape(-1, width)

    ffn_in_two = reduced(two[3], order_a)
    ffn_out_two = reduced_rows(two[4], order_b)

    grad_out = b16(stream)
    grad_conv_out = dot_over(active_conv, grad_out)
    grad_pw_out = row_total(grad_out)
    silu_back = jax.vjp(jax.nn.silu, normed)[1]
    grad_normed = silu_back(dot_back(grad_out, wc_out))[0]
    scaled = (conv_rows - row_mean) * inverse
    totals = stats_sum(
        jnp.concatenate(
            [
                jnp.sum(grad_normed, axis=0).reshape(-1, 128),
                jnp.sum(grad_normed * scaled, axis=0).reshape(-1, 128),
            ],
            0,
        ),
        2,
    )
    beta, gamma = totals[:lanes].reshape(features), totals[lanes:].reshape(features)
    gamma_row = gain_rows[3]
    grad_conv = inverse * (
        grad_normed * gamma_row
        - mask_col * (gamma_row * beta + scaled * (gamma_row * gamma)) / frames
    )
    tail_back = jax.vjp(lambda pre, taps: gated_conv(pre, mask_col, taps), pre_conv, kernel)[1]
    grad_pre_single, grad_kernel = tail_back(grad_conv)
    grad_pre = b16(grad_pre_single)
    grad_conv_in = dot_over(hidden_conv, grad_pre)
    grad_pw_in = row_total(grad_pre)
    conv_norm_back = jax.vjp(norm_rows, rows_two, gain_rows[2], bias_rows[8])[1]
    grad_rows, grad_gain_conv, grad_bias_conv = conv_norm_back(dot_back(grad_pre, wc_in))
    stream = stream + grad_rows

    def scattered(total):
        return f32(lax.psum_scatter(b16(total), "shard", scatter_dimension=1, tiled=True))

    conv_out_red = reduced(scattered(grad_conv_out), order_a)
    conv_in_red = reduced(scattered(grad_conv_in), order_b)

    grad_out = b16(stream)
    grad_w_out = dot_over(mixed_own, grad_out)
    grad_b_out = row_total(grad_out)
    grad_mixed = b16(dot_back(grad_out, w_out))
    slots = []
    for j in range(ns):
        part = lax.dynamic_slice_in_dim(grad_mixed, (shard ^ j) * width, width, 1)
        slots.append(part if j == 0 else swap(part, "shard", j))
    grad_qkv = [0.0, 0.0, 0.0]
    grad_w_pos = 0.0
    grad_uv = 0.0
    grad_q_bias = grad_x_bias = 0.0
    sums = []
    for half, (hidden, lens, soft, with_u, with_v, key, value) in enumerate(saved_mix):
        grad = jnp.concatenate(slots[2 * half : 2 * half + 2], 0)
        dq, dk, dx, dp, duv = attend_back(
            lens, grad, soft, with_u, with_v, key, value, proj_b, length, heads
        )
        for at, part in enumerate((dq, dk, dx)):
            grad_qkv[at] = grad_qkv[at] + dot_over(hidden, part)
        for at in range(dp.shape[0]):
            grad_w_pos = grad_w_pos + dot_over(table_b, dp[at])
        grad_uv = grad_uv + jnp.sum(duv, axis=0)
        grad_q_bias = grad_q_bias + row_total(dq)
        grad_x_bias = grad_x_bias + row_total(dx)
        sums.append(
            dot_back(dq, qkv_proj[0]) + dot_back(dk, qkv_proj[1]) + dot_back(dx, qkv_proj[2])
        )
    norm_back = jax.vjp(norm_rows, rows_one, gain_rows[1], bias_rows[2])[1]
    grad_rows, grad_gain_mix, grad_bias_mix = norm_back(scatter_slots(*sums))
    stream = stream + grad_rows
    pos_red = reduced(grad_w_pos, order_a)
    q_red = reduced(grad_qkv[0], order_b)
    k_red = reduced(grad_qkv[1], order_a)
    x_red = reduced(grad_qkv[2], order_b)
    out_red = reduced(scattered(grad_w_out), order_a)

    one = ffn_back(
        b16(0.5 * stream), rows_in, saved_one, w_in[0], w_rows[0], gain_rows[0], bias_rows[0]
    )
    stream = stream + one[0]
    ffn_in_one = reduced(one[3], order_a)
    ffn_out_one = reduced_rows(one[4], order_b)

    wide = jnp.stack(
        [
            one[1], grad_gain_mix, grad_gain_conv, two[1], grad_gain_last,
            one[2], one[6], grad_bias_mix, grad_b_out, grad_bias_conv,
            grad_pw_in[:features], grad_pw_in[features:], grad_pw_out, two[2], two[6], grad_bias_last,
        ]
        + [grad_kernel[t] for t in range(grad_kernel.shape[0])]
        + [jnp.zeros((features,), jnp.float32)] * 3
    )
    wide = wide.reshape(wide.shape[0], ns, width).transpose(1, 0, 2)
    hidden_bias = jnp.stack([one[5], two[5]]).reshape(-1, width)
    local = jnp.concatenate(
        [grad_q_bias[None], grad_x_bias[None], grad_uv[0:2], hidden_bias], 0
    )
    local = jnp.pad(local, [(0, -local.shape[0] % 8), (0, 0)])
    vec = vector_sum(wide, local, 3)
    mine = lax.dynamic_slice_in_dim(jnp.stack([gamma, beta]), shard * width, width, 1)
    base = wide.shape[1]
    out_gains = jnp.stack([vec[0], vec[1], vec[2], mine[0], vec[3], vec[4]])
    out_biases = jnp.stack(
        [
            vec[5], vec[6], vec[7], vec[base], vec[base + 1], vec[8], vec[base + 2], vec[base + 3],
            vec[9], vec[10], vec[11], mine[1], vec[12], vec[13], vec[14], vec[15],
        ]
    )
    out_kernel = vec[16:21]
    out_hidden = vec[base + 4 : base + 4 + hidden_bias.shape[0]].reshape(2, -1)
    return (
        result[None],
        stream[None],
        f32(jnp.stack([ffn_in_one, ffn_in_two])),
        f32(jnp.stack([ffn_out_one, ffn_out_two])),
        out_hidden,
        f32(jnp.stack([q_red, k_red, x_red])),
        f32(pos_red),
        f32(out_red),
        f32(conv_in_red),
        f32(conv_out_red),
        out_kernel,
        out_gains,
        out_biases,
    )


def solution(mesh):
    rows = P(("batch", "shard"), None, None)
    cube, flat = P(None, None, "shard"), P(None, "shard")
    return jax.shard_map(
        body,
        mesh=mesh,
        in_specs=(rows, rows, P(("batch", "shard")), cube, cube, flat, cube)
        + (flat,) * 7,
        out_specs=(rows, rows, cube, cube, flat, cube) + (flat,) * 7,
        check_vma=False,
    )
```

```python
import functools
import math

import jax
import jax.numpy as jnp
from jax import lax
from jax.experimental import pallas as pl
from jax.experimental.pallas import tpu as pltpu
from jax.sharding import PartitionSpec as P

HEADS = 8
MESH = pl.DeviceIdType.MESH
epsilon = 1e-05


def f32(a):
    return a.astype(jnp.float32)


def b16(a):
    return a.astype(jnp.bfloat16)


def norm_rows(values_in, gain_row, bias_row):
    row_mean = jnp.mean(values_in, axis=-1, keepdims=True)
    centered = values_in - row_mean
    spread = jnp.mean(centered * centered, axis=-1, keepdims=True)
    return centered * lax.rsqrt(spread + epsilon) * gain_row + bias_row


def dot_rows(a, b):
    return jnp.dot(a, b, preferred_element_type=jnp.float32)


def dot_back(a, b):
    return lax.dot_general(a, b, (((1,), (1,)), ((), ())), preferred_element_type=jnp.float32)


def dot_over(a, b):
    return lax.dot_general(a, b, (((0,), (0,)), ((), ())), preferred_element_type=jnp.float32)


def row_total(a):
    return jnp.sum(f32(a), axis=0)


def position_table(length, features):
    columns = jnp.arange(2 * length - 1, dtype=jnp.float32)
    offsets = length - 1.0 - columns
    freq_rates = jnp.exp(
        jnp.arange(features // 2, dtype=jnp.float32) * (-2.0 * math.log(10000.0) / features)
    )
    angles = offsets[:, None] * freq_rates[None, :]
    return jnp.concatenate([jnp.sin(angles), jnp.cos(angles)], axis=1)


def depth_conv(gated_rows, kernel):
    length = gated_rows.shape[0]
    half_width = (kernel.shape[0] - 1) // 2
    padded = jnp.pad(gated_rows, [(half_width, half_width), (0, 0)])
    summed = padded[0:length] * kernel[0]
    for tap_index in range(1, kernel.shape[0]):
        summed = summed + padded[tap_index : tap_index + length] * kernel[tap_index]
    return summed


def gated_conv(pre_act, mask_col, kernel):
    features = pre_act.shape[1] // 2
    gated_rows = pre_act[:, :features] * jax.nn.sigmoid(pre_act[:, features:]) * mask_col
    return depth_conv(gated_rows, kernel)


def swap(x, axis, mask):
    n = lax.axis_size(axis)
    return lax.ppermute(x, axis, [(i, i ^ mask) for i in range(n)])


def gather_slots(own):
    far = swap(own, "shard", 2)
    near = swap(own, "shard", 1)
    diag = swap(far, "shard", 1)
    return (jnp.concatenate([own, near], 0), jnp.concatenate([far, diag], 0))


def scatter_slots(near_half, far_half):
    rows = near_half.shape[0] // 2
    got_far = swap(b16(far_half[rows:]), "shard", 1)
    sent = b16(far_half[:rows] + f32(got_far))
    got_near = swap(b16(near_half[rows:]), "shard", 1)
    crossed = swap(sent, "shard", 2)
    return near_half[:rows] + f32(got_near) + f32(crossed)


def true_order(pieces, me, axis):
    stacked = jnp.stack(pieces, 0)
    return jnp.concatenate(
        [lax.dynamic_index_in_dim(stacked, me ^ t, 0, keepdims=False) for t in range(len(pieces))],
        axis,
    )


def to_rows(cols, me):
    n = lax.axis_size("shard")
    rows = cols.shape[0] // n
    pieces = []
    for j in range(n):
        part = lax.dynamic_slice_in_dim(cols, (me ^ j) * rows, rows, 0)
        pieces.append(part if j == 0 else swap(part, "shard", j))
    return true_order(pieces, me, 1)


def peers_of(axis, index, count):
    return [{axis: lax.rem(index + j, count)} for j in range(1, count)]


def exchange(axis, index, count, source, landing, send_sem, recv_sem):
    copies = []
    for j in range(1, count):
        peer = lax.rem(index + j, count)
        copies.append(
            pltpu.make_async_remote_copy(
                src_ref=source,
                dst_ref=landing.at[index],
                send_sem=send_sem.at[j],
                recv_sem=recv_sem.at[j],
                device_id={axis: peer},
                device_id_type=MESH,
            )
        )
    return copies


def greet(sizes, places):
    barrier = pltpu.get_barrier_semaphore()
    total = 0
    for axis in ("shard", "batch"):
        for device in peers_of(axis, places[axis], sizes[axis]):
            pl.semaphore_signal(barrier, inc=1, device_id=device, device_id_type=MESH)
            total += 1
    pl.semaphore_wait(barrier, total)


def sum_slots(ref, count):
    total = ref[0]
    for j in range(1, count):
        total = total + ref[j]
    return total


def stats_body(ns, nb, x_ref, o_ref, land_s, mid, land_b, ss, rs, sb, rb):
    s, b = lax.axis_index("shard"), lax.axis_index("batch")
    greet({"shard": ns, "batch": nb}, {"shard": s, "batch": b})
    first = exchange("shard", s, ns, x_ref, land_s, ss, rs)
    for copy in first:
        copy.start()
    land_s[s] = x_ref[...]
    for copy in first:
        copy.wait()
    mid[...] = sum_slots(land_s, ns)
    second = exchange("batch", b, nb, mid, land_b, sb, rb)
    for copy in second:
        copy.start()
    land_b[b] = mid[...]
    for copy in second:
        copy.wait()
    o_ref[...] = sum_slots(land_b, nb)


def stats_sum(x, ident):
    ns, nb = lax.axis_size("shard"), lax.axis_size("batch")
    shape = x.shape
    return pl.pallas_call(
        functools.partial(stats_body, ns, nb),
        out_shape=jax.ShapeDtypeStruct(shape, jnp.float32),
        in_specs=[pl.BlockSpec(memory_space=pltpu.VMEM)],
        out_specs=pl.BlockSpec(memory_space=pltpu.VMEM),
        scratch_shapes=[
            pltpu.VMEM((ns,) + shape, jnp.float32),
            pltpu.VMEM(shape, jnp.float32),
            pltpu.VMEM((nb,) + shape, jnp.float32),
            pltpu.SemaphoreType.DMA((ns,)),
            pltpu.SemaphoreType.DMA((ns,)),
            pltpu.SemaphoreType.DMA((nb,)),
            pltpu.SemaphoreType.DMA((nb,)),
        ],
        compiler_params=pltpu.CompilerParams(collective_id=ident, has_side_effects=True),
        name="stats_sum_%d" % ident,
    )(x)


def vector_body(ns, nb, w_ref, l_ref, o_ref, land_s, mid, land_b, ss, rs, sb, rb):
    s, b = lax.axis_index("shard"), lax.axis_index("batch")
    greet({"shard": ns, "batch": nb}, {"shard": s, "batch": b})
    rows = w_ref.shape[1]
    copies = []
    for j in range(1, ns):
        peer = lax.rem(s + j, ns)
        copies.append(
            pltpu.make_async_remote_copy(
                src_ref=w_ref.at[peer],
                dst_ref=land_s.at[s],
                send_sem=ss.at[j],
                recv_sem=rs.at[j],
                device_id={"shard": peer},
                device_id_type=MESH,
            )
        )
    for copy in copies:
        copy.start()
    land_s[s] = w_ref[s]
    for copy in copies:
        copy.wait()
    mid[0:rows] = sum_slots(land_s, ns)
    mid[rows:] = l_ref[...]
    second = exchange("batch", b, nb, mid, land_b, sb, rb)
    for copy in second:
        copy.start()
    land_b[b] = mid[...]
    for copy in second:
        copy.wait()
    o_ref[...] = sum_slots(land_b, nb)


def vector_sum(wide, local, ident):
    ns, nb = lax.axis_size("shard"), lax.axis_size("batch")
    _, r, c = wide.shape
    rows = r + local.shape[0]
    return pl.pallas_call(
        functools.partial(vector_body, ns, nb),
        out_shape=jax.ShapeDtypeStruct((rows, c), jnp.float32),
        in_specs=[pl.BlockSpec(memory_space=pltpu.VMEM)] * 2,
        out_specs=pl.BlockSpec(memory_space=pltpu.VMEM),
        scratch_shapes=[
            pltpu.VMEM((ns, r, c), jnp.float32),
            pltpu.VMEM((rows, c), jnp.float32),
            pltpu.VMEM((nb, rows, c), jnp.float32),
            pltpu.SemaphoreType.DMA((ns,)),
            pltpu.SemaphoreType.DMA((ns,)),
            pltpu.SemaphoreType.DMA((nb,)),
            pltpu.SemaphoreType.DMA((nb,)),
        ],
        compiler_params=pltpu.CompilerParams(collective_id=ident, has_side_effects=True),
        name="vector_sum",
    )(wide, local)


class Chunk:
    def __init__(self, at, source, row, rows, columns, first, count):
        self.at, self.source, self.row, self.rows, self.columns = at, source, row, rows, columns
        extra = [(1 << k, k) for k in range(3, count.bit_length() - 1)]
        line = (6, 1)
        if first == "near":
            self.pre, self.post = [(1, 0)], [line] + extra
        else:
            self.pre, self.post = [], [line, (1, 0)] + extra
        size, self.landings = rows, []
        for _ in self.pre:
            size //= 2
            self.landings.append((size, columns))
        self.landings.append((size, columns))
        for _ in self.post:
            size //= 2
            self.landings.append((size, columns))
        self.steps = len(self.landings)


def bit_of(value, k):
    return lax.rem(lax.div(value, 1 << k), 2)


def flip_bits(value, mask):
    out = value
    k = 0
    while (1 << k) <= mask:
        if mask & (1 << k):
            out = out + (1 - 2 * bit_of(value, k)) * (1 << k)
        k += 1
    return out


class Mover:
    def __init__(self, chunk, batch, source, total, landings, sems, finish):
        self.c, self.b = chunk, batch
        self.source, self.total, self.landings, self.sems = source, total, landings, sems
        lo, hi = bit_of(batch, 1), bit_of(batch, 2)
        self.inner = lo != hi
        self.ended = lo == hi
        self.finish = finish
        self.stages = []
        self.build()

    def copy(self, at, src, dst, mask):
        send, recv = self.sems
        return pltpu.make_async_remote_copy(
            src_ref=src,
            dst_ref=dst,
            send_sem=send.at[self.c.at, at],
            recv_sem=recv.at[self.c.at, at],
            device_id={"batch": flip_bits(self.b, mask)},
            device_id_type=MESH,
        )

    def rows(self, ref, start, size):
        start = start if isinstance(start, int) else pl.multiple_of(start, 16)
        return ref.at[pl.ds(start, size)]

    def build(self):
        c = self.c
        held = lambda off, size: self.rows(self.total, off, size)
        here, base = self.source, c.row
        off, size, step = 0, c.rows, 0
        plan, trail = [], []
        sequence = [("all",) + p for p in c.pre] + [("fold", 2, None)]
        sequence += [("inner",) + p for p in c.post]
        for kind, mask, sel in sequence:
            landing = self.landings[step]
            if kind == "fold":
                own = self.rows(here, base, size)
                cp = self.copy(step, own, landing, mask)
            else:
                size //= 2
                mine = bit_of(self.b, sel)
                cp = self.copy(step, self.rows(here, base + (1 - mine) * size, size), landing, mask)
                own = self.rows(here, base + mine * size, size)
                off = off + mine * size
            trail.append((kind, mask, off, size))
            step += 1
            out = landing if step < len(sequence) else held(off, size)
            plan.append((kind, cp, (own, landing, out)))
            here, base = landing, 0
        for kind, mask, off, size in reversed(trail):
            cp = self.copy(step, held(off, size), held(off, size), mask)
            plan.append(("unfold" if kind == "fold" else kind, cp, None))
            step += 1
        self.plan = plan

    def begin(self, k):
        kind, cp, _ = self.plan[k]
        if kind == "all":
            cp.start()
        elif kind == "fold":
            pl.when(self.ended)(cp.start)
        else:
            pl.when(self.inner)(cp.start)

    def end(self, k):
        kind, cp, add = self.plan[k]

        def gather():
            if add is not None:
                own, landing, out = add
                out[...] = b16(f32(own[...]) + f32(landing[...]))

        if kind == "all":
            cp.wait()
            gather()
        elif kind in ("fold", "unfold"):
            sender, taker = (
                (self.ended, self.inner) if kind == "fold" else (self.inner, self.ended)
            )
            pl.when(sender)(cp.wait_send)

            @pl.when(taker)
            def _():
                cp.wait_recv()
                gather()
        else:

            @pl.when(self.inner)
            def _():
                cp.wait()
                gather()

    def advance(self, k):
        if k > 0:
            self.end(k - 1)
        if k < len(self.plan):
            self.begin(k)
        else:
            self.finish(self.c)


def tail_body(specs, chunks, ns, n_in, n_out, *refs):
    ins, outs = refs[:n_in], refs[n_in : n_in + n_out]
    scratch = list(refs[n_in + n_out :])
    send, recv, turn_send, turn_recv, out_sem = scratch[:5]
    stage, turned = scratch[5], scratch[6]
    rest = scratch[7:]
    shard, batch = lax.axis_index("shard"), lax.axis_index("batch")
    barrier = pltpu.get_barrier_semaphore()
    greeted = [{"batch": flip_bits(batch, m)} for m in specs["masks"]]
    greeted += [{"shard": flip_bits(shard, m)} for m in range(1, ns)]
    for device in greeted:
        pl.semaphore_signal(barrier, inc=1, device_id=device, device_id_type=MESH)
    pl.semaphore_wait(barrier, len(greeted))
    pending = {}
    used = [0]

    def put(value, target):
        slot = used[0] % 2
        used[0] += 1
        if slot in pending:
            pending.pop(slot).wait()
        rows, columns = value.shape
        place = stage.at[slot, pl.ds(0, rows), pl.ds(0, columns)]
        place[...] = f32(value)
        copy = pltpu.make_async_copy(place, target, out_sem.at[slot])
        copy.start()
        pending[slot] = copy

    late = []

    def finish(total):
        def go(c):
            kind, out, lead = specs["arrays"][c.source]
            if kind == "plain":
                target = outs[out] if lead is None else outs[out].at[lead]
                half = c.rows // specs["parts"]
                for p in range(specs["parts"]):
                    put(total[p * half : (p + 1) * half], target.at[pl.ds(c.row + p * half, half)])
                return
            columns = c.columns // ns
            copies = []
            for j in range(1, ns):
                peer = flip_bits(shard, j)
                copies.append(
                    pltpu.make_async_remote_copy(
                        src_ref=total.at[:, pl.ds(pl.multiple_of(peer * columns, 128), columns)],
                        dst_ref=turned.at[lead, shard, pl.ds(c.row, c.rows)],
                        send_sem=turn_send.at[c.at, j],
                        recv_sem=turn_recv.at[c.at, j],
                        device_id={"shard": peer},
                        device_id_type=MESH,
                    )
                )
                copies[-1].start()
            turned[lead, shard, c.row : c.row + c.rows] = total[
                :, pl.ds(pl.multiple_of(shard * columns, 128), columns)
            ]

            def after():
                for copy in copies:
                    copy.wait()
                height = specs["height"]
                for t in range(ns):
                    put(
                        turned[lead, t, c.row : c.row + c.rows],
                        outs[out].at[lead, pl.ds(t * height + c.row, c.rows)],
                    )

            late.append(after)

        return go

    movers, k = [], 0
    for c in chunks:
        total = rest[k]
        landings = rest[k + 1 : k + 1 + c.steps]
        k += 1 + c.steps
        movers.append(Mover(c, batch, ins[c.source], total, landings, (send, recv), finish(total)))
    lag = specs["lag"]
    depth = max(len(m.plan) for m in movers) + 1
    rounds = depth + (len(movers) - 1) // lag
    for r in range(rounds):
        waiting = late[:]
        late.clear()
        for i, m in enumerate(movers):
            k = r - i // lag
            if 0 <= k <= len(m.plan):
                m.advance(k)
        for after in waiting:
            after()
    for after in late:
        after()
    for slot in sorted(pending):
        pending[slot].wait()


def tail_sum(arrays, kinds, outputs, firsts, chunk_rows, ident):
    ns, nb = lax.axis_size("shard"), lax.axis_size("batch")
    chunks = []
    for i, a in enumerate(arrays):
        step = chunk_rows[i]
        for row in range(0, a.shape[0], step):
            chunks.append(Chunk(len(chunks), i, row, step, a.shape[1], firsts[len(chunks) % len(firsts)], nb))
    masks = [1, 2, 6] + [1 << k for k in range(3, nb.bit_length() - 1)]
    depth = max(2 * c.steps for c in chunks)
    specs = dict(arrays=kinds, masks=masks, parts=2, height=arrays[0].shape[0], lag=2)
    scratch = [
        pltpu.SemaphoreType.DMA((len(chunks), depth)),
        pltpu.SemaphoreType.DMA((len(chunks), depth)),
        pltpu.SemaphoreType.DMA((len(chunks), ns)),
        pltpu.SemaphoreType.DMA((len(chunks), ns)),
        pltpu.SemaphoreType.DMA((2,)),
        pltpu.VMEM((2, 512, 1024), jnp.float32),
        pltpu.VMEM((2, ns, arrays[0].shape[0], arrays[0].shape[1] // ns), jnp.bfloat16),
    ]
    for c in chunks:
        scratch.append(pltpu.VMEM((c.rows, c.columns), jnp.bfloat16))
        scratch += [pltpu.VMEM(shape, jnp.bfloat16) for shape in c.landings]
    return pl.pallas_call(
        functools.partial(tail_body, specs, chunks, ns, len(arrays), len(outputs)),
        out_shape=[jax.ShapeDtypeStruct(s, jnp.float32) for s in outputs],
        in_specs=[pl.BlockSpec(memory_space=pltpu.VMEM)] * len(arrays),
        out_specs=[pl.BlockSpec(memory_space=pl.ANY)] * len(outputs),
        scratch_shapes=scratch,
        compiler_params=pltpu.CompilerParams(
            collective_id=ident, has_side_effects=True, vmem_limit_bytes=60 << 20
        ),
        name="tail_sum",
    )(*arrays)


def attend_body(heads, size, scale, len_ref, u_ref, v_ref, k_ref, x_ref, p_ref, mix_ref, soft_ref):
    live = len_ref[pl.program_id(0)]
    length = u_ref.shape[0]
    for h in range(heads):
        cols = slice(h * size, (h + 1) * size)
        wide = dot_back(v_ref[:, cols], p_ref[:, cols])
        moved = pltpu.roll(wide, length + 1, 1, stride=1, stride_axis=0)[:, :length]
        raw = dot_back(u_ref[:, cols], k_ref[:, cols]) + moved
        keys = lax.broadcasted_iota(jnp.int32, (length, length), 1)
        scores = jnp.where(keys < live, raw * scale, -1e30)
        top = jnp.max(scores, axis=-1, keepdims=True)
        grown = jnp.exp(scores - top)
        soft = grown / jnp.sum(grown, axis=-1, keepdims=True)
        soft_ref[:, h * length : (h + 1) * length] = soft
        mix_ref[:, cols] = b16(dot_rows(b16(soft), x_ref[:, cols]))


def attend(lens, with_u, with_v, key, value, proj, length, heads):
    rows, width = with_u.shape
    size = width // heads
    items = rows // length
    block = pl.BlockSpec((length, width), lambda i, n: (i, 0))
    return pl.pallas_call(
        functools.partial(attend_body, heads, size, 1.0 / math.sqrt(size)),
        grid_spec=pltpu.PrefetchScalarGridSpec(
            num_scalar_prefetch=1,
            grid=(items,),
            in_specs=[block, block, block, block, pl.BlockSpec(proj.shape, lambda i, n: (0, 0))],
            out_specs=[block, pl.BlockSpec((length, heads * length), lambda i, n: (i, 0))],
        ),
        out_shape=[
            jax.ShapeDtypeStruct((rows, width), jnp.bfloat16),
            jax.ShapeDtypeStruct((rows, heads * length), jnp.float32),
        ],
        compiler_params=pltpu.CompilerParams(vmem_limit_bytes=32 << 20),
        name="attend",
        cost_estimate=pl.CostEstimate(
            flops=8 * rows * length * width, transcendentals=rows * length * heads, bytes_accessed=rows * width * 10
        ),
    )(lens, with_u, with_v, key, value, proj)


def attend_back_body(
    heads, size, scale, len_ref, g_ref, soft_ref, u_ref, v_ref, k_ref, x_ref, p_ref,
    dq_ref, dk_ref, dx_ref, dp_ref, sum_ref,
):
    item = pl.program_id(0)
    live = len_ref[item]
    length = u_ref.shape[0]
    at_row = lax.broadcasted_iota(jnp.int32, (length, length), 0)
    at_col = lax.broadcasted_iota(jnp.int32, (length, length), 1)
    flip = b16(f32(at_row + at_col == length - 1))
    for h in range(heads):
        cols = slice(h * size, (h + 1) * size)
        soft = soft_ref[:, h * length : (h + 1) * length]
        grad = g_ref[:, cols]
        grad_soft = dot_back(grad, x_ref[:, cols])
        dx_ref[:, cols] = b16(dot_over(b16(soft), grad))
        grad_scores = soft * (grad_soft - jnp.sum(grad_soft * soft, axis=-1, keepdims=True))
        raw = b16(jnp.where(at_col < live, grad_scores, 0.0) * scale)
        grad_u = dot_rows(raw, k_ref[:, cols])
        dk_ref[:, cols] = b16(dot_over(raw, u_ref[:, cols]))
        turned = dot_rows(flip, raw)
        wide = jnp.concatenate([turned, jnp.zeros_like(turned)], 1)
        wide = b16(pltpu.roll(wide, 0, 1, stride=1, stride_axis=0))
        grad_v_turned = dot_rows(wide, p_ref[:, cols])
        v_turned = b16(dot_rows(flip, v_ref[:, cols]))
        dp_ref[0, :, cols] = b16(dot_over(wide, v_turned))
        high = b16(grad_v_turned)
        low = b16(grad_v_turned - f32(high))
        grad_v = dot_rows(flip, high) + dot_rows(flip, low)
        dq_ref[:, cols] = b16(grad_u + grad_v)
        total = jnp.concatenate(
            [
                jnp.sum(grad_u, axis=0, keepdims=True),
                jnp.sum(grad_v_turned, axis=0, keepdims=True),
                jnp.zeros((6, size), jnp.float32),
            ],
            0,
        )
        sum_ref[0, :, cols] = total


def attend_back(lens, grad, soft, with_u, with_v, key, value, proj, length, heads):
    rows, width = with_u.shape
    size = width // heads
    items = rows // length
    block = pl.BlockSpec((length, width), lambda i, n: (i, 0))
    return pl.pallas_call(
        functools.partial(attend_back_body, heads, size, 1.0 / math.sqrt(size)),
        grid_spec=pltpu.PrefetchScalarGridSpec(
            num_scalar_prefetch=1,
            grid=(items,),
            in_specs=[
                block,
                pl.BlockSpec((length, heads * length), lambda i, n: (i, 0)),
                block, block, block, block,
                pl.BlockSpec(proj.shape, lambda i, n: (0, 0)),
            ],
            out_specs=[
                block, block, block,
                pl.BlockSpec((1,) + proj.shape, lambda i, n: (i, 0, 0)),
                pl.BlockSpec((1, 8, width), lambda i, n: (i, 0, 0)),
            ],
        ),
        out_shape=[
            jax.ShapeDtypeStruct((rows, width), jnp.bfloat16),
            jax.ShapeDtypeStruct((rows, width), jnp.bfloat16),
            jax.ShapeDtypeStruct((rows, width), jnp.bfloat16),
            jax.ShapeDtypeStruct((items,) + proj.shape, jnp.bfloat16),
            jax.ShapeDtypeStruct((items, 8, width), jnp.float32),
        ],
        compiler_params=pltpu.CompilerParams(vmem_limit_bytes=32 << 20),
        name="attend_back",
        cost_estimate=pl.CostEstimate(
            flops=26 * rows * length * width, transcendentals=0, bytes_accessed=rows * width * 30
        ),
    )(lens, grad, soft, with_u, with_v, key, value, proj)


def ffn_forward(rows_in, w_in, w_rows, b_in, gain_row, norm_bias):
    halves = gather_slots(b16(norm_rows(rows_in, gain_row, norm_bias)))
    saved, sums = [], []
    for hidden in halves:
        pre = dot_rows(hidden, w_in) + b_in
        active = b16(jax.nn.silu(pre))
        sums.append(dot_rows(active, w_rows))
        saved.append((hidden, pre, active))
    return scatter_slots(*sums), saved


def ffn_back(grad_own, rows_in, saved, w_in, w_rows, gain_row, norm_bias):
    halves = gather_slots(grad_own)
    grad_in = grad_out = grad_b = 0.0
    sums = []
    for grad, (hidden, pre, active) in zip(halves, saved):
        silu_back = jax.vjp(jax.nn.silu, pre)[1]
        grad_pre = b16(silu_back(dot_back(grad, w_rows))[0])
        sums.append(dot_back(grad_pre, w_in))
        grad_out = grad_out + dot_over(active, grad)
        grad_in = grad_in + dot_over(hidden, grad_pre)
        grad_b = grad_b + row_total(grad_pre)
    norm_back = jax.vjp(norm_rows, rows_in, gain_row, norm_bias)[1]
    grad_rows, grad_gain, grad_bias = norm_back(scatter_slots(*sums))
    return grad_rows, grad_gain, grad_bias, grad_in, grad_out, grad_b, row_total(grad_own)


def body(
    tokens, cotangent, lengths, ffn_in, ffn_out, ffn_bias, qkv_proj, pos_proj, out_proj,
    conv_in, conv_out, depthwise, norm_gains, biases,
):
    _, length, features = tokens.shape
    shard, batch = lax.axis_index("shard"), lax.axis_index("batch")
    ns, nb = lax.axis_size("shard"), lax.axis_size("batch")
    width = features // ns
    heads = HEADS // ns
    rows_in = tokens[0]
    grads_in = cotangent[0]

    own_length = jnp.broadcast_to(b16(f32(lengths))[:, None], (1, width))
    packed = jnp.concatenate([norm_gains, biases, depthwise, own_length], 0)
    packed = f32(lax.all_gather(packed, "shard", axis=1, tiled=True))
    gain_rows, bias_rows = packed[0:6], packed[6:22]
    kernel = packed[22:27]
    group_lengths = packed[27].reshape(ns, width)[:, 0].astype(jnp.int32)
    slot_lengths = jnp.stack(
        [lax.dynamic_index_in_dim(group_lengths, shard ^ j, 0, keepdims=False) for j in range(ns)]
    )
    own_biases = f32(biases)
    mask_col = f32(lax.broadcasted_iota(jnp.int32, (length, 1), 0) < lengths[0])
    w_rows = [to_rows(ffn_out[0], shard), to_rows(ffn_out[1], shard)]
    w_in = [ffn_in[0], ffn_in[1]]
    b_in = f32(ffn_bias)

    branch, saved_one = ffn_forward(rows_in, w_in[0], w_rows[0], b_in[0], gain_rows[0], bias_rows[0])
    rows_one = rows_in + 0.5 * (branch + bias_rows[1])

    table_b = b16(position_table(length, features))
    table_b = jnp.pad(table_b, [(0, 1), (0, 0)])
    proj_b = b16(dot_rows(table_b, pos_proj))
    w_out = lax.all_gather(out_proj, "shard", axis=1, tiled=True)
    wc_in = lax.all_gather(conv_in, "shard", axis=1, tiled=True)
    wc_out = lax.all_gather(conv_out, "shard", axis=1, tiled=True)

    halves = gather_slots(b16(norm_rows(rows_one, gain_rows[1], bias_rows[2])))
    saved_mix = []
    mixed = []
    for half, hidden in enumerate(halves):
        query = dot_rows(hidden, qkv_proj[0]) + own_biases[3]
        key = b16(dot_rows(hidden, qkv_proj[1]))
        value = b16(dot_rows(hidden, qkv_proj[2]) + own_biases[4])
        with_u = b16(query + own_biases[6])
        with_v = b16(query + own_biases[7])
        lens = slot_lengths[2 * half : 2 * half + 2]
        mix, soft = attend(lens, with_u, with_v, key, value, proj_b, length, heads)
        mixed += [mix[:length], mix[length:]]
        saved_mix.append((hidden, lens, soft, with_u, with_v, key, value))
    pieces = [mixed[0]] + [swap(mixed[j], "shard", j) for j in range(1, ns)]
    mixed_own = true_order(pieces, shard, 1)
    rows_two = rows_one + (dot_rows(mixed_own, w_out) + bias_rows[5])

    hidden_conv = b16(norm_rows(rows_two, gain_rows[2], bias_rows[8]))
    pre_conv = dot_rows(hidden_conv, wc_in) + jnp.concatenate([bias_rows[9], bias_rows[10]])
    conv_rows = gated_conv(pre_conv, mask_col, kernel)
    sums = jnp.concatenate(
        [
            jnp.sum(conv_rows * mask_col, axis=0).reshape(-1, 128),
            jnp.sum(conv_rows * conv_rows * mask_col, axis=0).reshape(-1, 128),
            jnp.broadcast_to(f32(lengths)[:, None], (8, 128)),
        ],
        0,
    )
    sums = stats_sum(sums, 1)
    lanes = features // 128
    frames = sums[2 * lanes, 0]
    row_mean = sums[:lanes].reshape(features) / frames
    inverse = lax.rsqrt(
        sums[lanes : 2 * lanes].reshape(features) / frames - row_mean * row_mean + epsilon
    )
    normed = (conv_rows - row_mean) * inverse * gain_rows[3] + bias_rows[11]
    active_conv = b16(jax.nn.silu(normed))
    rows_three = rows_two + (dot_rows(active_conv, wc_out) + bias_rows[12])

    branch, saved_two = ffn_forward(
        rows_three, w_in[1], w_rows[1], b_in[1], gain_rows[4], bias_rows[13]
    )
    rows_four = rows_three + 0.5 * (branch + bias_rows[14])
    result = norm_rows(rows_four, gain_rows[5], bias_rows[15]) * mask_col

    final_back = jax.vjp(norm_rows, rows_four, gain_rows[5], bias_rows[15])[1]
    stream, grad_gain_last, grad_bias_last = final_back(grads_in * mask_col)
    two = ffn_back(
        b16(0.5 * stream), rows_three, saved_two, w_in[1], w_rows[1], gain_rows[4], bias_rows[13]
    )
    stream = stream + two[0]

    grad_out = b16(stream)
    grad_conv_out = dot_over(active_conv, grad_out)
    grad_pw_out = row_total(grad_out)
    silu_back = jax.vjp(jax.nn.silu, normed)[1]
    grad_normed = silu_back(dot_back(grad_out, wc_out))[0]
    scaled = (conv_rows - row_mean) * inverse
    totals = stats_sum(
        jnp.concatenate(
            [
                jnp.sum(grad_normed, axis=0).reshape(-1, 128),
                jnp.sum(grad_normed * scaled, axis=0).reshape(-1, 128),
            ],
            0,
        ),
        2,
    )
    beta, gamma = totals[:lanes].reshape(features), totals[lanes:].reshape(features)
    gamma_row = gain_rows[3]
    grad_conv = inverse * (
        grad_normed * gamma_row
        - mask_col * (gamma_row * beta + scaled * (gamma_row * gamma)) / frames
    )
    tail_back = jax.vjp(lambda pre, taps: gated_conv(pre, mask_col, taps), pre_conv, kernel)[1]
    grad_pre_single, grad_kernel = tail_back(grad_conv)
    grad_pre = b16(grad_pre_single)
    grad_conv_in = dot_over(hidden_conv, grad_pre)
    grad_pw_in = row_total(grad_pre)
    conv_norm_back = jax.vjp(norm_rows, rows_two, gain_rows[2], bias_rows[8])[1]
    grad_rows, grad_gain_conv, grad_bias_conv = conv_norm_back(dot_back(grad_pre, wc_in))
    stream = stream + grad_rows

    def scattered(total):
        return lax.psum_scatter(b16(total), "shard", scatter_dimension=1, tiled=True)

    conv_out_part = scattered(grad_conv_out)
    conv_in_part = scattered(grad_conv_in)

    grad_out = b16(stream)
    grad_w_out = dot_over(mixed_own, grad_out)
    grad_b_out = row_total(grad_out)
    grad_mixed = b16(dot_back(grad_out, w_out))
    slots = []
    for j in range(ns):
        part = lax.dynamic_slice_in_dim(grad_mixed, (shard ^ j) * width, width, 1)
        slots.append(part if j == 0 else swap(part, "shard", j))
    grad_qkv = [0.0, 0.0, 0.0]
    grad_w_pos = 0.0
    grad_uv = 0.0
    grad_q_bias = grad_x_bias = 0.0
    sums = []
    for half, (hidden, lens, soft, with_u, with_v, key, value) in enumerate(saved_mix):
        grad = jnp.concatenate(slots[2 * half : 2 * half + 2], 0)
        dq, dk, dx, dp, duv = attend_back(
            lens, grad, soft, with_u, with_v, key, value, proj_b, length, heads
        )
        for at, part in enumerate((dq, dk, dx)):
            grad_qkv[at] = grad_qkv[at] + dot_over(hidden, part)
        for at in range(dp.shape[0]):
            grad_w_pos = grad_w_pos + dot_over(table_b, dp[at])
        grad_uv = grad_uv + jnp.sum(duv, axis=0)
        grad_q_bias = grad_q_bias + row_total(dq)
        grad_x_bias = grad_x_bias + row_total(dx)
        sums.append(
            dot_back(dq, qkv_proj[0]) + dot_back(dk, qkv_proj[1]) + dot_back(dx, qkv_proj[2])
        )
    norm_back = jax.vjp(norm_rows, rows_one, gain_rows[1], bias_rows[2])[1]
    grad_rows, grad_gain_mix, grad_bias_mix = norm_back(scatter_slots(*sums))
    stream = stream + grad_rows
    out_part = scattered(grad_w_out)

    one = ffn_back(
        b16(0.5 * stream), rows_in, saved_one, w_in[0], w_rows[0], gain_rows[0], bias_rows[0]
    )
    stream = stream + one[0]
    tall, deep = one[3].shape[0], one[3].shape[1]
    sums = tail_sum(
        [b16(two[4]), b16(two[3]), conv_in_part, conv_out_part]
        + [b16(g) for g in grad_qkv]
        + [b16(grad_w_pos), out_part, b16(one[4]), b16(one[3])],
        [("turn", 1, 1), ("plain", 0, 1), ("plain", 5, None), ("plain", 6, None)]
        + [("plain", 2, at) for at in range(3)]
        + [("plain", 3, None), ("plain", 4, None), ("turn", 1, 0), ("plain", 0, 0)],
        [
            (2, tall, deep), (2, ns * deep, width), (3, tall, width), (tall, width), (tall, width),
            conv_in_part.shape, conv_out_part.shape,
        ],
        ["near", "line"],
        [512, 512, tall, tall, tall, tall, tall, tall, tall, 512, 512],
        4,
    )

    wide = jnp.stack(
        [
            one[1], grad_gain_mix, grad_gain_conv, two[1], grad_gain_last,
            one[2], one[6], grad_bias_mix, grad_b_out, grad_bias_conv,
            grad_pw_in[:features], grad_pw_in[features:], grad_pw_out, two[2], two[6], grad_bias_last,
        ]
        + [grad_kernel[t] for t in range(grad_kernel.shape[0])]
        + [jnp.zeros((features,), jnp.float32)] * 3
    )
    wide = wide.reshape(wide.shape[0], ns, width).transpose(1, 0, 2)
    hidden_bias = jnp.stack([one[5], two[5]]).reshape(-1, width)
    local = jnp.concatenate(
        [grad_q_bias[None], grad_x_bias[None], grad_uv[0:2], hidden_bias], 0
    )
    local = jnp.pad(local, [(0, -local.shape[0] % 8), (0, 0)])
    vec = vector_sum(wide, local, 3)
    mine = lax.dynamic_slice_in_dim(jnp.stack([gamma, beta]), shard * width, width, 1)
    base = wide.shape[1]
    out_gains = jnp.stack([vec[0], vec[1], vec[2], mine[0], vec[3], vec[4]])
    out_biases = jnp.stack(
        [
            vec[5], vec[6], vec[7], vec[base], vec[base + 1], vec[8], vec[base + 2], vec[base + 3],
            vec[9], vec[10], vec[11], mine[1], vec[12], vec[13], vec[14], vec[15],
        ]
    )
    out_kernel = vec[16:21]
    out_hidden = vec[base + 4 : base + 4 + hidden_bias.shape[0]].reshape(2, -1)
    return (
        result[None],
        stream[None],
        sums[0],
        sums[1],
        out_hidden,
        sums[2],
        sums[3],
        sums[4],
        sums[5],
        sums[6],
        out_kernel,
        out_gains,
        out_biases,
    )


def solution(mesh):
    rows = P(("batch", "shard"), None, None)
    cube, flat = P(None, None, "shard"), P(None, "shard")
    return jax.shard_map(
        body,
        mesh=mesh,
        in_specs=(rows, rows, P(("batch", "shard")), cube, cube, flat, cube)
        + (flat,) * 7,
        out_specs=(rows, rows, cube, cube, flat, cube) + (flat,) * 7,
        check_vma=False,
    )
```

```python
import functools
import math

import jax
import jax.numpy as jnp
from jax import lax
from jax.experimental import pallas as pl
from jax.experimental.pallas import tpu as pltpu
from jax.sharding import PartitionSpec as P

HEADS = 8
MESH = pl.DeviceIdType.MESH
epsilon = 1e-05


def f32(a):
    return a.astype(jnp.float32)


def b16(a):
    return a.astype(jnp.bfloat16)


def norm_rows(values_in, gain_row, bias_row):
    row_mean = jnp.mean(values_in, axis=-1, keepdims=True)
    centered = values_in - row_mean
    spread = jnp.mean(centered * centered, axis=-1, keepdims=True)
    return centered * lax.rsqrt(spread + epsilon) * gain_row + bias_row


def dot_rows(a, b):
    return jnp.dot(a, b, preferred_element_type=jnp.float32)


def dot_back(a, b):
    return lax.dot_general(a, b, (((1,), (1,)), ((), ())), preferred_element_type=jnp.float32)


def dot_over(a, b):
    return lax.dot_general(a, b, (((0,), (0,)), ((), ())), preferred_element_type=jnp.float32)


def row_total(a):
    return jnp.sum(f32(a), axis=0)


def position_table(length, features):
    columns = jnp.arange(2 * length - 1, dtype=jnp.float32)
    offsets = length - 1.0 - columns
    freq_rates = jnp.exp(
        jnp.arange(features // 2, dtype=jnp.float32) * (-2.0 * math.log(10000.0) / features)
    )
    angles = offsets[:, None] * freq_rates[None, :]
    return jnp.concatenate([jnp.sin(angles), jnp.cos(angles)], axis=1)


def depth_conv(gated_rows, kernel):
    length = gated_rows.shape[0]
    half_width = (kernel.shape[0] - 1) // 2
    padded = jnp.pad(gated_rows, [(half_width, half_width), (0, 0)])
    summed = padded[0:length] * kernel[0]
    for tap_index in range(1, kernel.shape[0]):
        summed = summed + padded[tap_index : tap_index + length] * kernel[tap_index]
    return summed


def gated_conv(pre_act, mask_col, kernel):
    features = pre_act.shape[1] // 2
    gated_rows = pre_act[:, :features] * jax.nn.sigmoid(pre_act[:, features:]) * mask_col
    return depth_conv(gated_rows, kernel)


def swap(x, axis, mask):
    n = lax.axis_size(axis)
    return lax.ppermute(x, axis, [(i, i ^ mask) for i in range(n)])


def gather_slots(own):
    far = swap(own, "shard", 2)
    near = swap(own, "shard", 1)
    diag = swap(far, "shard", 1)
    return (jnp.concatenate([own, near], 0), jnp.concatenate([far, diag], 0))


def scatter_slots(near_half, far_half):
    rows = near_half.shape[0] // 2
    got_far = swap(b16(far_half[rows:]), "shard", 1)
    sent = b16(far_half[:rows] + f32(got_far))
    got_near = swap(b16(near_half[rows:]), "shard", 1)
    crossed = swap(sent, "shard", 2)
    return near_half[:rows] + f32(got_near) + f32(crossed)


def true_order(pieces, me, axis):
    stacked = jnp.stack(pieces, 0)
    return jnp.concatenate(
        [lax.dynamic_index_in_dim(stacked, me ^ t, 0, keepdims=False) for t in range(len(pieces))],
        axis,
    )


def to_rows(cols, me):
    n = lax.axis_size("shard")
    rows = cols.shape[0] // n
    pieces = []
    for j in range(n):
        part = lax.dynamic_slice_in_dim(cols, (me ^ j) * rows, rows, 0)
        pieces.append(part if j == 0 else swap(part, "shard", j))
    return true_order(pieces, me, 1)


def peers_of(axis, index, count):
    return [{axis: lax.rem(index + j, count)} for j in range(1, count)]


def exchange(axis, index, count, source, landing, send_sem, recv_sem):
    copies = []
    for j in range(1, count):
        peer = lax.rem(index + j, count)
        copies.append(
            pltpu.make_async_remote_copy(
                src_ref=source,
                dst_ref=landing.at[index],
                send_sem=send_sem.at[j],
                recv_sem=recv_sem.at[j],
                device_id={axis: peer},
                device_id_type=MESH,
            )
        )
    return copies


def greet(sizes, places):
    barrier = pltpu.get_barrier_semaphore()
    total = 0
    for axis in ("shard", "batch"):
        for device in peers_of(axis, places[axis], sizes[axis]):
            pl.semaphore_signal(barrier, inc=1, device_id=device, device_id_type=MESH)
            total += 1
    pl.semaphore_wait(barrier, total)


def sum_slots(ref, count):
    total = ref[0]
    for j in range(1, count):
        total = total + ref[j]
    return total


def stats_body(ns, nb, x_ref, o_ref, land_s, mid, land_b, ss, rs, sb, rb):
    s, b = lax.axis_index("shard"), lax.axis_index("batch")
    greet({"shard": ns, "batch": nb}, {"shard": s, "batch": b})
    first = exchange("shard", s, ns, x_ref, land_s, ss, rs)
    for copy in first:
        copy.start()
    land_s[s] = x_ref[...]
    for copy in first:
        copy.wait()
    mid[...] = sum_slots(land_s, ns)
    second = exchange("batch", b, nb, mid, land_b, sb, rb)
    for copy in second:
        copy.start()
    land_b[b] = mid[...]
    for copy in second:
        copy.wait()
    o_ref[...] = sum_slots(land_b, nb)


def stats_sum(x, ident):
    ns, nb = lax.axis_size("shard"), lax.axis_size("batch")
    shape = x.shape
    return pl.pallas_call(
        functools.partial(stats_body, ns, nb),
        out_shape=jax.ShapeDtypeStruct(shape, jnp.float32),
        in_specs=[pl.BlockSpec(memory_space=pltpu.VMEM)],
        out_specs=pl.BlockSpec(memory_space=pltpu.VMEM),
        scratch_shapes=[
            pltpu.VMEM((ns,) + shape, jnp.float32),
            pltpu.VMEM(shape, jnp.float32),
            pltpu.VMEM((nb,) + shape, jnp.float32),
            pltpu.SemaphoreType.DMA((ns,)),
            pltpu.SemaphoreType.DMA((ns,)),
            pltpu.SemaphoreType.DMA((nb,)),
            pltpu.SemaphoreType.DMA((nb,)),
        ],
        compiler_params=pltpu.CompilerParams(collective_id=ident, has_side_effects=True),
        name="stats_sum_%d" % ident,
    )(x)


def vector_body(ns, nb, w_ref, l_ref, o_ref, land_s, mid, land_b, ss, rs, sb, rb):
    s, b = lax.axis_index("shard"), lax.axis_index("batch")
    greet({"shard": ns, "batch": nb}, {"shard": s, "batch": b})
    rows = w_ref.shape[1]
    copies = []
    for j in range(1, ns):
        peer = lax.rem(s + j, ns)
        copies.append(
            pltpu.make_async_remote_copy(
                src_ref=w_ref.at[peer],
                dst_ref=land_s.at[s],
                send_sem=ss.at[j],
                recv_sem=rs.at[j],
                device_id={"shard": peer},
                device_id_type=MESH,
            )
        )
    for copy in copies:
        copy.start()
    land_s[s] = w_ref[s]
    for copy in copies:
        copy.wait()
    mid[0:rows] = sum_slots(land_s, ns)
    mid[rows:] = l_ref[...]
    second = exchange("batch", b, nb, mid, land_b, sb, rb)
    for copy in second:
        copy.start()
    land_b[b] = mid[...]
    for copy in second:
        copy.wait()
    o_ref[...] = sum_slots(land_b, nb)


def vector_sum(wide, local, ident):
    ns, nb = lax.axis_size("shard"), lax.axis_size("batch")
    _, r, c = wide.shape
    rows = r + local.shape[0]
    return pl.pallas_call(
        functools.partial(vector_body, ns, nb),
        out_shape=jax.ShapeDtypeStruct((rows, c), jnp.float32),
        in_specs=[pl.BlockSpec(memory_space=pltpu.VMEM)] * 2,
        out_specs=pl.BlockSpec(memory_space=pltpu.VMEM),
        scratch_shapes=[
            pltpu.VMEM((ns, r, c), jnp.float32),
            pltpu.VMEM((rows, c), jnp.float32),
            pltpu.VMEM((nb, rows, c), jnp.float32),
            pltpu.SemaphoreType.DMA((ns,)),
            pltpu.SemaphoreType.DMA((ns,)),
            pltpu.SemaphoreType.DMA((nb,)),
            pltpu.SemaphoreType.DMA((nb,)),
        ],
        compiler_params=pltpu.CompilerParams(collective_id=ident, has_side_effects=True),
        name="vector_sum",
    )(wide, local)


class Chunk:
    def __init__(self, at, source, row, rows, columns, first, count):
        self.at, self.source, self.row, self.rows, self.columns = at, source, row, rows, columns
        extra = [(1 << k, k) for k in range(3, count.bit_length() - 1)]
        line = (6, 1)
        if first == "near":
            self.pre, self.post = [(1, 0)], [line] + extra
        else:
            self.pre, self.post = [], [line, (1, 0)] + extra
        size, self.landings = rows, []
        for _ in self.pre:
            size //= 2
            self.landings.append((size, columns))
        self.landings.append((size, columns))
        for _ in self.post:
            size //= 2
            self.landings.append((size, columns))
        self.steps = len(self.landings)


def bit_of(value, k):
    return lax.rem(lax.div(value, 1 << k), 2)


def flip_bits(value, mask):
    out = value
    k = 0
    while (1 << k) <= mask:
        if mask & (1 << k):
            out = out + (1 - 2 * bit_of(value, k)) * (1 << k)
        k += 1
    return out


class Mover:
    def __init__(self, chunk, batch, source, total, landings, sems, finish):
        self.c, self.b = chunk, batch
        self.source, self.total, self.landings, self.sems = source, total, landings, sems
        lo, hi = bit_of(batch, 1), bit_of(batch, 2)
        self.inner = lo != hi
        self.ended = lo == hi
        self.finish = finish
        self.stages = []
        self.build()

    def copy(self, at, src, dst, mask):
        send, recv = self.sems
        return pltpu.make_async_remote_copy(
            src_ref=src,
            dst_ref=dst,
            send_sem=send.at[self.c.at, at],
            recv_sem=recv.at[self.c.at, at],
            device_id={"batch": flip_bits(self.b, mask)},
            device_id_type=MESH,
        )

    def rows(self, ref, start, size):
        start = start if isinstance(start, int) else pl.multiple_of(start, 16)
        return ref.at[pl.ds(start, size)]

    def build(self):
        c = self.c
        held = lambda off, size: self.rows(self.total, off, size)
        here, base = self.source, c.row
        off, size, step = 0, c.rows, 0
        plan, trail = [], []
        sequence = [("all",) + p for p in c.pre] + [("fold", 2, None)]
        sequence += [("inner",) + p for p in c.post]
        for kind, mask, sel in sequence:
            landing = self.landings[step]
            if kind == "fold":
                own = self.rows(here, base, size)
                cp = self.copy(step, own, landing, mask)
            else:
                size //= 2
                mine = bit_of(self.b, sel)
                cp = self.copy(step, self.rows(here, base + (1 - mine) * size, size), landing, mask)
                own = self.rows(here, base + mine * size, size)
                off = off + mine * size
            trail.append((kind, mask, off, size))
            step += 1
            out = landing if step < len(sequence) else held(off, size)
            plan.append((kind, cp, (own, landing, out)))
            here, base = landing, 0
        for kind, mask, off, size in reversed(trail):
            cp = self.copy(step, held(off, size), held(off, size), mask)
            plan.append(("unfold" if kind == "fold" else kind, cp, None))
            step += 1
        self.plan = plan

    def begin(self, k):
        kind, cp, _ = self.plan[k]
        if kind == "all":
            cp.start()
        elif kind == "fold":
            pl.when(self.ended)(cp.start)
        else:
            pl.when(self.inner)(cp.start)

    def end(self, k):
        kind, cp, add = self.plan[k]

        def gather():
            if add is not None:
                own, landing, out = add
                out[...] = b16(f32(own[...]) + f32(landing[...]))

        if kind == "all":
            cp.wait()
            gather()
        elif kind in ("fold", "unfold"):
            sender, taker = (
                (self.ended, self.inner) if kind == "fold" else (self.inner, self.ended)
            )
            pl.when(sender)(cp.wait_send)

            @pl.when(taker)
            def _():
                cp.wait_recv()
                gather()
        else:

            @pl.when(self.inner)
            def _():
                cp.wait()
                gather()

    def advance(self, k):
        if k > 0:
            self.end(k - 1)
        if k < len(self.plan):
            self.begin(k)
        else:
            self.finish(self.c)


def tail_body(specs, chunks, ns, n_in, n_out, *refs):
    ins, outs = refs[:n_in], refs[n_in : n_in + n_out]
    scratch = list(refs[n_in + n_out :])
    send, recv, turn_send, turn_recv, out_sem = scratch[:5]
    stage, turned = scratch[5], scratch[6]
    rest = scratch[7:]
    shard, batch = lax.axis_index("shard"), lax.axis_index("batch")
    barrier = pltpu.get_barrier_semaphore()
    greeted = [{"batch": flip_bits(batch, m)} for m in specs["masks"]]
    greeted += [{"shard": flip_bits(shard, m)} for m in range(1, ns)]
    for device in greeted:
        pl.semaphore_signal(barrier, inc=1, device_id=device, device_id_type=MESH)
    pl.semaphore_wait(barrier, len(greeted))
    pending = {}
    used = [0]

    def put(value, target):
        slot = used[0] % 2
        used[0] += 1
        if slot in pending:
            pending.pop(slot).wait()
        rows, columns = value.shape
        place = stage.at[slot, pl.ds(0, rows), pl.ds(0, columns)]
        place[...] = f32(value)
        copy = pltpu.make_async_copy(place, target, out_sem.at[slot])
        copy.start()
        pending[slot] = copy

    late = []

    def finish(total):
        def go(c):
            kind, out, lead = specs["arrays"][c.source]
            if kind == "plain":
                target = outs[out] if lead is None else outs[out].at[lead]
                half = c.rows // specs["parts"]
                for p in range(specs["parts"]):
                    put(total[p * half : (p + 1) * half], target.at[pl.ds(c.row + p * half, half)])
                return
            columns = c.columns // ns
            copies = []
            for j in range(1, ns):
                peer = flip_bits(shard, j)
                copies.append(
                    pltpu.make_async_remote_copy(
                        src_ref=total.at[:, pl.ds(pl.multiple_of(peer * columns, 128), columns)],
                        dst_ref=turned.at[lead, shard, pl.ds(c.row, c.rows)],
                        send_sem=turn_send.at[c.at, j],
                        recv_sem=turn_recv.at[c.at, j],
                        device_id={"shard": peer},
                        device_id_type=MESH,
                    )
                )
                copies[-1].start()
            turned[lead, shard, c.row : c.row + c.rows] = total[
                :, pl.ds(pl.multiple_of(shard * columns, 128), columns)
            ]

            def after():
                for copy in copies:
                    copy.wait()
                height = specs["height"]
                for t in range(ns):
                    put(
                        turned[lead, t, c.row : c.row + c.rows],
                        outs[out].at[lead, pl.ds(t * height + c.row, c.rows)],
                    )

            late.append(after)

        return go

    movers, k = [], 0
    for c in chunks:
        total = rest[k]
        landings = rest[k + 1 : k + 1 + c.steps]
        k += 1 + c.steps
        movers.append(Mover(c, batch, ins[c.source], total, landings, (send, recv), finish(total)))
    lag = specs["lag"]
    depth = max(len(m.plan) for m in movers) + 1
    rounds = depth + (len(movers) - 1) // lag
    for r in range(rounds):
        waiting = late[:]
        late.clear()
        for i, m in enumerate(movers):
            k = r - i // lag
            if 0 <= k <= len(m.plan):
                m.advance(k)
        for after in waiting:
            after()
    for after in late:
        after()
    for slot in sorted(pending):
        pending[slot].wait()


def tail_sum(arrays, kinds, outputs, firsts, chunk_rows, ident):
    ns, nb = lax.axis_size("shard"), lax.axis_size("batch")
    chunks = []
    for i, a in enumerate(arrays):
        step = chunk_rows[i]
        for row in range(0, a.shape[0], step):
            chunks.append(Chunk(len(chunks), i, row, step, a.shape[1], firsts[len(chunks) % len(firsts)], nb))
    masks = [1, 2, 6] + [1 << k for k in range(3, nb.bit_length() - 1)]
    depth = max(2 * c.steps for c in chunks)
    specs = dict(arrays=kinds, masks=masks, parts=2, height=arrays[0].shape[0], lag=2)
    scratch = [
        pltpu.SemaphoreType.DMA((len(chunks), depth)),
        pltpu.SemaphoreType.DMA((len(chunks), depth)),
        pltpu.SemaphoreType.DMA((len(chunks), ns)),
        pltpu.SemaphoreType.DMA((len(chunks), ns)),
        pltpu.SemaphoreType.DMA((2,)),
        pltpu.VMEM((2, 512, 1024), jnp.float32),
        pltpu.VMEM((2, ns, arrays[0].shape[0], arrays[0].shape[1] // ns), jnp.bfloat16),
    ]
    for c in chunks:
        scratch.append(pltpu.VMEM((c.rows, c.columns), jnp.bfloat16))
        scratch += [pltpu.VMEM(shape, jnp.bfloat16) for shape in c.landings]
    return pl.pallas_call(
        functools.partial(tail_body, specs, chunks, ns, len(arrays), len(outputs)),
        out_shape=[jax.ShapeDtypeStruct(s, jnp.float32) for s in outputs],
        in_specs=[pl.BlockSpec(memory_space=pltpu.VMEM)] * len(arrays),
        out_specs=[pl.BlockSpec(memory_space=pl.ANY)] * len(outputs),
        scratch_shapes=scratch,
        compiler_params=pltpu.CompilerParams(
            collective_id=ident, has_side_effects=True, vmem_limit_bytes=60 << 20
        ),
        name="tail_sum",
    )(*arrays)


def attend_body(heads, size, scale, len_ref, u_ref, v_ref, k_ref, x_ref, p_ref, mix_ref, soft_ref):
    live = len_ref[pl.program_id(0)]
    length = u_ref.shape[0]
    for h in range(heads):
        cols = slice(h * size, (h + 1) * size)
        wide = dot_back(v_ref[:, cols], p_ref[:, cols])
        moved = pltpu.roll(wide, length + 1, 1, stride=1, stride_axis=0)[:, :length]
        raw = dot_back(u_ref[:, cols], k_ref[:, cols]) + moved
        keys = lax.broadcasted_iota(jnp.int32, (length, length), 1)
        scores = jnp.where(keys < live, raw * scale, -1e30)
        top = jnp.max(scores, axis=-1, keepdims=True)
        grown = jnp.exp(scores - top)
        soft = grown / jnp.sum(grown, axis=-1, keepdims=True)
        soft_ref[:, h * length : (h + 1) * length] = soft
        mix_ref[:, cols] = b16(dot_rows(b16(soft), x_ref[:, cols]))


def attend(lens, with_u, with_v, key, value, proj, length, heads):
    rows, width = with_u.shape
    size = width // heads
    items = rows // length
    block = pl.BlockSpec((length, width), lambda i, n: (i, 0))
    return pl.pallas_call(
        functools.partial(attend_body, heads, size, 1.0 / math.sqrt(size)),
        grid_spec=pltpu.PrefetchScalarGridSpec(
            num_scalar_prefetch=1,
            grid=(items,),
            in_specs=[block, block, block, block, pl.BlockSpec(proj.shape, lambda i, n: (0, 0))],
            out_specs=[block, pl.BlockSpec((length, heads * length), lambda i, n: (i, 0))],
        ),
        out_shape=[
            jax.ShapeDtypeStruct((rows, width), jnp.bfloat16),
            jax.ShapeDtypeStruct((rows, heads * length), jnp.float32),
        ],
        compiler_params=pltpu.CompilerParams(vmem_limit_bytes=32 << 20),
        name="attend",
        cost_estimate=pl.CostEstimate(
            flops=8 * rows * length * width, transcendentals=rows * length * heads, bytes_accessed=rows * width * 10
        ),
    )(lens, with_u, with_v, key, value, proj)


def attend_back_body(
    heads, size, scale, len_ref, g_ref, soft_ref, u_ref, v_ref, k_ref, x_ref, p_ref,
    dq_ref, dk_ref, dx_ref, dp_ref, sum_ref,
):
    item = pl.program_id(0)
    live = len_ref[item]
    length = u_ref.shape[0]
    at_row = lax.broadcasted_iota(jnp.int32, (length, length), 0)
    at_col = lax.broadcasted_iota(jnp.int32, (length, length), 1)
    flip = b16(f32(at_row + at_col == length - 1))
    for h in range(heads):
        cols = slice(h * size, (h + 1) * size)
        soft = soft_ref[:, h * length : (h + 1) * length]
        grad = g_ref[:, cols]
        grad_soft = dot_back(grad, x_ref[:, cols])
        dx_ref[:, cols] = b16(dot_over(b16(soft), grad))
        grad_scores = soft * (grad_soft - jnp.sum(grad_soft * soft, axis=-1, keepdims=True))
        raw = b16(jnp.where(at_col < live, grad_scores, 0.0) * scale)
        grad_u = dot_rows(raw, k_ref[:, cols])
        dk_ref[:, cols] = b16(dot_over(raw, u_ref[:, cols]))
        turned = dot_rows(flip, raw)
        wide = jnp.concatenate([turned, jnp.zeros_like(turned)], 1)
        wide = b16(pltpu.roll(wide, 0, 1, stride=1, stride_axis=0))
        grad_v_turned = dot_rows(wide, p_ref[:, cols])
        v_turned = b16(dot_rows(flip, v_ref[:, cols]))
        dp_ref[0, :, cols] = b16(dot_over(wide, v_turned))
        high = b16(grad_v_turned)
        low = b16(grad_v_turned - f32(high))
        grad_v = dot_rows(flip, high) + dot_rows(flip, low)
        dq_ref[:, cols] = b16(grad_u + grad_v)
        total = jnp.concatenate(
            [
                jnp.sum(grad_u, axis=0, keepdims=True),
                jnp.sum(grad_v_turned, axis=0, keepdims=True),
                jnp.zeros((6, size), jnp.float32),
            ],
            0,
        )
        sum_ref[0, :, cols] = total


def attend_back(lens, grad, soft, with_u, with_v, key, value, proj, length, heads):
    rows, width = with_u.shape
    size = width // heads
    items = rows // length
    block = pl.BlockSpec((length, width), lambda i, n: (i, 0))
    return pl.pallas_call(
        functools.partial(attend_back_body, heads, size, 1.0 / math.sqrt(size)),
        grid_spec=pltpu.PrefetchScalarGridSpec(
            num_scalar_prefetch=1,
            grid=(items,),
            in_specs=[
                block,
                pl.BlockSpec((length, heads * length), lambda i, n: (i, 0)),
                block, block, block, block,
                pl.BlockSpec(proj.shape, lambda i, n: (0, 0)),
            ],
            out_specs=[
                block, block, block,
                pl.BlockSpec((1,) + proj.shape, lambda i, n: (i, 0, 0)),
                pl.BlockSpec((1, 8, width), lambda i, n: (i, 0, 0)),
            ],
        ),
        out_shape=[
            jax.ShapeDtypeStruct((rows, width), jnp.bfloat16),
            jax.ShapeDtypeStruct((rows, width), jnp.bfloat16),
            jax.ShapeDtypeStruct((rows, width), jnp.bfloat16),
            jax.ShapeDtypeStruct((items,) + proj.shape, jnp.bfloat16),
            jax.ShapeDtypeStruct((items, 8, width), jnp.float32),
        ],
        compiler_params=pltpu.CompilerParams(vmem_limit_bytes=32 << 20),
        name="attend_back",
        cost_estimate=pl.CostEstimate(
            flops=26 * rows * length * width, transcendentals=0, bytes_accessed=rows * width * 30
        ),
    )(lens, grad, soft, with_u, with_v, key, value, proj)


class Links:
    def __init__(self, send, recv):
        self.send, self.recv, self.count = send, recv, 0
        s = lax.axis_index("shard")
        self.shard = s
        self.near = {"shard": flip_bits(s, 1)}
        self.far = {"shard": flip_bits(s, 2)}
        self.across = {"shard": flip_bits(s, 3)}

    def greet(self, devices):
        barrier = pltpu.get_barrier_semaphore()
        for device in devices:
            pl.semaphore_signal(barrier, inc=1, device_id=device, device_id_type=MESH)
        pl.semaphore_wait(barrier, len(devices))

    def go(self, src, dst, device):
        at = self.count
        self.count += 1
        copy = pltpu.make_async_remote_copy(
            src_ref=src, dst_ref=dst, send_sem=self.send.at[at], recv_sem=self.recv.at[at],
            device_id=device, device_id_type=MESH,
        )
        copy.start()
        return copy


def gather_work_scatter(links, x, work, part, send, land, cross, land_cross):
    half = x.shape[1] // 2
    out = [
        links.go(x.at[0, pl.ds(h * half, half)], x.at[2 + h, pl.ds(0, half)], links.far)
        for h in range(2)
    ]
    near = links.go(x.at[0], x.at[1], links.near)

    def keep(cols, value):
        part[0, :, cols] = value

    work(0, keep)
    near.wait()

    def give(cols, value):
        send[0, :, cols] = b16(value[:half])
        send[1, :, cols] = b16(value[half:])

    work(1, give)
    last = [links.go(send.at[pl.ds(0, 2)], land.at[pl.ds(0, 2)], links.near)]
    for h in range(2):
        out[h].wait()
        on = links.go(x.at[2 + h, pl.ds(0, half)], x.at[2 + h, pl.ds(half, half)], links.near)
        on.wait()

        def split(cols, value, h=h):
            part[1, h * half : (h + 1) * half, cols] = value[:half]
            send[2 + h, :, cols] = b16(value[half:])

        work(2 + h, split)
        back = links.go(send.at[2 + h], land.at[2 + h], links.near)
        back.wait()
        cross[h] = b16(part[1, h * half : (h + 1) * half] + f32(land[2 + h]))
        last.append(links.go(cross.at[h], land_cross.at[h], links.far))

    def settle():
        for copy in last:
            copy.wait()

    def total(h):
        rows = slice(h * half, (h + 1) * half)
        return part[0, rows] + f32(land[h]) + f32(land_cross[h])

    return settle, total


def gws_scratch(rows, columns):
    half = rows // 2
    return [
        pltpu.VMEM((2, rows, columns), jnp.float32),
        pltpu.VMEM((4, half, columns), jnp.bfloat16),
        pltpu.VMEM((4, half, columns), jnp.bfloat16),
        pltpu.VMEM((2, half, columns), jnp.bfloat16),
        pltpu.VMEM((2, half, columns), jnp.bfloat16),
        pltpu.SemaphoreType.DMA((16,)),
        pltpu.SemaphoreType.DMA((16,)),
    ]


def tiles(total, size):
    def over(body):
        pl.loop(0, total // size)(
            lambda n: body(pl.ds(pl.multiple_of(n * size, size), size))
        )

    return over


def ffn_forward_body(
    rows_ref, vec_ref, b_ref, w_in, w_rows, out_ref, hid, act, slope,
    part, send, land, cross, land_cross, send_sem, recv_sem,
):
    links = Links(send_sem, recv_sem)
    links.greet([links.near, links.far])
    vec = vec_ref[...]
    hid[0] = b16(norm_rows(rows_ref[...], vec[0:1], vec[1:2]))
    columns = hid.shape[2]

    def work(block, emit):
        @tiles(w_in.shape[1], 512)
        def _(cols):
            pre = dot_rows(hid[block], w_in[:, cols]) + b_ref[:, cols]
            gate = jax.nn.sigmoid(pre)
            act[block, :, cols] = b16(pre * gate)
            slope[block, :, cols] = b16(gate * (1.0 + pre * (1.0 - gate)))

        @tiles(columns, 512)
        def _(cols):
            emit(cols, dot_rows(act[block], w_rows[:, cols]))

    settle, total = gather_work_scatter(links, hid, work, part, send, land, cross, land_cross)
    settle()
    half = rows_ref.shape[0] // 2
    for h in range(2):
        rows = slice(h * half, (h + 1) * half)
        out_ref[rows] = rows_ref[rows] + 0.5 * (total(h) + vec[2:3])


VMEM_SPEC = pl.BlockSpec(memory_space=pltpu.VMEM)


def ffn_forward(rows_in, w_in, w_rows, b_in, gain_row, norm_bias, out_bias, ident):
    rows, features = rows_in.shape
    hidden = w_in.shape[1]
    vec = jnp.concatenate(
        [gain_row[None], norm_bias[None], out_bias[None], jnp.zeros((5, features), jnp.float32)], 0
    )
    shape = lambda c: jax.ShapeDtypeStruct((4, rows, c), jnp.bfloat16)
    out, hid, act, slope = pl.pallas_call(
        ffn_forward_body,
        out_shape=[
            jax.ShapeDtypeStruct((rows, features), jnp.float32),
            shape(features), shape(hidden), shape(hidden),
        ],
        in_specs=[VMEM_SPEC] * 5,
        out_specs=[VMEM_SPEC] * 4,
        scratch_shapes=gws_scratch(rows, features),
        compiler_params=pltpu.CompilerParams(
            collective_id=ident, has_side_effects=True, vmem_limit_bytes=40 << 20
        ),
        name="ffn_forward_%d" % ident,
    )(rows_in, vec, b_in[None], w_in, w_rows)
    return out, (hid, act, slope)


def norm_parts(rows):
    row_mean = jnp.mean(rows, axis=-1, keepdims=True)
    centered = rows - row_mean
    inverse = lax.rsqrt(jnp.mean(centered * centered, axis=-1, keepdims=True) + epsilon)
    return centered * inverse, inverse


def norm_slope(grad, scaled, inverse, gain):
    inner = grad * gain
    return inverse * (
        inner
        - jnp.mean(inner, axis=-1, keepdims=True)
        - scaled * jnp.mean(inner * scaled, axis=-1, keepdims=True)
    )


def ffn_back_body(
    stream_ref, rows_ref, vec_ref, hid, act, slope, w_in, w_rows,
    out_ref, gw_in, gw_out, sums_ref,
    grad, inner, part, send, land, cross, land_cross, send_sem, recv_sem,
):
    links = Links(send_sem, recv_sem)
    links.greet([links.near, links.far])
    grad[0] = b16(0.5 * stream_ref[...])
    columns = grad.shape[2]
    hidden = w_in.shape[1]

    def work(block, emit):
        @tiles(hidden, 512)
        def _(cols):
            wide = dot_back(grad[block], w_rows[cols, :])
            inner[block, :, cols] = b16(wide * f32(slope[block, :, cols]))

        @tiles(columns, 512)
        def _(cols):
            emit(cols, dot_back(inner[block], w_in[cols, :]))

    settle, total = gather_work_scatter(links, grad, work, part, send, land, cross, land_cross)
    rows = stream_ref.shape[0]
    flat = lambda ref: ref[...].reshape(4 * rows, ref.shape[2])

    @tiles(hidden, 256)
    def _(cols):
        left = act[:, :, cols].reshape(4 * rows, 256)
        gw_out[cols, :] = b16(dot_over(left, flat(grad)))

    @tiles(hidden, 256)
    def _(cols):
        right = inner[:, :, cols].reshape(4 * rows, 256)
        gw_in[:, cols] = b16(dot_over(flat(hid), right))
        sums_ref[3:4, cols] = jnp.sum(f32(right), axis=0, keepdims=True)

    settle()
    vec = vec_ref[...]
    sums_ref[0:3, :] = jnp.zeros((3, columns), jnp.float32)
    sums_ref[4:8, :] = jnp.zeros((4, columns), jnp.float32)
    sums_ref[2:3, :] = jnp.sum(f32(grad[0]), axis=0, keepdims=True)
    half = rows // 2
    for h in range(2):
        at = slice(h * half, (h + 1) * half)
        scaled, inverse = norm_parts(rows_ref[at])
        given = total(h)
        out_ref[at] = stream_ref[at] + norm_slope(given, scaled, inverse, vec[0:1])
        sums_ref[0:1, :] += jnp.sum(given * scaled, axis=0, keepdims=True)
        sums_ref[1:2, :] += jnp.sum(given, axis=0, keepdims=True)


def ffn_back(stream, rows_in, saved, w_in, w_rows, gain_row, ident):
    rows, features = rows_in.shape
    hidden = w_in.shape[1]
    hid, act, slope = saved
    vec = jnp.broadcast_to(gain_row[None], (8, features))
    return pl.pallas_call(
        ffn_back_body,
        out_shape=[
            jax.ShapeDtypeStruct((rows, features), jnp.float32),
            jax.ShapeDtypeStruct((features, hidden), jnp.bfloat16),
            jax.ShapeDtypeStruct((hidden, features), jnp.bfloat16),
            jax.ShapeDtypeStruct((8, features), jnp.float32),
        ],
        in_specs=[VMEM_SPEC] * 8,
        out_specs=[VMEM_SPEC] * 4,
        scratch_shapes=[
            pltpu.VMEM((4, rows, features), jnp.bfloat16),
            pltpu.VMEM((4, rows, hidden), jnp.bfloat16),
        ]
        + gws_scratch(rows, features),
        compiler_params=pltpu.CompilerParams(
            collective_id=ident, has_side_effects=True, vmem_limit_bytes=48 << 20
        ),
        name="ffn_back_%d" % ident,
    )(stream, rows_in, vec, hid, act, slope, w_in, w_rows)


def body(
    tokens, cotangent, lengths, ffn_in, ffn_out, ffn_bias, qkv_proj, pos_proj, out_proj,
    conv_in, conv_out, depthwise, norm_gains, biases,
):
    _, length, features = tokens.shape
    shard, batch = lax.axis_index("shard"), lax.axis_index("batch")
    ns, nb = lax.axis_size("shard"), lax.axis_size("batch")
    width = features // ns
    heads = HEADS // ns
    rows_in = tokens[0]
    grads_in = cotangent[0]

    own_length = jnp.broadcast_to(b16(f32(lengths))[:, None], (1, width))
    packed = jnp.concatenate([norm_gains, biases, depthwise, own_length], 0)
    packed = f32(lax.all_gather(packed, "shard", axis=1, tiled=True))
    gain_rows, bias_rows = packed[0:6], packed[6:22]
    kernel = packed[22:27]
    group_lengths = packed[27].reshape(ns, width)[:, 0].astype(jnp.int32)
    slot_lengths = jnp.stack(
        [lax.dynamic_index_in_dim(group_lengths, shard ^ j, 0, keepdims=False) for j in range(ns)]
    )
    own_biases = f32(biases)
    mask_col = f32(lax.broadcasted_iota(jnp.int32, (length, 1), 0) < lengths[0])
    w_rows = [to_rows(ffn_out[0], shard), to_rows(ffn_out[1], shard)]
    w_in = [ffn_in[0], ffn_in[1]]
    b_in = f32(ffn_bias)

    rows_one, saved_one = ffn_forward(
        rows_in, w_in[0], w_rows[0], b_in[0], gain_rows[0], bias_rows[0], bias_rows[1], 5
    )

    table_b = b16(position_table(length, features))
    table_b = jnp.pad(table_b, [(0, 1), (0, 0)])
    proj_b = b16(dot_rows(table_b, pos_proj))
    w_out = lax.all_gather(out_proj, "shard", axis=1, tiled=True)
    wc_in = lax.all_gather(conv_in, "shard", axis=1, tiled=True)
    wc_out = lax.all_gather(conv_out, "shard", axis=1, tiled=True)

    halves = gather_slots(b16(norm_rows(rows_one, gain_rows[1], bias_rows[2])))
    saved_mix = []
    mixed = []
    for half, hidden in enumerate(halves):
        query = dot_rows(hidden, qkv_proj[0]) + own_biases[3]
        key = b16(dot_rows(hidden, qkv_proj[1]))
        value = b16(dot_rows(hidden, qkv_proj[2]) + own_biases[4])
        with_u = b16(query + own_biases[6])
        with_v = b16(query + own_biases[7])
        lens = slot_lengths[2 * half : 2 * half + 2]
        mix, soft = attend(lens, with_u, with_v, key, value, proj_b, length, heads)
        mixed += [mix[:length], mix[length:]]
        saved_mix.append((hidden, lens, soft, with_u, with_v, key, value))
    pieces = [mixed[0]] + [swap(mixed[j], "shard", j) for j in range(1, ns)]
    mixed_own = true_order(pieces, shard, 1)
    rows_two = rows_one + (dot_rows(mixed_own, w_out) + bias_rows[5])

    hidden_conv = b16(norm_rows(rows_two, gain_rows[2], bias_rows[8]))
    pre_conv = dot_rows(hidden_conv, wc_in) + jnp.concatenate([bias_rows[9], bias_rows[10]])
    conv_rows = gated_conv(pre_conv, mask_col, kernel)
    sums = jnp.concatenate(
        [
            jnp.sum(conv_rows * mask_col, axis=0).reshape(-1, 128),
            jnp.sum(conv_rows * conv_rows * mask_col, axis=0).reshape(-1, 128),
            jnp.broadcast_to(f32(lengths)[:, None], (8, 128)),
        ],
        0,
    )
    sums = stats_sum(sums, 1)
    lanes = features // 128
    frames = sums[2 * lanes, 0]
    row_mean = sums[:lanes].reshape(features) / frames
    inverse = lax.rsqrt(
        sums[lanes : 2 * lanes].reshape(features) / frames - row_mean * row_mean + epsilon
    )
    normed = (conv_rows - row_mean) * inverse * gain_rows[3] + bias_rows[11]
    active_conv = b16(jax.nn.silu(normed))
    rows_three = rows_two + (dot_rows(active_conv, wc_out) + bias_rows[12])

    rows_four, saved_two = ffn_forward(
        rows_three, w_in[1], w_rows[1], b_in[1], gain_rows[4], bias_rows[13], bias_rows[14], 6
    )
    result = norm_rows(rows_four, gain_rows[5], bias_rows[15]) * mask_col

    final_back = jax.vjp(norm_rows, rows_four, gain_rows[5], bias_rows[15])[1]
    stream, grad_gain_last, grad_bias_last = final_back(grads_in * mask_col)
    stream, two_in, two_out, two_sums = ffn_back(
        stream, rows_three, saved_two, w_in[1], w_rows[1], gain_rows[4], 7
    )

    grad_out = b16(stream)
    grad_conv_out = dot_over(active_conv, grad_out)
    grad_pw_out = row_total(grad_out)
    silu_back = jax.vjp(jax.nn.silu, normed)[1]
    grad_normed = silu_back(dot_back(grad_out, wc_out))[0]
    scaled = (conv_rows - row_mean) * inverse
    totals = stats_sum(
        jnp.concatenate(
            [
                jnp.sum(grad_normed, axis=0).reshape(-1, 128),
                jnp.sum(grad_normed * scaled, axis=0).reshape(-1, 128),
            ],
            0,
        ),
        2,
    )
    beta, gamma = totals[:lanes].reshape(features), totals[lanes:].reshape(features)
    gamma_row = gain_rows[3]
    grad_conv = inverse * (
        grad_normed * gamma_row
        - mask_col * (gamma_row * beta + scaled * (gamma_row * gamma)) / frames
    )
    tail_back = jax.vjp(lambda pre, taps: gated_conv(pre, mask_col, taps), pre_conv, kernel)[1]
    grad_pre_single, grad_kernel = tail_back(grad_conv)
    grad_pre = b16(grad_pre_single)
    grad_conv_in = dot_over(hidden_conv, grad_pre)
    grad_pw_in = row_total(grad_pre)
    conv_norm_back = jax.vjp(norm_rows, rows_two, gain_rows[2], bias_rows[8])[1]
    grad_rows, grad_gain_conv, grad_bias_conv = conv_norm_back(dot_back(grad_pre, wc_in))
    stream = stream + grad_rows

    def scattered(total):
        return lax.psum_scatter(b16(total), "shard", scatter_dimension=1, tiled=True)

    conv_out_part = scattered(grad_conv_out)
    conv_in_part = scattered(grad_conv_in)

    grad_out = b16(stream)
    grad_w_out = dot_over(mixed_own, grad_out)
    grad_b_out = row_total(grad_out)
    grad_mixed = b16(dot_back(grad_out, w_out))
    slots = []
    for j in range(ns):
        part = lax.dynamic_slice_in_dim(grad_mixed, (shard ^ j) * width, width, 1)
        slots.append(part if j == 0 else swap(part, "shard", j))
    grad_qkv = [0.0, 0.0, 0.0]
    grad_w_pos = 0.0
    grad_uv = 0.0
    grad_q_bias = grad_x_bias = 0.0
    sums = []
    for half, (hidden, lens, soft, with_u, with_v, key, value) in enumerate(saved_mix):
        grad = jnp.concatenate(slots[2 * half : 2 * half + 2], 0)
        dq, dk, dx, dp, duv = attend_back(
            lens, grad, soft, with_u, with_v, key, value, proj_b, length, heads
        )
        for at, part in enumerate((dq, dk, dx)):
            grad_qkv[at] = grad_qkv[at] + dot_over(hidden, part)
        for at in range(dp.shape[0]):
            grad_w_pos = grad_w_pos + dot_over(table_b, dp[at])
        grad_uv = grad_uv + jnp.sum(duv, axis=0)
        grad_q_bias = grad_q_bias + row_total(dq)
        grad_x_bias = grad_x_bias + row_total(dx)
        sums.append(
            dot_back(dq, qkv_proj[0]) + dot_back(dk, qkv_proj[1]) + dot_back(dx, qkv_proj[2])
        )
    norm_back = jax.vjp(norm_rows, rows_one, gain_rows[1], bias_rows[2])[1]
    grad_rows, grad_gain_mix, grad_bias_mix = norm_back(scatter_slots(*sums))
    stream = stream + grad_rows
    out_part = scattered(grad_w_out)

    stream, one_in, one_out, one_sums = ffn_back(
        stream, rows_in, saved_one, w_in[0], w_rows[0], gain_rows[0], 8
    )
    tall, deep = one_in.shape
    sums = tail_sum(
        [two_out, two_in, conv_in_part, conv_out_part]
        + [b16(g) for g in grad_qkv]
        + [b16(grad_w_pos), out_part, one_out, one_in],
        [("turn", 1, 1), ("plain", 0, 1), ("plain", 5, None), ("plain", 6, None)]
        + [("plain", 2, at) for at in range(3)]
        + [("plain", 3, None), ("plain", 4, None), ("turn", 1, 0), ("plain", 0, 0)],
        [
            (2, tall, deep), (2, ns * deep, width), (3, tall, width), (tall, width), (tall, width),
            conv_in_part.shape, conv_out_part.shape,
        ],
        ["near", "line"],
        [512, 512, tall, tall, tall, tall, tall, tall, tall, 512, 512],
        4,
    )

    wide = jnp.stack(
        [
            one_sums[0], grad_gain_mix, grad_gain_conv, two_sums[0], grad_gain_last,
            one_sums[1], one_sums[2], grad_bias_mix, grad_b_out, grad_bias_conv,
            grad_pw_in[:features], grad_pw_in[features:], grad_pw_out, two_sums[1], two_sums[2],
            grad_bias_last,
        ]
        + [grad_kernel[t] for t in range(grad_kernel.shape[0])]
        + [jnp.zeros((features,), jnp.float32)] * 3
    )
    wide = wide.reshape(wide.shape[0], ns, width).transpose(1, 0, 2)
    hidden_bias = jnp.stack([one_sums[3], two_sums[3]]).reshape(-1, width)
    local = jnp.concatenate(
        [grad_q_bias[None], grad_x_bias[None], grad_uv[0:2], hidden_bias], 0
    )
    local = jnp.pad(local, [(0, -local.shape[0] % 8), (0, 0)])
    vec = vector_sum(wide, local, 3)
    mine = lax.dynamic_slice_in_dim(jnp.stack([gamma, beta]), shard * width, width, 1)
    base = wide.shape[1]
    out_gains = jnp.stack([vec[0], vec[1], vec[2], mine[0], vec[3], vec[4]])
    out_biases = jnp.stack(
        [
            vec[5], vec[6], vec[7], vec[base], vec[base + 1], vec[8], vec[base + 2], vec[base + 3],
            vec[9], vec[10], vec[11], mine[1], vec[12], vec[13], vec[14], vec[15],
        ]
    )
    out_kernel = vec[16:21]
    out_hidden = vec[base + 4 : base + 4 + hidden_bias.shape[0]].reshape(2, -1)
    return (
        result[None],
        stream[None],
        sums[0],
        sums[1],
        out_hidden,
        sums[2],
        sums[3],
        sums[4],
        sums[5],
        sums[6],
        out_kernel,
        out_gains,
        out_biases,
    )


def solution(mesh):
    rows = P(("batch", "shard"), None, None)
    cube, flat = P(None, None, "shard"), P(None, "shard")
    return jax.shard_map(
        body,
        mesh=mesh,
        in_specs=(rows, rows, P(("batch", "shard")), cube, cube, flat, cube)
        + (flat,) * 7,
        out_specs=(rows, rows, cube, cube, flat, cube) + (flat,) * 7,
        check_vma=False,
    )
```

```python
import functools
import math

import jax
import jax.numpy as jnp
from jax import lax
from jax.experimental import pallas as pl
from jax.experimental.pallas import tpu as pltpu
from jax.sharding import PartitionSpec as P

HEADS = 8
MESH = pl.DeviceIdType.MESH
VMEM_SPEC = pl.BlockSpec(memory_space=pltpu.VMEM)
epsilon = 1e-05


def f32(a):
    return a.astype(jnp.float32)


def b16(a):
    return a.astype(jnp.bfloat16)


def norm_rows(values_in, gain_row, bias_row):
    row_mean = jnp.mean(values_in, axis=-1, keepdims=True)
    centered = values_in - row_mean
    spread = jnp.mean(centered * centered, axis=-1, keepdims=True)
    return centered * lax.rsqrt(spread + epsilon) * gain_row + bias_row


def dot_rows(a, b):
    return jnp.dot(a, b, preferred_element_type=jnp.float32)


def dot_back(a, b):
    return lax.dot_general(a, b, (((1,), (1,)), ((), ())), preferred_element_type=jnp.float32)


def dot_over(a, b):
    return lax.dot_general(a, b, (((0,), (0,)), ((), ())), preferred_element_type=jnp.float32)


def exchange(axis, index, count, source, landing, send_sem, recv_sem):
    copies = []
    for j in range(1, count):
        peer = lax.rem(index + j, count)
        copies.append(
            pltpu.make_async_remote_copy(
                src_ref=source,
                dst_ref=landing.at[index],
                send_sem=send_sem.at[j],
                recv_sem=recv_sem.at[j],
                device_id={axis: peer},
                device_id_type=MESH,
            )
        )
    return copies


def sum_slots(ref, count):
    total = ref[0]
    for j in range(1, count):
        total = total + ref[j]
    return total


class Chunk:
    def __init__(self, at, source, row, rows, columns, first, count):
        self.at, self.source, self.row, self.rows, self.columns = at, source, row, rows, columns
        extra = [(1 << k, k) for k in range(3, count.bit_length() - 1)]
        line = (6, 1)
        if first == "near":
            self.pre, self.post = [(1, 0)], [line] + extra
        else:
            self.pre, self.post = [], [line, (1, 0)] + extra
        size, self.landings = rows, []
        for _ in self.pre:
            size //= 2
            self.landings.append((size, columns))
        self.landings.append((size, columns))
        for _ in self.post:
            size //= 2
            self.landings.append((size, columns))
        self.steps = len(self.landings)


def bit_of(value, k):
    return lax.rem(lax.div(value, 1 << k), 2)


def flip_bits(value, mask):
    out = value
    k = 0
    while (1 << k) <= mask:
        if mask & (1 << k):
            out = out + (1 - 2 * bit_of(value, k)) * (1 << k)
        k += 1
    return out


class Mover:
    def __init__(self, chunk, batch, source, base, held, landings, sems, finish, early):
        self.c, self.b = chunk, batch
        self.source, self.base, self.held, self.landings, self.sems = source, base, held, landings, sems
        lo, hi = bit_of(batch, 1), bit_of(batch, 2)
        self.inner = lo != hi
        self.ended = lo == hi
        self.finish, self.early = finish, early
        self.build()

    def copy(self, at, src, dst, mask):
        send, recv = self.sems
        return pltpu.make_async_remote_copy(
            src_ref=src,
            dst_ref=dst,
            send_sem=send.at[self.c.at, at],
            recv_sem=recv.at[self.c.at, at],
            device_id={"batch": flip_bits(self.b, mask)},
            device_id_type=MESH,
        )

    def build(self):
        c = self.c
        held = self.held
        here, base = self.source, self.base
        off, size, step = 0, c.rows, 0
        plan, trail = [], []
        sequence = [("all",) + p for p in c.pre] + [("fold", 2, None)]
        sequence += [("inner",) + p for p in c.post]
        for kind, mask, sel in sequence:
            landing = self.landings[step]
            if kind == "fold":
                own = row_view(here, base, size)
                cp = self.copy(step, own, landing, mask)
            else:
                size //= 2
                mine = bit_of(self.b, sel)
                cp = self.copy(step, row_view(here, base + (1 - mine) * size, size), landing, mask)
                own = row_view(here, base + mine * size, size)
                off = off + mine * size
            trail.append((kind, mask, off, size))
            step += 1
            out = landing if step < len(sequence) else held(off, size)
            plan.append((kind, cp, (own, landing, out)))
            here, base = landing, 0
        for kind, mask, off, size in reversed(trail):
            cp = self.copy(step, held(off, size), held(off, size), mask)
            plan.append(("unfold" if kind == "fold" else kind, cp, None))
            step += 1
        self.plan = plan
        self.depth = len(plan) + len(self.early)

    def begin(self, k):
        kind, cp, _ = self.plan[k]
        if kind == "all":
            cp.start()
        elif kind == "fold":
            pl.when(self.ended)(cp.start)
        else:
            pl.when(self.inner)(cp.start)

    def end(self, k):
        kind, cp, add = self.plan[k]

        def gather():
            if add is not None:
                own, landing, out = add
                out[...] = b16(f32(own[...]) + f32(landing[...]))

        if kind == "all":
            cp.wait()
            gather()
        elif kind in ("fold", "unfold"):
            sender, taker = (
                (self.ended, self.inner) if kind == "fold" else (self.inner, self.ended)
            )
            pl.when(sender)(cp.wait_send)

            @pl.when(taker)
            def _():
                cp.wait_recv()
                gather()
        else:

            @pl.when(self.inner)
            def _():
                cp.wait()
                gather()

    def advance(self, k):
        if k < len(self.early):
            self.early[k]()
            return
        k -= len(self.early)
        if k > 0:
            self.end(k - 1)
        elif self.early:
            self.settle_early()
        if k < len(self.plan):
            self.begin(k)
        else:
            self.finish(self.c)


def row_view(ref, start, size):
    start = start if isinstance(start, int) else pl.multiple_of(start, 16 if size % 16 == 0 else 8)
    return ref.at[pl.ds(start, size)]


def column_block(index, columns):
    return pl.ds(pl.multiple_of(index * columns, 128), columns)


class Rider:
    def __init__(self, batch, send, recv, first):
        self.b, self.send, self.recv, self.at = batch, send, recv, first

    def go(self, src, dst, bit):
        copy = pltpu.make_async_remote_copy(
            src_ref=src, dst_ref=dst, send_sem=self.send.at[self.at], recv_sem=self.recv.at[self.at],
            device_id={"batch": flip_bits(self.b, 1 << bit)}, device_id_type=MESH,
        )
        self.at += 1
        copy.start()
        return copy

    def halve(self, source, landing, bit):
        half = landing.shape[0]
        mine = bit_of(self.b, bit)
        copy = self.go(row_view(source, (1 - mine) * half, half), landing, bit)

        def end():
            copy.wait()
            own = row_view(source, mine * half, half)
            landing[...] = b16(f32(own[...]) + f32(landing[...]))

        return end

    def double(self, source, target, bit):
        half = source.shape[0]
        there = row_view(target, bit_of(self.b, bit) * half, half)
        copy = self.go(source, there, bit)
        there[...] = source[...]
        return copy.wait

    def chain(self, refs, bits, move):
        ends, stages = [], []
        for i, bit in enumerate(bits):

            def stage(i=i, bit=bit):
                if ends:
                    ends.pop()()
                ends.append(move(refs[i], refs[i + 1], bit))

            stages.append(stage)
        stages.append(lambda: ends.pop()())
        return stages


def ride_orders(count):
    bits = list(range(count.bit_length() - 1))
    return bits, [1, 0] + bits[2:]


def tail_body(specs, chunks, ns, nb, n_in, n_out, *refs):
    ins, refs = refs[:n_in], refs[n_in:]
    ridden, refs = refs[:2], refs[2:]
    (one_sums, mix_sums, two_sums, conv_sums, own_sums), refs = refs[:5], refs[5:]
    outs, refs = refs[:n_out], refs[n_out:]
    (o_gains, o_biases, o_taps, o_hidden), refs = refs[:4], refs[4:]
    send, recv, turn_send, turn_recv, pre_send, pre_recv, ride_send, ride_recv = refs[:8]
    ss, rs, sb, rb, wide, land_s, mid, land_b, ride_fin = refs[8:17]
    rest = list(refs[17:])
    shard, batch = lax.axis_index("shard"), lax.axis_index("batch")
    barrier = pltpu.get_barrier_semaphore()
    greeted = [{"batch": lax.rem(batch + j, nb)} for j in range(1, nb)]
    greeted += [{"shard": flip_bits(shard, m)} for m in range(1, ns)]
    for device in greeted:
        pl.semaphore_signal(barrier, inc=1, device_id=device, device_id_type=MESH)
    width = own_sums.shape[1]
    for t in range(ns):
        cols = slice(t * width, (t + 1) * width)
        wide[t, 0:3, :] = one_sums[0:3, cols]
        wide[t, 3:6, :] = mix_sums[0:3, cols]
        wide[t, 6:9, :] = two_sums[0:3, cols]
        wide[t, 9:14, :] = conv_sums[0:5, cols]
        wide[t, 14:19, :] = conv_sums[8:13, cols]
        wide[t, 19:21, :] = two_sums[4:6, cols]
        wide[t, 21:24, :] = jnp.zeros((3, width), jnp.float32)
    pl.semaphore_wait(barrier, len(greeted))

    vector_copies = []
    for j in range(1, ns):
        peer = lax.rem(shard + j, ns)
        copy = pltpu.make_async_remote_copy(
            src_ref=wide.at[peer], dst_ref=land_s.at[shard], send_sem=ss.at[j], recv_sem=rs.at[j],
            device_id={"shard": peer}, device_id_type=MESH,
        )
        copy.start()
        vector_copies.append(copy)
    land_s[shard] = wide[shard]

    def vectors_on():
        for copy in vector_copies:
            copy.wait()
        mid[0:24, :] = sum_slots(land_s, ns)
        mid[24:28, :] = own_sums[0:4, :]
        per = one_sums.shape[1] // width
        for t in range(per):
            cols = slice(t * width, (t + 1) * width)
            mid[28 + t : 29 + t, :] = one_sums[3:4, cols]
            mid[28 + per + t : 29 + per + t, :] = two_sums[3:4, cols]
        mid[28 + 2 * per :, :] = jnp.zeros((mid.shape[0] - 28 - 2 * per, width), jnp.float32)
        vector_copies[:] = exchange("batch", batch, nb, mid, land_b, sb, rb)
        for copy in vector_copies:
            copy.start()
        land_b[batch] = mid[...]

    def vectors_out():
        for copy in vector_copies:
            copy.wait()
        vec = sum_slots(land_b, nb)
        row = lambda k: vec[k : k + 1]
        mine = conv_sums[5:7, column_block(shard, width)]
        gains = [row(0), row(3), row(9), mine[0:1], row(6), row(19)]
        order = [1, 2, 4, 24, 25, 5, 26, 27, 10, 11, 12, None, 13, 7, 8, 20]
        for k, value in enumerate(gains):
            o_gains[k : k + 1, :] = value
        for k, at in enumerate(order):
            o_biases[k : k + 1, :] = mine[1:2] if at is None else row(at)
        o_taps[...] = vec[14:19]
        per = o_hidden.shape[1] // width
        for k in range(2):
            for t in range(per):
                at = 28 + k * per + t
                o_hidden[k : k + 1, t * width : (t + 1) * width] = row(at)

    late = []

    def turn(c_at, total, row, rows, out, lead):
        target = outs[out] if lead is None else outs[out].at[lead]
        columns = target.shape[1]
        height = target.shape[0] // ns
        there = row_view(target, shard * height + row, rows)
        copies = []
        for j in range(1, ns):
            peer = flip_bits(shard, j)
            copy = pltpu.make_async_remote_copy(
                src_ref=total.at[:, column_block(peer, columns)],
                dst_ref=there,
                send_sem=turn_send.at[c_at, j],
                recv_sem=turn_recv.at[c_at, j],
                device_id={"shard": peer},
                device_id_type=MESH,
            )
            copy.start()
            copies.append(copy)
        there[...] = total[:, column_block(shard, columns)]
        late.extend(copies)

    rides = []
    orders = ride_orders(nb)
    plain_target = outs[0].at[1]
    rider_a = Rider(batch, ride_send, ride_recv, 0)
    rider_b = Rider(batch, ride_send, ride_recv, 1)
    end_a = rider_a.double(ridden[0], plain_target, orders[0][0])
    end_b = rider_b.double(ridden[1], ride_fin, orders[1][0])

    movers = []
    for c in chunks:
        kind, out, lead = specs["arrays"][c.source]
        source, base, early, settle = ins[c.source], c.row, [], None
        if kind == "gather":
            near_land, far_land = rest.pop(0), rest.pop(0)
            whole, columns, rows = ins[c.source], c.columns, pl.ds(c.row, c.rows)
            far = flip_bits(shard, 2)
            state = {}

            def pre(at, src, dst, mask, c=c):
                copy = pltpu.make_async_remote_copy(
                    src_ref=src, dst_ref=dst, send_sem=pre_send.at[c.at, at], recv_sem=pre_recv.at[c.at, at],
                    device_id={"shard": flip_bits(shard, mask)}, device_id_type=MESH,
                )
                copy.start()
                return copy

            def first(near_land=near_land, whole=whole, columns=columns, rows=rows, state=state, pre=pre):
                state["n"] = [
                    pre(i, whole.at[rows, column_block(flip_bits(shard, m), columns)], near_land.at[i], 1)
                    for i, m in enumerate((1, 3))
                ]

            def second(
                near_land=near_land, far_land=far_land, whole=whole, columns=columns, rows=rows, state=state,
                pre=pre, far=far,
            ):
                for copy in state["n"]:
                    copy.wait()
                near_land[1] = b16(f32(near_land[1]) + f32(whole[rows, column_block(far, columns)]))
                state["f"] = pre(2, near_land.at[1], far_land, 2)

            def settle(
                near_land=near_land, far_land=far_land, whole=whole, columns=columns, rows=rows, state=state,
            ):
                state["f"].wait()
                far_land[...] = b16(
                    f32(far_land[...]) + f32(near_land[0]) + f32(whole[rows, column_block(shard, columns)])
                )

            early = [first, second]
            source, base = far_land, 0
        if kind == "turn":
            total = rest.pop(0)
            held = lambda off, size, total=total: row_view(total, off, size)

            def finish(c, total=total, out=out, lead=lead):
                turn(c.at, total, c.row, c.rows, out, lead)
        else:
            target = outs[out] if lead is None else outs[out].at[lead]
            held = lambda off, size, target=target, c=c: row_view(target, c.row + off, size)

            def finish(c):
                pass
        landings = [rest.pop(0) for _ in range(c.steps)]
        m = Mover(c, batch, source, base, held, landings, (send, recv), finish, early)
        m.settle_early = settle
        movers.append(m)
    starts, lag = [], specs["lag"]
    for i, m in enumerate(movers):
        starts.append(max(0, i // lag - len(m.early)))
    rounds = max(s + m.depth + 1 for s, m in zip(starts, movers))
    for r in range(rounds):
        if r == 1:
            vectors_on()
        if r == 2:
            end_b()
            turn(len(chunks), ride_fin, 0, ride_fin.shape[0], 1, 1)
        if r == 3:
            vectors_out()
            end_a()
        for s, m in zip(starts, movers):
            if 0 <= r - s <= m.depth:
                m.advance(r - s)
    for copy in late:
        copy.wait()


def tail_sum(arrays, ridden, sums, kinds, outputs, firsts, chunk_rows, hidden, ident):
    ns, nb = lax.axis_size("shard"), lax.axis_size("batch")
    low, full = jnp.bfloat16, jnp.float32
    chunks = []
    for i, a in enumerate(arrays):
        step = chunk_rows[i]
        columns = a.shape[1] // ns if kinds[i][0] == "gather" else a.shape[1]
        for row in range(0, a.shape[0], step):
            chunks.append(Chunk(len(chunks), i, row, step, columns, firsts[len(chunks) % len(firsts)], nb))
    depth = max(2 * c.steps for c in chunks)
    specs = dict(arrays=kinds, lag=2)
    width = sums[-1].shape[1]
    per = hidden // width
    small = -(-(28 + 2 * per) // 8) * 8
    dma = pltpu.SemaphoreType.DMA
    n = len(chunks)
    scratch = [
        dma((n, depth)), dma((n, depth)), dma((n + 1, ns)), dma((n + 1, ns)), dma((n, 3)), dma((n, 3)),
        dma((2,)), dma((2,)), dma((ns,)), dma((ns,)), dma((nb,)), dma((nb,)),
        pltpu.VMEM((ns, 24, width), full), pltpu.VMEM((ns, 24, width), full),
        pltpu.VMEM((small, width), full), pltpu.VMEM((nb, small, width), full),
        pltpu.VMEM((2 * ridden[1].shape[0], ridden[1].shape[1]), low),
    ]
    for c in chunks:
        if kinds[c.source][0] == "gather":
            scratch += [pltpu.VMEM((2, c.rows, c.columns), low), pltpu.VMEM((c.rows, c.columns), low)]
        if kinds[c.source][0] == "turn":
            scratch.append(pltpu.VMEM((c.rows, c.columns), low))
        scratch += [pltpu.VMEM(shape, low) for shape in c.landings]
    shape = jax.ShapeDtypeStruct
    shapes = [shape(s, low) for s in outputs]
    shapes += [shape((6, width), full), shape((16, width), full), shape((5, width), full), shape((2, hidden), full)]
    operands = list(arrays) + list(ridden) + list(sums)
    return pl.pallas_call(
        functools.partial(tail_body, specs, chunks, ns, nb, len(arrays), len(outputs)),
        out_shape=shapes,
        in_specs=[VMEM_SPEC] * len(operands),
        out_specs=[VMEM_SPEC] * len(shapes),
        scratch_shapes=scratch,
        compiler_params=pltpu.CompilerParams(
            collective_id=ident, has_side_effects=True, vmem_limit_bytes=62 << 20
        ),
        name="tail_sum",
    )(*operands)


class Links:
    def __init__(self, send, recv):
        self.send, self.recv, self.count = send, recv, 0
        s = lax.axis_index("shard")
        self.shard = s
        self.near = {"shard": flip_bits(s, 1)}
        self.far = {"shard": flip_bits(s, 2)}
        self.across = {"shard": flip_bits(s, 3)}

    def greet(self, devices):
        barrier = pltpu.get_barrier_semaphore()
        for device in devices:
            pl.semaphore_signal(barrier, inc=1, device_id=device, device_id_type=MESH)
        pl.semaphore_wait(barrier, len(devices))

    def go(self, src, dst, device):
        at = self.count
        self.count += 1
        copy = pltpu.make_async_remote_copy(
            src_ref=src, dst_ref=dst, send_sem=self.send.at[at], recv_sem=self.recv.at[at],
            device_id=device, device_id_type=MESH,
        )
        copy.start()
        return copy


def gather_work_scatter(links, x, work, part, send, land, cross, land_cross, tick=None):
    half = x.shape[1] // 2
    out = [
        links.go(x.at[0, pl.ds(h * half, half)], x.at[2 + h, pl.ds(0, half)], links.far)
        for h in range(2)
    ]
    near = links.go(x.at[0], x.at[1], links.near)

    def keep(cols, value):
        part[0, :, cols] = value

    work(0, keep)
    near.wait()

    def give(cols, value):
        send[0, :, cols] = b16(value[:half])
        send[1, :, cols] = b16(value[half:])

    work(1, give)
    last = [links.go(send.at[pl.ds(0, 2)], land.at[pl.ds(0, 2)], links.near)]
    if tick is not None:
        tick()
    for h in range(2):
        out[h].wait()
        on = links.go(x.at[2 + h, pl.ds(0, half)], x.at[2 + h, pl.ds(half, half)], links.near)
        on.wait()

        def split(cols, value, h=h):
            part[1, h * half : (h + 1) * half, cols] = value[:half]
            send[2 + h, :, cols] = b16(value[half:])

        work(2 + h, split)
        back = links.go(send.at[2 + h], land.at[2 + h], links.near)
        back.wait()
        cross[h] = b16(part[1, h * half : (h + 1) * half] + f32(land[2 + h]))
        last.append(links.go(cross.at[h], land_cross.at[h], links.far))

    def settle():
        for copy in last:
            copy.wait()

    def total(h):
        rows = slice(h * half, (h + 1) * half)
        return part[0, rows] + f32(land[h]) + f32(land_cross[h])

    return settle, total


def gws_scratch(rows, columns):
    half = rows // 2
    return [
        pltpu.VMEM((2, rows, columns), jnp.float32),
        pltpu.VMEM((4, half, columns), jnp.bfloat16),
        pltpu.VMEM((4, half, columns), jnp.bfloat16),
        pltpu.VMEM((2, half, columns), jnp.bfloat16),
        pltpu.VMEM((2, half, columns), jnp.bfloat16),
        pltpu.SemaphoreType.DMA((16,)),
        pltpu.SemaphoreType.DMA((16,)),
    ]


def tiles(total, size):
    def over(body):
        pl.loop(0, total // size)(
            lambda n: body(pl.ds(pl.multiple_of(n * size, size), size))
        )

    return over


def ffn_forward_body(
    which, at_rows, rows_ref, pack, b_ref, w_rows, ffn_in, out_ref, hid, act, slope,
    part, send, land, cross, land_cross, send_sem, recv_sem, w_in, local_sem,
):
    links = Links(send_sem, recv_sem)
    load = pltpu.make_async_copy(ffn_in.at[which], w_in, local_sem)
    load.start()
    links.greet([links.near, links.far])
    hid[0] = b16(
        norm_rows(rows_ref[...], vector_row(pack, at_rows[0]), vector_row(pack, at_rows[1]))
    )
    load.wait()
    columns = hid.shape[2]

    def work(block, emit):
        @tiles(w_in.shape[1], 512)
        def _(cols):
            pre = dot_rows(hid[block], w_in[:, cols]) + b_ref[which : which + 1, cols]
            gate = jax.nn.sigmoid(pre)
            act[block, :, cols] = b16(pre * gate)
            slope[block, :, cols] = b16(gate * (1.0 + pre * (1.0 - gate)))

        @tiles(columns, 512)
        def _(cols):
            emit(cols, dot_rows(act[block], w_rows[:, cols]))

    settle, total = gather_work_scatter(links, hid, work, part, send, land, cross, land_cross)
    settle()
    half = rows_ref.shape[0] // 2
    for h in range(2):
        rows = slice(h * half, (h + 1) * half)
        out_ref[rows] = rows_ref[rows] + 0.5 * (total(h) + vector_row(pack, at_rows[2]))


def ffn_forward(rows_in, pack, b_in, w_rows, ffn_in, which, at_rows, ident):
    rows, features = rows_in.shape
    hidden = ffn_in.shape[2]
    shape = lambda c: jax.ShapeDtypeStruct((4, rows, c), jnp.bfloat16)
    out, hid, act, slope = pl.pallas_call(
        functools.partial(ffn_forward_body, which, at_rows),
        out_shape=[
            jax.ShapeDtypeStruct((rows, features), jnp.float32),
            shape(features), shape(hidden), shape(hidden),
        ],
        in_specs=[VMEM_SPEC] * 4 + [pl.BlockSpec(memory_space=pl.ANY)],
        out_specs=[VMEM_SPEC] * 4,
        scratch_shapes=gws_scratch(rows, features)
        + [pltpu.VMEM((features, hidden), jnp.bfloat16), pltpu.SemaphoreType.DMA],
        compiler_params=pltpu.CompilerParams(
            collective_id=ident, has_side_effects=True, vmem_limit_bytes=40 << 20
        ),
        name="ffn_forward",
    )(rows_in, pack, b_in, w_rows, ffn_in)
    return out, (hid, act, slope)


def norm_parts(rows):
    row_mean = jnp.mean(rows, axis=-1, keepdims=True)
    centered = rows - row_mean
    inverse = lax.rsqrt(jnp.mean(centered * centered, axis=-1, keepdims=True) + epsilon)
    return centered * inverse, inverse


def norm_slope(grad, scaled, inverse, gain):
    inner = grad * gain
    return inverse * (
        inner
        - jnp.mean(inner, axis=-1, keepdims=True)
        - scaled * jnp.mean(inner * scaled, axis=-1, keepdims=True)
    )


def ffn_back_body(which, gain_at, nb, *refs):
    stages = []
    if which == 1:
        last_rows, cotangent, *refs = refs
        rows_ref, pack, hid, act, slope, w_rows, ffn_in, result, out_ref, gw_in, gw_out, sums_ref, *refs = refs
        stream_ref, *refs = refs
    else:
        stream_ref, ride_a, ride_b, *refs = refs
        rows_ref, pack, hid, act, slope, w_rows, ffn_in, out_ref, gw_in, gw_out, sums_ref, *refs = refs
        out_a, out_b, ride_send, ride_recv, *refs = refs
    grad, inner, part, send, land, cross, land_cross, send_sem, recv_sem, w_in, local_sem, *refs = refs
    links = Links(send_sem, recv_sem)
    load = pltpu.make_async_copy(ffn_in.at[which], w_in, local_sem)
    load.start()
    batch = lax.axis_index("batch")
    orders = ride_orders(nb)
    devices = [links.near, links.far]
    if which == 0:
        devices += [{"batch": flip_bits(batch, 1 << k)} for k in orders[0]]
    links.greet(devices)
    if which == 0:
        steps = len(orders[0]) - 1
        for at, (start, end) in enumerate(((ride_a, out_a), (ride_b, out_b))):
            rider = Rider(batch, ride_send, ride_recv, at * steps)
            between = refs[at * (steps - 1) : (at + 1) * (steps - 1)]
            stages.append(
                rider.chain([start, *between, end], orders[at][:0:-1], rider.double)
            )
    else:
        live = f32(pack[links.shard, 27:28, 0:1])
        mask = f32(f32(lax.broadcasted_iota(jnp.int32, (rows_ref.shape[0], 1), 0)) < live)
        scaled, inverse = norm_parts(last_rows[...])
        gain = vector_row(pack, 5)
        result[...] = (scaled * gain + vector_row(pack, 21)) * mask
        given = cotangent[...] * mask
        stream_ref[...] = norm_slope(given, scaled, inverse, gain)
        ends = (
            jnp.sum(given * scaled, axis=0, keepdims=True),
            jnp.sum(given, axis=0, keepdims=True),
        )

    def tick():
        for chain in stages:
            if chain:
                chain.pop(0)()

    tick()
    grad[0] = b16(0.5 * stream_ref[...])
    load.wait()
    columns = grad.shape[2]
    hidden = w_in.shape[1]

    def work(block, emit):
        @tiles(hidden, 512)
        def _(cols):
            wide = dot_back(grad[block], w_rows[cols, :])
            inner[block, :, cols] = b16(wide * f32(slope[block, :, cols]))

        @tiles(columns, 512)
        def _(cols):
            emit(cols, dot_back(inner[block], w_in[cols, :]))

    settle, total = gather_work_scatter(
        links, grad, work, part, send, land, cross, land_cross, None
    )
    tick()
    rows = stream_ref.shape[0]
    flat = lambda ref: ref[...].reshape(4 * rows, ref.shape[2])

    @tiles(hidden, 256)
    def _(cols):
        left = act[:, :, cols].reshape(4 * rows, 256)
        gw_out[cols, :] = b16(dot_over(left, flat(grad)))

    @tiles(hidden, 256)
    def _(cols):
        right = inner[:, :, cols].reshape(4 * rows, 256)
        gw_in[:, cols] = b16(dot_over(flat(hid), right))
        sums_ref[3:4, cols] = jnp.sum(f32(right), axis=0, keepdims=True)

    settle()
    for chain in stages:
        while chain:
            chain.pop(0)()
    gain = vector_row(pack, gain_at)
    sums_ref[0:3, :] = jnp.zeros((3, columns), jnp.float32)
    sums_ref[4:8, :] = jnp.zeros((4, columns), jnp.float32)
    if which == 1:
        sums_ref[4:5, :], sums_ref[5:6, :] = ends
    sums_ref[2:3, :] = jnp.sum(f32(grad[0]), axis=0, keepdims=True)
    half = rows // 2
    for h in range(2):
        at = slice(h * half, (h + 1) * half)
        scaled, inverse = norm_parts(rows_ref[at])
        given = total(h)
        out_ref[at] = stream_ref[at] + norm_slope(given, scaled, inverse, gain)
        sums_ref[0:1, :] += jnp.sum(given * scaled, axis=0, keepdims=True)
        sums_ref[1:2, :] += jnp.sum(given, axis=0, keepdims=True)


def ffn_back(given, rows_in, pack, saved, w_rows, ffn_in, which, gain_at, ident):
    rows, features = rows_in.shape
    hidden = ffn_in.shape[2]
    nb = lax.axis_size("batch")
    low, full = jnp.bfloat16, jnp.float32
    shape = jax.ShapeDtypeStruct
    shapes = [
        shape((rows, features), full), shape((features, hidden), low), shape((hidden, features), low),
        shape((8, features), full),
    ]
    scratch = []
    if which == 1:
        shapes = [shape((rows, features), full)] + shapes
        scratch = [pltpu.VMEM((rows, features), full)]
    else:
        first, steps = given[1].shape[0], nb.bit_length() - 2
        shapes += [shape((first << steps, r.shape[1]), low) for r in given[1:]]
        scratch = [pltpu.SemaphoreType.DMA((2 * steps,)), pltpu.SemaphoreType.DMA((2 * steps,))]
    extra = []
    if which == 0:
        for r in given[1:]:
            extra += [pltpu.VMEM((first << k, r.shape[1]), low) for k in range(1, steps)]
    return pl.pallas_call(
        functools.partial(ffn_back_body, which, gain_at, nb),
        out_shape=shapes,
        in_specs=[VMEM_SPEC] * (len(given) + 6) + [pl.BlockSpec(memory_space=pl.ANY)],
        out_specs=[VMEM_SPEC] * len(shapes),
        scratch_shapes=scratch
        + [
            pltpu.VMEM((4, rows, features), low),
            pltpu.VMEM((4, rows, hidden), low),
        ]
        + gws_scratch(rows, features)
        + [pltpu.VMEM((features, hidden), low), pltpu.SemaphoreType.DMA]
        + extra,
        compiler_params=pltpu.CompilerParams(
            collective_id=ident, has_side_effects=True, vmem_limit_bytes=48 << 20
        ),
        name="ffn_back_%d" % which,
    )(*given, rows_in, pack, *saved, w_rows, ffn_in)


class Fetch:
    def __init__(self, links, batch, local_sem):
        self.links, self.side = links, bit_of(batch, 0)
        self.beside = {"batch": flip_bits(batch, 1)}
        self.local_sem = local_sem
        self.open = []
        self.stages = []

    def run(self):
        if self.stages:
            self.stages.pop(0)()

    def drain(self):
        while self.stages:
            self.run()

    def go(self, src, dst, device):
        return self.links.go(src, dst, device)

    def columns(self, source, target, at):
        links, (rows, columns) = self.links, source.shape
        half = rows // 2
        block = lambda s: pl.ds(pl.multiple_of(s * columns, 128), columns)
        mine = pl.ds(pl.multiple_of(self.side * half, 16), half)
        far_index = flip_bits(links.shard, 2)
        held = {}

        def first():
            held["own"] = pltpu.make_async_copy(source, target.at[:, block(links.shard)], self.local_sem.at[at])
            held["own"].start()
            held["far"] = self.go(source.at[mine], target.at[mine, block(links.shard)], links.far)
            held["near"] = self.go(source, target.at[:, block(links.shard)], links.near)

        def second():
            held["far"].wait()
            held["x"] = self.go(target.at[mine, block(far_index)], target.at[mine, block(far_index)], self.beside)

        def third():
            held["x"].wait()
            held["on"] = self.go(target.at[:, block(far_index)], target.at[:, block(far_index)], links.near)

        def fourth():
            held["on"].wait()
            held["near"].wait()
            held["own"].wait()

        return [first, second, third, fourth]

    def rows(self, source, target, at, pieces):
        links, (rows, width) = self.links, target.shape
        columns = source.shape[1]
        half = rows // 2
        size = half // pieces
        block = lambda s: pl.ds(pl.multiple_of(s * columns, 128), columns)
        part = lambda base, p: pl.ds(pl.multiple_of(base + self.side * half + p * size, 16), size)
        held = {}
        far, across = flip_bits(links.shard, 2), flip_bits(links.shard, 3)
        near = flip_bits(links.shard, 1)
        whole = lambda t: pl.ds(pl.multiple_of(t * rows, 16), rows)

        def first():
            held["own"] = pltpu.make_async_copy(
                source.at[whole(links.shard)], target.at[:, block(links.shard)], self.local_sem.at[at]
            )
            held["own"].start()
            for p in range(pieces):
                for name, t, device in (("f", far, links.far), ("a", across, links.across)):
                    held[name, p] = self.go(
                        source.at[part(t * rows, p)], target.at[part(0, p), block(links.shard)], device
                    )
            held["near"] = self.go(source.at[whole(near)], target.at[:, block(links.shard)], links.near)

        def middle(p):
            def run():
                for name, t in (("f", far), ("a", across)):
                    held[name, p].wait()
                    at_p = target.at[part(0, p), block(t)]
                    held[name, p] = self.go(at_p, at_p, self.beside)

            return run

        def last():
            for p in range(pieces):
                held["f", p].wait()
                held["a", p].wait()
            held["near"].wait()
            held["own"].wait()

        return [first] + [middle(p) for p in range(pieces)] + [last]


def vector_row(pack, row):
    return f32(jnp.concatenate([pack[t, row : row + 1, :] for t in range(pack.shape[0])], 1))


def scatter_late(links, work, part, send, land, cross, land_cross):
    half = send.shape[1]
    backs = []
    for h in range(2):

        def split(cols, value, h=h):
            part[1, h * half : (h + 1) * half, cols] = value[:half]
            send[2 + h, :, cols] = b16(value[half:])

        work(2 + h, split)
        backs.append(links.go(send.at[2 + h], land.at[2 + h], links.near))
    last = []
    for h in range(2):
        backs[h].wait()
        cross[h] = b16(part[1, h * half : (h + 1) * half] + f32(land[2 + h]))
        last.append(links.go(cross.at[h], land_cross.at[h], links.far))

    def give(cols, value):
        send[0, :, cols] = b16(value[:half])
        send[1, :, cols] = b16(value[half:])

    work(1, give)
    last.append(links.go(send.at[pl.ds(0, 2)], land.at[pl.ds(0, 2)], links.near))

    def keep(cols, value):
        part[0, :, cols] = value

    work(0, keep)

    def settle():
        for copy in last:
            copy.wait()

    def total(h):
        rows = slice(h * half, (h + 1) * half)
        return part[0, rows] + f32(land[h]) + f32(land_cross[h])

    return settle, total


def opening_body(
    rows_ref, pack_in, b_ref, base_ref, pos_ref, ffn_in, ffn_out, out_proj,
    out_ref, hid, act, slope, pack, w_rows, table, proj, w_out,
    w_in, part, send, land, cross, land_cross, send_sem, recv_sem, local_sem,
):
    batch = lax.axis_index("batch")
    links = Links(send_sem, recv_sem)
    fetch = Fetch(links, batch, local_sem)
    load = pltpu.make_async_copy(ffn_in.at[0], w_in, local_sem.at[0])
    load.start()
    links.greet([links.near, links.far, links.across, fetch.beside])
    small = [
        links.go(pack_in, pack.at[links.shard], device)
        for device in (links.far, links.across, links.near)
    ]
    down = fetch.rows(ffn_out.at[0], w_rows, 1, 4)
    down.pop(0)()
    pack[links.shard] = pack_in[...]
    for copy in small:
        copy.wait()
    rows, features = rows_ref.shape
    hid[0] = b16(norm_rows(rows_ref[...], vector_row(pack, 0), vector_row(pack, 6)))
    half = rows // 2
    out = [
        links.go(hid.at[0, pl.ds(h * half, half)], hid.at[2 + h, pl.ds(0, half)], links.far)
        for h in range(2)
    ]
    near = links.go(hid.at[0], hid.at[1], links.near)
    load.wait()

    def up(block):
        @tiles(w_in.shape[1], 512)
        def _(cols):
            pre = dot_rows(hid[block], w_in[:, cols]) + b_ref[0:1, cols]
            gate = jax.nn.sigmoid(pre)
            act[block, :, cols] = b16(pre * gate)
            slope[block, :, cols] = b16(gate * (1.0 + pre * (1.0 - gate)))

    up(0)
    down.pop(0)()
    near.wait()
    up(1)
    lanes = features // 2

    @pl.loop(0, table.shape[0] // 16)
    def _(i):
        at = pl.ds(pl.multiple_of(i * 16, 16), 16)
        s_a, c_a = base_ref[pl.ds(16 + i, 1), 0:lanes], base_ref[pl.ds(16 + i, 1), lanes:]
        s_b, c_b = base_ref[0:16, 0:lanes], base_ref[0:16, lanes:]
        table[at, 0:lanes] = b16(s_a * c_b + c_a * s_b)
        table[at, lanes:] = b16(c_a * c_b - s_a * s_b)

    proj[...] = b16(dot_rows(table[...], pos_ref[...]))
    down.pop(0)()
    other = fetch.columns(out_proj, w_out, 2)
    for h in range(2):
        out[h].wait()
        on = links.go(hid.at[2 + h, pl.ds(0, half)], hid.at[2 + h, pl.ds(half, half)], links.near)
        on.wait()
        up(2 + h)
        down.pop(0)()
        if h == 0:
            other.pop(0)()
    while down:
        down.pop(0)()
    other.pop(0)()

    def work(block, emit):
        @tiles(features, 512)
        def _(cols):
            emit(cols, dot_rows(act[block], w_rows[:, cols]))

    settle, total = scatter_late(links, work, part, send, land, cross, land_cross)
    while other:
        other.pop(0)()
    settle()
    bias = vector_row(pack, 7)
    for h in range(2):
        at = slice(h * half, (h + 1) * half)
        out_ref[at] = rows_ref[at] + 0.5 * (total(h) + bias)


ANY_SPEC = pl.BlockSpec(memory_space=pl.ANY)


def link_scratch(count, local):
    return [
        pltpu.SemaphoreType.DMA((count,)),
        pltpu.SemaphoreType.DMA((count,)),
        pltpu.SemaphoreType.DMA((local,)),
    ]


def opening(rows_in, pack_in, b_in, base, pos_proj, ffn_in, ffn_out, out_proj, ident):
    ns = lax.axis_size("shard")
    rows, features = rows_in.shape
    hidden = ffn_in.shape[2]
    shape = jax.ShapeDtypeStruct
    low = jnp.bfloat16
    positions = 2 * rows
    return pl.pallas_call(
        opening_body,
        out_shape=[
            shape((rows, features), jnp.float32),
            shape((4, rows, features), low), shape((4, rows, hidden), low), shape((4, rows, hidden), low),
            shape((ns,) + pack_in.shape, low),
            shape((hidden, features), low),
            shape((positions, features), low),
            shape((positions, pos_proj.shape[1]), low),
            shape((features, features), low),
        ],
        in_specs=[VMEM_SPEC] * 5 + [ANY_SPEC] * 3,
        out_specs=[VMEM_SPEC] * 8 + [ANY_SPEC],
        scratch_shapes=[pltpu.VMEM((features, hidden), low)]
        + gws_scratch(rows, features)[:5]
        + link_scratch(48, 4),
        compiler_params=pltpu.CompilerParams(
            collective_id=ident, has_side_effects=True, vmem_limit_bytes=40 << 20
        ),
        name="opening",
    )(rows_in, pack_in, b_in, base, pos_proj, ffn_in, ffn_out, out_proj)


def mix_body(
    heads, size, rows_ref, pack, own_ref, w_qkv, proj, w_out, conv_in,
    out_ref, hid, with_u, with_v, key, value, soft_ref, mix, wc_in,
    turned, send_sem, recv_sem, local_sem,
):
    batch = lax.axis_index("batch")
    links = Links(send_sem, recv_sem)
    fetch = Fetch(links, batch, local_sem)
    scale = 1.0 / math.sqrt(size)
    rows, features = rows_ref.shape
    half = rows // 2
    links.greet([links.near, links.far, links.across, fetch.beside])
    hid[0] = b16(norm_rows(rows_ref[...], vector_row(pack, 1), vector_row(pack, 8)))
    out = [
        links.go(hid.at[0, pl.ds(h * half, half)], hid.at[2, pl.ds(h * half, half)], links.far)
        for h in range(2)
    ]
    near = links.go(hid.at[0], hid.at[1], links.near)
    own = f32(own_ref[...])
    keys = f32(lax.broadcasted_iota(jnp.int32, (rows, rows), 1))

    def attend(slot):
        hidden = hid[slot]
        query = dot_rows(hidden, w_qkv[0]) + own[3:4]
        with_u[slot] = b16(query + own[6:7])
        with_v[slot] = b16(query + own[7:8])
        key[slot] = b16(dot_rows(hidden, w_qkv[1]))
        value[slot] = b16(dot_rows(hidden, w_qkv[2]) + own[4:5])
        live = f32(pack[flip_bits(links.shard, slot), 27:28, 0:1])
        for h in range(heads):
            cols = slice(h * size, (h + 1) * size)
            wide = dot_back(with_v[slot, :, cols], proj[:, cols])
            moved = pltpu.roll(wide, rows + 1, 1, stride=1, stride_axis=0)[:, :rows]
            raw = dot_back(with_u[slot, :, cols], key[slot, :, cols]) + moved
            scores = jnp.where(keys < live, raw * scale, -1e30)
            grown = jnp.exp(scores - jnp.max(scores, axis=-1, keepdims=True))
            soft = grown / jnp.sum(grown, axis=-1, keepdims=True)
            soft_ref[slot, :, h * rows : (h + 1) * rows] = soft
            mix[slot, :, cols] = b16(dot_rows(b16(soft), value[slot, :, cols]))

    last = []
    attend(0)
    turned[links.shard] = mix[0]
    near.wait()
    attend(1)
    last.append(links.go(mix.at[1], turned.at[links.shard], links.near))
    on = []
    for h in range(2):
        out[h].wait()
        part = hid.at[2, pl.ds(h * half, half)]
        on.append(links.go(part, hid.at[3, pl.ds(h * half, half)], links.near))
    other = fetch.columns(conv_in, wc_in, 0)
    other.pop(0)()
    attend(2)
    last.append(links.go(mix.at[2], turned.at[links.shard], links.far))
    for copy in on:
        copy.wait()
    attend(3)
    last.append(links.go(mix.at[3], turned.at[links.shard], links.across))
    other.pop(0)()
    for copy in last:
        copy.wait()
    bias = vector_row(pack, 11)
    width = mix.shape[2]
    total = rows_ref[...] + bias
    for t in range(turned.shape[0]):
        total = total + dot_rows(turned[t], w_out[t * width : (t + 1) * width])
    out_ref[...] = total
    while other:
        other.pop(0)()


def mix_forward(rows_in, pack, own_biases, qkv_proj, proj, w_out, conv_in, heads, ident):
    ns = lax.axis_size("shard")
    rows, features = rows_in.shape
    width = features // ns
    shape = jax.ShapeDtypeStruct
    low = jnp.bfloat16
    narrow = shape((ns, rows, width), low)
    return pl.pallas_call(
        functools.partial(mix_body, heads, width // heads),
        out_shape=[
            shape((rows, features), jnp.float32), shape((ns, rows, features), low),
            narrow, narrow, narrow, narrow,
            shape((ns, rows, heads * rows), jnp.float32),
            narrow,
            shape((conv_in.shape[0], ns * conv_in.shape[1]), low),
        ],
        in_specs=[VMEM_SPEC] * 6 + [ANY_SPEC],
        out_specs=[VMEM_SPEC] * 8 + [ANY_SPEC],
        scratch_shapes=[pltpu.VMEM((ns, rows, width), low)] + link_scratch(16, 2),
        compiler_params=pltpu.CompilerParams(
            collective_id=ident, has_side_effects=True, vmem_limit_bytes=40 << 20
        ),
        name="mix_forward",
    )(rows_in, pack, own_biases, qkv_proj, proj, w_out, conv_in)


def pack_rows(ref, at, row):
    for i in range(row.shape[1] // 128):
        ref[at + i : at + i + 1, :] = row[:, i * 128 : (i + 1) * 128]


def unpack_rows(value, at, lanes):
    return jnp.concatenate([value[at + i : at + i + 1, :] for i in range(lanes)], 1)


def everywhere(links, nb, source, mid, land_s, land_b, result, small, sems):
    s, b = links.shard, lax.axis_index("batch")
    ns = land_s.shape[0]
    ss, rs, sb, rb = sems
    first = exchange("shard", s, ns, source, land_s, ss, rs)
    for copy in first:
        copy.start()
    land_s[s] = source[...]
    for copy in first:
        copy.wait()
    mid[...] = sum_slots(land_s, ns)
    second = exchange("batch", b, nb, mid, land_b, sb, rb)
    for copy in second:
        copy.start()
    land_b[b] = mid[...]
    small()
    for copy in second:
        copy.wait()
    return sum_slots(land_b, nb)


def conv_body(
    nb, rows_ref, pack, w_in, conv_out, ffn_out,
    out_ref, hid, open_ref, gate_ref, gated_ref, scaled_ref, act, slope, stats, w_out, w_rows,
    padded, source, mid, land_s, land_b, ss, rs, sb, rb, send_sem, recv_sem, local_sem,
):
    batch = lax.axis_index("batch")
    links = Links(send_sem, recv_sem)
    fetch = Fetch(links, batch, local_sem)
    rows, features = rows_ref.shape
    ns = land_s.shape[0]
    links.greet(
        [links.near, links.far, links.across]
        + [{"batch": lax.rem(batch + j, nb)} for j in range(1, nb)]
    )
    out_fetch = fetch.columns(conv_out, w_out, 0)
    out_fetch.pop(0)()
    live = f32(pack[links.shard, 27:28, 0:1])
    mask = f32(f32(lax.broadcasted_iota(jnp.int32, (rows, 1), 0)) < live)
    hid[...] = b16(norm_rows(rows_ref[...], vector_row(pack, 2), vector_row(pack, 14)))
    bias_v, bias_g = vector_row(pack, 15), vector_row(pack, 16)
    lead = 8
    tile = 512
    padded[0:lead, :] = jnp.zeros((lead, features), jnp.float32)
    padded[lead + rows :, :] = jnp.zeros((lead, features), jnp.float32)
    for n in range(features // tile):
        cols = slice(n * tile, (n + 1) * tile)
        left = dot_rows(hid[...], w_in[:, cols]) + bias_v[:, cols]
        right = dot_rows(hid[...], w_in[:, features + n * tile : features + (n + 1) * tile])
        gate = jax.nn.sigmoid(right + bias_g[:, cols])
        opened = gate * mask
        gated = left * opened
        open_ref[:, cols] = b16(opened)
        gate_ref[:, cols] = b16(gated * (1.0 - gate))
        gated_ref[:, cols] = b16(gated)
        padded[lead : lead + rows, cols] = gated
    out_fetch.pop(0)()
    down = fetch.rows(ffn_out.at[1], w_rows, 1, 1)
    down.pop(0)()
    taps = 5
    total = 0.0
    for k in range(taps):
        at = lead - (taps - 1) // 2 + k
        total = total + padded[at : at + rows, :] * vector_row(pack, 22 + k)
    live_total = total * mask
    lanes = features // 128
    pack_rows(source, 0, jnp.sum(live_total, axis=0, keepdims=True))
    pack_rows(source, lanes, jnp.sum(live_total * total, axis=0, keepdims=True))
    source[2 * lanes : 2 * lanes + 8, :] = jnp.broadcast_to(live, (8, 128))
    scaled_ref[...] = total

    sums = everywhere(links, nb, source, mid, land_s, land_b, None, out_fetch.pop(0), (ss, rs, sb, rb))
    frames = sums[2 * lanes : 2 * lanes + 1, 0:1]
    mean = unpack_rows(sums, 0, lanes) / frames
    inverse = lax.rsqrt(unpack_rows(sums, lanes, lanes) / frames - mean * mean + epsilon)
    stats[0:1, :] = inverse
    stats[1:2, :] = jnp.broadcast_to(frames, (1, features))
    stats[2:8, :] = jnp.zeros((6, features), jnp.float32)
    scaled = (scaled_ref[...] - mean) * inverse
    scaled_ref[...] = scaled
    normed = scaled * vector_row(pack, 3) + vector_row(pack, 17)
    gate = jax.nn.sigmoid(normed)
    act[...] = b16(normed * gate)
    slope[...] = b16(gate * (1.0 + normed * (1.0 - gate)))
    out_fetch.pop(0)()
    down.pop(0)()
    out_ref[...] = rows_ref[...] + (dot_rows(act[...], w_out[...]) + vector_row(pack, 18))
    down.pop(0)()


def conv_forward(rows_in, pack, w_in, conv_out, ffn_out, ident):
    ns, nb = lax.axis_size("shard"), lax.axis_size("batch")
    rows, features = rows_in.shape
    shape = jax.ShapeDtypeStruct
    low, full = jnp.bfloat16, jnp.float32
    plain = shape((rows, features), low)
    small = (24, 128)
    return pl.pallas_call(
        functools.partial(conv_body, nb),
        out_shape=[
            shape((rows, features), full), plain, plain, plain, plain,
            shape((rows, features), full), plain, plain, shape((8, features), full),
            shape((features, features), low),
            shape((ffn_out.shape[1] // ns, features), low),
        ],
        in_specs=[VMEM_SPEC] * 3 + [ANY_SPEC] * 2,
        out_specs=[VMEM_SPEC] * 10 + [ANY_SPEC],
        scratch_shapes=[
            pltpu.VMEM((rows + 16, features), full),
            pltpu.VMEM(small, full), pltpu.VMEM(small, full),
            pltpu.VMEM((ns,) + small, full), pltpu.VMEM((nb,) + small, full),
            pltpu.SemaphoreType.DMA((ns,)), pltpu.SemaphoreType.DMA((ns,)),
            pltpu.SemaphoreType.DMA((nb,)), pltpu.SemaphoreType.DMA((nb,)),
        ]
        + link_scratch(16, 3),
        compiler_params=pltpu.CompilerParams(
            collective_id=ident, has_side_effects=True, vmem_limit_bytes=40 << 20
        ),
        name="conv_forward",
    )(rows_in, pack, w_in, conv_out, ffn_out)


def conv_back_body(
    nb, stream_ref, rows_ref, pack, w_in, w_out, hid, open_ref, gate_ref, gated_ref, scaled_ref, act, slope, stats,
    ride_a, ride_b, out_ref, gw_out, gw_in, sums_ref, half_a, half_b,
    padded, normed, grad, inner, source, mid, land_s, land_b, ss, rs, sb, rb, send_sem, recv_sem,
):
    batch = lax.axis_index("batch")
    links = Links(send_sem, recv_sem)
    rows, features = rows_ref.shape
    links.greet(
        [links.near, links.far, links.across]
        + [{"batch": lax.rem(batch + j, nb)} for j in range(1, nb)]
    )
    orders = ride_orders(nb)
    ride = [
        Rider(batch, send_sem, recv_sem, at).halve(source_ref, landing, orders[at][0])
        for at, (source_ref, landing) in enumerate(((ride_a, half_a), (ride_b, half_b)))
    ]
    lanes = features // 128
    lead, tile, taps = 8, 512, 5
    grad[...] = b16(stream_ref[...])
    gain = vector_row(pack, 3)
    sums_ref[...] = jnp.zeros_like(sums_ref)
    for n in range(features // tile):
        cols = slice(n * tile, (n + 1) * tile)
        value = dot_back(grad[...], w_out[cols, :]) * f32(slope[:, cols])
        normed[:, cols] = value
        for at, total in (
            (0, jnp.sum(value, axis=0, keepdims=True)),
            (lanes, jnp.sum(value * scaled_ref[:, cols], axis=0, keepdims=True)),
        ):
            for i in range(tile // 128):
                row = at + n * (tile // 128) + i
                source[row : row + 1, :] = total[:, i * 128 : (i + 1) * 128]

    def meanwhile():
        @tiles(features, 256)
        def _(cols):
            gw_out[cols, :] = b16(dot_over(act[:, cols], grad[...]))

        sums_ref[4:5, :] = jnp.sum(f32(grad[...]), axis=0, keepdims=True)

    sums = everywhere(links, nb, source, mid, land_s, land_b, None, meanwhile, (ss, rs, sb, rb))
    beta, gamma = unpack_rows(sums, 0, lanes), unpack_rows(sums, lanes, lanes)
    sums_ref[5:6, :] = gamma
    sums_ref[6:7, :] = beta
    inverse, frames = stats[0:1, :], stats[1:2, 0:1]
    live = f32(pack[links.shard, 27:28, 0:1])
    mask = f32(f32(lax.broadcasted_iota(jnp.int32, (rows, 1), 0)) < live)
    padded[0:lead, :] = jnp.zeros((lead, features), jnp.float32)
    padded[lead + rows :, :] = jnp.zeros((lead, features), jnp.float32)
    padded[lead : lead + rows, :] = inverse * (
        normed[...] * gain - mask * (gain * beta + scaled_ref[...] * (gain * gamma)) / frames
    )
    given = 0.0
    gated = f32(gated_ref[...])
    for k in range(taps):
        at = lead + (taps - 1) // 2 - k
        moved = padded[at : at + rows, :]
        given = given + moved * vector_row(pack, 22 + k)
        sums_ref[8 + k : 9 + k, :] = jnp.sum(moved * gated, axis=0, keepdims=True)
    left = b16(given * f32(open_ref[...]))
    right = b16(given * f32(gate_ref[...]))
    inner[:, 0:features] = left
    inner[:, features:] = right
    sums_ref[2:3, :] = jnp.sum(f32(left), axis=0, keepdims=True)
    sums_ref[3:4, :] = jnp.sum(f32(right), axis=0, keepdims=True)
    total = dot_back(inner[...], w_in[...])
    scaled, inverse = norm_parts(rows_ref[...])
    out_ref[...] = stream_ref[...] + norm_slope(total, scaled, inverse, vector_row(pack, 2))
    sums_ref[0:1, :] = jnp.sum(total * scaled, axis=0, keepdims=True)
    sums_ref[1:2, :] = jnp.sum(total, axis=0, keepdims=True)

    @tiles(2 * features, 512)
    def _(cols):
        gw_in[:, cols] = b16(dot_over(hid[...], inner[:, cols]))

    for end in ride:
        end()


def conv_back(stream, rows_in, pack, w_in, w_out, saved, ridden, ident):
    ns, nb = lax.axis_size("shard"), lax.axis_size("batch")
    rows, features = rows_in.shape
    shape = jax.ShapeDtypeStruct
    low, full = jnp.bfloat16, jnp.float32
    small = (2 * features // 128, 128)
    return pl.pallas_call(
        functools.partial(conv_back_body, nb),
        out_shape=[
            shape((rows, features), full), shape((features, features), low),
            shape((features, 2 * features), low), shape((16, features), full),
        ]
        + [shape((r.shape[0] // 2, r.shape[1]), low) for r in ridden],
        in_specs=[VMEM_SPEC] * 15,
        out_specs=[VMEM_SPEC] * 6,
        scratch_shapes=[
            pltpu.VMEM((rows + 16, features), full), pltpu.VMEM((rows, features), full),
            pltpu.VMEM((rows, features), low), pltpu.VMEM((rows, 2 * features), low),
            pltpu.VMEM(small, full), pltpu.VMEM(small, full),
            pltpu.VMEM((ns,) + small, full), pltpu.VMEM((nb,) + small, full),
            pltpu.SemaphoreType.DMA((ns,)), pltpu.SemaphoreType.DMA((ns,)),
            pltpu.SemaphoreType.DMA((nb,)), pltpu.SemaphoreType.DMA((nb,)),
        ]
        + link_scratch(4, 1)[:2],
        compiler_params=pltpu.CompilerParams(
            collective_id=ident, has_side_effects=True, vmem_limit_bytes=48 << 20
        ),
        name="conv_back",
    )(stream, rows_in, pack, w_in, w_out, *saved, *ridden)


def mix_back_body(
    heads, size, nb, stream_ref, rows_ref, pack, hid, with_u, with_v, key, value, soft_ref, mix, table, proj,
    w_qkv, w_out, ride_a, ride_b, out_ref, gw_qkv, gw_pos, gw_out, sums_ref, own_sums, out_a, out_b,
    grad, dq, dk, dx, dp, part, send, land, cross, land_cross, send_sem, recv_sem, ride_send, ride_recv, *between,
):
    links = Links(send_sem, recv_sem)
    batch = lax.axis_index("batch")
    orders = ride_orders(nb)
    steps = len(orders[0]) - 1
    scale = 1.0 / math.sqrt(size)
    rows, features = rows_ref.shape
    half = rows // 2
    width = mix.shape[2]
    links.greet([links.near, links.far] + [{"batch": flip_bits(batch, 1 << k)} for k in orders[0]])
    stages = []
    for at, (start, end) in enumerate(((ride_a, out_a), (ride_b, out_b))):
        rider = Rider(batch, ride_send, ride_recv, at * steps)
        middle = between[at * (steps - 1) : (at + 1) * (steps - 1)]
        stages.append(rider.chain([start, *middle, end], orders[at][1:], rider.halve))

    def tick():
        for chain in stages:
            if chain:
                chain.pop(0)()

    tick()
    grad[0] = b16(stream_ref[...])
    out = [
        links.go(grad.at[0, pl.ds(h * half, half)], grad.at[2, pl.ds(h * half, half)], links.far)
        for h in range(2)
    ]
    near = links.go(grad.at[0], grad.at[1], links.near)
    at_row = lax.broadcasted_iota(jnp.int32, (rows, rows), 0)
    at_col = lax.broadcasted_iota(jnp.int32, (rows, rows), 1)
    flip = b16(f32(at_row + at_col == rows - 1))
    keys = f32(at_col)
    mine = pl.ds(pl.multiple_of(links.shard * width, 16), width)
    own_sums[...] = jnp.zeros_like(own_sums)

    def work(slot, emit):
        mixed = b16(dot_back(grad[slot], w_out[mine, :]))
        live = f32(pack[flip_bits(links.shard, slot), 27:28, 0:1])
        for h in range(heads):
            cols = slice(h * size, (h + 1) * size)
            soft = soft_ref[slot, :, h * rows : (h + 1) * rows]
            given = mixed[:, cols]
            grad_soft = dot_back(given, value[slot, :, cols])
            dx[slot, :, cols] = b16(dot_over(b16(soft), given))
            grad_scores = soft * (grad_soft - jnp.sum(grad_soft * soft, axis=-1, keepdims=True))
            raw = b16(jnp.where(keys < live, grad_scores, 0.0) * scale)
            grad_u = dot_rows(raw, key[slot, :, cols])
            dk[slot, :, cols] = b16(dot_over(raw, with_u[slot, :, cols]))
            turned = dot_rows(flip, raw)
            wide = jnp.concatenate([turned, jnp.zeros_like(turned)], 1)
            wide = b16(pltpu.roll(wide, 0, 1, stride=1, stride_axis=0))
            grad_v = dot_rows(wide, proj[:, cols])
            v_turned = b16(dot_rows(flip, with_v[slot, :, cols]))
            dp[slot, :, cols] = b16(dot_over(wide, v_turned))
            own_sums[2:3, cols] += jnp.sum(grad_u, axis=0, keepdims=True)
            own_sums[3:4, cols] += jnp.sum(grad_v, axis=0, keepdims=True)
            high = b16(grad_v)
            rest = b16(grad_v - f32(high))
            dq[slot, :, cols] = b16(grad_u + (dot_rows(flip, high) + dot_rows(flip, rest)))
        own_sums[0:1, :] += jnp.sum(f32(dq[slot]), axis=0, keepdims=True)
        own_sums[1:2, :] += jnp.sum(f32(dx[slot]), axis=0, keepdims=True)

        @tiles(features, 512)
        def _(cols):
            emit(
                cols,
                dot_back(dq[slot], w_qkv[0, cols, :])
                + dot_back(dk[slot], w_qkv[1, cols, :])
                + dot_back(dx[slot], w_qkv[2, cols, :]),
            )

    def keep(cols, value):
        part[0, :, cols] = value

    def keep_far(cols, value):
        part[1, :, cols] = value

    def give(cols, value):
        send[0, :, cols] = b16(value[:half])
        send[1, :, cols] = b16(value[half:])

    def give_far(cols, value):
        send[2, :, cols] = b16(value[:half])
        send[3, :, cols] = b16(value[half:])

    work(0, keep)
    near.wait()
    work(1, give)
    last = [links.go(send.at[pl.ds(0, 2)], land.at[pl.ds(0, 2)], links.near)]
    on = []
    for h in range(2):
        out[h].wait()
        there = pl.ds(h * half, half)
        on.append(links.go(grad.at[2, there], grad.at[3, there], links.near))
    for copy in on:
        copy.wait()
    tick()
    work(3, give_far)
    back = links.go(send.at[pl.ds(2, 2)], land.at[pl.ds(2, 2)], links.near)
    work(2, keep_far)
    back.wait()
    for h in range(2):
        cross[h] = b16(part[1, h * half : (h + 1) * half] + f32(land[2 + h]))
        last.append(links.go(cross.at[h], land_cross.at[h], links.far))
    flat = lambda ref: ref[...].reshape(4 * rows, ref.shape[2])
    for at, ref in enumerate((dq, dk, dx)):
        right = flat(ref)

        @tiles(features, 256)
        def _(cols, at=at, right=right):
            left = hid[:, :, cols].reshape(4 * rows, 256)
            gw_qkv[at, cols, :] = b16(dot_over(left, right))

    @tiles(features, 256)
    def _(cols):
        total = dot_over(table[:, cols], dp[0])
        for slot in range(1, 4):
            total = total + dot_over(table[:, cols], dp[slot])
        gw_pos[cols, :] = b16(total)

    gw_out[...] = b16(dot_over(flat(mix), flat(grad)))
    for copy in last:
        copy.wait()
    for chain in stages:
        while chain:
            chain.pop(0)()
    sums_ref[...] = jnp.zeros_like(sums_ref)
    sums_ref[2:3, :] = jnp.sum(f32(grad[0]), axis=0, keepdims=True)
    gain = vector_row(pack, 1)
    for h in range(2):
        at = slice(h * half, (h + 1) * half)
        given = part[0, at] + f32(land[h]) + f32(land_cross[h])
        scaled, inverse = norm_parts(rows_ref[at])
        out_ref[at] = stream_ref[at] + norm_slope(given, scaled, inverse, gain)
        sums_ref[0:1, :] += jnp.sum(given * scaled, axis=0, keepdims=True)
        sums_ref[1:2, :] += jnp.sum(given, axis=0, keepdims=True)


def mix_back(stream, rows_in, pack, saved, table, proj, w_qkv, w_out, ridden, heads, ident):
    rows, features = rows_in.shape
    hid, with_u, with_v, key, value, soft, mix = saved
    width = mix.shape[2]
    shape = jax.ShapeDtypeStruct
    low, full = jnp.bfloat16, jnp.float32
    narrow = pltpu.VMEM((4, rows, width), low)
    nb = lax.axis_size("batch")
    steps = nb.bit_length() - 2
    dma = pltpu.SemaphoreType.DMA((2 * steps,))
    between = []
    for r in ridden:
        between += [pltpu.VMEM((r.shape[0] >> k, r.shape[1]), low) for k in range(1, steps)]
    return pl.pallas_call(
        functools.partial(mix_back_body, heads, width // heads, nb),
        out_shape=[
            shape((rows, features), full), shape((3, features, width), low), shape((features, width), low),
            shape((width, features), low), shape((8, features), full), shape((8, width), full),
        ]
        + [shape((r.shape[0] >> steps, r.shape[1]), low) for r in ridden],
        in_specs=[VMEM_SPEC] * 16,
        out_specs=[VMEM_SPEC] * 8,
        scratch_shapes=[
            pltpu.VMEM((4, rows, features), low), narrow, narrow, narrow,
            pltpu.VMEM((4, 2 * rows, width), low),
        ]
        + gws_scratch(rows, features)
        + [dma, dma]
        + between,
        compiler_params=pltpu.CompilerParams(
            collective_id=ident, has_side_effects=True, vmem_limit_bytes=48 << 20
        ),
        name="mix_back",
    )(stream, rows_in, pack, *saved, table, proj, w_qkv, w_out, *ridden)


def body(
    tokens, cotangent, lengths, ffn_in, ffn_out, ffn_bias, qkv_proj, pos_proj, out_proj,
    conv_in, conv_out, depthwise, norm_gains, biases,
):
    _, length, features = tokens.shape
    ns, nb = lax.axis_size("shard"), lax.axis_size("batch")
    width = features // ns
    heads = HEADS // ns
    rows_in = tokens[0]

    own_length = jnp.broadcast_to(b16(f32(lengths))[:, None], (5, width))
    pack_in = jnp.concatenate([norm_gains, biases, depthwise, own_length], 0)
    b_in = f32(ffn_bias)

    rates = jnp.exp(
        jnp.arange(features // 2, dtype=jnp.float32) * (-2.0 * math.log(10000.0) / features)
    )
    turns = jnp.concatenate(
        [
            length - 1.0 - jnp.arange(16, dtype=jnp.float32),
            -16.0 * jnp.arange(2 * length // 16, dtype=jnp.float32),
        ]
    )
    angles = turns[:, None] * rates[None, :]
    base = jnp.concatenate([jnp.sin(angles), jnp.cos(angles)], 1)
    rows_one, *saved_one, pack, w_rows_one, table, proj, w_out = opening(
        rows_in, pack_in, b_in, base, pos_proj, ffn_in, ffn_out, out_proj, 5
    )
    rows_two, hid, with_u, with_v, key, value, soft, mix, wc_in = mix_forward(
        rows_one, pack, biases, qkv_proj, proj, w_out, conv_in, heads, 9
    )
    saved_mix = (hid, with_u, with_v, key, value, soft, mix)
    rows_three, *saved_conv, wc_out, w_rows_two = conv_forward(
        rows_two, pack, wc_in, conv_out, ffn_out, 10
    )
    rows_four, saved_two = ffn_forward(
        rows_three, pack, b_in, w_rows_two, ffn_in, 1, (4, 19, 20), 6
    )

    result, stream, two_in, two_out, two_sums = ffn_back(
        (rows_four, cotangent[0]), rows_three, pack, saved_two, w_rows_two, ffn_in, 1, 4, 7
    )
    stream, grad_conv_out, grad_conv_in, conv_sums, *ridden = conv_back(
        stream, rows_two, pack, wc_in, wc_out, saved_conv, (two_in, two_out), 11
    )
    stream, grad_qkv, grad_pos, grad_out, mix_sums, own_sums, *ridden = mix_back(
        stream, rows_one, pack, saved_mix, table, proj, qkv_proj, w_out, ridden, heads, 12
    )
    stream, one_in, one_out, one_sums, *ridden = ffn_back(
        (stream, *ridden), rows_in, pack, saved_one, w_rows_one, ffn_in, 0, 0, 8
    )
    tall, deep = one_in.shape
    piece = max(256, 8 * nb)
    *sums, out_gains, out_biases, out_taps, out_hidden = tail_sum(
        [grad_out, one_out, one_in] + [grad_qkv[at] for at in range(3)] + [grad_pos, grad_conv_in, grad_conv_out],
        ridden,
        [one_sums, mix_sums, two_sums, conv_sums, own_sums],
        [("turn", 4, None), ("turn", 1, 0), ("plain", 0, 0)]
        + [("plain", 2, at) for at in range(3)]
        + [("plain", 3, None), ("gather", 5, None), ("gather", 6, None)],
        [
            (2, tall, deep), (2, ns * deep, width), (3, tall, width), (tall, width), (tall, width),
            (tall, 2 * width), (tall, width),
        ],
        ["near", "line"],
        [width, piece, piece, tall, tall, tall, tall, 2 * piece, tall],
        deep,
        4,
    )
    return (
        result[None],
        stream[None],
        f32(sums[0]),
        f32(sums[1]),
        out_hidden,
        f32(sums[2]),
        f32(sums[3]),
        f32(sums[4]),
        f32(sums[5]),
        f32(sums[6]),
        out_taps,
        out_gains,
        out_biases,
    )


def solution(mesh):
    rows = P(("batch", "shard"), None, None)
    cube, flat = P(None, None, "shard"), P(None, "shard")
    return jax.shard_map(
        body,
        mesh=mesh,
        in_specs=(rows, rows, P(("batch", "shard")), cube, cube, flat, cube)
        + (flat,) * 7,
        out_specs=(rows, rows, cube, cube, flat, cube) + (flat,) * 7,
        check_vma=False,
    )
```

```python
import functools
import math

import jax
import jax.numpy as jnp
from jax import lax
from jax.experimental import pallas as pl
from jax.experimental.pallas import tpu as pltpu
from jax.sharding import PartitionSpec as P

HEADS = 8
MESH = pl.DeviceIdType.MESH
VMEM_SPEC = pl.BlockSpec(memory_space=pltpu.VMEM)
HBM_SPEC = pl.BlockSpec(memory_space=pltpu.HBM)
epsilon = 1e-05


def f32(a):
    return a.astype(jnp.float32)


def b16(a):
    return a.astype(jnp.bfloat16)


def norm_rows(values_in, gain_row, bias_row):
    row_mean = jnp.mean(values_in, axis=-1, keepdims=True)
    centered = values_in - row_mean
    spread = jnp.mean(centered * centered, axis=-1, keepdims=True)
    return centered * lax.rsqrt(spread + epsilon) * gain_row + bias_row


def dot_rows(a, b):
    return jnp.dot(a, b, preferred_element_type=jnp.float32)


def dot_back(a, b):
    return lax.dot_general(a, b, (((1,), (1,)), ((), ())), preferred_element_type=jnp.float32)


def dot_over(a, b):
    return lax.dot_general(a, b, (((0,), (0,)), ((), ())), preferred_element_type=jnp.float32)


def exchange(axis, index, count, source, landing, send_sem, recv_sem):
    copies = []
    for j in range(1, count):
        peer = lax.rem(index + j, count)
        copies.append(
            pltpu.make_async_remote_copy(
                src_ref=source,
                dst_ref=landing.at[index],
                send_sem=send_sem.at[j],
                recv_sem=recv_sem.at[j],
                device_id={axis: peer},
                device_id_type=MESH,
            )
        )
    return copies


def sum_slots(ref, count):
    total = ref[0]
    for j in range(1, count):
        total = total + ref[j]
    return total


class Chunk:
    def __init__(self, at, source, row, rows, columns, first, count):
        self.at, self.source, self.row, self.rows, self.columns = at, source, row, rows, columns
        extra = [(1 << k, k) for k in range(3, count.bit_length() - 1)]
        line = (6, 1)
        if first == "near":
            self.pre, self.post = [(1, 0)], [line] + extra
        else:
            self.pre, self.post = [], [line, (1, 0)] + extra
        size, self.landings = rows, []
        for _ in self.pre:
            size //= 2
            self.landings.append((size, columns))
        self.landings.append((size, columns))
        for _ in self.post:
            size //= 2
            self.landings.append((size, columns))
        self.steps = len(self.landings)


def bit_of(value, k):
    return lax.rem(lax.div(value, 1 << k), 2)


def flip_bits(value, mask):
    out = value
    k = 0
    while (1 << k) <= mask:
        if mask & (1 << k):
            out = out + (1 - 2 * bit_of(value, k)) * (1 << k)
        k += 1
    return out


class Mover:
    def __init__(self, chunk, batch, source, base, held, landings, sems, finish, early):
        self.c, self.b = chunk, batch
        self.source, self.base, self.held, self.landings, self.sems = source, base, held, landings, sems
        lo, hi = bit_of(batch, 1), bit_of(batch, 2)
        self.inner = lo != hi
        self.ended = lo == hi
        self.finish, self.early = finish, early
        self.build()

    def copy(self, at, src, dst, mask):
        send, recv = self.sems
        return pltpu.make_async_remote_copy(
            src_ref=src,
            dst_ref=dst,
            send_sem=send.at[self.c.at, at],
            recv_sem=recv.at[self.c.at, at],
            device_id={"batch": flip_bits(self.b, mask)},
            device_id_type=MESH,
        )

    def build(self):
        c = self.c
        held = self.held
        here, base = self.source, self.base
        off, size, step = 0, c.rows, 0
        plan, trail = [], []
        sequence = [("all",) + p for p in c.pre] + [("fold", 2, None)]
        sequence += [("inner",) + p for p in c.post]
        for kind, mask, sel in sequence:
            landing = self.landings[step]
            if kind == "fold":
                own = row_view(here, base, size)
                cp = self.copy(step, own, landing, mask)
            else:
                size //= 2
                mine = bit_of(self.b, sel)
                cp = self.copy(step, row_view(here, base + (1 - mine) * size, size), landing, mask)
                own = row_view(here, base + mine * size, size)
                off = off + mine * size
            trail.append((kind, mask, off, size))
            step += 1
            out = landing if step < len(sequence) else held(off, size)
            plan.append((kind, cp, (own, landing, out)))
            here, base = landing, 0
        for kind, mask, off, size in reversed(trail):
            cp = self.copy(step, held(off, size), held(off, size), mask)
            plan.append(("unfold" if kind == "fold" else kind, cp, None))
            step += 1
        self.plan = plan
        self.depth = len(plan) + len(self.early)

    def begin(self, k):
        kind, cp, _ = self.plan[k]
        if kind == "all":
            cp.start()
        elif kind == "fold":
            pl.when(self.ended)(cp.start)
        else:
            pl.when(self.inner)(cp.start)

    def end(self, k):
        kind, cp, add = self.plan[k]

        def gather():
            if add is not None:
                own, landing, out = add
                out[...] = b16(f32(own[...]) + f32(landing[...]))

        if kind == "all":
            cp.wait()
            gather()
        elif kind in ("fold", "unfold"):
            sender, taker = (
                (self.ended, self.inner) if kind == "fold" else (self.inner, self.ended)
            )
            pl.when(sender)(cp.wait_send)

            @pl.when(taker)
            def _():
                cp.wait_recv()
                gather()
        else:

            @pl.when(self.inner)
            def _():
                cp.wait()
                gather()

    def advance(self, k):
        if k < len(self.early):
            self.early[k]()
            return
        k -= len(self.early)
        if k > 0:
            self.end(k - 1)
        elif self.early:
            self.settle_early()
        if k < len(self.plan):
            self.begin(k)
        else:
            self.finish(self.c)


def row_view(ref, start, size):
    start = start if isinstance(start, int) else pl.multiple_of(start, 16 if size % 16 == 0 else 8)
    return ref.at[pl.ds(start, size)]


def column_block(index, columns):
    return pl.ds(pl.multiple_of(index * columns, 128), columns)


class Rider:
    def __init__(self, batch, send, recv, first):
        self.b, self.send, self.recv, self.at = batch, send, recv, first

    def go(self, src, dst, bit):
        copy = pltpu.make_async_remote_copy(
            src_ref=src, dst_ref=dst, send_sem=self.send.at[self.at], recv_sem=self.recv.at[self.at],
            device_id={"batch": flip_bits(self.b, 1 << bit)}, device_id_type=MESH,
        )
        self.at += 1
        copy.start()
        return copy

    def halve_pieces(self, source, landing, bit, pieces):
        half = landing.shape[0]
        size = half // pieces
        mine = bit_of(self.b, bit)
        copies = []

        def start(p):
            copies.append(
                self.go(
                    row_view(source, (1 - mine) * half + p * size, size), row_view(landing, p * size, size), bit
                )
            )

        def end():
            for copy in copies:
                copy.wait()
            own = row_view(source, mine * half, half)
            landing[...] = b16(f32(own[...]) + f32(landing[...]))

        return start, end

    def halve(self, source, landing, bit):
        half = landing.shape[0]
        mine = bit_of(self.b, bit)
        copy = self.go(row_view(source, (1 - mine) * half, half), landing, bit)

        def end():
            copy.wait()
            own = row_view(source, mine * half, half)
            landing[...] = b16(f32(own[...]) + f32(landing[...]))

        return end

    def double(self, source, target, bit):
        half = source.shape[0]
        there = row_view(target, bit_of(self.b, bit) * half, half)
        copy = self.go(source, there, bit)
        there[...] = source[...]
        return copy.wait

    def chain(self, refs, bits, move):
        ends, stages = [], []
        for i, bit in enumerate(bits):

            def stage(i=i, bit=bit):
                if ends:
                    ends.pop()()
                ends.append(move(refs[i], refs[i + 1], bit))

            stages.append(stage)
        stages.append(lambda: ends.pop()())
        return stages


def ride_orders(count):
    bits = list(range(count.bit_length() - 1))
    return bits, [1, 0] + bits[2:]


def tail_body(specs, chunks, ns, nb, n_in, n_out, *refs):
    ins, refs = refs[:n_in], refs[n_in:]
    ridden, refs = refs[:2], refs[2:]
    (one_sums, mix_sums, two_sums, conv_sums, own_sums), refs = refs[:5], refs[5:]
    outs, refs = refs[:n_out], refs[n_out:]
    (o_gains, o_biases, o_taps, o_hidden), refs = refs[:4], refs[4:]
    send, recv, turn_send, turn_recv, pre_send, pre_recv, ride_send, ride_recv = refs[:8]
    ss, rs, sb, rb, wide, land_s, mid, land_b, ride_fin = refs[8:17]
    rest = list(refs[17:])
    shard, batch = lax.axis_index("shard"), lax.axis_index("batch")
    barrier = pltpu.get_barrier_semaphore()
    greeted = [{"batch": lax.rem(batch + j, nb)} for j in range(1, nb)]
    greeted += [{"shard": flip_bits(shard, m)} for m in range(1, ns)]
    for device in greeted:
        pl.semaphore_signal(barrier, inc=1, device_id=device, device_id_type=MESH)
    width = own_sums.shape[1]
    for t in range(ns):
        cols = slice(t * width, (t + 1) * width)
        wide[t, 0:3, :] = one_sums[0:3, cols]
        wide[t, 3:6, :] = mix_sums[0:3, cols]
        wide[t, 6:9, :] = two_sums[0:3, cols]
        wide[t, 9:14, :] = conv_sums[0:5, cols]
        wide[t, 14:19, :] = conv_sums[8:13, cols]
        wide[t, 19:21, :] = two_sums[4:6, cols]
        wide[t, 21:24, :] = jnp.zeros((3, width), jnp.float32)
    pl.semaphore_wait(barrier, len(greeted))

    vector_copies = []
    for j in range(1, ns):
        peer = lax.rem(shard + j, ns)
        copy = pltpu.make_async_remote_copy(
            src_ref=wide.at[peer], dst_ref=land_s.at[shard], send_sem=ss.at[j], recv_sem=rs.at[j],
            device_id={"shard": peer}, device_id_type=MESH,
        )
        copy.start()
        vector_copies.append(copy)
    land_s[shard] = wide[shard]

    def vectors_on():
        for copy in vector_copies:
            copy.wait()
        mid[0:24, :] = sum_slots(land_s, ns)
        mid[24:28, :] = own_sums[0:4, :]
        per = one_sums.shape[1] // width
        for t in range(per):
            cols = slice(t * width, (t + 1) * width)
            mid[28 + t : 29 + t, :] = one_sums[3:4, cols]
            mid[28 + per + t : 29 + per + t, :] = two_sums[3:4, cols]
        mid[28 + 2 * per :, :] = jnp.zeros((mid.shape[0] - 28 - 2 * per, width), jnp.float32)
        vector_copies[:] = exchange("batch", batch, nb, mid, land_b, sb, rb)
        for copy in vector_copies:
            copy.start()
        land_b[batch] = mid[...]

    def vectors_out():
        for copy in vector_copies:
            copy.wait()
        vec = sum_slots(land_b, nb)
        row = lambda k: vec[k : k + 1]
        mine = conv_sums[5:7, column_block(shard, width)]
        gains = [row(0), row(3), row(9), mine[0:1], row(6), row(19)]
        order = [1, 2, 4, 24, 25, 5, 26, 27, 10, 11, 12, None, 13, 7, 8, 20]
        for k, value in enumerate(gains):
            o_gains[k : k + 1, :] = value
        for k, at in enumerate(order):
            o_biases[k : k + 1, :] = mine[1:2] if at is None else row(at)
        o_taps[...] = vec[14:19]
        per = o_hidden.shape[1] // width
        for k in range(2):
            for t in range(per):
                at = 28 + k * per + t
                o_hidden[k : k + 1, t * width : (t + 1) * width] = row(at)

    late = []

    def turn(c_at, total, row, rows, out, lead):
        target = outs[out] if lead is None else outs[out].at[lead]
        columns = target.shape[1]
        height = target.shape[0] // ns
        there = row_view(target, shard * height + row, rows)
        copies = []
        for j in range(1, ns):
            peer = flip_bits(shard, j)
            copy = pltpu.make_async_remote_copy(
                src_ref=total.at[:, column_block(peer, columns)],
                dst_ref=there,
                send_sem=turn_send.at[c_at, j],
                recv_sem=turn_recv.at[c_at, j],
                device_id={"shard": peer},
                device_id_type=MESH,
            )
            copy.start()
            copies.append(copy)
        there[...] = total[:, column_block(shard, columns)]
        late.extend(copies)

    rides = []
    orders = ride_orders(nb)
    plain_target = outs[0].at[1]
    rider_a = Rider(batch, ride_send, ride_recv, 0)
    rider_b = Rider(batch, ride_send, ride_recv, 1)
    end_a = rider_a.double(ridden[0], plain_target, orders[0][0])
    end_b = rider_b.double(ridden[1], ride_fin, orders[1][0])

    movers = []
    for c in chunks:
        kind, out, lead = specs["arrays"][c.source]
        source, base, early, settle = ins[c.source], c.row, [], None
        if kind == "gather":
            near_land, far_land = rest.pop(0), rest.pop(0)
            whole, columns, rows = ins[c.source], c.columns, pl.ds(c.row, c.rows)
            far = flip_bits(shard, 2)
            state = {}

            def pre(at, src, dst, mask, c=c):
                copy = pltpu.make_async_remote_copy(
                    src_ref=src, dst_ref=dst, send_sem=pre_send.at[c.at, at], recv_sem=pre_recv.at[c.at, at],
                    device_id={"shard": flip_bits(shard, mask)}, device_id_type=MESH,
                )
                copy.start()
                return copy

            def first(near_land=near_land, whole=whole, columns=columns, rows=rows, state=state, pre=pre):
                state["n"] = [
                    pre(i, whole.at[rows, column_block(flip_bits(shard, m), columns)], near_land.at[i], 1)
                    for i, m in enumerate((1, 3))
                ]

            def second(
                near_land=near_land, far_land=far_land, whole=whole, columns=columns, rows=rows, state=state,
                pre=pre, far=far,
            ):
                for copy in state["n"]:
                    copy.wait()
                near_land[1] = b16(f32(near_land[1]) + f32(whole[rows, column_block(far, columns)]))
                state["f"] = pre(2, near_land.at[1], far_land, 2)

            def settle(
                near_land=near_land, far_land=far_land, whole=whole, columns=columns, rows=rows, state=state,
            ):
                state["f"].wait()
                far_land[...] = b16(
                    f32(far_land[...]) + f32(near_land[0]) + f32(whole[rows, column_block(shard, columns)])
                )

            early = [first, second]
            source, base = far_land, 0
        if kind == "turn":
            total = rest.pop(0)
            held = lambda off, size, total=total: row_view(total, off, size)

            def finish(c, total=total, out=out, lead=lead):
                turn(c.at, total, c.row, c.rows, out, lead)
        else:
            target = outs[out] if lead is None else outs[out].at[lead]
            held = lambda off, size, target=target, c=c: row_view(target, c.row + off, size)

            def finish(c):
                pass
        landings = [rest.pop(0) for _ in range(c.steps)]
        m = Mover(c, batch, source, base, held, landings, (send, recv), finish, early)
        m.settle_early = settle
        movers.append(m)
    starts, lag = [], specs["lag"]
    for i, m in enumerate(movers):
        starts.append(max(0, i // lag - len(m.early)))
    rounds = max(s + m.depth + 1 for s, m in zip(starts, movers))
    for r in range(rounds):
        if r == 1:
            vectors_on()
        if r == 2:
            end_b()
            turn(len(chunks), ride_fin, 0, ride_fin.shape[0], 1, 1)
        if r == 3:
            vectors_out()
            end_a()
        for s, m in zip(starts, movers):
            if 0 <= r - s <= m.depth:
                m.advance(r - s)
    for copy in late:
        copy.wait()


def tail_sum(arrays, ridden, sums, kinds, outputs, firsts, chunk_rows, hidden, ident):
    ns, nb = lax.axis_size("shard"), lax.axis_size("batch")
    low, full = jnp.bfloat16, jnp.float32
    chunks = []
    for i, a in enumerate(arrays):
        step = chunk_rows[i]
        columns = a.shape[1] // ns if kinds[i][0] == "gather" else a.shape[1]
        for row in range(0, a.shape[0], step):
            chunks.append(Chunk(len(chunks), i, row, step, columns, firsts[len(chunks) % len(firsts)], nb))
    depth = max(2 * c.steps for c in chunks)
    specs = dict(arrays=kinds, lag=2)
    width = sums[-1].shape[1]
    per = hidden // width
    small = -(-(28 + 2 * per) // 8) * 8
    dma = pltpu.SemaphoreType.DMA
    n = len(chunks)
    scratch = [
        dma((n, depth)), dma((n, depth)), dma((n + 1, ns)), dma((n + 1, ns)), dma((n, 3)), dma((n, 3)),
        dma((2,)), dma((2,)), dma((ns,)), dma((ns,)), dma((nb,)), dma((nb,)),
        pltpu.VMEM((ns, 24, width), full), pltpu.VMEM((ns, 24, width), full),
        pltpu.VMEM((small, width), full), pltpu.VMEM((nb, small, width), full),
        pltpu.VMEM((2 * ridden[1].shape[0], ridden[1].shape[1]), low),
    ]
    for c in chunks:
        if kinds[c.source][0] == "gather":
            scratch += [pltpu.VMEM((2, c.rows, c.columns), low), pltpu.VMEM((c.rows, c.columns), low)]
        if kinds[c.source][0] == "turn":
            scratch.append(pltpu.VMEM((c.rows, c.columns), low))
        scratch += [pltpu.VMEM(shape, low) for shape in c.landings]
    shape = jax.ShapeDtypeStruct
    shapes = [shape(s, low) for s in outputs]
    shapes += [shape((6, width), full), shape((16, width), full), shape((5, width), full), shape((2, hidden), full)]
    operands = list(arrays) + list(ridden) + list(sums)
    return pl.pallas_call(
        functools.partial(tail_body, specs, chunks, ns, nb, len(arrays), len(outputs)),
        out_shape=shapes,
        in_specs=[VMEM_SPEC] * len(operands),
        out_specs=[VMEM_SPEC] * len(shapes),
        scratch_shapes=scratch,
        compiler_params=pltpu.CompilerParams(
            collective_id=ident, has_side_effects=True, vmem_limit_bytes=62 << 20
        ),
        name="tail_sum",
    )(*operands)


class Links:
    def __init__(self, send, recv):
        self.send, self.recv, self.count = send, recv, 0
        s = lax.axis_index("shard")
        self.shard = s
        self.near = {"shard": flip_bits(s, 1)}
        self.far = {"shard": flip_bits(s, 2)}
        self.across = {"shard": flip_bits(s, 3)}

    def greet(self, devices):
        barrier = pltpu.get_barrier_semaphore()
        for device in devices:
            pl.semaphore_signal(barrier, inc=1, device_id=device, device_id_type=MESH)
        pl.semaphore_wait(barrier, len(devices))

    def go(self, src, dst, device):
        at = self.count
        self.count += 1
        copy = pltpu.make_async_remote_copy(
            src_ref=src, dst_ref=dst, send_sem=self.send.at[at], recv_sem=self.recv.at[at],
            device_id=device, device_id_type=MESH,
        )
        copy.start()
        return copy


def gather_work_scatter(links, x, work, part, send, land, cross, land_cross, tick=None):
    half = x.shape[1] // 2
    out = [
        links.go(x.at[0, pl.ds(h * half, half)], x.at[2 + h, pl.ds(0, half)], links.far)
        for h in range(2)
    ]
    near = links.go(x.at[0], x.at[1], links.near)

    def keep(cols, value):
        part[0, :, cols] = value

    work(0, keep)
    near.wait()

    def give(cols, value):
        send[0, :, cols] = b16(value[:half])
        send[1, :, cols] = b16(value[half:])

    work(1, give)
    last = [links.go(send.at[pl.ds(0, 2)], land.at[pl.ds(0, 2)], links.near)]
    if tick is not None:
        tick()
    for h in range(2):
        out[h].wait()
        on = links.go(x.at[2 + h, pl.ds(0, half)], x.at[2 + h, pl.ds(half, half)], links.near)
        on.wait()

        def split(cols, value, h=h):
            part[1, h * half : (h + 1) * half, cols] = value[:half]
            send[2 + h, :, cols] = b16(value[half:])

        work(2 + h, split)
        back = links.go(send.at[2 + h], land.at[2 + h], links.near)
        back.wait()
        cross[h] = b16(part[1, h * half : (h + 1) * half] + f32(land[2 + h]))
        last.append(links.go(cross.at[h], land_cross.at[h], links.far))

    def settle():
        for copy in last:
            copy.wait()

    def total(h):
        rows = slice(h * half, (h + 1) * half)
        return part[0, rows] + f32(land[h]) + f32(land_cross[h])

    return settle, total


def gws_scratch(rows, columns):
    half = rows // 2
    return [
        pltpu.VMEM((2, rows, columns), jnp.float32),
        pltpu.VMEM((4, half, columns), jnp.bfloat16),
        pltpu.VMEM((4, half, columns), jnp.bfloat16),
        pltpu.VMEM((2, half, columns), jnp.bfloat16),
        pltpu.VMEM((2, half, columns), jnp.bfloat16),
        pltpu.SemaphoreType.DMA((16,)),
        pltpu.SemaphoreType.DMA((16,)),
    ]


def tiles(total, size):
    def over(body):
        pl.loop(0, total // size)(
            lambda n: body(pl.ds(pl.multiple_of(n * size, size), size))
        )

    return over


def ffn_forward_body(
    which, at_rows, rows_ref, pack, b_ref, w_rows, ffn_in, out_ref, hid_out, act_out, slope_out,
    hid, act, slope, part, send, land, cross, land_cross, send_sem, recv_sem, w_in, local_sem, flush_sem,
):
    flush = Flush(flush_sem)
    links = Links(send_sem, recv_sem)
    load = pltpu.make_async_copy(ffn_in.at[which], w_in, local_sem)
    load.start()
    links.greet([links.near, links.far])
    hid[0] = b16(
        norm_rows(rows_ref[...], vector_row(pack, at_rows[0]), vector_row(pack, at_rows[1]))
    )
    load.wait()
    columns = hid.shape[2]

    def work(block, emit):
        @tiles(w_in.shape[1], 512)
        def _(cols):
            pre = dot_rows(hid[block], w_in[:, cols]) + b_ref[which : which + 1, cols]
            gate = jax.nn.sigmoid(pre)
            act[block, :, cols] = b16(pre * gate)
            slope[block, :, cols] = b16(gate * (1.0 + pre * (1.0 - gate)))

        @tiles(columns, 512)
        def _(cols):
            emit(cols, dot_rows(act[block], w_rows[:, cols]))

    settle, total = gather_work_scatter(links, hid, work, part, send, land, cross, land_cross)
    for pair in ((hid, hid_out), (act, act_out), (slope, slope_out)):
        flush.go(*pair)
    settle()
    half = rows_ref.shape[0] // 2
    for h in range(2):
        rows = slice(h * half, (h + 1) * half)
        out_ref[rows] = rows_ref[rows] + 0.5 * (total(h) + vector_row(pack, at_rows[2]))
    flush.settle()


def ffn_forward(rows_in, pack, b_in, w_rows, ffn_in, which, at_rows, ident):
    rows, features = rows_in.shape
    hidden = ffn_in.shape[2]
    shape = lambda c: jax.ShapeDtypeStruct((4, rows, c), jnp.bfloat16)
    out, hid, act, slope = pl.pallas_call(
        functools.partial(ffn_forward_body, which, at_rows),
        out_shape=[
            jax.ShapeDtypeStruct((rows, features), jnp.float32),
            shape(features), shape(hidden), shape(hidden),
        ],
        in_specs=[VMEM_SPEC] * 4 + [pl.BlockSpec(memory_space=pl.ANY)],
        out_specs=[VMEM_SPEC] + [HBM_SPEC] * 3,
        scratch_shapes=[pltpu.VMEM((4, rows, c), jnp.bfloat16) for c in (features, hidden, hidden)]
        + gws_scratch(rows, features)
        + [
            pltpu.VMEM((features, hidden), jnp.bfloat16), pltpu.SemaphoreType.DMA, pltpu.SemaphoreType.DMA((3,)),
        ],
        compiler_params=pltpu.CompilerParams(
            collective_id=ident, has_side_effects=True, vmem_limit_bytes=60 << 20
        ),
        name="ffn_forward",
    )(rows_in, pack, b_in, w_rows, ffn_in)
    return out, (hid, act, slope)


def norm_parts(rows):
    row_mean = jnp.mean(rows, axis=-1, keepdims=True)
    centered = rows - row_mean
    inverse = lax.rsqrt(jnp.mean(centered * centered, axis=-1, keepdims=True) + epsilon)
    return centered * inverse, inverse


def norm_slope(grad, scaled, inverse, gain):
    inner = grad * gain
    return inverse * (
        inner
        - jnp.mean(inner, axis=-1, keepdims=True)
        - scaled * jnp.mean(inner * scaled, axis=-1, keepdims=True)
    )


def ffn_back_body(which, gain_at, nb, *refs):
    stages = []
    if which == 1:
        last_rows, cotangent, *refs = refs
        rows_ref, pack, hid, act, slope, w_rows, ffn_in, result, out_ref, gw_in, gw_out, sums_ref, *refs = refs
        stream_ref, *refs = refs
    else:
        stream_ref, ride_a, ride_b, *refs = refs
        rows_ref, pack, hid, act, slope, w_rows, ffn_in, out_ref, gw_in, gw_out, sums_ref, *refs = refs
        out_a, out_b, ride_send, ride_recv, *refs = refs
    grad, inner, part, send, land, cross, land_cross, send_sem, recv_sem, w_in, local_sem, *refs = refs
    links = Links(send_sem, recv_sem)
    load = pltpu.make_async_copy(ffn_in.at[which], w_in, local_sem)
    load.start()
    batch = lax.axis_index("batch")
    orders = ride_orders(nb)
    devices = [links.near, links.far]
    if which == 0:
        devices += [{"batch": flip_bits(batch, 1 << k)} for k in orders[0]]
    links.greet(devices)
    if which == 0:
        steps = len(orders[0]) - 1
        for at, (start, end) in enumerate(((ride_a, out_a), (ride_b, out_b))):
            rider = Rider(batch, ride_send, ride_recv, at * steps)
            between = refs[at * (steps - 1) : (at + 1) * (steps - 1)]
            stages.append(
                rider.chain([start, *between, end], orders[at][:0:-1], rider.double)
            )
    else:
        live = f32(pack[links.shard, 27:28, 0:1])
        mask = f32(f32(lax.broadcasted_iota(jnp.int32, (rows_ref.shape[0], 1), 0)) < live)
        scaled, inverse = norm_parts(last_rows[...])
        gain = vector_row(pack, 5)
        result[...] = (scaled * gain + vector_row(pack, 21)) * mask
        given = cotangent[...] * mask
        stream_ref[...] = norm_slope(given, scaled, inverse, gain)
        ends = (
            jnp.sum(given * scaled, axis=0, keepdims=True),
            jnp.sum(given, axis=0, keepdims=True),
        )

    def tick():
        for chain in stages:
            if chain:
                chain.pop(0)()

    tick()
    grad[0] = b16(0.5 * stream_ref[...])
    load.wait()
    columns = grad.shape[2]
    hidden = w_in.shape[1]

    def work(block, emit):
        @tiles(hidden, 512)
        def _(cols):
            wide = dot_back(grad[block], w_rows[cols, :])
            inner[block, :, cols] = b16(wide * f32(slope[block, :, cols]))

        @tiles(columns, 512)
        def _(cols):
            emit(cols, dot_back(inner[block], w_in[cols, :]))

    settle, total = gather_work_scatter(
        links, grad, work, part, send, land, cross, land_cross, None
    )
    rows = stream_ref.shape[0]
    flat = lambda ref: ref[...].reshape(4 * rows, ref.shape[2])

    @tiles(hidden, 256)
    def _(cols):
        left = act[:, :, cols].reshape(4 * rows, 256)
        gw_out[cols, :] = b16(dot_over(left, flat(grad)))

    tick()

    @tiles(hidden, 256)
    def _(cols):
        right = inner[:, :, cols].reshape(4 * rows, 256)
        gw_in[:, cols] = b16(dot_over(flat(hid), right))
        sums_ref[3:4, cols] = jnp.sum(f32(right), axis=0, keepdims=True)

    settle()
    gain = vector_row(pack, gain_at)
    sums_ref[0:3, :] = jnp.zeros((3, columns), jnp.float32)
    sums_ref[4:8, :] = jnp.zeros((4, columns), jnp.float32)
    if which == 1:
        sums_ref[4:5, :], sums_ref[5:6, :] = ends
    sums_ref[2:3, :] = jnp.sum(f32(grad[0]), axis=0, keepdims=True)
    half = rows // 2
    for h in range(2):
        at = slice(h * half, (h + 1) * half)
        scaled, inverse = norm_parts(rows_ref[at])
        given = total(h)
        out_ref[at] = stream_ref[at] + norm_slope(given, scaled, inverse, gain)
        sums_ref[0:1, :] += jnp.sum(given * scaled, axis=0, keepdims=True)
        sums_ref[1:2, :] += jnp.sum(given, axis=0, keepdims=True)
    for chain in stages:
        while chain:
            chain.pop(0)()


def ffn_back(given, rows_in, pack, saved, w_rows, ffn_in, which, gain_at, ident):
    rows, features = rows_in.shape
    hidden = ffn_in.shape[2]
    nb = lax.axis_size("batch")
    low, full = jnp.bfloat16, jnp.float32
    shape = jax.ShapeDtypeStruct
    shapes = [
        shape((rows, features), full), shape((features, hidden), low), shape((hidden, features), low),
        shape((8, features), full),
    ]
    scratch = []
    if which == 1:
        shapes = [shape((rows, features), full)] + shapes
        scratch = [pltpu.VMEM((rows, features), full)]
    else:
        first, steps = given[1].shape[0], nb.bit_length() - 2
        shapes += [shape((first << steps, r.shape[1]), low) for r in given[1:]]
        scratch = [pltpu.SemaphoreType.DMA((2 * steps,)), pltpu.SemaphoreType.DMA((2 * steps,))]
    extra = []
    if which == 0:
        for r in given[1:]:
            extra += [pltpu.VMEM((first << k, r.shape[1]), low) for k in range(1, steps)]
    return pl.pallas_call(
        functools.partial(ffn_back_body, which, gain_at, nb),
        out_shape=shapes,
        in_specs=[VMEM_SPEC] * (len(given) + 6) + [pl.BlockSpec(memory_space=pl.ANY)],
        out_specs=[VMEM_SPEC] * len(shapes),
        scratch_shapes=scratch
        + [
            pltpu.VMEM((4, rows, features), low),
            pltpu.VMEM((4, rows, hidden), low),
        ]
        + gws_scratch(rows, features)
        + [pltpu.VMEM((features, hidden), low), pltpu.SemaphoreType.DMA]
        + extra,
        compiler_params=pltpu.CompilerParams(
            collective_id=ident, has_side_effects=True, vmem_limit_bytes=60 << 20
        ),
        name="ffn_back_%d" % which,
    )(*given, rows_in, pack, *saved, w_rows, ffn_in)


class Fetch:
    def __init__(self, links, batch, local_sem):
        self.links, self.local_sem = links, local_sem
        self.quarter = bit_of(batch, 0) + 2 * bit_of(batch, 1)
        self.peers = [{"batch": flip_bits(batch, 1)}, {"batch": flip_bits(batch, 2)}]

    def flow(self, source_rows, target, blocks, rows):
        links, size, held = self.links, rows // 8, {}
        span = lambda q, p: pl.ds(pl.multiple_of(q * (2 * size) + p * size, 16), size)
        mine = self.quarter
        own = blocks[0]

        def first():
            for p in range(2):
                for t, device, _ in blocks[1:]:
                    held["y", p, t] = links.go(
                        source_rows(t, mine * (2 * size) + p * size, size),
                        target.at[span(mine, p), own],
                        device,
                    )

        def pass_on(p, q, t, block, way):
            there = target.at[span(q, p), block]
            return links.go(there, there, self.peers[way])

        def second(p):
            def run():
                for t, _, block in blocks[1:]:
                    held["y", p, t].wait()
                    held["a", p, t] = pass_on(p, mine, t, block, p)

            return run

        def third(p):
            def run():
                other = flip_bits(mine, 1 << p)
                for t, _, block in blocks[1:]:
                    held["a", p, t].wait()
                    held["b", p, t] = pass_on(p, mine, t, block, 1 - p)
                    held["c", p, t] = pass_on(p, other, t, block, 1 - p)

            return run

        def last():
            for p in range(2):
                for t, _, _ in blocks[1:]:
                    held["b", p, t].wait()
                    held["c", p, t].wait()

        return [first, second(0), second(1), third(0), third(1), last]

    def columns(self, source, target, at):
        links, (rows, columns) = self.links, source.shape
        far = flip_bits(links.shard, 2)
        own = column_block(links.shard, columns)
        far_block = column_block(far, columns)
        row = lambda t, start, size: source.at[pl.ds(pl.multiple_of(start, 16), size)]
        stages = self.flow(row, target, [own, (2, links.far, far_block)], rows)
        held = {}

        def first():
            stages[0]()
            held["own"] = pltpu.make_async_copy(source, target.at[:, own], self.local_sem.at[at])
            held["own"].start()
            held["near"] = links.go(source, target.at[:, own], links.near)

        def pass_near():
            stages[-1]()
            held["on"] = links.go(target.at[:, far_block], target.at[:, far_block], links.near)

        def finish():
            held["on"].wait()
            held["near"].wait()
            held["own"].wait()

        return [first] + stages[1:-1] + [pass_near, finish]

    def rows(self, source, target, at):
        links, rows = self.links, target.shape[0]
        columns = source.shape[1]
        index = [flip_bits(links.shard, m) for m in range(4)]
        own = column_block(links.shard, columns)
        row = lambda m, start, size: source.at[pl.ds(pl.multiple_of(index[m] * rows + start, 16), size)]
        blocks = [own] + [
            (m, device, column_block(index[m], columns)) for m, device in ((2, links.far), (3, links.across))
        ]
        stages = self.flow(row, target, blocks, rows)
        held = {}

        def first():
            stages[0]()
            held["own"] = pltpu.make_async_copy(row(0, 0, rows), target.at[:, own], self.local_sem.at[at])
            held["own"].start()
            held["near"] = links.go(row(1, 0, rows), target.at[:, own], links.near)

        def last():
            stages[-1]()
            held["near"].wait()
            held["own"].wait()

        return [first] + stages[1:-1] + [last]


class Flush:
    def __init__(self, sem):
        self.sem, self.open = sem, []

    def go(self, src, dst):
        copy = pltpu.make_async_copy(src, dst, self.sem.at[len(self.open)])
        copy.start()
        self.open.append(copy)

    def settle(self):
        for copy in self.open:
            copy.wait()


def vector_row(pack, row):
    return f32(jnp.concatenate([pack[t, row : row + 1, :] for t in range(pack.shape[0])], 1))


def scatter_late(links, work, part, send, land, cross, land_cross):
    half = send.shape[1]
    backs = []
    for h in range(2):

        def split(cols, value, h=h):
            part[1, h * half : (h + 1) * half, cols] = value[:half]
            send[2 + h, :, cols] = b16(value[half:])

        work(2 + h, split)
        backs.append(links.go(send.at[2 + h], land.at[2 + h], links.near))
    last = []
    for h in range(2):
        backs[h].wait()
        cross[h] = b16(part[1, h * half : (h + 1) * half] + f32(land[2 + h]))
        last.append(links.go(cross.at[h], land_cross.at[h], links.far))

    def give(cols, value):
        send[0, :, cols] = b16(value[:half])
        send[1, :, cols] = b16(value[half:])

    work(1, give)
    last.append(links.go(send.at[pl.ds(0, 2)], land.at[pl.ds(0, 2)], links.near))

    def keep(cols, value):
        part[0, :, cols] = value

    work(0, keep)

    def settle():
        for copy in last:
            copy.wait()

    def total(h):
        rows = slice(h * half, (h + 1) * half)
        return part[0, rows] + f32(land[h]) + f32(land_cross[h])

    return settle, total


def opening_body(
    rows_ref, pack_in, b_ref, base_ref, pos_ref, ffn_in, ffn_out, out_proj,
    out_ref, pack, table, proj, w_out, hid_out, act_out, slope_out, w_rows_out,
    hid, act, slope, w_rows, w_in, part, send, land, cross, land_cross, send_sem, recv_sem, local_sem, flush_sem,
):
    flush = Flush(flush_sem)
    batch = lax.axis_index("batch")
    links = Links(send_sem, recv_sem)
    fetch = Fetch(links, batch, local_sem)
    load = pltpu.make_async_copy(ffn_in.at[0], w_in, local_sem.at[0])
    load.start()
    links.greet([links.near, links.far, links.across] + fetch.peers)
    small = [
        links.go(pack_in, pack.at[links.shard], device)
        for device in (links.far, links.across, links.near)
    ]
    down = fetch.rows(ffn_out.at[0], w_rows, 1)
    down.pop(0)()
    pack[links.shard] = pack_in[...]
    for copy in small:
        copy.wait()
    rows, features = rows_ref.shape
    hid[0] = b16(norm_rows(rows_ref[...], vector_row(pack, 0), vector_row(pack, 6)))
    half = rows // 2
    out = [
        links.go(hid.at[0, pl.ds(h * half, half)], hid.at[2 + h, pl.ds(0, half)], links.far)
        for h in range(2)
    ]
    near = links.go(hid.at[0], hid.at[1], links.near)
    load.wait()

    def up(block):
        @tiles(w_in.shape[1], 512)
        def _(cols):
            pre = dot_rows(hid[block], w_in[:, cols]) + b_ref[0:1, cols]
            gate = jax.nn.sigmoid(pre)
            act[block, :, cols] = b16(pre * gate)
            slope[block, :, cols] = b16(gate * (1.0 + pre * (1.0 - gate)))

    up(0)
    near.wait()
    up(1)
    down.pop(0)()
    down.pop(0)()
    lanes = features // 2

    @pl.loop(0, table.shape[0] // 16)
    def _(i):
        at = pl.ds(pl.multiple_of(i * 16, 16), 16)
        s_a, c_a = base_ref[pl.ds(16 + i, 1), 0:lanes], base_ref[pl.ds(16 + i, 1), lanes:]
        s_b, c_b = base_ref[0:16, 0:lanes], base_ref[0:16, lanes:]
        table[at, 0:lanes] = b16(s_a * c_b + c_a * s_b)
        table[at, lanes:] = b16(c_a * c_b - s_a * s_b)

    proj[...] = b16(dot_rows(table[...], pos_ref[...]))
    other = fetch.columns(out_proj, w_out, 2)
    for h in range(2):
        out[h].wait()
        on = links.go(hid.at[2 + h, pl.ds(0, half)], hid.at[2 + h, pl.ds(half, half)], links.near)
        on.wait()
        if h == 1:
            other.pop(0)()
        up(2 + h)
        down.pop(0)()
    for pair in ((hid, hid_out), (act, act_out), (slope, slope_out)):
        flush.go(*pair)
    while down:
        down.pop(0)()
    flush.go(w_rows, w_rows_out)

    def work(block, emit):
        @tiles(features, 512)
        def _(cols):
            emit(cols, dot_rows(act[block], w_rows[:, cols]))

    settle, total = scatter_late(links, work, part, send, land, cross, land_cross)
    while other:
        other.pop(0)()
    settle()
    bias = vector_row(pack, 7)
    for h in range(2):
        at = slice(h * half, (h + 1) * half)
        out_ref[at] = rows_ref[at] + 0.5 * (total(h) + bias)
    flush.settle()


ANY_SPEC = pl.BlockSpec(memory_space=pl.ANY)


def link_scratch(count, local):
    return [
        pltpu.SemaphoreType.DMA((count,)),
        pltpu.SemaphoreType.DMA((count,)),
        pltpu.SemaphoreType.DMA((local,)),
    ]


def opening(rows_in, pack_in, b_in, base, pos_proj, ffn_in, ffn_out, out_proj, ident):
    ns = lax.axis_size("shard")
    rows, features = rows_in.shape
    hidden = ffn_in.shape[2]
    shape = jax.ShapeDtypeStruct
    low = jnp.bfloat16
    positions = 2 * rows
    return pl.pallas_call(
        opening_body,
        out_shape=[
            shape((rows, features), jnp.float32),
            shape((ns,) + pack_in.shape, low),
            shape((positions, features), low),
            shape((positions, pos_proj.shape[1]), low),
            shape((features, features), low),
            shape((4, rows, features), low), shape((4, rows, hidden), low), shape((4, rows, hidden), low),
            shape((hidden, features), low),
        ],
        in_specs=[VMEM_SPEC] * 5 + [ANY_SPEC] * 3,
        out_specs=[VMEM_SPEC] * 5 + [HBM_SPEC] * 4,
        scratch_shapes=[
            pltpu.VMEM((4, rows, features), low), pltpu.VMEM((4, rows, hidden), low),
            pltpu.VMEM((4, rows, hidden), low), pltpu.VMEM((hidden, features), low),
            pltpu.VMEM((features, hidden), low),
        ]
        + gws_scratch(rows, features)[:5]
        + link_scratch(48, 4)
        + [pltpu.SemaphoreType.DMA((4,))],
        compiler_params=pltpu.CompilerParams(
            collective_id=ident, has_side_effects=True, vmem_limit_bytes=60 << 20
        ),
        name="opening",
    )(rows_in, pack_in, b_in, base, pos_proj, ffn_in, ffn_out, out_proj)


def mix_body(
    heads, size, rows_ref, pack, own_ref, w_qkv, proj, w_out, conv_in,
    out_ref, with_u, with_v, key, value, mix, wc_in, hid_out, soft_out,
    hid, soft_ref, turned, send_sem, recv_sem, local_sem, flush_sem,
):
    flush = Flush(flush_sem)
    batch = lax.axis_index("batch")
    links = Links(send_sem, recv_sem)
    fetch = Fetch(links, batch, local_sem)
    scale = 1.0 / math.sqrt(size)
    rows, features = rows_ref.shape
    half = rows // 2
    links.greet([links.near, links.far, links.across] + fetch.peers)
    hid[0] = b16(norm_rows(rows_ref[...], vector_row(pack, 1), vector_row(pack, 8)))
    out = [
        links.go(hid.at[0, pl.ds(h * half, half)], hid.at[2, pl.ds(h * half, half)], links.far)
        for h in range(2)
    ]
    near = links.go(hid.at[0], hid.at[1], links.near)
    own = f32(own_ref[...])
    keys = f32(lax.broadcasted_iota(jnp.int32, (rows, rows), 1))

    def attend(slot):
        hidden = hid[slot]
        query = dot_rows(hidden, w_qkv[0]) + own[3:4]
        with_u[slot] = b16(query + own[6:7])
        with_v[slot] = b16(query + own[7:8])
        key[slot] = b16(dot_rows(hidden, w_qkv[1]))
        value[slot] = b16(dot_rows(hidden, w_qkv[2]) + own[4:5])
        live = f32(pack[flip_bits(links.shard, slot), 27:28, 0:1])
        for h in range(heads):
            cols = slice(h * size, (h + 1) * size)
            wide = dot_back(with_v[slot, :, cols], proj[:, cols])
            moved = pltpu.roll(wide, rows + 1, 1, stride=1, stride_axis=0)[:, :rows]
            raw = dot_back(with_u[slot, :, cols], key[slot, :, cols]) + moved
            scores = jnp.where(keys < live, raw * scale, -1e30)
            grown = jnp.exp(scores - jnp.max(scores, axis=-1, keepdims=True))
            soft = grown / jnp.sum(grown, axis=-1, keepdims=True)
            soft_ref[slot, :, h * rows : (h + 1) * rows] = soft
            mix[slot, :, cols] = b16(dot_rows(b16(soft), value[slot, :, cols]))

    last = []
    attend(0)
    turned[links.shard] = mix[0]
    near.wait()
    attend(1)
    last.append(links.go(mix.at[1], turned.at[links.shard], links.near))
    on = []
    for h in range(2):
        out[h].wait()
        part = hid.at[2, pl.ds(h * half, half)]
        on.append(links.go(part, hid.at[3, pl.ds(h * half, half)], links.near))
    other = fetch.columns(conv_in, wc_in, 0)
    other.pop(0)()
    attend(2)
    last.append(links.go(mix.at[2], turned.at[links.shard], links.far))
    other.pop(0)()
    other.pop(0)()
    for copy in on:
        copy.wait()
    flush.go(hid, hid_out)
    attend(3)
    last.append(links.go(mix.at[3], turned.at[links.shard], links.across))
    flush.go(soft_ref, soft_out)
    other.pop(0)()
    other.pop(0)()
    for copy in last:
        copy.wait()
    bias = vector_row(pack, 11)
    width = mix.shape[2]
    total = rows_ref[...] + bias
    for t in range(turned.shape[0]):
        total = total + dot_rows(turned[t], w_out[t * width : (t + 1) * width])
    out_ref[...] = total
    while other:
        other.pop(0)()
    flush.settle()


def mix_forward(rows_in, pack, own_biases, qkv_proj, proj, w_out, conv_in, heads, ident):
    ns = lax.axis_size("shard")
    rows, features = rows_in.shape
    width = features // ns
    shape = jax.ShapeDtypeStruct
    low = jnp.bfloat16
    narrow = shape((ns, rows, width), low)
    return pl.pallas_call(
        functools.partial(mix_body, heads, width // heads),
        out_shape=[
            shape((rows, features), jnp.float32),
            narrow, narrow, narrow, narrow, narrow,
            shape((conv_in.shape[0], ns * conv_in.shape[1]), low),
            shape((ns, rows, features), low),
            shape((ns, rows, heads * rows), jnp.float32),
        ],
        in_specs=[VMEM_SPEC] * 6 + [ANY_SPEC],
        out_specs=[VMEM_SPEC] * 7 + [HBM_SPEC] * 2,
        scratch_shapes=[
            pltpu.VMEM((ns, rows, features), low),
            pltpu.VMEM((ns, rows, heads * rows), jnp.float32),
            pltpu.VMEM((ns, rows, width), low),
        ]
        + link_scratch(24, 2)
        + [pltpu.SemaphoreType.DMA((2,))],
        compiler_params=pltpu.CompilerParams(
            collective_id=ident, has_side_effects=True, vmem_limit_bytes=60 << 20
        ),
        name="mix_forward",
    )(rows_in, pack, own_biases, qkv_proj, proj, w_out, conv_in)


def pack_rows(ref, at, row):
    for i in range(row.shape[1] // 128):
        ref[at + i : at + i + 1, :] = row[:, i * 128 : (i + 1) * 128]


def unpack_rows(value, at, lanes):
    return jnp.concatenate([value[at + i : at + i + 1, :] for i in range(lanes)], 1)


def everywhere(links, nb, source, mid, land_s, land_b, result, small, sems):
    s, b = links.shard, lax.axis_index("batch")
    ns = land_s.shape[0]
    ss, rs, sb, rb = sems
    first = exchange("shard", s, ns, source, land_s, ss, rs)
    for copy in first:
        copy.start()
    land_s[s] = source[...]
    for copy in first:
        copy.wait()
    mid[...] = sum_slots(land_s, ns)
    second = exchange("batch", b, nb, mid, land_b, sb, rb)
    for copy in second:
        copy.start()
    land_b[b] = mid[...]
    small()
    for copy in second:
        copy.wait()
    return sum_slots(land_b, nb)


def conv_body(
    nb, rows_ref, pack, w_in, conv_out, ffn_out,
    out_ref, hid, open_ref, gate_ref, gated_ref, scaled_ref, act, slope, stats, w_out, w_rows,
    padded, source, mid, land_s, land_b, ss, rs, sb, rb, send_sem, recv_sem, local_sem,
):
    batch = lax.axis_index("batch")
    links = Links(send_sem, recv_sem)
    fetch = Fetch(links, batch, local_sem)
    rows, features = rows_ref.shape
    ns = land_s.shape[0]
    links.greet(
        [links.near, links.far, links.across]
        + [{"batch": lax.rem(batch + j, nb)} for j in range(1, nb)]
    )
    out_fetch = fetch.columns(conv_out, w_out, 0)
    out_fetch.pop(0)()
    down = fetch.rows(ffn_out.at[1], w_rows, 1)
    down.pop(0)()
    live = f32(pack[links.shard, 27:28, 0:1])
    mask = f32(f32(lax.broadcasted_iota(jnp.int32, (rows, 1), 0)) < live)
    hid[...] = b16(norm_rows(rows_ref[...], vector_row(pack, 2), vector_row(pack, 14)))
    bias_v, bias_g = vector_row(pack, 15), vector_row(pack, 16)
    lead = 8
    tile = 512
    padded[0:lead, :] = jnp.zeros((lead, features), jnp.float32)
    padded[lead + rows :, :] = jnp.zeros((lead, features), jnp.float32)
    for n in range(features // tile):
        cols = slice(n * tile, (n + 1) * tile)
        left = dot_rows(hid[...], w_in[:, cols]) + bias_v[:, cols]
        right = dot_rows(hid[...], w_in[:, features + n * tile : features + (n + 1) * tile])
        gate = jax.nn.sigmoid(right + bias_g[:, cols])
        opened = gate * mask
        gated = left * opened
        open_ref[:, cols] = b16(opened)
        gate_ref[:, cols] = b16(gated * (1.0 - gate))
        gated_ref[:, cols] = b16(gated)
        padded[lead : lead + rows, cols] = gated
    for _ in range(4):
        out_fetch.pop(0)()
    taps = 5
    total = 0.0
    for k in range(taps):
        at = lead - (taps - 1) // 2 + k
        total = total + padded[at : at + rows, :] * vector_row(pack, 22 + k)
    live_total = total * mask
    lanes = features // 128
    pack_rows(source, 0, jnp.sum(live_total, axis=0, keepdims=True))
    pack_rows(source, lanes, jnp.sum(live_total * total, axis=0, keepdims=True))
    source[2 * lanes : 2 * lanes + 8, :] = jnp.broadcast_to(live, (8, 128))
    scaled_ref[...] = total

    sums = everywhere(links, nb, source, mid, land_s, land_b, None, out_fetch.pop(0), (ss, rs, sb, rb))
    down.pop(0)()
    down.pop(0)()
    frames = sums[2 * lanes : 2 * lanes + 1, 0:1]
    mean = unpack_rows(sums, 0, lanes) / frames
    inverse = lax.rsqrt(unpack_rows(sums, lanes, lanes) / frames - mean * mean + epsilon)
    stats[0:1, :] = inverse
    stats[1:2, :] = jnp.broadcast_to(frames, (1, features))
    stats[2:8, :] = jnp.zeros((6, features), jnp.float32)
    scaled = (scaled_ref[...] - mean) * inverse
    scaled_ref[...] = scaled
    normed = scaled * vector_row(pack, 3) + vector_row(pack, 17)
    gate = jax.nn.sigmoid(normed)
    act[...] = b16(normed * gate)
    slope[...] = b16(gate * (1.0 + normed * (1.0 - gate)))
    while out_fetch:
        out_fetch.pop(0)()
    down.pop(0)()
    out_ref[...] = rows_ref[...] + (dot_rows(act[...], w_out[...]) + vector_row(pack, 18))
    while down:
        down.pop(0)()


def conv_forward(rows_in, pack, w_in, conv_out, ffn_out, ident):
    ns, nb = lax.axis_size("shard"), lax.axis_size("batch")
    rows, features = rows_in.shape
    shape = jax.ShapeDtypeStruct
    low, full = jnp.bfloat16, jnp.float32
    plain = shape((rows, features), low)
    small = (24, 128)
    return pl.pallas_call(
        functools.partial(conv_body, nb),
        out_shape=[
            shape((rows, features), full), plain, plain, plain, plain,
            shape((rows, features), full), plain, plain, shape((8, features), full),
            shape((features, features), low),
            shape((ffn_out.shape[1] // ns, features), low),
        ],
        in_specs=[VMEM_SPEC] * 3 + [ANY_SPEC] * 2,
        out_specs=[VMEM_SPEC] * 11,
        scratch_shapes=[
            pltpu.VMEM((rows + 16, features), full),
            pltpu.VMEM(small, full), pltpu.VMEM(small, full),
            pltpu.VMEM((ns,) + small, full), pltpu.VMEM((nb,) + small, full),
            pltpu.SemaphoreType.DMA((ns,)), pltpu.SemaphoreType.DMA((ns,)),
            pltpu.SemaphoreType.DMA((nb,)), pltpu.SemaphoreType.DMA((nb,)),
        ]
        + link_scratch(32, 3),
        compiler_params=pltpu.CompilerParams(
            collective_id=ident, has_side_effects=True, vmem_limit_bytes=60 << 20
        ),
        name="conv_forward",
    )(rows_in, pack, w_in, conv_out, ffn_out)


def conv_back_body(
    nb, stream_ref, rows_ref, pack, w_in, w_out, hid, open_ref, gate_ref, gated_ref, scaled_ref, act, slope, stats,
    ride_a, ride_b, out_ref, gw_out, gw_in, sums_ref, half_a, half_b,
    padded, normed, grad, inner, source, mid, land_s, land_b, ss, rs, sb, rb, send_sem, recv_sem,
):
    batch = lax.axis_index("batch")
    links = Links(send_sem, recv_sem)
    rows, features = rows_ref.shape
    links.greet(
        [links.near, links.far, links.across]
        + [{"batch": lax.rem(batch + j, nb)} for j in range(1, nb)]
    )
    orders = ride_orders(nb)
    pieces = 4
    ride = [
        Rider(batch, send_sem, recv_sem, at * pieces).halve_pieces(source_ref, landing, orders[at][0], pieces)
        for at, (source_ref, landing) in enumerate(((ride_a, half_a), (ride_b, half_b)))
    ]
    for start, _ in ride:
        start(0)
    lanes = features // 128
    lead, tile, taps = 8, 512, 5
    grad[...] = b16(stream_ref[...])
    gain = vector_row(pack, 3)
    sums_ref[...] = jnp.zeros_like(sums_ref)
    for n in range(features // tile):
        cols = slice(n * tile, (n + 1) * tile)
        value = dot_back(grad[...], w_out[cols, :]) * f32(slope[:, cols])
        normed[:, cols] = value
        for at, total in (
            (0, jnp.sum(value, axis=0, keepdims=True)),
            (lanes, jnp.sum(value * scaled_ref[:, cols], axis=0, keepdims=True)),
        ):
            for i in range(tile // 128):
                row = at + n * (tile // 128) + i
                source[row : row + 1, :] = total[:, i * 128 : (i + 1) * 128]

    def meanwhile():
        @tiles(features, 256)
        def _(cols):
            gw_out[cols, :] = b16(dot_over(act[:, cols], grad[...]))

        sums_ref[4:5, :] = jnp.sum(f32(grad[...]), axis=0, keepdims=True)

    sums = everywhere(links, nb, source, mid, land_s, land_b, None, meanwhile, (ss, rs, sb, rb))
    beta, gamma = unpack_rows(sums, 0, lanes), unpack_rows(sums, lanes, lanes)
    for p in range(1, pieces):
        for start, _ in ride:
            start(p)
    sums_ref[5:6, :] = gamma
    sums_ref[6:7, :] = beta
    inverse, frames = stats[0:1, :], stats[1:2, 0:1]
    live = f32(pack[links.shard, 27:28, 0:1])
    mask = f32(f32(lax.broadcasted_iota(jnp.int32, (rows, 1), 0)) < live)
    padded[0:lead, :] = jnp.zeros((lead, features), jnp.float32)
    padded[lead + rows :, :] = jnp.zeros((lead, features), jnp.float32)
    padded[lead : lead + rows, :] = inverse * (
        normed[...] * gain - mask * (gain * beta + scaled_ref[...] * (gain * gamma)) / frames
    )
    given = 0.0
    gated = f32(gated_ref[...])
    for k in range(taps):
        at = lead + (taps - 1) // 2 - k
        moved = padded[at : at + rows, :]
        given = given + moved * vector_row(pack, 22 + k)
        sums_ref[8 + k : 9 + k, :] = jnp.sum(moved * gated, axis=0, keepdims=True)
    left = b16(given * f32(open_ref[...]))
    right = b16(given * f32(gate_ref[...]))
    inner[:, 0:features] = left
    inner[:, features:] = right
    sums_ref[2:3, :] = jnp.sum(f32(left), axis=0, keepdims=True)
    sums_ref[3:4, :] = jnp.sum(f32(right), axis=0, keepdims=True)
    total = dot_back(inner[...], w_in[...])
    scaled, inverse = norm_parts(rows_ref[...])
    out_ref[...] = stream_ref[...] + norm_slope(total, scaled, inverse, vector_row(pack, 2))
    sums_ref[0:1, :] = jnp.sum(total * scaled, axis=0, keepdims=True)
    sums_ref[1:2, :] = jnp.sum(total, axis=0, keepdims=True)

    @tiles(2 * features, 512)
    def _(cols):
        gw_in[:, cols] = b16(dot_over(hid[...], inner[:, cols]))

    for _, end in ride:
        end()


def conv_back(stream, rows_in, pack, w_in, w_out, saved, ridden, ident):
    ns, nb = lax.axis_size("shard"), lax.axis_size("batch")
    rows, features = rows_in.shape
    shape = jax.ShapeDtypeStruct
    low, full = jnp.bfloat16, jnp.float32
    small = (2 * features // 128, 128)
    return pl.pallas_call(
        functools.partial(conv_back_body, nb),
        out_shape=[
            shape((rows, features), full), shape((features, features), low),
            shape((features, 2 * features), low), shape((16, features), full),
        ]
        + [shape((r.shape[0] // 2, r.shape[1]), low) for r in ridden],
        in_specs=[VMEM_SPEC] * 15,
        out_specs=[VMEM_SPEC] * 6,
        scratch_shapes=[
            pltpu.VMEM((rows + 16, features), full), pltpu.VMEM((rows, features), full),
            pltpu.VMEM((rows, features), low), pltpu.VMEM((rows, 2 * features), low),
            pltpu.VMEM(small, full), pltpu.VMEM(small, full),
            pltpu.VMEM((ns,) + small, full), pltpu.VMEM((nb,) + small, full),
            pltpu.SemaphoreType.DMA((ns,)), pltpu.SemaphoreType.DMA((ns,)),
            pltpu.SemaphoreType.DMA((nb,)), pltpu.SemaphoreType.DMA((nb,)),
        ]
        + link_scratch(8, 1)[:2],
        compiler_params=pltpu.CompilerParams(
            collective_id=ident, has_side_effects=True, vmem_limit_bytes=60 << 20
        ),
        name="conv_back",
    )(stream, rows_in, pack, w_in, w_out, *saved, *ridden)


def mix_back_body(
    heads, size, nb, stream_ref, rows_ref, pack, hid, with_u, with_v, key, value, soft_ref, mix, table, proj,
    w_qkv, w_out, ride_a, ride_b, out_ref, gw_qkv, gw_pos, gw_out, sums_ref, own_sums, out_a, out_b,
    grad, dq, dk, dx, dp, part, send, land, cross, land_cross, send_sem, recv_sem, ride_send, ride_recv, *between,
):
    links = Links(send_sem, recv_sem)
    batch = lax.axis_index("batch")
    orders = ride_orders(nb)
    steps = len(orders[0]) - 1
    scale = 1.0 / math.sqrt(size)
    rows, features = rows_ref.shape
    half = rows // 2
    width = mix.shape[2]
    links.greet([links.near, links.far] + [{"batch": flip_bits(batch, 1 << k)} for k in orders[0]])
    stages = []
    for at, (start, end) in enumerate(((ride_a, out_a), (ride_b, out_b))):
        rider = Rider(batch, ride_send, ride_recv, at * steps)
        middle = between[at * (steps - 1) : (at + 1) * (steps - 1)]
        stages.append(rider.chain([start, *middle, end], orders[at][1:], rider.halve))

    def tick():
        for chain in stages:
            if chain:
                chain.pop(0)()

    tick()
    grad[0] = b16(stream_ref[...])
    out = [
        links.go(grad.at[0, pl.ds(h * half, half)], grad.at[2, pl.ds(h * half, half)], links.far)
        for h in range(2)
    ]
    near = links.go(grad.at[0], grad.at[1], links.near)
    at_row = lax.broadcasted_iota(jnp.int32, (rows, rows), 0)
    at_col = lax.broadcasted_iota(jnp.int32, (rows, rows), 1)
    flip = b16(f32(at_row + at_col == rows - 1))
    keys = f32(at_col)
    mine = pl.ds(pl.multiple_of(links.shard * width, 16), width)
    own_sums[...] = jnp.zeros_like(own_sums)

    def work(slot, emit):
        mixed = b16(dot_back(grad[slot], w_out[mine, :]))
        live = f32(pack[flip_bits(links.shard, slot), 27:28, 0:1])
        for h in range(heads):
            cols = slice(h * size, (h + 1) * size)
            soft = soft_ref[slot, :, h * rows : (h + 1) * rows]
            given = mixed[:, cols]
            grad_soft = dot_back(given, value[slot, :, cols])
            dx[slot, :, cols] = b16(dot_over(b16(soft), given))
            grad_scores = soft * (grad_soft - jnp.sum(grad_soft * soft, axis=-1, keepdims=True))
            raw = b16(jnp.where(keys < live, grad_scores, 0.0) * scale)
            grad_u = dot_rows(raw, key[slot, :, cols])
            dk[slot, :, cols] = b16(dot_over(raw, with_u[slot, :, cols]))
            turned = dot_rows(flip, raw)
            wide = jnp.concatenate([turned, jnp.zeros_like(turned)], 1)
            wide = b16(pltpu.roll(wide, 0, 1, stride=1, stride_axis=0))
            grad_v = dot_rows(wide, proj[:, cols])
            v_turned = b16(dot_rows(flip, with_v[slot, :, cols]))
            dp[slot, :, cols] = b16(dot_over(wide, v_turned))
            own_sums[2:3, cols] += jnp.sum(grad_u, axis=0, keepdims=True)
            own_sums[3:4, cols] += jnp.sum(grad_v, axis=0, keepdims=True)
            high = b16(grad_v)
            rest = b16(grad_v - f32(high))
            dq[slot, :, cols] = b16(grad_u + (dot_rows(flip, high) + dot_rows(flip, rest)))
        own_sums[0:1, :] += jnp.sum(f32(dq[slot]), axis=0, keepdims=True)
        own_sums[1:2, :] += jnp.sum(f32(dx[slot]), axis=0, keepdims=True)

        @tiles(features, 512)
        def _(cols):
            emit(
                cols,
                dot_back(dq[slot], w_qkv[0, cols, :])
                + dot_back(dk[slot], w_qkv[1, cols, :])
                + dot_back(dx[slot], w_qkv[2, cols, :]),
            )

    def keep(cols, value):
        part[0, :, cols] = value

    def keep_far(cols, value):
        part[1, :, cols] = value

    def give(cols, value):
        send[0, :, cols] = b16(value[:half])
        send[1, :, cols] = b16(value[half:])

    def give_far(cols, value):
        send[2, :, cols] = b16(value[:half])
        send[3, :, cols] = b16(value[half:])

    work(0, keep)
    near.wait()
    work(1, give)
    last = [links.go(send.at[pl.ds(0, 2)], land.at[pl.ds(0, 2)], links.near)]
    tick()
    on = []
    for h in range(2):
        out[h].wait()
        there = pl.ds(h * half, half)
        on.append(links.go(grad.at[2, there], grad.at[3, there], links.near))
    for copy in on:
        copy.wait()
    work(3, give_far)
    back = links.go(send.at[pl.ds(2, 2)], land.at[pl.ds(2, 2)], links.near)
    work(2, keep_far)
    back.wait()
    for h in range(2):
        cross[h] = b16(part[1, h * half : (h + 1) * half] + f32(land[2 + h]))
        last.append(links.go(cross.at[h], land_cross.at[h], links.far))
    flat = lambda ref: ref[...].reshape(4 * rows, ref.shape[2])
    for at, ref in enumerate((dq, dk, dx)):
        right = flat(ref)

        @tiles(features, 256)
        def _(cols, at=at, right=right):
            left = hid[:, :, cols].reshape(4 * rows, 256)
            gw_qkv[at, cols, :] = b16(dot_over(left, right))

    @tiles(features, 256)
    def _(cols):
        total = dot_over(table[:, cols], dp[0])
        for slot in range(1, 4):
            total = total + dot_over(table[:, cols], dp[slot])
        gw_pos[cols, :] = b16(total)

    gw_out[...] = b16(dot_over(flat(mix), flat(grad)))
    for copy in last:
        copy.wait()
    sums_ref[...] = jnp.zeros_like(sums_ref)
    sums_ref[2:3, :] = jnp.sum(f32(grad[0]), axis=0, keepdims=True)
    gain = vector_row(pack, 1)
    for h in range(2):
        at = slice(h * half, (h + 1) * half)
        given = part[0, at] + f32(land[h]) + f32(land_cross[h])
        scaled, inverse = norm_parts(rows_ref[at])
        out_ref[at] = stream_ref[at] + norm_slope(given, scaled, inverse, gain)
        sums_ref[0:1, :] += jnp.sum(given * scaled, axis=0, keepdims=True)
        sums_ref[1:2, :] += jnp.sum(given, axis=0, keepdims=True)
    for chain in stages:
        while chain:
            chain.pop(0)()


def mix_back(stream, rows_in, pack, saved, table, proj, w_qkv, w_out, ridden, heads, ident):
    rows, features = rows_in.shape
    hid, with_u, with_v, key, value, soft, mix = saved
    width = mix.shape[2]
    shape = jax.ShapeDtypeStruct
    low, full = jnp.bfloat16, jnp.float32
    narrow = pltpu.VMEM((4, rows, width), low)
    nb = lax.axis_size("batch")
    steps = nb.bit_length() - 2
    dma = pltpu.SemaphoreType.DMA((2 * steps,))
    between = []
    for r in ridden:
        between += [pltpu.VMEM((r.shape[0] >> k, r.shape[1]), low) for k in range(1, steps)]
    return pl.pallas_call(
        functools.partial(mix_back_body, heads, width // heads, nb),
        out_shape=[
            shape((rows, features), full), shape((3, features, width), low), shape((features, width), low),
            shape((width, features), low), shape((8, features), full), shape((8, width), full),
        ]
        + [shape((r.shape[0] >> steps, r.shape[1]), low) for r in ridden],
        in_specs=[VMEM_SPEC] * 16,
        out_specs=[VMEM_SPEC] * 8,
        scratch_shapes=[
            pltpu.VMEM((4, rows, features), low), narrow, narrow, narrow,
            pltpu.VMEM((4, 2 * rows, width), low),
        ]
        + gws_scratch(rows, features)
        + [dma, dma]
        + between,
        compiler_params=pltpu.CompilerParams(
            collective_id=ident, has_side_effects=True, vmem_limit_bytes=60 << 20
        ),
        name="mix_back",
    )(stream, rows_in, pack, *saved, table, proj, w_qkv, w_out, *ridden)


def body(
    tokens, cotangent, lengths, ffn_in, ffn_out, ffn_bias, qkv_proj, pos_proj, out_proj,
    conv_in, conv_out, depthwise, norm_gains, biases,
):
    _, length, features = tokens.shape
    ns, nb = lax.axis_size("shard"), lax.axis_size("batch")
    width = features // ns
    heads = HEADS // ns
    rows_in = tokens[0]

    own_length = jnp.broadcast_to(b16(f32(lengths))[:, None], (5, width))
    pack_in = jnp.concatenate([norm_gains, biases, depthwise, own_length], 0)
    b_in = f32(ffn_bias)

    rates = jnp.exp(
        jnp.arange(features // 2, dtype=jnp.float32) * (-2.0 * math.log(10000.0) / features)
    )
    turns = jnp.concatenate(
        [
            length - 1.0 - jnp.arange(16, dtype=jnp.float32),
            -16.0 * jnp.arange(2 * length // 16, dtype=jnp.float32),
        ]
    )
    angles = turns[:, None] * rates[None, :]
    base = jnp.concatenate([jnp.sin(angles), jnp.cos(angles)], 1)
    rows_one, pack, table, proj, w_out, *saved_one, w_rows_one = opening(
        rows_in, pack_in, b_in, base, pos_proj, ffn_in, ffn_out, out_proj, 5
    )
    rows_two, with_u, with_v, key, value, mix, wc_in, hid, soft = mix_forward(
        rows_one, pack, biases, qkv_proj, proj, w_out, conv_in, heads, 9
    )
    saved_mix = (hid, with_u, with_v, key, value, soft, mix)
    rows_three, *saved_conv, wc_out, w_rows_two = conv_forward(
        rows_two, pack, wc_in, conv_out, ffn_out, 10
    )
    rows_four, saved_two = ffn_forward(
        rows_three, pack, b_in, w_rows_two, ffn_in, 1, (4, 19, 20), 6
    )

    result, stream, two_in, two_out, two_sums = ffn_back(
        (rows_four, cotangent[0]), rows_three, pack, saved_two, w_rows_two, ffn_in, 1, 4, 7
    )
    stream, grad_conv_out, grad_conv_in, conv_sums, *ridden = conv_back(
        stream, rows_two, pack, wc_in, wc_out, saved_conv, (two_in, two_out), 11
    )
    stream, grad_qkv, grad_pos, grad_out, mix_sums, own_sums, *ridden = mix_back(
        stream, rows_one, pack, saved_mix, table, proj, qkv_proj, w_out, ridden, heads, 12
    )
    stream, one_in, one_out, one_sums, *ridden = ffn_back(
        (stream, *ridden), rows_in, pack, saved_one, w_rows_one, ffn_in, 0, 0, 8
    )
    tall, deep = one_in.shape
    piece = max(128, 8 * nb)
    *sums, out_gains, out_biases, out_taps, out_hidden = tail_sum(
        [grad_out, one_out, one_in] + [grad_qkv[at] for at in range(3)] + [grad_pos, grad_conv_in, grad_conv_out],
        ridden,
        [one_sums, mix_sums, two_sums, conv_sums, own_sums],
        [("turn", 4, None), ("turn", 1, 0), ("plain", 0, 0)]
        + [("plain", 2, at) for at in range(3)]
        + [("plain", 3, None), ("gather", 5, None), ("gather", 6, None)],
        [
            (2, tall, deep), (2, ns * deep, width), (3, tall, width), (tall, width), (tall, width),
            (tall, 2 * width), (tall, width),
        ],
        ["near", "line"],
        [width, piece, piece] + [min(tall, 4 * piece)] * 4 + [2 * piece, min(tall, 4 * piece)],
        deep,
        4,
    )
    return (
        result[None],
        stream[None],
        f32(sums[0]),
        f32(sums[1]),
        out_hidden,
        f32(sums[2]),
        f32(sums[3]),
        f32(sums[4]),
        f32(sums[5]),
        f32(sums[6]),
        out_taps,
        out_gains,
        out_biases,
    )


def solution(mesh):
    rows = P(("batch", "shard"), None, None)
    cube, flat = P(None, None, "shard"), P(None, "shard")
    return jax.shard_map(
        body,
        mesh=mesh,
        in_specs=(rows, rows, P(("batch", "shard")), cube, cube, flat, cube)
        + (flat,) * 7,
        out_specs=(rows, rows, cube, cube, flat, cube) + (flat,) * 7,
        check_vma=False,
    )
```

```python
import functools
import math

import jax
import jax.numpy as jnp
from jax import lax
from jax.experimental import pallas as pl
from jax.experimental.pallas import tpu as pltpu
from jax.sharding import PartitionSpec as P

HEADS = 8
MESH = pl.DeviceIdType.MESH
VMEM_SPEC = pl.BlockSpec(memory_space=pltpu.VMEM)
HBM_SPEC = pl.BlockSpec(memory_space=pltpu.HBM)
epsilon = 1e-05


def f32(a):
    return a.astype(jnp.float32)


def b16(a):
    return a.astype(jnp.bfloat16)


def norm_rows(values_in, gain_row, bias_row):
    row_mean = jnp.mean(values_in, axis=-1, keepdims=True)
    centered = values_in - row_mean
    spread = jnp.mean(centered * centered, axis=-1, keepdims=True)
    return centered * lax.rsqrt(spread + epsilon) * gain_row + bias_row


def dot_rows(a, b):
    return jnp.dot(a, b, preferred_element_type=jnp.float32)


def dot_back(a, b):
    return lax.dot_general(a, b, (((1,), (1,)), ((), ())), preferred_element_type=jnp.float32)


def dot_over(a, b):
    return lax.dot_general(a, b, (((0,), (0,)), ((), ())), preferred_element_type=jnp.float32)


def exchange(axis, index, count, source, landing, send_sem, recv_sem):
    copies = []
    for j in range(1, count):
        peer = lax.rem(index + j, count)
        copies.append(
            pltpu.make_async_remote_copy(
                src_ref=source,
                dst_ref=landing.at[index],
                send_sem=send_sem.at[j],
                recv_sem=recv_sem.at[j],
                device_id={axis: peer},
                device_id_type=MESH,
            )
        )
    return copies


def sum_slots(ref, count):
    total = ref[0]
    for j in range(1, count):
        total = total + ref[j]
    return total


class Chunk:
    def __init__(self, at, source, row, rows, columns, first, count):
        self.at, self.source, self.row, self.rows, self.columns = at, source, row, rows, columns
        extra = [(1 << k, k) for k in range(3, count.bit_length() - 1)]
        line = (6, 1)
        if first == "near":
            self.pre, self.post = [(1, 0)], [line] + extra
        else:
            self.pre, self.post = [], [line, (1, 0)] + extra
        size, self.landings = rows, []
        for _ in self.pre:
            size //= 2
            self.landings.append((size, columns))
        self.landings.append((size, columns))
        for _ in self.post:
            size //= 2
            self.landings.append((size, columns))
        self.steps = len(self.landings)


def bit_of(value, k):
    return lax.rem(lax.div(value, 1 << k), 2)


def flip_bits(value, mask):
    out = value
    k = 0
    while (1 << k) <= mask:
        if mask & (1 << k):
            out = out + (1 - 2 * bit_of(value, k)) * (1 << k)
        k += 1
    return out


class Mover:
    def __init__(self, chunk, batch, source, base, held, landings, sems, finish, early):
        self.c, self.b = chunk, batch
        self.source, self.base, self.held, self.landings, self.sems = source, base, held, landings, sems
        lo, hi = bit_of(batch, 1), bit_of(batch, 2)
        self.inner = lo != hi
        self.ended = lo == hi
        self.finish, self.early = finish, early
        self.build()

    def copy(self, at, src, dst, mask):
        send, recv = self.sems
        return pltpu.make_async_remote_copy(
            src_ref=src,
            dst_ref=dst,
            send_sem=send.at[self.c.at, at],
            recv_sem=recv.at[self.c.at, at],
            device_id={"batch": flip_bits(self.b, mask)},
            device_id_type=MESH,
        )

    def build(self):
        c = self.c
        held = self.held
        here, base = self.source, self.base
        off, size, step = 0, c.rows, 0
        plan, trail = [], []
        sequence = [("all",) + p for p in c.pre] + [("fold", 2, None)]
        sequence += [("inner",) + p for p in c.post]
        for kind, mask, sel in sequence:
            landing = self.landings[step]
            if kind == "fold":
                own = row_view(here, base, size)
                cp = self.copy(step, own, landing, mask)
            else:
                size //= 2
                mine = bit_of(self.b, sel)
                cp = self.copy(step, row_view(here, base + (1 - mine) * size, size), landing, mask)
                own = row_view(here, base + mine * size, size)
                off = off + mine * size
            trail.append((kind, mask, off, size))
            step += 1
            out = landing if step < len(sequence) else held(off, size)
            plan.append((kind, cp, (own, landing, out)))
            here, base = landing, 0
        for kind, mask, off, size in reversed(trail):
            cp = self.copy(step, held(off, size), held(off, size), mask)
            plan.append(("unfold" if kind == "fold" else kind, cp, None))
            step += 1
        self.plan = plan
        self.depth = len(plan) + len(self.early)

    def begin(self, k):
        kind, cp, _ = self.plan[k]
        if kind == "all":
            cp.start()
        elif kind == "fold":
            pl.when(self.ended)(cp.start)
        else:
            pl.when(self.inner)(cp.start)

    def end(self, k):
        kind, cp, add = self.plan[k]

        def gather():
            if add is not None:
                own, landing, out = add
                out[...] = b16(f32(own[...]) + f32(landing[...]))

        if kind == "all":
            cp.wait()
            gather()
        elif kind in ("fold", "unfold"):
            sender, taker = (
                (self.ended, self.inner) if kind == "fold" else (self.inner, self.ended)
            )
            pl.when(sender)(cp.wait_send)

            @pl.when(taker)
            def _():
                cp.wait_recv()
                gather()
        else:

            @pl.when(self.inner)
            def _():
                cp.wait()
                gather()

    def advance(self, k):
        if k < len(self.early):
            self.early[k]()
            return
        k -= len(self.early)
        if k > 0:
            self.end(k - 1)
        elif self.early:
            self.settle_early()
        if k < len(self.plan):
            self.begin(k)
        else:
            self.finish(self.c)


def row_view(ref, start, size):
    start = start if isinstance(start, int) else pl.multiple_of(start, 16 if size % 16 == 0 else 8)
    return ref.at[pl.ds(start, size)]


def column_block(index, columns):
    return pl.ds(pl.multiple_of(index * columns, 128), columns)


class Rider:
    def __init__(self, batch, send, recv, first):
        self.b, self.send, self.recv, self.at = batch, send, recv, first

    def go(self, src, dst, bit):
        copy = pltpu.make_async_remote_copy(
            src_ref=src, dst_ref=dst, send_sem=self.send.at[self.at], recv_sem=self.recv.at[self.at],
            device_id={"batch": flip_bits(self.b, 1 << bit)}, device_id_type=MESH,
        )
        self.at += 1
        copy.start()
        return copy

    def halve_pieces(self, source, landing, bit, pieces, half):
        size = half // pieces
        mine = bit_of(self.b, bit)
        copies = []

        def start(p):
            copies.append(
                self.go(
                    row_view(source, (1 - mine) * half + p * size, size), row_view(landing, p * size, size), bit
                )
            )

        def settle():
            for copy in copies:
                copy.wait()

        return start, settle, row_view(source, mine * half, half)

    def halve(self, source, landing, bit):
        half = landing.shape[0]
        mine = bit_of(self.b, bit)
        copy = self.go(row_view(source, (1 - mine) * half, half), landing, bit)

        def end():
            copy.wait()
            own = row_view(source, mine * half, half)
            landing[...] = b16(f32(own[...]) + f32(landing[...]))

        return end

    def double(self, source, target, bit):
        half = source.shape[0]
        there = row_view(target, bit_of(self.b, bit) * half, half)
        copy = self.go(source, there, bit)
        there[...] = source[...]
        return copy.wait

    def chain(self, refs, bits, move):
        ends, stages = [], []
        for i, bit in enumerate(bits):

            def stage(i=i, bit=bit):
                if ends:
                    ends.pop()()
                ends.append(move(refs[i], refs[i + 1], bit))

            stages.append(stage)
        stages.append(lambda: ends.pop()())
        return stages


def ride_orders(count):
    bits = list(range(count.bit_length() - 1))
    return bits, [1, 0] + bits[2:]


def tail_body(specs, chunks, ns, nb, n_in, n_out, *refs):
    ins, refs = refs[:n_in], refs[n_in:]
    ridden, refs = refs[:2], refs[2:]
    (one_sums, mix_sums, two_sums, conv_sums, own_sums), refs = refs[:5], refs[5:]
    outs, refs = refs[:n_out], refs[n_out:]
    (o_gains, o_biases, o_taps, o_hidden), refs = refs[:4], refs[4:]
    send, recv, turn_send, turn_recv, pre_send, pre_recv, ride_send, ride_recv = refs[:8]
    ss, rs, sb, rb, wide, land_s, mid, land_b, ride_fin = refs[8:17]
    rest = list(refs[17:])
    shard, batch = lax.axis_index("shard"), lax.axis_index("batch")
    barrier = pltpu.get_barrier_semaphore()
    greeted = [{"batch": lax.rem(batch + j, nb)} for j in range(1, nb)]
    greeted += [{"shard": flip_bits(shard, m)} for m in range(1, ns)]
    for device in greeted:
        pl.semaphore_signal(barrier, inc=1, device_id=device, device_id_type=MESH)
    width = own_sums.shape[1]
    for t in range(ns):
        cols = slice(t * width, (t + 1) * width)
        wide[t, 0:3, :] = one_sums[0:3, cols]
        wide[t, 3:6, :] = mix_sums[0:3, cols]
        wide[t, 6:9, :] = two_sums[0:3, cols]
        wide[t, 9:14, :] = conv_sums[0:5, cols]
        wide[t, 14:19, :] = conv_sums[8:13, cols]
        wide[t, 19:21, :] = two_sums[4:6, cols]
        wide[t, 21:24, :] = jnp.zeros((3, width), jnp.float32)
    pl.semaphore_wait(barrier, len(greeted))

    vector_copies = []
    for j in range(1, ns):
        peer = lax.rem(shard + j, ns)
        copy = pltpu.make_async_remote_copy(
            src_ref=wide.at[peer], dst_ref=land_s.at[shard], send_sem=ss.at[j], recv_sem=rs.at[j],
            device_id={"shard": peer}, device_id_type=MESH,
        )
        copy.start()
        vector_copies.append(copy)
    land_s[shard] = wide[shard]

    def vectors_on():
        for copy in vector_copies:
            copy.wait()
        mid[0:24, :] = sum_slots(land_s, ns)
        mid[24:28, :] = own_sums[0:4, :]
        per = one_sums.shape[1] // width
        for t in range(per):
            cols = slice(t * width, (t + 1) * width)
            mid[28 + t : 29 + t, :] = one_sums[3:4, cols]
            mid[28 + per + t : 29 + per + t, :] = two_sums[3:4, cols]
        mid[28 + 2 * per :, :] = jnp.zeros((mid.shape[0] - 28 - 2 * per, width), jnp.float32)
        vector_copies[:] = exchange("batch", batch, nb, mid, land_b, sb, rb)
        for copy in vector_copies:
            copy.start()
        land_b[batch] = mid[...]

    def vectors_out():
        for copy in vector_copies:
            copy.wait()
        vec = sum_slots(land_b, nb)
        row = lambda k: vec[k : k + 1]
        mine = conv_sums[5:7, column_block(shard, width)]
        gains = [row(0), row(3), row(9), mine[0:1], row(6), row(19)]
        order = [1, 2, 4, 24, 25, 5, 26, 27, 10, 11, 12, None, 13, 7, 8, 20]
        for k, value in enumerate(gains):
            o_gains[k : k + 1, :] = value
        for k, at in enumerate(order):
            o_biases[k : k + 1, :] = mine[1:2] if at is None else row(at)
        o_taps[...] = vec[14:19]
        per = o_hidden.shape[1] // width
        for k in range(2):
            for t in range(per):
                at = 28 + k * per + t
                o_hidden[k : k + 1, t * width : (t + 1) * width] = row(at)

    late = []

    def turn(c_at, total, row, rows, out, lead):
        target = outs[out] if lead is None else outs[out].at[lead]
        columns = target.shape[1]
        height = target.shape[0] // ns
        there = row_view(target, shard * height + row, rows)
        copies = []
        for j in range(1, ns):
            peer = flip_bits(shard, j)
            copy = pltpu.make_async_remote_copy(
                src_ref=total.at[:, column_block(peer, columns)],
                dst_ref=there,
                send_sem=turn_send.at[c_at, j],
                recv_sem=turn_recv.at[c_at, j],
                device_id={"shard": peer},
                device_id_type=MESH,
            )
            copy.start()
            copies.append(copy)
        there[...] = total[:, column_block(shard, columns)]
        late.extend(copies)

    rides = []
    orders = ride_orders(nb)
    plain_target = outs[0].at[1]
    rider_a = Rider(batch, ride_send, ride_recv, 0)
    rider_b = Rider(batch, ride_send, ride_recv, 1)
    end_a = rider_a.double(ridden[0], plain_target, orders[0][0])
    end_b = rider_b.double(ridden[1], ride_fin, orders[1][0])

    movers = []
    for c in chunks:
        kind, out, lead = specs["arrays"][c.source]
        source, base, early, settle = ins[c.source], c.row, [], None
        if kind == "gather":
            near_land, far_land = rest.pop(0), rest.pop(0)
            whole, columns, rows = ins[c.source], c.columns, pl.ds(c.row, c.rows)
            far = flip_bits(shard, 2)
            state = {}

            def pre(at, src, dst, mask, c=c):
                copy = pltpu.make_async_remote_copy(
                    src_ref=src, dst_ref=dst, send_sem=pre_send.at[c.at, at], recv_sem=pre_recv.at[c.at, at],
                    device_id={"shard": flip_bits(shard, mask)}, device_id_type=MESH,
                )
                copy.start()
                return copy

            def first(near_land=near_land, whole=whole, columns=columns, rows=rows, state=state, pre=pre):
                state["n"] = [
                    pre(i, whole.at[rows, column_block(flip_bits(shard, m), columns)], near_land.at[i], 1)
                    for i, m in enumerate((1, 3))
                ]

            def second(
                near_land=near_land, far_land=far_land, whole=whole, columns=columns, rows=rows, state=state,
                pre=pre, far=far,
            ):
                for copy in state["n"]:
                    copy.wait()
                near_land[1] = b16(f32(near_land[1]) + f32(whole[rows, column_block(far, columns)]))
                state["f"] = pre(2, near_land.at[1], far_land, 2)

            def settle(
                near_land=near_land, far_land=far_land, whole=whole, columns=columns, rows=rows, state=state,
            ):
                state["f"].wait()
                far_land[...] = b16(
                    f32(far_land[...]) + f32(near_land[0]) + f32(whole[rows, column_block(shard, columns)])
                )

            early = [first, second]
            source, base = far_land, 0
        if kind == "turn":
            total = rest.pop(0)
            held = lambda off, size, total=total: row_view(total, off, size)

            def finish(c, total=total, out=out, lead=lead):
                turn(c.at, total, c.row, c.rows, out, lead)
        else:
            target = outs[out] if lead is None else outs[out].at[lead]
            held = lambda off, size, target=target, c=c: row_view(target, c.row + off, size)

            def finish(c):
                pass
        landings = [rest.pop(0) for _ in range(c.steps)]
        m = Mover(c, batch, source, base, held, landings, (send, recv), finish, early)
        m.settle_early = settle
        movers.append(m)
    starts, lag = [], specs["lag"]
    for i, m in enumerate(movers):
        starts.append(max(0, i // lag - len(m.early)))
    rounds = max(s + m.depth + 1 for s, m in zip(starts, movers))
    for r in range(rounds):
        if r == 1:
            vectors_on()
        if r == 2:
            end_b()
            turn(len(chunks), ride_fin, 0, ride_fin.shape[0], 1, 1)
        if r == 3:
            vectors_out()
            end_a()
        for s, m in zip(starts, movers):
            if 0 <= r - s <= m.depth:
                m.advance(r - s)
    for copy in late:
        copy.wait()


def tail_sum(arrays, ridden, sums, kinds, outputs, firsts, chunk_rows, hidden, ident):
    ns, nb = lax.axis_size("shard"), lax.axis_size("batch")
    low, full = jnp.bfloat16, jnp.float32
    chunks = []
    for i, a in enumerate(arrays):
        step = chunk_rows[i]
        columns = a.shape[1] // ns if kinds[i][0] == "gather" else a.shape[1]
        for row in range(0, a.shape[0], step):
            chunks.append(Chunk(len(chunks), i, row, step, columns, firsts[len(chunks) % len(firsts)], nb))
    depth = max(2 * c.steps for c in chunks)
    specs = dict(arrays=kinds, lag=2)
    width = sums[-1].shape[1]
    per = hidden // width
    small = -(-(28 + 2 * per) // 8) * 8
    dma = pltpu.SemaphoreType.DMA
    n = len(chunks)
    scratch = [
        dma((n, depth)), dma((n, depth)), dma((n + 1, ns)), dma((n + 1, ns)), dma((n, 3)), dma((n, 3)),
        dma((2,)), dma((2,)), dma((ns,)), dma((ns,)), dma((nb,)), dma((nb,)),
        pltpu.VMEM((ns, 24, width), full), pltpu.VMEM((ns, 24, width), full),
        pltpu.VMEM((small, width), full), pltpu.VMEM((nb, small, width), full),
        pltpu.VMEM((2 * ridden[1].shape[0], ridden[1].shape[1]), low),
    ]
    for c in chunks:
        if kinds[c.source][0] == "gather":
            scratch += [pltpu.VMEM((2, c.rows, c.columns), low), pltpu.VMEM((c.rows, c.columns), low)]
        if kinds[c.source][0] == "turn":
            scratch.append(pltpu.VMEM((c.rows, c.columns), low))
        scratch += [pltpu.VMEM(shape, low) for shape in c.landings]
    shape = jax.ShapeDtypeStruct
    shapes = [shape(s, low) for s in outputs]
    shapes += [shape((6, width), full), shape((16, width), full), shape((5, width), full), shape((2, hidden), full)]
    operands = list(arrays) + list(ridden) + list(sums)
    return pl.pallas_call(
        functools.partial(tail_body, specs, chunks, ns, nb, len(arrays), len(outputs)),
        out_shape=shapes,
        in_specs=[VMEM_SPEC] * len(operands),
        out_specs=[VMEM_SPEC] * len(shapes),
        scratch_shapes=scratch,
        compiler_params=pltpu.CompilerParams(
            collective_id=ident, has_side_effects=True, vmem_limit_bytes=62 << 20
        ),
        name="tail_sum",
    )(*operands)


class Links:
    def __init__(self, send, recv):
        self.send, self.recv, self.count = send, recv, 0
        s = lax.axis_index("shard")
        self.shard = s
        self.near = {"shard": flip_bits(s, 1)}
        self.far = {"shard": flip_bits(s, 2)}
        self.across = {"shard": flip_bits(s, 3)}

    def greet(self, devices):
        barrier = pltpu.get_barrier_semaphore()
        for device in devices:
            pl.semaphore_signal(barrier, inc=1, device_id=device, device_id_type=MESH)
        pl.semaphore_wait(barrier, len(devices))

    def go(self, src, dst, device):
        at = self.count
        self.count += 1
        copy = pltpu.make_async_remote_copy(
            src_ref=src, dst_ref=dst, send_sem=self.send.at[at], recv_sem=self.recv.at[at],
            device_id=device, device_id_type=MESH,
        )
        copy.start()
        return copy


def sums_scratch(rows, columns):
    half = rows // 2
    return [
        pltpu.VMEM((2, rows, columns), jnp.float32),
        pltpu.VMEM((4, half, columns), jnp.bfloat16),
        pltpu.VMEM((4, half, columns), jnp.bfloat16),
        pltpu.VMEM((2, half, columns), jnp.bfloat16),
        pltpu.VMEM((2, half, columns), jnp.bfloat16),
    ]


class Sums:
    def __init__(self, links, refs):
        self.links = links
        self.part, self.send, self.land, self.cross, self.land_cross = refs
        self.half = self.send.shape[1]
        self.near, self.crossing, self.backs = None, [], []

    def rows(self, h):
        return slice(h * self.half, (h + 1) * self.half)

    def keep(self, cols, value):
        self.part[0, :, cols] = value

    def keep_far(self, cols, value):
        self.part[1, :, cols] = value

    def give(self, cols, value):
        self.send[0, :, cols] = b16(value[: self.half])
        self.send[1, :, cols] = b16(value[self.half :])

    def give_far(self, cols, value):
        self.send[2, :, cols] = b16(value[: self.half])
        self.send[3, :, cols] = b16(value[self.half :])

    def split(self, h):
        def emit(cols, value):
            self.part[1, self.rows(h), cols] = value[: self.half]
            self.send[2 + h, :, cols] = b16(value[self.half :])

        return emit

    def send_near(self):
        both = pl.ds(0, 2)
        self.near = self.links.go(self.send.at[both], self.land.at[both], self.links.near)

    def send_back(self, h):
        self.backs.append(self.links.go(self.send.at[2 + h], self.land.at[2 + h], self.links.near))

    def send_cross(self, h):
        self.backs[h].wait()
        self.cross[h] = b16(self.part[1, self.rows(h)] + f32(self.land[2 + h]))
        self.crossing.append(self.links.go(self.cross.at[h], self.land_cross.at[h], self.links.far))

    def arrive(self, h):
        if self.near is not None:
            self.near.wait()
            self.near = None
        self.crossing[h].wait()
        return self.part[0, self.rows(h)] + f32(self.land[h]) + f32(self.land_cross[h])


def gather_work_scatter(links, x, fill, work, refs):
    sums = Sums(links, refs)
    half = x.shape[1] // 2
    out = []
    for h in range(2):
        fill(h)
        out.append(links.go(x.at[0, pl.ds(h * half, half)], x.at[2 + h, pl.ds(0, half)], links.far))
    near = links.go(x.at[0], x.at[1], links.near)
    work(0, sums.keep)
    near.wait()
    work(1, sums.give)
    sums.send_near()
    for h in range(2):
        out[h].wait()
        on = links.go(x.at[2 + h, pl.ds(0, half)], x.at[2 + h, pl.ds(half, half)], links.near)
        on.wait()
        work(2 + h, sums.split(h))
        sums.send_back(h)
        sums.send_cross(h)
    return sums


def tiles(total, size):
    def over(body):
        pl.loop(0, total // size)(
            lambda n: body(pl.ds(pl.multiple_of(n * size, size), size))
        )

    return over


def norm_parts(rows):
    row_mean = jnp.mean(rows, axis=-1, keepdims=True)
    centered = rows - row_mean
    inverse = lax.rsqrt(jnp.mean(centered * centered, axis=-1, keepdims=True) + epsilon)
    return centered * inverse, inverse


def norm_slope(grad, scaled, inverse, gain):
    inner = grad * gain
    return inverse * (
        inner
        - jnp.mean(inner, axis=-1, keepdims=True)
        - scaled * jnp.mean(inner * scaled, axis=-1, keepdims=True)
    )


def column_sum(value):
    return jnp.sum(value, axis=0, keepdims=True)


def ffn_up(hid, act, slope, w_in, b_ref, which):
    def run(block):
        @tiles(w_in.shape[1], 512)
        def _(cols):
            pre = dot_rows(hid[block], w_in[:, cols]) + b_ref[which : which + 1, cols]
            gate = jax.nn.sigmoid(pre)
            act[block, :, cols] = b16(pre * gate)
            slope[block, :, cols] = b16(gate * (1.0 + pre * (1.0 - gate)))

    return run


def ffn_down(act, w_rows):
    def run(block, emit):
        @tiles(w_rows.shape[1], 512)
        def _(cols):
            emit(cols, dot_rows(act[block], w_rows[:, cols]))

    return run


def ffn_inward(grad, inner, slope, w_in, w_rows):
    def run(block, emit):
        @tiles(w_in.shape[1], 512)
        def _(cols):
            wide = dot_back(grad[block], w_rows[cols, :])
            inner[block, :, cols] = b16(wide * f32(slope[block, :, cols]))

        @tiles(w_in.shape[0], 512)
        def _(cols):
            emit(cols, dot_back(inner[block], w_in[cols, :]))

    return run


def flat(ref):
    return ref[...].reshape(ref.shape[0] * ref.shape[1], ref.shape[2])


def flat_columns(ref, cols, size):
    return ref[:, :, cols].reshape(ref.shape[0] * ref.shape[1], size)


def weight_out(act, grad, gw_out):
    @tiles(act.shape[2], 256)
    def _(cols):
        gw_out[cols, :] = b16(dot_over(flat_columns(act, cols, 256), flat(grad)))


def weight_in(hid, inner, gw_in, sums_ref):
    @tiles(inner.shape[2], 256)
    def _(cols):
        right = flat_columns(inner, cols, 256)
        gw_in[:, cols] = b16(dot_over(flat(hid), right))
        sums_ref[3:4, cols] = column_sum(f32(right))


class Fetch:
    def __init__(self, links, batch, local_sem):
        self.links, self.local_sem = links, local_sem
        self.quarter = bit_of(batch, 0) + 2 * bit_of(batch, 1)
        self.peers = [{"batch": flip_bits(batch, 1)}, {"batch": flip_bits(batch, 2)}]

    def flow(self, source_rows, target, blocks, rows):
        links, size, held = self.links, rows // 8, {}
        span = lambda q, p: pl.ds(pl.multiple_of(q * (2 * size) + p * size, 16), size)
        mine = self.quarter
        own = blocks[0]

        def first():
            for p in range(2):
                for t, device, _ in blocks[1:]:
                    held["y", p, t] = links.go(
                        source_rows(t, mine * (2 * size) + p * size, size),
                        target.at[span(mine, p), own],
                        device,
                    )

        def pass_on(p, q, t, block, way):
            there = target.at[span(q, p), block]
            return links.go(there, there, self.peers[way])

        def second(p):
            def run():
                for t, _, block in blocks[1:]:
                    held["y", p, t].wait()
                    held["a", p, t] = pass_on(p, mine, t, block, p)

            return run

        def third(p):
            def run():
                other = flip_bits(mine, 1 << p)
                for t, _, block in blocks[1:]:
                    held["a", p, t].wait()
                    held["b", p, t] = pass_on(p, mine, t, block, 1 - p)
                    held["c", p, t] = pass_on(p, other, t, block, 1 - p)

            return run

        def last():
            for p in range(2):
                for t, _, _ in blocks[1:]:
                    held["b", p, t].wait()
                    held["c", p, t].wait()

        return [first, second(0), second(1), third(0), third(1), last]

    def columns(self, source, target, at):
        links, (rows, columns) = self.links, source.shape
        far = flip_bits(links.shard, 2)
        own = column_block(links.shard, columns)
        far_block = column_block(far, columns)
        row = lambda t, start, size: source.at[pl.ds(pl.multiple_of(start, 16), size)]
        stages = self.flow(row, target, [own, (2, links.far, far_block)], rows)
        held = {}

        def first():
            stages[0]()
            held["own"] = pltpu.make_async_copy(source, target.at[:, own], self.local_sem.at[at])
            held["own"].start()
            held["near"] = links.go(source, target.at[:, own], links.near)

        def pass_near():
            stages[-1]()
            held["on"] = links.go(target.at[:, far_block], target.at[:, far_block], links.near)

        def finish():
            held["on"].wait()
            held["near"].wait()
            held["own"].wait()

        return [first] + stages[1:-1] + [pass_near, finish]

    def rows(self, source, target, at):
        links, rows = self.links, target.shape[0]
        columns = source.shape[1]
        index = [flip_bits(links.shard, m) for m in range(4)]
        own = column_block(links.shard, columns)
        row = lambda m, start, size: source.at[pl.ds(pl.multiple_of(index[m] * rows + start, 16), size)]
        blocks = [own] + [
            (m, device, column_block(index[m], columns)) for m, device in ((2, links.far), (3, links.across))
        ]
        stages = self.flow(row, target, blocks, rows)
        held = {}

        def first():
            stages[0]()
            held["own"] = pltpu.make_async_copy(row(0, 0, rows), target.at[:, own], self.local_sem.at[at])
            held["own"].start()
            held["near"] = links.go(row(1, 0, rows), target.at[:, own], links.near)

        def last():
            stages[-1]()
            held["near"].wait()
            held["own"].wait()

        return [first] + stages[1:-1] + [last]


class Flush:
    def __init__(self, sem):
        self.sem, self.open = sem, []

    def go(self, src, dst):
        copy = pltpu.make_async_copy(src, dst, self.sem.at[len(self.open)])
        copy.start()
        self.open.append(copy)

    def settle(self):
        for copy in self.open:
            copy.wait()


def vector_row(pack, row):
    return f32(jnp.concatenate([pack[t, row : row + 1, :] for t in range(pack.shape[0])], 1))

def link_scratch(count, local):
    return [
        pltpu.SemaphoreType.DMA((count,)),
        pltpu.SemaphoreType.DMA((count,)),
        pltpu.SemaphoreType.DMA((local,)),
    ]


class Loads:
    def __init__(self, sem, pairs):
        self.open = []
        for at, (src, dst) in enumerate(pairs):
            copy = pltpu.make_async_copy(src, dst, sem.at[at])
            copy.start()
            self.open.append(copy)

    def need(self, *which):
        for at in which:
            if self.open[at] is not None:
                self.open[at].wait()
                self.open[at] = None


def front_body(
    heads, size,
    rows_ref, pack_in, b_ref, base_ref, own_ref, pos_hbm, qkv_hbm, ffn_in, ffn_out, out_proj, conv_in,
    one_ref, two_ref, pack, table, proj, with_u, with_v, key, value, mix, wc_in, w_mine,
    hid_out, act_out, slope_out, w_rows_out, hidden_out, soft_out,
    hid, act, slope, w_rows, w_in, w_out, pos_ref, w_qkv, hid_b, soft_ref, turned,
    part, send, land, cross, land_cross, send_sem, recv_sem, local_sem, load_sem, flush_sem,
):
    batch = lax.axis_index("batch")
    links = Links(send_sem, recv_sem)
    fetch = Fetch(links, batch, local_sem)
    flush = Flush(flush_sem)
    loads = Loads(load_sem, [(ffn_in.at[0], w_in), (pos_hbm, pos_ref), (qkv_hbm, w_qkv)])
    links.greet([links.near, links.far, links.across] + fetch.peers)
    small = [
        links.go(pack_in, pack.at[links.shard], device)
        for device in (links.far, links.across, links.near)
    ]
    down = fetch.rows(ffn_out.at[0], w_rows, 0)
    down.pop(0)()
    pack[links.shard] = pack_in[...]
    for copy in small:
        copy.wait()
    rows, features = rows_ref.shape
    hid[0] = b16(norm_rows(rows_ref[...], vector_row(pack, 0), vector_row(pack, 6)))
    half = rows // 2
    out = [
        links.go(hid.at[0, pl.ds(h * half, half)], hid.at[2 + h, pl.ds(0, half)], links.far)
        for h in range(2)
    ]
    near = links.go(hid.at[0], hid.at[1], links.near)
    up = ffn_up(hid, act, slope, w_in, b_ref, 0)
    loads.need(0)
    up(0)
    near.wait()
    up(1)
    down.pop(0)()
    down.pop(0)()
    lanes = features // 2

    @pl.loop(0, table.shape[0] // 16)
    def _(i):
        at = pl.ds(pl.multiple_of(i * 16, 16), 16)
        s_a, c_a = base_ref[pl.ds(16 + i, 1), 0:lanes], base_ref[pl.ds(16 + i, 1), lanes:]
        s_b, c_b = base_ref[0:16, 0:lanes], base_ref[0:16, lanes:]
        table[at, 0:lanes] = b16(s_a * c_b + c_a * s_b)
        table[at, lanes:] = b16(c_a * c_b - s_a * s_b)

    loads.need(1)
    proj[...] = b16(dot_rows(table[...], pos_ref[...]))
    other = fetch.columns(out_proj, w_out, 1)
    for h in range(2):
        out[h].wait()
        on = links.go(hid.at[2 + h, pl.ds(0, half)], hid.at[2 + h, pl.ds(half, half)], links.near)
        on.wait()
        if h == 1:
            other.pop(0)()
        up(2 + h)
        down.pop(0)()
    for pair in ((hid, hid_out), (act, act_out), (slope, slope_out)):
        flush.go(*pair)
    while down:
        down.pop(0)()
    flush.go(w_rows, w_rows_out)
    sums = Sums(links, (part, send, land, cross, land_cross))
    work = ffn_down(act, w_rows)
    for h in range(2):
        work(2 + h, sums.split(h))
        sums.send_back(h)
    for h in range(2):
        sums.send_cross(h)
    work(1, sums.give)
    sums.send_near()
    work(0, sums.keep)
    for _ in range(4):
        other.pop(0)()

    out_bias, gain, shift = vector_row(pack, 7), vector_row(pack, 1), vector_row(pack, 8)
    out = []
    for h in range(2):
        at = slice(h * half, (h + 1) * half)
        one = rows_ref[at] + 0.5 * (sums.arrive(h) + out_bias)
        one_ref[at] = one
        hid_b[0, at] = b16(norm_rows(one, gain, shift))
        there = pl.ds(h * half, half)
        out.append(links.go(hid_b.at[0, there], hid_b.at[2, there], links.far))
    near = links.go(hid_b.at[0], hid_b.at[1], links.near)
    while other:
        other.pop(0)()
    entering = fetch.columns(conv_in, wc_in, 2)
    own = f32(own_ref[...])
    keys = f32(lax.broadcasted_iota(jnp.int32, (rows, rows), 1))
    scale = 1.0 / math.sqrt(size)
    loads.need(2)

    def attend(slot):
        hidden = hid_b[slot]
        query = dot_rows(hidden, w_qkv[0]) + own[3:4]
        with_u[slot] = b16(query + own[6:7])
        with_v[slot] = b16(query + own[7:8])
        key[slot] = b16(dot_rows(hidden, w_qkv[1]))
        value[slot] = b16(dot_rows(hidden, w_qkv[2]) + own[4:5])
        live = f32(pack[flip_bits(links.shard, slot), 27:28, 0:1])
        for h in range(heads):
            cols = slice(h * size, (h + 1) * size)
            wide = dot_back(with_v[slot, :, cols], proj[:, cols])
            moved = pltpu.roll(wide, rows + 1, 1, stride=1, stride_axis=0)[:, :rows]
            raw = dot_back(with_u[slot, :, cols], key[slot, :, cols]) + moved
            scores = jnp.where(keys < live, raw * scale, -1e30)
            grown = jnp.exp(scores - jnp.max(scores, axis=-1, keepdims=True))
            soft = grown / jnp.sum(grown, axis=-1, keepdims=True)
            soft_ref[slot, :, h * rows : (h + 1) * rows] = soft
            mix[slot, :, cols] = b16(dot_rows(b16(soft), value[slot, :, cols]))

    last = []
    attend(0)
    turned[links.shard] = mix[0]
    near.wait()
    attend(1)
    last.append(links.go(mix.at[1], turned.at[links.shard], links.near))
    on = []
    for h in range(2):
        out[h].wait()
        there = pl.ds(h * half, half)
        on.append(links.go(hid_b.at[2, there], hid_b.at[3, there], links.near))
        if h == 0:
            entering.pop(0)()
    attend(2)
    last.append(links.go(mix.at[2], turned.at[links.shard], links.far))
    entering.pop(0)()
    entering.pop(0)()
    for copy in on:
        copy.wait()
    flush.go(hid_b, hidden_out)
    attend(3)
    last.append(links.go(mix.at[3], turned.at[links.shard], links.across))
    flush.go(soft_ref, soft_out)
    entering.pop(0)()
    entering.pop(0)()
    for copy in last:
        copy.wait()
    width = mix.shape[2]
    total = one_ref[...] + vector_row(pack, 11)
    for t in range(turned.shape[0]):
        total = total + dot_rows(turned[t], w_out[t * width : (t + 1) * width])
    two_ref[...] = total
    w_mine[...] = w_out[pl.ds(pl.multiple_of(links.shard * width, 16), width), :]
    while entering:
        entering.pop(0)()
    flush.settle()


def front(rows_in, pack_in, b_in, base, own_biases, pos_proj, qkv_proj, ffn_in, ffn_out, out_proj, conv_in, heads, ident):
    ns = lax.axis_size("shard")
    rows, features = rows_in.shape
    hidden = ffn_in.shape[2]
    width = features // ns
    low, full = jnp.bfloat16, jnp.float32
    shape, vmem = jax.ShapeDtypeStruct, pltpu.VMEM
    narrow = shape((ns, rows, width), low)
    dma = pltpu.SemaphoreType.DMA
    return pl.pallas_call(
        functools.partial(front_body, heads, width // heads),
        out_shape=[
            shape((rows, features), full), shape((rows, features), full),
            shape((ns,) + pack_in.shape, low),
            shape((2 * rows, features), low), shape((2 * rows, width), low),
            narrow, narrow, narrow, narrow, narrow,
            shape((conv_in.shape[0], ns * conv_in.shape[1]), low),
            shape((width, features), low),
            shape((4, rows, features), low), shape((4, rows, hidden), low), shape((4, rows, hidden), low),
            shape((hidden, features), low),
            shape((ns, rows, features), low),
            shape((ns, rows, heads * rows), full),
        ],
        in_specs=[VMEM_SPEC] * 5 + [HBM_SPEC] * 6,
        out_specs=[VMEM_SPEC] * 12 + [HBM_SPEC] * 6,
        scratch_shapes=[
            vmem((4, rows, features), low), vmem((4, rows, hidden), low), vmem((4, rows, hidden), low),
            vmem((hidden, features), low), vmem((features, hidden), low), vmem((features, features), low),
            vmem(pos_proj.shape, low), vmem(qkv_proj.shape, low),
            vmem((ns, rows, features), low), vmem((ns, rows, heads * rows), full), vmem((ns, rows, width), low),
        ]
        + sums_scratch(rows, features)
        + link_scratch(72, 3)
        + [dma((3,)), dma((6,))],
        compiler_params=pltpu.CompilerParams(
            collective_id=ident, has_side_effects=True, vmem_limit_bytes=60 << 20
        ),
        name="front",
    )(rows_in, pack_in, b_in, base, own_biases, pos_proj, qkv_proj, ffn_in, ffn_out, out_proj, conv_in)


def middle_body(
    nb, early, rows_ref, pack, b_ref, w_rows, cotangent_hbm, ffn_in,
    result, out_ref, gw_in, gw_out, sums_ref, early_a, early_b,
    hid, act, slope, grad, inner, w_in, cotangent, stream, *refs,
):
    first, second, refs = refs[:5], refs[5:10], refs[10:]
    send_sem, recv_sem, ride_send, ride_recv, load_sem = refs
    batch = lax.axis_index("batch")
    links = Links(send_sem, recv_sem)
    loads = Loads(load_sem, [(ffn_in.at[1], w_in), (cotangent_hbm, cotangent)])
    orders = ride_orders(nb)
    links.greet([links.near, links.far] + [{"batch": flip_bits(batch, 1 << k)} for k in range(2)])
    rows, features = rows_ref.shape
    half = rows // 2
    gain, shift = vector_row(pack, 4), vector_row(pack, 19)

    def fill(h):
        at = slice(h * half, (h + 1) * half)
        hid[0, at] = b16(norm_rows(rows_ref[at], gain, shift))

    up, down = ffn_up(hid, act, slope, w_in, b_ref, 1), ffn_down(act, w_rows)

    def work(block, emit):
        loads.need(0)
        up(block)
        down(block, emit)

    sums = gather_work_scatter(links, hid, fill, work, first)
    last_gain, last_shift, out_bias = vector_row(pack, 5), vector_row(pack, 21), vector_row(pack, 20)
    live = f32(pack[links.shard, 27:28, 0:1])
    mask = f32(f32(lax.broadcasted_iota(jnp.int32, (rows, 1), 0)) < live)
    loads.need(1)
    ends = []

    def turn_back(h):
        at = slice(h * half, (h + 1) * half)
        scaled, inverse = norm_parts(rows_ref[at] + 0.5 * (sums.arrive(h) + out_bias))
        result[at] = (scaled * last_gain + last_shift) * mask[at]
        given = cotangent[at] * mask[at]
        slide = norm_slope(given, scaled, inverse, last_gain)
        stream[at] = slide
        grad[0, at] = b16(0.5 * slide)
        ends.append((column_sum(given * scaled), column_sum(given)))

    back = gather_work_scatter(
        links, grad, turn_back, ffn_inward(grad, inner, slope, w_in, w_rows), second
    )
    pieces = 4
    riders = [
        Rider(batch, ride_send, ride_recv, at * early).halve_pieces(
            (gw_in, gw_out)[at], (early_a, early_b)[at], orders[at][0], pieces, gw_in.shape[0] // 2
        )
        for at in range(2)
    ]
    weight_out(act, grad, gw_out)
    for p in range(early):
        riders[1][0](p)
    weight_in(hid, inner, gw_in, sums_ref)
    for p in range(early):
        riders[0][0](p)
    sums_ref[0:3, :] = jnp.zeros((3, features), jnp.float32)
    sums_ref[2:3, :] = column_sum(f32(grad[0]))
    sums_ref[4:5, :] = ends[0][0] + ends[1][0]
    sums_ref[5:6, :] = ends[0][1] + ends[1][1]
    sums_ref[6:8, :] = jnp.zeros((2, features), jnp.float32)
    for h in range(2):
        at = slice(h * half, (h + 1) * half)
        scaled, inverse = norm_parts(rows_ref[at])
        given = back.arrive(h)
        out_ref[at] = stream[at] + norm_slope(given, scaled, inverse, gain)
        sums_ref[0:1, :] += column_sum(given * scaled)
        sums_ref[1:2, :] += column_sum(given)
    for _, settle, _ in riders:
        settle()


EARLY = 1


def middle(rows_in, pack, b_in, w_rows, cotangent, ffn_in, ident):
    rows, features = rows_in.shape
    hidden = ffn_in.shape[2]
    nb = lax.axis_size("batch")
    low, full = jnp.bfloat16, jnp.float32
    shape, vmem = jax.ShapeDtypeStruct, pltpu.VMEM
    dma = pltpu.SemaphoreType.DMA
    piece = features // 8
    return pl.pallas_call(
        functools.partial(middle_body, nb, EARLY),
        out_shape=[
            shape((rows, features), full), shape((rows, features), full),
            shape((features, hidden), low), shape((hidden, features), low), shape((8, features), full),
            shape((EARLY * piece, hidden), low), shape((EARLY * piece, features), low),
        ],
        in_specs=[VMEM_SPEC] * 4 + [HBM_SPEC] * 2,
        out_specs=[VMEM_SPEC] * 7,
        scratch_shapes=[
            vmem((4, rows, features), low), vmem((4, rows, hidden), low), vmem((4, rows, hidden), low),
            vmem((4, rows, features), low), vmem((4, rows, hidden), low), vmem((features, hidden), low),
            vmem((rows, features), full), vmem((rows, features), full),
        ]
        + sums_scratch(rows, features)
        + sums_scratch(rows, features)
        + [dma((20,)), dma((20,)), dma((2 * EARLY,)), dma((2 * EARLY,)), dma((2,))],
        compiler_params=pltpu.CompilerParams(
            collective_id=ident, has_side_effects=True, vmem_limit_bytes=60 << 20
        ),
        name="middle",
    )(rows_in, pack, b_in, w_rows, cotangent, ffn_in)


def pack_rows(ref, at, row):
    for i in range(row.shape[1] // 128):
        ref[at + i : at + i + 1, :] = row[:, i * 128 : (i + 1) * 128]


def unpack_rows(value, at, lanes):
    return jnp.concatenate([value[at + i : at + i + 1, :] for i in range(lanes)], 1)


def everywhere(links, nb, source, mid, land_s, land_b, result, small, sems):
    s, b = links.shard, lax.axis_index("batch")
    ns = land_s.shape[0]
    ss, rs, sb, rb = sems
    first = exchange("shard", s, ns, source, land_s, ss, rs)
    for copy in first:
        copy.start()
    land_s[s] = source[...]
    for copy in first:
        copy.wait()
    mid[...] = sum_slots(land_s, ns)
    second = exchange("batch", b, nb, mid, land_b, sb, rb)
    for copy in second:
        copy.start()
    land_b[b] = mid[...]
    small()
    for copy in second:
        copy.wait()
    return sum_slots(land_b, nb)


def conv_body(
    nb, rows_ref, pack, w_in, conv_out, ffn_out,
    out_ref, hid, open_ref, gate_ref, gated_ref, scaled_ref, act, slope, stats, w_out, w_rows,
    padded, source, mid, land_s, land_b, ss, rs, sb, rb, send_sem, recv_sem, local_sem,
):
    batch = lax.axis_index("batch")
    links = Links(send_sem, recv_sem)
    fetch = Fetch(links, batch, local_sem)
    rows, features = rows_ref.shape
    ns = land_s.shape[0]
    links.greet(
        [links.near, links.far, links.across]
        + [{"batch": lax.rem(batch + j, nb)} for j in range(1, nb)]
    )
    out_fetch = fetch.columns(conv_out, w_out, 0)
    out_fetch.pop(0)()
    down = fetch.rows(ffn_out.at[1], w_rows, 1)
    down.pop(0)()
    live = f32(pack[links.shard, 27:28, 0:1])
    mask = f32(f32(lax.broadcasted_iota(jnp.int32, (rows, 1), 0)) < live)
    hid[...] = b16(norm_rows(rows_ref[...], vector_row(pack, 2), vector_row(pack, 14)))
    bias_v, bias_g = vector_row(pack, 15), vector_row(pack, 16)
    lead = 8
    tile = 512
    padded[0:lead, :] = jnp.zeros((lead, features), jnp.float32)
    padded[lead + rows :, :] = jnp.zeros((lead, features), jnp.float32)
    for n in range(features // tile):
        cols = slice(n * tile, (n + 1) * tile)
        left = dot_rows(hid[...], w_in[:, cols]) + bias_v[:, cols]
        right = dot_rows(hid[...], w_in[:, features + n * tile : features + (n + 1) * tile])
        gate = jax.nn.sigmoid(right + bias_g[:, cols])
        opened = gate * mask
        gated = left * opened
        open_ref[:, cols] = b16(opened)
        gate_ref[:, cols] = b16(gated * (1.0 - gate))
        gated_ref[:, cols] = b16(gated)
        padded[lead : lead + rows, cols] = gated
    for _ in range(4):
        out_fetch.pop(0)()
    taps = 5
    total = 0.0
    for k in range(taps):
        at = lead - (taps - 1) // 2 + k
        total = total + padded[at : at + rows, :] * vector_row(pack, 22 + k)
    live_total = total * mask
    lanes = features // 128
    pack_rows(source, 0, jnp.sum(live_total, axis=0, keepdims=True))
    pack_rows(source, lanes, jnp.sum(live_total * total, axis=0, keepdims=True))
    source[2 * lanes : 2 * lanes + 8, :] = jnp.broadcast_to(live, (8, 128))
    scaled_ref[...] = total

    sums = everywhere(links, nb, source, mid, land_s, land_b, None, out_fetch.pop(0), (ss, rs, sb, rb))
    down.pop(0)()
    down.pop(0)()
    frames = sums[2 * lanes : 2 * lanes + 1, 0:1]
    mean = unpack_rows(sums, 0, lanes) / frames
    inverse = lax.rsqrt(unpack_rows(sums, lanes, lanes) / frames - mean * mean + epsilon)
    stats[0:1, :] = inverse
    stats[1:2, :] = jnp.broadcast_to(frames, (1, features))
    stats[2:8, :] = jnp.zeros((6, features), jnp.float32)
    scaled = (scaled_ref[...] - mean) * inverse
    scaled_ref[...] = scaled
    normed = scaled * vector_row(pack, 3) + vector_row(pack, 17)
    gate = jax.nn.sigmoid(normed)
    act[...] = b16(normed * gate)
    slope[...] = b16(gate * (1.0 + normed * (1.0 - gate)))
    while out_fetch:
        out_fetch.pop(0)()
    down.pop(0)()
    out_ref[...] = rows_ref[...] + (dot_rows(act[...], w_out[...]) + vector_row(pack, 18))
    while down:
        down.pop(0)()


def conv_forward(rows_in, pack, w_in, conv_out, ffn_out, ident):
    ns, nb = lax.axis_size("shard"), lax.axis_size("batch")
    rows, features = rows_in.shape
    shape = jax.ShapeDtypeStruct
    low, full = jnp.bfloat16, jnp.float32
    plain = shape((rows, features), low)
    small = (24, 128)
    return pl.pallas_call(
        functools.partial(conv_body, nb),
        out_shape=[
            shape((rows, features), full), plain, plain, plain, plain,
            shape((rows, features), full), plain, plain, shape((8, features), full),
            shape((features, features), low),
            shape((ffn_out.shape[1] // ns, features), low),
        ],
        in_specs=[VMEM_SPEC] * 3 + [HBM_SPEC] * 2,
        out_specs=[VMEM_SPEC] * 11,
        scratch_shapes=[
            pltpu.VMEM((rows + 16, features), full),
            pltpu.VMEM(small, full), pltpu.VMEM(small, full),
            pltpu.VMEM((ns,) + small, full), pltpu.VMEM((nb,) + small, full),
            pltpu.SemaphoreType.DMA((ns,)), pltpu.SemaphoreType.DMA((ns,)),
            pltpu.SemaphoreType.DMA((nb,)), pltpu.SemaphoreType.DMA((nb,)),
        ]
        + link_scratch(32, 3),
        compiler_params=pltpu.CompilerParams(
            collective_id=ident, has_side_effects=True, vmem_limit_bytes=60 << 20
        ),
        name="conv_forward",
    )(rows_in, pack, w_in, conv_out, ffn_out)


def conv_back_body(
    nb, stream_ref, rows_ref, pack, w_in, w_out, hid, open_ref, gate_ref, gated_ref, scaled_ref, act, slope, stats,
    ride_a, ride_b, early_a, early_b, out_ref, gw_out, gw_in, sums_ref, half_a, half_b,
    padded, normed, grad, inner, source, mid, land_s, land_b, ss, rs, sb, rb, send_sem, recv_sem,
):
    batch = lax.axis_index("batch")
    links = Links(send_sem, recv_sem)
    rows, features = rows_ref.shape
    links.greet(
        [links.near, links.far, links.across]
        + [{"batch": lax.rem(batch + j, nb)} for j in range(1, nb)]
    )
    orders = ride_orders(nb)
    pieces = 4
    ride = [
        Rider(batch, send_sem, recv_sem, at * pieces).halve_pieces(
            source_ref, landing, orders[at][0], pieces, landing.shape[0]
        )
        for at, (source_ref, landing) in enumerate(((ride_a, half_a), (ride_b, half_b)))
    ]
    for start, _, _ in ride:
        start(EARLY)
    lanes = features // 128
    lead, tile, taps = 8, 512, 5
    grad[...] = b16(stream_ref[...])
    gain = vector_row(pack, 3)
    sums_ref[...] = jnp.zeros_like(sums_ref)
    for n in range(features // tile):
        cols = slice(n * tile, (n + 1) * tile)
        value = dot_back(grad[...], w_out[cols, :]) * f32(slope[:, cols])
        normed[:, cols] = value
        for at, total in (
            (0, jnp.sum(value, axis=0, keepdims=True)),
            (lanes, jnp.sum(value * scaled_ref[:, cols], axis=0, keepdims=True)),
        ):
            for i in range(tile // 128):
                row = at + n * (tile // 128) + i
                source[row : row + 1, :] = total[:, i * 128 : (i + 1) * 128]

    def meanwhile():
        @tiles(features, 256)
        def _(cols):
            gw_out[cols, :] = b16(dot_over(act[:, cols], grad[...]))

        sums_ref[4:5, :] = jnp.sum(f32(grad[...]), axis=0, keepdims=True)

    sums = everywhere(links, nb, source, mid, land_s, land_b, None, meanwhile, (ss, rs, sb, rb))
    beta, gamma = unpack_rows(sums, 0, lanes), unpack_rows(sums, lanes, lanes)
    for p in range(EARLY + 1, pieces):
        for start, _, _ in ride:
            start(p)
    sums_ref[5:6, :] = gamma
    sums_ref[6:7, :] = beta
    inverse, frames = stats[0:1, :], stats[1:2, 0:1]
    live = f32(pack[links.shard, 27:28, 0:1])
    mask = f32(f32(lax.broadcasted_iota(jnp.int32, (rows, 1), 0)) < live)
    padded[0:lead, :] = jnp.zeros((lead, features), jnp.float32)
    padded[lead + rows :, :] = jnp.zeros((lead, features), jnp.float32)
    padded[lead : lead + rows, :] = inverse * (
        normed[...] * gain - mask * (gain * beta + scaled_ref[...] * (gain * gamma)) / frames
    )
    given = 0.0
    gated = f32(gated_ref[...])
    for k in range(taps):
        at = lead + (taps - 1) // 2 - k
        moved = padded[at : at + rows, :]
        given = given + moved * vector_row(pack, 22 + k)
        sums_ref[8 + k : 9 + k, :] = jnp.sum(moved * gated, axis=0, keepdims=True)
    left = b16(given * f32(open_ref[...]))
    right = b16(given * f32(gate_ref[...]))
    inner[:, 0:features] = left
    inner[:, features:] = right
    sums_ref[2:3, :] = jnp.sum(f32(left), axis=0, keepdims=True)
    sums_ref[3:4, :] = jnp.sum(f32(right), axis=0, keepdims=True)
    total = dot_back(inner[...], w_in[...])
    scaled, inverse = norm_parts(rows_ref[...])
    out_ref[...] = stream_ref[...] + norm_slope(total, scaled, inverse, vector_row(pack, 2))
    sums_ref[0:1, :] = jnp.sum(total * scaled, axis=0, keepdims=True)
    sums_ref[1:2, :] = jnp.sum(total, axis=0, keepdims=True)

    @tiles(2 * features, 512)
    def _(cols):
        gw_in[:, cols] = b16(dot_over(hid[...], inner[:, cols]))

    for (_, settle, own), landing, early in zip(ride, (half_a, half_b), (early_a, early_b)):
        settle()
        done = early.shape[0]
        landing[0:done] = b16(f32(own[0:done]) + f32(early[...]))
        landing[done:] = b16(f32(own[done:]) + f32(landing[done:]))


def conv_back(stream, rows_in, pack, w_in, w_out, saved, ridden, early, ident):
    ns, nb = lax.axis_size("shard"), lax.axis_size("batch")
    rows, features = rows_in.shape
    shape = jax.ShapeDtypeStruct
    low, full = jnp.bfloat16, jnp.float32
    small = (2 * features // 128, 128)
    return pl.pallas_call(
        functools.partial(conv_back_body, nb),
        out_shape=[
            shape((rows, features), full), shape((features, features), low),
            shape((features, 2 * features), low), shape((16, features), full),
        ]
        + [shape((r.shape[0] // 2, r.shape[1]), low) for r in ridden],
        in_specs=[VMEM_SPEC] * 17,
        out_specs=[VMEM_SPEC] * 6,
        scratch_shapes=[
            pltpu.VMEM((rows + 16, features), full), pltpu.VMEM((rows, features), full),
            pltpu.VMEM((rows, features), low), pltpu.VMEM((rows, 2 * features), low),
            pltpu.VMEM(small, full), pltpu.VMEM(small, full),
            pltpu.VMEM((ns,) + small, full), pltpu.VMEM((nb,) + small, full),
            pltpu.SemaphoreType.DMA((ns,)), pltpu.SemaphoreType.DMA((ns,)),
            pltpu.SemaphoreType.DMA((nb,)), pltpu.SemaphoreType.DMA((nb,)),
        ]
        + link_scratch(8, 1)[:2],
        compiler_params=pltpu.CompilerParams(
            collective_id=ident, has_side_effects=True, vmem_limit_bytes=60 << 20
        ),
        name="conv_back",
    )(stream, rows_in, pack, w_in, w_out, *saved, *ridden, *early)


def rear_body(
    heads, size, nb, stream_ref, rows_ref, pack, hid_b, with_u, with_v, key, value, soft_ref, mix, table, proj,
    w_qkv, w_mine, ride_a, ride_b, start_hbm, hid_hbm, act_hbm, slope_hbm, w_rows_hbm, ffn_in,
    out_ref, gw_qkv, gw_pos, gw_mix, mix_sums, own_sums, gw_in, gw_out, sums_ref, out_a, out_b,
    grad, dq, dk, dx, dp, stream, grad_b, inner, start, hid, act, slope, w_rows, w_in, *refs,
):
    first, second, refs = refs[:5], refs[5:10], refs[10:]
    send_sem, recv_sem, ride_send, ride_recv, load_sem, *between = refs
    links = Links(send_sem, recv_sem)
    batch = lax.axis_index("batch")
    loads = Loads(
        load_sem,
        [
            (slope_hbm, slope), (w_rows_hbm, w_rows), (ffn_in.at[0], w_in), (act_hbm, act), (hid_hbm, hid),
            (start_hbm, start),
        ],
    )
    orders = ride_orders(nb)
    steps = len(orders[0]) - 1
    scale = 1.0 / math.sqrt(size)
    rows, features = rows_ref.shape
    half = rows // 2
    links.greet([links.near, links.far] + [{"batch": flip_bits(batch, 1 << k)} for k in orders[0]])
    inward, outward = [], []
    count = 2 * steps - 1
    for at, (begin, end) in enumerate(((ride_a, out_a), (ride_b, out_b))):
        middle_refs = between[at * count : (at + 1) * count]
        down_refs = [begin, *middle_refs[:steps]]
        up_refs = [*middle_refs[steps - 1 :], end]
        rider = Rider(batch, ride_send, ride_recv, at * 2 * steps)
        inward.append(rider.chain(down_refs, orders[at][1:], rider.halve))
        rider = Rider(batch, ride_send, ride_recv, at * 2 * steps + steps)
        outward.append(rider.chain(up_refs, orders[at][:0:-1], rider.double))

    def tick(chains):
        for chain in chains:
            if chain:
                chain.pop(0)()

    tick(inward)
    grad[0] = b16(stream_ref[...])
    out = [
        links.go(grad.at[0, pl.ds(h * half, half)], grad.at[2, pl.ds(h * half, half)], links.far)
        for h in range(2)
    ]
    near = links.go(grad.at[0], grad.at[1], links.near)
    at_row = lax.broadcasted_iota(jnp.int32, (rows, rows), 0)
    at_col = lax.broadcasted_iota(jnp.int32, (rows, rows), 1)
    flip = b16(f32(at_row + at_col == rows - 1))
    keys = f32(at_col)
    own_sums[...] = jnp.zeros_like(own_sums)

    def work(slot, emit):
        mixed = b16(dot_back(grad[slot], w_mine[...]))
        live = f32(pack[flip_bits(links.shard, slot), 27:28, 0:1])
        for h in range(heads):
            cols = slice(h * size, (h + 1) * size)
            soft = soft_ref[slot, :, h * rows : (h + 1) * rows]
            given = mixed[:, cols]
            grad_soft = dot_back(given, value[slot, :, cols])
            dx[slot, :, cols] = b16(dot_over(b16(soft), given))
            grad_scores = soft * (grad_soft - jnp.sum(grad_soft * soft, axis=-1, keepdims=True))
            raw = b16(jnp.where(keys < live, grad_scores, 0.0) * scale)
            grad_u = dot_rows(raw, key[slot, :, cols])
            dk[slot, :, cols] = b16(dot_over(raw, with_u[slot, :, cols]))
            turned = dot_rows(flip, raw)
            wide = jnp.concatenate([turned, jnp.zeros_like(turned)], 1)
            wide = b16(pltpu.roll(wide, 0, 1, stride=1, stride_axis=0))
            grad_v = dot_rows(wide, proj[:, cols])
            v_turned = b16(dot_rows(flip, with_v[slot, :, cols]))
            dp[slot, :, cols] = b16(dot_over(wide, v_turned))
            own_sums[2:3, cols] += column_sum(grad_u)
            own_sums[3:4, cols] += column_sum(grad_v)
            high = b16(grad_v)
            rest = b16(grad_v - f32(high))
            dq[slot, :, cols] = b16(grad_u + (dot_rows(flip, high) + dot_rows(flip, rest)))
        own_sums[0:1, :] += column_sum(f32(dq[slot]))
        own_sums[1:2, :] += column_sum(f32(dx[slot]))

        @tiles(features, 512)
        def _(cols):
            emit(
                cols,
                dot_back(dq[slot], w_qkv[0, cols, :])
                + dot_back(dk[slot], w_qkv[1, cols, :])
                + dot_back(dx[slot], w_qkv[2, cols, :]),
            )

    sums = Sums(links, first)
    work(0, sums.keep)
    near.wait()
    work(1, sums.give)
    sums.send_near()
    tick(inward)
    on = []
    for h in range(2):
        out[h].wait()
        there = pl.ds(h * half, half)
        on.append(links.go(grad.at[2, there], grad.at[3, there], links.near))
    for copy in on:
        copy.wait()
    work(3, sums.give_far)
    for h in range(2):
        sums.send_back(h)
    work(2, sums.keep_far)
    for h in range(2):
        sums.send_cross(h)
    for at, ref in enumerate((dq, dk, dx)):
        right = flat(ref)

        @tiles(features, 256)
        def _(cols, at=at, right=right):
            gw_qkv[at, cols, :] = b16(dot_over(flat_columns(hid_b, cols, 256), right))

    @tiles(features, 256)
    def _(cols):
        total = dot_over(table[:, cols], dp[0])
        for slot in range(1, 4):
            total = total + dot_over(table[:, cols], dp[slot])
        gw_pos[cols, :] = b16(total)

    gw_mix[...] = b16(dot_over(flat(mix), flat(grad)))
    mix_sums[...] = jnp.zeros_like(mix_sums)
    mix_sums[2:3, :] = column_sum(f32(grad[0]))
    gain = vector_row(pack, 1)

    def fill(h):
        at = slice(h * half, (h + 1) * half)
        given = sums.arrive(h)
        scaled, inverse = norm_parts(rows_ref[at])
        slide = stream_ref[at] + norm_slope(given, scaled, inverse, gain)
        stream[at] = slide
        grad_b[0, at] = b16(0.5 * slide)
        mix_sums[0:1, :] += column_sum(given * scaled)
        mix_sums[1:2, :] += column_sum(given)

    step = ffn_inward(grad_b, inner, slope, w_in, w_rows)

    def back_work(block, emit):
        loads.need(0, 1, 2)
        if block == 1:
            for chain in inward:
                while chain:
                    chain.pop(0)()
            tick(outward)
        step(block, emit)

    back = gather_work_scatter(links, grad_b, fill, back_work, second)
    loads.need(3, 4, 5)
    weight_out(act, grad_b, gw_out)
    tick(outward)
    weight_in(hid, inner, gw_in, sums_ref)
    sums_ref[0:3, :] = jnp.zeros((3, features), jnp.float32)
    sums_ref[2:3, :] = column_sum(f32(grad_b[0]))
    sums_ref[4:8, :] = jnp.zeros((4, features), jnp.float32)
    gain = vector_row(pack, 0)
    for h in range(2):
        at = slice(h * half, (h + 1) * half)
        scaled, inverse = norm_parts(start[at])
        given = back.arrive(h)
        out_ref[at] = stream[at] + norm_slope(given, scaled, inverse, gain)
        sums_ref[0:1, :] += column_sum(given * scaled)
        sums_ref[1:2, :] += column_sum(given)
    for chain in outward:
        while chain:
            chain.pop(0)()


def rear(stream, rows_one, pack, saved_mix, table, proj, w_qkv, w_mine, ridden, rows_in, saved, w_rows, ffn_in, heads, ident):
    rows, features = rows_one.shape
    hidden = ffn_in.shape[2]
    width = proj.shape[1]
    nb = lax.axis_size("batch")
    steps = nb.bit_length() - 2
    low, full = jnp.bfloat16, jnp.float32
    shape, vmem = jax.ShapeDtypeStruct, pltpu.VMEM
    dma = pltpu.SemaphoreType.DMA
    narrow = vmem((4, rows, width), low)
    between = []
    for r in ridden:
        sizes = [r.shape[0] >> k for k in range(1, steps + 1)]
        between += [vmem((size, r.shape[1]), low) for size in sizes + sizes[-2::-1]]
    return pl.pallas_call(
        functools.partial(rear_body, heads, width // heads, nb),
        out_shape=[
            shape((rows, features), full), shape((3, features, width), low), shape((features, width), low),
            shape((width, features), low), shape((8, features), full), shape((8, width), full),
            shape((features, hidden), low), shape((hidden, features), low), shape((8, features), full),
        ]
        + [shape(r.shape, low) for r in ridden],
        in_specs=[VMEM_SPEC] * 16 + [HBM_SPEC] * 6,
        out_specs=[VMEM_SPEC] * 11,
        scratch_shapes=[
            vmem((4, rows, features), low), narrow, narrow, narrow, vmem((4, 2 * rows, width), low),
            vmem((rows, features), full), vmem((4, rows, features), low), vmem((4, rows, hidden), low),
            vmem((rows, features), full), vmem((4, rows, features), low), vmem((4, rows, hidden), low),
            vmem((4, rows, hidden), low), vmem((hidden, features), low), vmem((features, hidden), low),
        ]
        + sums_scratch(rows, features)
        + sums_scratch(rows, features)
        + [dma((24,)), dma((24,)), dma((4 * steps,)), dma((4 * steps,)), dma((6,))]
        + between,
        compiler_params=pltpu.CompilerParams(
            collective_id=ident, has_side_effects=True, vmem_limit_bytes=62 << 20
        ),
        name="rear",
    )(stream, rows_one, pack, *saved_mix, table, proj, w_qkv, w_mine, *ridden, rows_in, *saved, w_rows, ffn_in)


def body(
    tokens, cotangent, lengths, ffn_in, ffn_out, ffn_bias, qkv_proj, pos_proj, out_proj,
    conv_in, conv_out, depthwise, norm_gains, biases,
):
    _, length, features = tokens.shape
    ns, nb = lax.axis_size("shard"), lax.axis_size("batch")
    width = features // ns
    heads = HEADS // ns
    rows_in = tokens[0]

    own_length = jnp.broadcast_to(b16(f32(lengths))[:, None], (5, width))
    pack_in = jnp.concatenate([norm_gains, biases, depthwise, own_length], 0)
    b_in = f32(ffn_bias)

    rates = jnp.exp(
        jnp.arange(features // 2, dtype=jnp.float32) * (-2.0 * math.log(10000.0) / features)
    )
    turns = jnp.concatenate(
        [
            length - 1.0 - jnp.arange(16, dtype=jnp.float32),
            -16.0 * jnp.arange(2 * length // 16, dtype=jnp.float32),
        ]
    )
    angles = turns[:, None] * rates[None, :]
    base = jnp.concatenate([jnp.sin(angles), jnp.cos(angles)], 1)
    (
        rows_one, rows_two, pack, table, proj, with_u, with_v, key, value, mix, wc_in, w_mine,
        *saved_one, w_rows_one, hidden_mix, soft,
    ) = front(
        rows_in, pack_in, b_in, base, biases, pos_proj, qkv_proj, ffn_in, ffn_out, out_proj, conv_in, heads, 5
    )
    saved_mix = (hidden_mix, with_u, with_v, key, value, soft, mix)
    rows_three, *saved_conv, wc_out, w_rows_two = conv_forward(
        rows_two, pack, wc_in, conv_out, ffn_out, 10
    )
    result, stream, two_in, two_out, two_sums, *early = middle(
        rows_three, pack, b_in, w_rows_two, cotangent[0], ffn_in, 6
    )

    stream, grad_conv_out, grad_conv_in, conv_sums, *ridden = conv_back(
        stream, rows_two, pack, wc_in, wc_out, saved_conv, (two_in, two_out), early, 11
    )
    stream, grad_qkv, grad_pos, grad_out, mix_sums, own_sums, one_in, one_out, one_sums, *ridden = rear(
        stream, rows_one, pack, saved_mix, table, proj, qkv_proj, w_mine, ridden, rows_in, saved_one, w_rows_one,
        ffn_in, heads, 12
    )
    tall, deep = one_in.shape
    piece = max(128, 8 * nb)
    *sums, out_gains, out_biases, out_taps, out_hidden = tail_sum(
        [grad_out, one_out, one_in] + [grad_qkv[at] for at in range(3)] + [grad_pos, grad_conv_in, grad_conv_out],
        ridden,
        [one_sums, mix_sums, two_sums, conv_sums, own_sums],
        [("turn", 4, None), ("turn", 1, 0), ("plain", 0, 0)]
        + [("plain", 2, at) for at in range(3)]
        + [("plain", 3, None), ("gather", 5, None), ("gather", 6, None)],
        [
            (2, tall, deep), (2, ns * deep, width), (3, tall, width), (tall, width), (tall, width),
            (tall, 2 * width), (tall, width),
        ],
        ["near", "line"],
        [width, piece, piece] + [min(tall, 4 * piece)] * 4 + [2 * piece, min(tall, 4 * piece)],
        deep,
        4,
    )
    return (
        result[None],
        stream[None],
        f32(sums[0]),
        f32(sums[1]),
        out_hidden,
        f32(sums[2]),
        f32(sums[3]),
        f32(sums[4]),
        f32(sums[5]),
        f32(sums[6]),
        out_taps,
        out_gains,
        out_biases,
    )


def solution(mesh):
    rows = P(("batch", "shard"), None, None)
    cube, flat = P(None, None, "shard"), P(None, "shard")
    return jax.shard_map(
        body,
        mesh=mesh,
        in_specs=(rows, rows, P(("batch", "shard")), cube, cube, flat, cube)
        + (flat,) * 7,
        out_specs=(rows, rows, cube, cube, flat, cube) + (flat,) * 7,
        check_vma=False,
    )
```

```python
import functools
import math

import jax
import jax.numpy as jnp
from jax import lax
from jax.experimental import pallas as pl
from jax.experimental.pallas import tpu as pltpu
from jax.sharding import PartitionSpec as P

HEADS = 8
MESH = pl.DeviceIdType.MESH
VMEM_SPEC = pl.BlockSpec(memory_space=pltpu.VMEM)
HBM_SPEC = pl.BlockSpec(memory_space=pltpu.HBM)
epsilon = 1e-05


def f32(a):
    return a.astype(jnp.float32)


def b16(a):
    return a.astype(jnp.bfloat16)


def norm_rows(values_in, gain_row, bias_row):
    row_mean = jnp.mean(values_in, axis=-1, keepdims=True)
    centered = values_in - row_mean
    spread = jnp.mean(centered * centered, axis=-1, keepdims=True)
    return centered * lax.rsqrt(spread + epsilon) * gain_row + bias_row


def dot_rows(a, b):
    return jnp.dot(a, b, preferred_element_type=jnp.float32)


def dot_back(a, b):
    return lax.dot_general(a, b, (((1,), (1,)), ((), ())), preferred_element_type=jnp.float32)


def dot_over(a, b):
    return lax.dot_general(a, b, (((0,), (0,)), ((), ())), preferred_element_type=jnp.float32)


def exchange(axis, index, count, source, landing, send_sem, recv_sem):
    copies = []
    for j in range(1, count):
        peer = lax.rem(index + j, count)
        copies.append(
            pltpu.make_async_remote_copy(
                src_ref=source,
                dst_ref=landing.at[index],
                send_sem=send_sem.at[j],
                recv_sem=recv_sem.at[j],
                device_id={axis: peer},
                device_id_type=MESH,
            )
        )
    return copies


def sum_slots(ref, count):
    total = ref[0]
    for j in range(1, count):
        total = total + ref[j]
    return total


class Loads:
    def __init__(self, sem, pairs):
        self.open = []
        for at, (src, dst) in enumerate(pairs):
            copy = pltpu.make_async_copy(src, dst, sem.at[at])
            copy.start()
            self.open.append(copy)

    def need(self, *which):
        for at in which:
            if self.open[at] is not None:
                self.open[at].wait()
                self.open[at] = None


class Flush:
    def __init__(self, sem):
        self.sem, self.open = sem, []

    def go(self, src, dst):
        copy = pltpu.make_async_copy(src, dst, self.sem.at[len(self.open)])
        copy.start()
        self.open.append(copy)

    def settle(self):
        for copy in self.open:
            copy.wait()


class Chunk:
    def __init__(self, at, source, row, rows, columns, first, count):
        self.at, self.source, self.row, self.rows, self.columns = at, source, row, rows, columns
        extra = [(1 << k, k) for k in range(3, count.bit_length() - 1)]
        line = (6, 1)
        if first == "near":
            self.pre, self.post = [(1, 0)], [line] + extra
        else:
            self.pre, self.post = [], [line, (1, 0)] + extra
        size, self.landings = rows, []
        for _ in self.pre:
            size //= 2
            self.landings.append((size, columns))
        self.landings.append((size, columns))
        for _ in self.post:
            size //= 2
            self.landings.append((size, columns))
        self.steps = len(self.landings)


def bit_of(value, k):
    return lax.rem(lax.div(value, 1 << k), 2)


def flip_bits(value, mask):
    out = value
    k = 0
    while (1 << k) <= mask:
        if mask & (1 << k):
            out = out + (1 - 2 * bit_of(value, k)) * (1 << k)
        k += 1
    return out


class Mover:
    def __init__(self, chunk, batch, source, base, held, landings, sems, finish, early):
        self.c, self.b = chunk, batch
        self.source, self.base, self.held, self.landings, self.sems = source, base, held, landings, sems
        lo, hi = bit_of(batch, 1), bit_of(batch, 2)
        self.inner = lo != hi
        self.ended = lo == hi
        self.finish, self.early = finish, early
        self.build()

    def copy(self, at, src, dst, mask):
        send, recv = self.sems
        return pltpu.make_async_remote_copy(
            src_ref=src,
            dst_ref=dst,
            send_sem=send.at[self.c.at, at],
            recv_sem=recv.at[self.c.at, at],
            device_id={"batch": flip_bits(self.b, mask)},
            device_id_type=MESH,
        )

    def build(self):
        c = self.c
        held = self.held
        here, base = self.source, self.base
        off, size, step = 0, c.rows, 0
        plan, trail = [], []
        sequence = [("all",) + p for p in c.pre] + [("fold", 2, None)]
        sequence += [("inner",) + p for p in c.post]
        for kind, mask, sel in sequence:
            landing = self.landings[step]
            if kind == "fold":
                own = row_view(here, base, size)
                cp = self.copy(step, own, landing, mask)
            else:
                size //= 2
                mine = bit_of(self.b, sel)
                cp = self.copy(step, row_view(here, base + (1 - mine) * size, size), landing, mask)
                own = row_view(here, base + mine * size, size)
                off = off + mine * size
            trail.append((kind, mask, off, size))
            step += 1
            out = landing if step < len(sequence) else held(off, size)
            plan.append((kind, cp, (own, landing, out)))
            here, base = landing, 0
        for kind, mask, off, size in reversed(trail):
            cp = self.copy(step, held(off, size), held(off, size), mask)
            plan.append(("unfold" if kind == "fold" else kind, cp, None))
            step += 1
        self.plan = plan
        self.depth = len(plan) + len(self.early)

    def begin(self, k):
        kind, cp, _ = self.plan[k]
        if kind == "all":
            cp.start()
        elif kind == "fold":
            pl.when(self.ended)(cp.start)
        else:
            pl.when(self.inner)(cp.start)

    def end(self, k):
        kind, cp, add = self.plan[k]

        def gather():
            if add is not None:
                own, landing, out = add
                out[...] = b16(f32(own[...]) + f32(landing[...]))

        if kind == "all":
            cp.wait()
            gather()
        elif kind in ("fold", "unfold"):
            sender, taker = (
                (self.ended, self.inner) if kind == "fold" else (self.inner, self.ended)
            )
            pl.when(sender)(cp.wait_send)

            @pl.when(taker)
            def _():
                cp.wait_recv()
                gather()
        else:

            @pl.when(self.inner)
            def _():
                cp.wait()
                gather()

    def advance(self, k):
        if k < len(self.early):
            self.early[k]()
            return
        k -= len(self.early)
        if k > 0:
            self.end(k - 1)
        elif self.early:
            self.settle_early()
        if k < len(self.plan):
            self.begin(k)
        else:
            self.finish(self.c)


def row_view(ref, start, size):
    start = start if isinstance(start, int) else pl.multiple_of(start, 16 if size % 16 == 0 else 8)
    return ref.at[pl.ds(start, size)]


def column_block(index, columns):
    return pl.ds(pl.multiple_of(index * columns, 128), columns)


class Rider:
    def __init__(self, batch, send, recv, first):
        self.b, self.send, self.recv, self.at = batch, send, recv, first

    def go(self, src, dst, bit):
        copy = pltpu.make_async_remote_copy(
            src_ref=src, dst_ref=dst, send_sem=self.send.at[self.at], recv_sem=self.recv.at[self.at],
            device_id={"batch": flip_bits(self.b, 1 << bit)}, device_id_type=MESH,
        )
        self.at += 1
        copy.start()
        return copy

    def halve_pieces(self, source, landing, bit, pieces, half):
        size = half // pieces
        mine = bit_of(self.b, bit)
        copies = []

        def start(p):
            copies.append(
                self.go(
                    row_view(source, (1 - mine) * half + p * size, size), row_view(landing, p * size, size), bit
                )
            )

        def settle():
            for copy in copies:
                copy.wait()

        return start, settle, row_view(source, mine * half, half)

    def halve(self, source, landing, bit):
        half = landing.shape[0]
        mine = bit_of(self.b, bit)
        copy = self.go(row_view(source, (1 - mine) * half, half), landing, bit)

        def end():
            copy.wait()
            own = row_view(source, mine * half, half)
            landing[...] = b16(f32(own[...]) + f32(landing[...]))

        return end

    def double(self, source, target, bit):
        half = source.shape[0]
        there = row_view(target, bit_of(self.b, bit) * half, half)
        copy = self.go(source, there, bit)
        there[...] = source[...]
        return copy.wait

    def chain(self, refs, bits, move):
        ends, stages = [], []
        for i, bit in enumerate(bits):

            def stage(i=i, bit=bit):
                if ends:
                    ends.pop()()
                ends.append(move(refs[i], refs[i + 1], bit))

            stages.append(stage)
        stages.append(lambda: ends.pop()())
        return stages


def ride_orders(count):
    bits = list(range(count.bit_length() - 1))
    return bits, [1, 0] + bits[2:]


def tail_body(specs, chunks, ns, nb, n_in, n_out, *refs):
    (one_sums, mix_sums, two_sums, conv_sums, own_sums), refs = refs[:5], refs[5:]
    given, refs = refs[: n_in + 2], refs[n_in + 2 :]
    outs_hbm, refs = refs[:n_out], refs[n_out:]
    (o_gains, o_biases, o_taps, o_hidden), refs = refs[:4], refs[4:]
    send, recv, turn_send, turn_recv, pre_send, pre_recv, ride_send, ride_recv = refs[:8]
    ss, rs, sb, rb, wide, land_s, mid, land_b, ride_fin, load_sem = refs[8:18]
    shard, batch = lax.axis_index("shard"), lax.axis_index("batch")
    flush = Flush(refs[18])
    outs = refs[19 : 19 + n_out]
    rest = list(refs[19 + n_out :])
    pairs, ins, blocks = [], [], {}
    for i, ref in enumerate(given):
        if i < n_in and specs["arrays"][i][0] == "gather":
            pair = []
            for index in (shard, flip_bits(shard, 2)):
                held_block = rest.pop(0)
                pairs.append((ref.at[:, column_block(index, held_block.shape[1])], held_block))
                pair.append(held_block)
            blocks[i] = (pair, (len(pairs) - 2, len(pairs) - 1))
            ins.append(ref)
        else:
            held_ref = rest.pop(0)
            pairs.append((ref, held_ref))
            blocks[i] = (None, (len(pairs) - 1,))
            ins.append(held_ref)
    loads = Loads(load_sem, pairs)
    ins, ridden = ins[:n_in], ins[n_in:]
    shard, batch = lax.axis_index("shard"), lax.axis_index("batch")
    barrier = pltpu.get_barrier_semaphore()
    greeted = [{"batch": lax.rem(batch + j, nb)} for j in range(1, nb)]
    greeted += [{"shard": flip_bits(shard, m)} for m in range(1, ns)]
    for device in greeted:
        pl.semaphore_signal(barrier, inc=1, device_id=device, device_id_type=MESH)
    width = own_sums.shape[1]
    for t in range(ns):
        cols = slice(t * width, (t + 1) * width)
        wide[t, 0:3, :] = one_sums[0:3, cols]
        wide[t, 3:6, :] = mix_sums[0:3, cols]
        wide[t, 6:9, :] = two_sums[0:3, cols]
        wide[t, 9:14, :] = conv_sums[0:5, cols]
        wide[t, 14:19, :] = conv_sums[8:13, cols]
        wide[t, 19:21, :] = two_sums[4:6, cols]
        wide[t, 21:24, :] = jnp.zeros((3, width), jnp.float32)
    pl.semaphore_wait(barrier, len(greeted))

    vector_copies = []
    for j in range(1, ns):
        peer = lax.rem(shard + j, ns)
        copy = pltpu.make_async_remote_copy(
            src_ref=wide.at[peer], dst_ref=land_s.at[shard], send_sem=ss.at[j], recv_sem=rs.at[j],
            device_id={"shard": peer}, device_id_type=MESH,
        )
        copy.start()
        vector_copies.append(copy)
    land_s[shard] = wide[shard]

    def vectors_on():
        for copy in vector_copies:
            copy.wait()
        mid[0:24, :] = sum_slots(land_s, ns)
        mid[24:28, :] = own_sums[0:4, :]
        per = one_sums.shape[1] // width
        for t in range(per):
            cols = slice(t * width, (t + 1) * width)
            mid[28 + t : 29 + t, :] = one_sums[3:4, cols]
            mid[28 + per + t : 29 + per + t, :] = two_sums[3:4, cols]
        mid[28 + 2 * per :, :] = jnp.zeros((mid.shape[0] - 28 - 2 * per, width), jnp.float32)
        vector_copies[:] = exchange("batch", batch, nb, mid, land_b, sb, rb)
        for copy in vector_copies:
            copy.start()
        land_b[batch] = mid[...]

    def vectors_out():
        for copy in vector_copies:
            copy.wait()
        vec = sum_slots(land_b, nb)
        row = lambda k: vec[k : k + 1]
        mine = conv_sums[5:7, column_block(shard, width)]
        gains = [row(0), row(3), row(9), mine[0:1], row(6), row(19)]
        order = [1, 2, 4, 24, 25, 5, 26, 27, 10, 11, 12, None, 13, 7, 8, 20]
        for k, value in enumerate(gains):
            o_gains[k : k + 1, :] = value
        for k, at in enumerate(order):
            o_biases[k : k + 1, :] = mine[1:2] if at is None else row(at)
        o_taps[...] = vec[14:19]
        per = o_hidden.shape[1] // width
        for k in range(2):
            for t in range(per):
                at = 28 + k * per + t
                o_hidden[k : k + 1, t * width : (t + 1) * width] = row(at)

    late = []

    def leave(out, lead, start, rows):
        src, dst = outs[out], outs_hbm[out]
        if lead is not None:
            src, dst = src.at[lead], dst.at[lead]
        flush.go(src.at[pl.ds(start, rows)], dst.at[pl.ds(start, rows)])

    def turn(c_at, total, row, rows, out, lead):
        target = outs[out] if lead is None else outs[out].at[lead]
        columns = target.shape[1]
        height = target.shape[0] // ns
        there = row_view(target, shard * height + row, rows)
        copies = []
        for j in range(1, ns):
            peer = flip_bits(shard, j)
            copy = pltpu.make_async_remote_copy(
                src_ref=total.at[:, column_block(peer, columns)],
                dst_ref=there,
                send_sem=turn_send.at[c_at, j],
                recv_sem=turn_recv.at[c_at, j],
                device_id={"shard": peer},
                device_id_type=MESH,
            )
            copy.start()
            copies.append(copy)
        there[...] = total[:, column_block(shard, columns)]

        def after():
            for copy in copies:
                copy.wait()
            for t in range(ns):
                leave(out, lead, t * height + row, rows)

        late.append(after)

    rides = []
    orders = ride_orders(nb)
    plain_target = outs[0].at[1]
    rider_a = Rider(batch, ride_send, ride_recv, 0)
    rider_b = Rider(batch, ride_send, ride_recv, 1)
    loads.need(*blocks[n_in][1], *blocks[n_in + 1][1])
    end_a = rider_a.double(ridden[0], plain_target, orders[0][0])
    end_b = rider_b.double(ridden[1], ride_fin, orders[1][0])

    movers = []
    for c in chunks:
        kind, out, lead = specs["arrays"][c.source]
        source, base, early, settle = ins[c.source], c.row, [], None
        if kind == "gather":
            near_land, far_land = rest.pop(0), rest.pop(0)
            whole, columns, rows = ins[c.source], c.columns, pl.ds(c.row, c.rows)
            own_block, far_block = blocks[c.source][0]
            state = {}

            def pre(at, src, dst, mask, c=c):
                copy = pltpu.make_async_remote_copy(
                    src_ref=src, dst_ref=dst, send_sem=pre_send.at[c.at, at], recv_sem=pre_recv.at[c.at, at],
                    device_id={"shard": flip_bits(shard, mask)}, device_id_type=MESH,
                )
                copy.start()
                return copy

            def first(near_land=near_land, whole=whole, columns=columns, rows=rows, state=state, pre=pre):
                state["n"] = [
                    pre(i, whole.at[rows, column_block(flip_bits(shard, m), columns)], near_land.at[i], 1)
                    for i, m in enumerate((1, 3))
                ]

            def second(
                near_land=near_land, far_land=far_land, far_block=far_block, rows=rows, state=state, pre=pre,
            ):
                for copy in state["n"]:
                    copy.wait()
                near_land[1] = b16(f32(near_land[1]) + f32(far_block[rows]))
                state["f"] = pre(2, near_land.at[1], far_land, 2)

            def settle(
                near_land=near_land, far_land=far_land, own_block=own_block, rows=rows, state=state,
            ):
                state["f"].wait()
                far_land[...] = b16(
                    f32(far_land[...]) + f32(near_land[0]) + f32(own_block[rows])
                )

            early = [first, second]
            source, base = far_land, 0
        if kind == "turn":
            total = rest.pop(0)
            held = lambda off, size, total=total: row_view(total, off, size)

            def finish(c, total=total, out=out, lead=lead):
                turn(c.at, total, c.row, c.rows, out, lead)
        else:
            target = outs[out] if lead is None else outs[out].at[lead]
            held = lambda off, size, target=target, c=c: row_view(target, c.row + off, size)

            def finish(c, out=out, lead=lead):
                leave(out, lead, c.row, c.rows)
        landings = [rest.pop(0) for _ in range(c.steps)]
        m = Mover(c, batch, source, base, held, landings, (send, recv), finish, early)
        m.settle_early = settle
        movers.append(m)
    starts, lag = [], specs["lag"]
    for i, m in enumerate(movers):
        starts.append(max(0, i // lag - len(m.early)))
    rounds = max(s + m.depth + 1 for s, m in zip(starts, movers))
    for r in range(rounds):
        ready, late[:] = late[:], []
        if r == 1:
            vectors_on()
        if r == 2:
            end_b()
            turn(len(chunks), ride_fin, 0, ride_fin.shape[0], 1, 1)
        if r == 3:
            vectors_out()
            end_a()
            leave(0, 1, 0, outs[0].shape[1])
        for s, m in zip(starts, movers):
            if 0 <= r - s <= m.depth:
                loads.need(*blocks[m.c.source][1])
                m.advance(r - s)
        for after in ready:
            after()
    for after in late:
        after()
    flush.settle()


def tail_sum(arrays, ridden, sums, kinds, outputs, firsts, chunk_rows, hidden, ident):
    ns, nb = lax.axis_size("shard"), lax.axis_size("batch")
    low, full = jnp.bfloat16, jnp.float32
    chunks = []
    for i, a in enumerate(arrays):
        step = chunk_rows[i]
        columns = a.shape[1] // ns if kinds[i][0] == "gather" else a.shape[1]
        for row in range(0, a.shape[0], step):
            chunks.append(Chunk(len(chunks), i, row, step, columns, firsts[len(chunks) % len(firsts)], nb))
    depth = max(2 * c.steps for c in chunks)
    specs = dict(arrays=kinds, lag=2)
    width = sums[-1].shape[1]
    per = hidden // width
    small = -(-(28 + 2 * per) // 8) * 8
    dma = pltpu.SemaphoreType.DMA
    n = len(chunks)
    scratch = [
        dma((n, depth)), dma((n, depth)), dma((n + 1, ns)), dma((n + 1, ns)), dma((n, 3)), dma((n, 3)),
        dma((2,)), dma((2,)), dma((ns,)), dma((ns,)), dma((nb,)), dma((nb,)),
        pltpu.VMEM((ns, 24, width), full), pltpu.VMEM((ns, 24, width), full),
        pltpu.VMEM((small, width), full), pltpu.VMEM((nb, small, width), full),
        pltpu.VMEM((2 * ridden[1].shape[0], ridden[1].shape[1]), low),
        dma((2 * len(arrays) + 2,)),
        dma(((ns + 1) * (n + 1) + 1,)),
    ]
    scratch += [pltpu.VMEM(o, low) for o in outputs]
    for i, a in enumerate(list(arrays) + list(ridden)):
        if i < len(arrays) and kinds[i][0] == "gather":
            scratch += [pltpu.VMEM((a.shape[0], a.shape[1] // ns), low)] * 2
        else:
            scratch.append(pltpu.VMEM(a.shape, low))
    for c in chunks:
        if kinds[c.source][0] == "gather":
            scratch += [pltpu.VMEM((2, c.rows, c.columns), low), pltpu.VMEM((c.rows, c.columns), low)]
        if kinds[c.source][0] == "turn":
            scratch.append(pltpu.VMEM((c.rows, c.columns), low))
        scratch += [pltpu.VMEM(shape, low) for shape in c.landings]
    shape = jax.ShapeDtypeStruct
    shapes = [shape(s, low) for s in outputs]
    shapes += [shape((6, width), full), shape((16, width), full), shape((5, width), full), shape((2, hidden), full)]
    operands = list(sums) + list(arrays) + list(ridden)
    return pl.pallas_call(
        functools.partial(tail_body, specs, chunks, ns, nb, len(arrays), len(outputs)),
        out_shape=shapes,
        in_specs=[VMEM_SPEC] * len(sums) + [HBM_SPEC] * (len(arrays) + 2),
        out_specs=[HBM_SPEC] * len(outputs) + [VMEM_SPEC] * 4,
        scratch_shapes=scratch,
        compiler_params=pltpu.CompilerParams(
            collective_id=ident, has_side_effects=True, vmem_limit_bytes=60 << 20
        ),
        name="tail_sum",
    )(*operands)


def widen_body(count, others, slots, *refs):
    n = count + others
    ins, outs = refs[:n], refs[n : 2 * n]
    stages, in_sem, out_sem, pass_sem = refs[2 * n : -3], refs[-3], refs[-2], refs[-1]
    passed = []
    for at in range(others):
        passed.append(pltpu.make_async_copy(ins[count + at], outs[count + at], pass_sem.at[at]))
        passed[-1].start()
    half = len(stages) // 2
    items, used = [], {}
    for src, dst in zip(ins[:count], outs[:count]):
        for lead in range(src.shape[0]) if len(src.shape) == 3 else [None]:
            source = src if lead is None else src.at[lead]
            target = dst if lead is None else dst.at[lead]
            rows, columns = source.shape
            kind = [k.shape[2] for k in stages[:half]].index(columns)
            size = stages[kind].shape[1]
            for row in range(0, rows, size):
                slot = used.get(kind, 0) % slots
                used[kind] = used.get(kind, 0) + 1
                items.append((source.at[pl.ds(row, size)], target.at[pl.ds(row, size)], kind, slot))
    items.sort(key=lambda item: item[2])
    loads, stores = {}, {}

    def load(i):
        if i < len(items):
            source, _, kind, slot = items[i]
            loads[i] = pltpu.make_async_copy(source, stages[kind].at[slot], in_sem.at[kind, slot])
            loads[i].start()

    ahead = slots - 1
    for i in range(ahead):
        load(i)
    for i, (_, target, kind, slot) in enumerate(items):
        loads[i].wait()
        if (kind, slot) in stores:
            stores.pop((kind, slot)).wait()
        narrow, wide = stages[kind].at[slot], stages[half + kind].at[slot]

        @pl.loop(0, narrow.shape[0] // 64)
        def _(k, narrow=narrow, wide=wide):
            part = pl.ds(pl.multiple_of(k * 64, 64), 64)
            wide[part] = f32(narrow[part])

        stores[kind, slot] = pltpu.make_async_copy(wide, target, out_sem.at[kind, slot])
        stores[kind, slot].start()
        load(i + ahead)
    for copy in list(stores.values()) + passed:
        copy.wait()


def widen(arrays, others):
    columns = sorted({a.shape[-1] for a in arrays})
    slots = 6
    least = lambda c: min([a.shape[-2] for a in arrays if a.shape[-1] == c] + [(256 * 1024) // c])
    stages = [pltpu.VMEM((slots, least(c), c), d) for d in (jnp.bfloat16, jnp.float32) for c in columns]
    dma = pltpu.SemaphoreType.DMA
    return pl.pallas_call(
        functools.partial(widen_body, len(arrays), len(others), slots),
        out_shape=[jax.ShapeDtypeStruct(a.shape, jnp.float32) for a in (*arrays, *others)],
        in_specs=[HBM_SPEC] * len(arrays) + [VMEM_SPEC] * len(others),
        out_specs=[HBM_SPEC] * (len(arrays) + len(others)),
        scratch_shapes=stages + [dma((len(columns), slots)), dma((len(columns), slots)), dma((len(others),))],
        compiler_params=pltpu.CompilerParams(vmem_limit_bytes=60 << 20),
        name="widen",
    )(*arrays, *others)


class Links:
    def __init__(self, send, recv):
        self.send, self.recv, self.count = send, recv, 0
        s = lax.axis_index("shard")
        self.shard = s
        self.near = {"shard": flip_bits(s, 1)}
        self.far = {"shard": flip_bits(s, 2)}
        self.across = {"shard": flip_bits(s, 3)}

    def greet(self, devices):
        barrier = pltpu.get_barrier_semaphore()
        for device in devices:
            pl.semaphore_signal(barrier, inc=1, device_id=device, device_id_type=MESH)
        pl.semaphore_wait(barrier, len(devices))

    def go(self, src, dst, device):
        at = self.count
        self.count += 1
        copy = pltpu.make_async_remote_copy(
            src_ref=src, dst_ref=dst, send_sem=self.send.at[at], recv_sem=self.recv.at[at],
            device_id=device, device_id_type=MESH,
        )
        copy.start()
        return copy


def sums_scratch(rows, columns):
    half = rows // 2
    return [
        pltpu.VMEM((2, rows, columns), jnp.float32),
        pltpu.VMEM((4, half, columns), jnp.bfloat16),
        pltpu.VMEM((4, half, columns), jnp.bfloat16),
        pltpu.VMEM((2, half, columns), jnp.bfloat16),
        pltpu.VMEM((2, half, columns), jnp.bfloat16),
    ]


class Sums:
    def __init__(self, links, refs):
        self.links = links
        self.part, self.send, self.land, self.cross, self.land_cross = refs
        self.half = self.send.shape[1]
        self.near, self.crossing, self.backs = None, [], []

    def rows(self, h):
        return slice(h * self.half, (h + 1) * self.half)

    def keep(self, cols, value):
        self.part[0, :, cols] = value

    def keep_far(self, cols, value):
        self.part[1, :, cols] = value

    def give(self, cols, value):
        self.send[0, :, cols] = b16(value[: self.half])
        self.send[1, :, cols] = b16(value[self.half :])

    def give_far(self, cols, value):
        self.send[2, :, cols] = b16(value[: self.half])
        self.send[3, :, cols] = b16(value[self.half :])

    def split(self, h):
        def emit(cols, value):
            self.part[1, self.rows(h), cols] = value[: self.half]
            self.send[2 + h, :, cols] = b16(value[self.half :])

        return emit

    def send_near(self):
        both = pl.ds(0, 2)
        self.near = self.links.go(self.send.at[both], self.land.at[both], self.links.near)

    def send_back(self, h):
        self.backs.append(self.links.go(self.send.at[2 + h], self.land.at[2 + h], self.links.near))

    def send_cross(self, h):
        self.backs[h].wait()
        self.cross[h] = b16(self.part[1, self.rows(h)] + f32(self.land[2 + h]))
        self.crossing.append(self.links.go(self.cross.at[h], self.land_cross.at[h], self.links.far))

    def arrive(self, h):
        if self.near is not None:
            self.near.wait()
            self.near = None
        self.crossing[h].wait()
        return self.part[0, self.rows(h)] + f32(self.land[h]) + f32(self.land_cross[h])


def gather_work_scatter(links, x, fill, work, refs):
    sums = Sums(links, refs)
    half = x.shape[1] // 2
    out = []
    for h in range(2):
        fill(h)
        out.append(links.go(x.at[0, pl.ds(h * half, half)], x.at[2 + h, pl.ds(0, half)], links.far))
    near = links.go(x.at[0], x.at[1], links.near)
    work(0, sums.keep)
    near.wait()
    work(1, sums.give)
    sums.send_near()
    for h in range(2):
        out[h].wait()
        on = links.go(x.at[2 + h, pl.ds(0, half)], x.at[2 + h, pl.ds(half, half)], links.near)
        on.wait()
        work(2 + h, sums.split(h))
        sums.send_back(h)
        sums.send_cross(h)
    return sums


def tiles(total, size):
    def over(body):
        pl.loop(0, total // size)(
            lambda n: body(pl.ds(pl.multiple_of(n * size, size), size))
        )

    return over


def norm_parts(rows):
    row_mean = jnp.mean(rows, axis=-1, keepdims=True)
    centered = rows - row_mean
    inverse = lax.rsqrt(jnp.mean(centered * centered, axis=-1, keepdims=True) + epsilon)
    return centered * inverse, inverse


def norm_slope(grad, scaled, inverse, gain):
    inner = grad * gain
    return inverse * (
        inner
        - jnp.mean(inner, axis=-1, keepdims=True)
        - scaled * jnp.mean(inner * scaled, axis=-1, keepdims=True)
    )


def column_sum(value):
    return jnp.sum(value, axis=0, keepdims=True)


def ffn_up(hid, act, slope, w_in, b_ref, which):
    def run(block):
        @tiles(w_in.shape[1], 512)
        def _(cols):
            pre = dot_rows(hid[block], w_in[:, cols]) + f32(b_ref[which : which + 1, cols])
            gate = jax.nn.sigmoid(pre)
            act[block, :, cols] = b16(pre * gate)
            slope[block, :, cols] = b16(gate * (1.0 + pre * (1.0 - gate)))

    return run


def ffn_down(act, w_rows):
    def run(block, emit):
        @tiles(w_rows.shape[1], 512)
        def _(cols):
            emit(cols, dot_rows(act[block], w_rows[:, cols]))

    return run


def ffn_inward(grad, inner, slope, w_in, w_rows):
    def run(block, emit):
        @tiles(w_in.shape[1], 512)
        def _(cols):
            wide = dot_back(grad[block], w_rows[cols, :])
            inner[block, :, cols] = b16(wide * f32(slope[block, :, cols]))

        @tiles(w_in.shape[0], 512)
        def _(cols):
            emit(cols, dot_back(inner[block], w_in[cols, :]))

    return run


def flat(ref):
    return ref[...].reshape(ref.shape[0] * ref.shape[1], ref.shape[2])


def flat_columns(ref, cols, size):
    return ref[:, :, cols].reshape(ref.shape[0] * ref.shape[1], size)


def weight_out(act, grad, gw_out):
    @tiles(act.shape[2], 256)
    def _(cols):
        gw_out[cols, :] = b16(dot_over(flat_columns(act, cols, 256), flat(grad)))


def weight_in(hid, inner, gw_in, sums_ref):
    @tiles(inner.shape[2], 256)
    def _(cols):
        right = flat_columns(inner, cols, 256)
        gw_in[:, cols] = b16(dot_over(flat(hid), right))
        sums_ref[3:4, cols] = column_sum(f32(right))


class Fetch:
    def __init__(self, links, batch, local_sem):
        self.links, self.local_sem = links, local_sem
        self.quarter = bit_of(batch, 0) + 2 * bit_of(batch, 1)
        self.peers = [{"batch": flip_bits(batch, 1)}, {"batch": flip_bits(batch, 2)}]

    def flow(self, source_rows, target, blocks, rows):
        links, size, held = self.links, rows // 8, {}
        span = lambda q, p: pl.ds(pl.multiple_of(q * (2 * size) + p * size, 16), size)
        mine = self.quarter
        own = blocks[0]

        def first():
            for p in range(2):
                for t, device, _ in blocks[1:]:
                    held["y", p, t] = links.go(
                        source_rows(t, mine * (2 * size) + p * size, size),
                        target.at[span(mine, p), own],
                        device,
                    )

        def pass_on(p, q, t, block, way):
            there = target.at[span(q, p), block]
            return links.go(there, there, self.peers[way])

        def second(p):
            def run():
                for t, _, block in blocks[1:]:
                    held["y", p, t].wait()
                    held["a", p, t] = pass_on(p, mine, t, block, p)

            return run

        def third(p):
            def run():
                other = flip_bits(mine, 1 << p)
                for t, _, block in blocks[1:]:
                    held["a", p, t].wait()
                    held["b", p, t] = pass_on(p, mine, t, block, 1 - p)
                    held["c", p, t] = pass_on(p, other, t, block, 1 - p)

            return run

        def last():
            for p in range(2):
                for t, _, _ in blocks[1:]:
                    held["b", p, t].wait()
                    held["c", p, t].wait()

        return [first, second(0), second(1), third(0), third(1), last]

    def columns(self, source, target, at):
        links, (rows, columns) = self.links, source.shape
        far = flip_bits(links.shard, 2)
        own = column_block(links.shard, columns)
        far_block = column_block(far, columns)
        row = lambda t, start, size: source.at[pl.ds(pl.multiple_of(start, 16), size)]
        stages = self.flow(row, target, [own, (2, links.far, far_block)], rows)
        held = {}

        def first():
            stages[0]()
            held["own"] = pltpu.make_async_copy(source, target.at[:, own], self.local_sem.at[at])
            held["own"].start()
            held["near"] = links.go(source, target.at[:, own], links.near)

        def pass_near():
            stages[-1]()
            held["on"] = links.go(target.at[:, far_block], target.at[:, far_block], links.near)

        def finish():
            held["on"].wait()
            held["near"].wait()
            held["own"].wait()

        return [first] + stages[1:-1] + [pass_near, finish]

    def rows(self, source, target, at):
        links, rows = self.links, target.shape[0]
        columns = source.shape[1]
        index = [flip_bits(links.shard, m) for m in range(4)]
        own = column_block(links.shard, columns)
        row = lambda m, start, size: source.at[pl.ds(pl.multiple_of(index[m] * rows + start, 16), size)]
        blocks = [own] + [
            (m, device, column_block(index[m], columns)) for m, device in ((2, links.far), (3, links.across))
        ]
        stages = self.flow(row, target, blocks, rows)
        held = {}

        def first():
            stages[0]()
            held["own"] = pltpu.make_async_copy(row(0, 0, rows), target.at[:, own], self.local_sem.at[at])
            held["own"].start()
            held["near"] = links.go(row(1, 0, rows), target.at[:, own], links.near)

        def last():
            stages[-1]()
            held["near"].wait()
            held["own"].wait()

        return [first] + stages[1:-1] + [last]


def vector_row(pack, row):
    return f32(jnp.concatenate([pack[t, row : row + 1, :] for t in range(pack.shape[0])], 1))

def link_scratch(count, local):
    return [
        pltpu.SemaphoreType.DMA((count,)),
        pltpu.SemaphoreType.DMA((count,)),
        pltpu.SemaphoreType.DMA((local,)),
    ]


def front_body(
    heads, size,
    rows_ref, gains_ref, own_ref, taps_ref, b_ref, base_ref, length_ref,
    pos_hbm, qkv_hbm, ffn_in, ffn_out, out_proj, conv_in, conv_out,
    one_ref, two_ref, pack, table, proj, with_u, with_v, key, value, mix, wc_in, w_mine, wc_out,
    hid_out, act_out, slope_out, w_rows_out, hidden_out, soft_out,
    hid, act, slope, w_rows, w_in, w_out, pos_ref, w_qkv, hid_b, soft_ref, turned,
    part, send, land, cross, land_cross, send_sem, recv_sem, local_sem, load_sem, flush_sem, pack_in,
):
    batch = lax.axis_index("batch")
    links = Links(send_sem, recv_sem)
    fetch = Fetch(links, batch, local_sem)
    flush = Flush(flush_sem)
    pack_in[0:6, :] = gains_ref[...]
    pack_in[6:22, :] = own_ref[...]
    pack_in[22:27, :] = taps_ref[...]
    pack_in[27:32, :] = b16(jnp.full((5, pack_in.shape[1]), length_ref[0], jnp.int32).astype(jnp.float32))
    loads = Loads(load_sem, [(ffn_in.at[0], w_in), (pos_hbm, pos_ref), (qkv_hbm, w_qkv)])
    links.greet([links.near, links.far, links.across] + fetch.peers)
    small = [
        links.go(pack_in, pack.at[links.shard], device)
        for device in (links.far, links.across, links.near)
    ]
    down = fetch.rows(ffn_out.at[0], w_rows, 0)
    down.pop(0)()
    pack[links.shard] = pack_in[...]
    for copy in small:
        copy.wait()
    rows, features = rows_ref.shape
    hid[0] = b16(norm_rows(rows_ref[...], vector_row(pack, 0), vector_row(pack, 6)))
    half = rows // 2
    out = [
        links.go(hid.at[0, pl.ds(h * half, half)], hid.at[2 + h, pl.ds(0, half)], links.far)
        for h in range(2)
    ]
    near = links.go(hid.at[0], hid.at[1], links.near)
    up = ffn_up(hid, act, slope, w_in, b_ref, 0)
    loads.need(0)
    up(0)
    near.wait()
    up(1)
    down.pop(0)()
    down.pop(0)()
    lanes = features // 2

    @pl.loop(0, table.shape[0] // 16)
    def _(i):
        at = pl.ds(pl.multiple_of(i * 16, 16), 16)
        s_a, c_a = base_ref[pl.ds(16 + i, 1), 0:lanes], base_ref[pl.ds(16 + i, 1), lanes:]
        s_b, c_b = base_ref[0:16, 0:lanes], base_ref[0:16, lanes:]
        table[at, 0:lanes] = b16(s_a * c_b + c_a * s_b)
        table[at, lanes:] = b16(c_a * c_b - s_a * s_b)

    loads.need(1)
    proj[...] = b16(dot_rows(table[...], pos_ref[...]))
    other = fetch.columns(out_proj, w_out, 1)
    leaving = fetch.columns(conv_out, wc_out, 3)
    for h in range(2):
        out[h].wait()
        on = links.go(hid.at[2 + h, pl.ds(0, half)], hid.at[2 + h, pl.ds(half, half)], links.near)
        on.wait()
        if h == 1:
            other.pop(0)()
            leaving.pop(0)()
        up(2 + h)
        down.pop(0)()
    for pair in ((hid, hid_out), (act, act_out), (slope, slope_out)):
        flush.go(*pair)
    while down:
        down.pop(0)()
    flush.go(w_rows, w_rows_out)
    sums = Sums(links, (part, send, land, cross, land_cross))
    work = ffn_down(act, w_rows)
    for h in range(2):
        work(2 + h, sums.split(h))
        sums.send_back(h)
    for h in range(2):
        sums.send_cross(h)
    work(1, sums.give)
    sums.send_near()
    work(0, sums.keep)
    for _ in range(4):
        other.pop(0)()
        leaving.pop(0)()

    out_bias, gain, shift = vector_row(pack, 7), vector_row(pack, 1), vector_row(pack, 8)
    out = []
    for h in range(2):
        at = slice(h * half, (h + 1) * half)
        one = rows_ref[at] + 0.5 * (sums.arrive(h) + out_bias)
        one_ref[at] = one
        hid_b[0, at] = b16(norm_rows(one, gain, shift))
        there = pl.ds(h * half, half)
        out.append(links.go(hid_b.at[0, there], hid_b.at[2, there], links.far))
    near = links.go(hid_b.at[0], hid_b.at[1], links.near)
    while other:
        other.pop(0)()
        leaving.pop(0)()
    entering = fetch.columns(conv_in, wc_in, 2)
    own = f32(own_ref[...])
    keys = f32(lax.broadcasted_iota(jnp.int32, (rows, rows), 1))
    scale = 1.0 / math.sqrt(size)
    loads.need(2)

    def attend(slot):
        hidden = hid_b[slot]
        query = dot_rows(hidden, w_qkv[0]) + own[3:4]
        with_u[slot] = b16(query + own[6:7])
        with_v[slot] = b16(query + own[7:8])
        key[slot] = b16(dot_rows(hidden, w_qkv[1]))
        value[slot] = b16(dot_rows(hidden, w_qkv[2]) + own[4:5])
        live = f32(pack[flip_bits(links.shard, slot), 27:28, 0:1])
        for h in range(heads):
            cols = slice(h * size, (h + 1) * size)
            wide = dot_back(with_v[slot, :, cols], proj[:, cols])
            moved = pltpu.roll(wide, rows + 1, 1, stride=1, stride_axis=0)[:, :rows]
            raw = dot_back(with_u[slot, :, cols], key[slot, :, cols]) + moved
            scores = jnp.where(keys < live, raw * scale, -1e30)
            grown = jnp.exp(scores - jnp.max(scores, axis=-1, keepdims=True))
            soft = grown / jnp.sum(grown, axis=-1, keepdims=True)
            soft_ref[slot, :, h * rows : (h + 1) * rows] = soft
            mix[slot, :, cols] = b16(dot_rows(b16(soft), value[slot, :, cols]))

    last = []
    attend(0)
    turned[links.shard] = mix[0]
    near.wait()
    attend(1)
    last.append(links.go(mix.at[1], turned.at[links.shard], links.near))
    on = []
    for h in range(2):
        out[h].wait()
        there = pl.ds(h * half, half)
        on.append(links.go(hid_b.at[2, there], hid_b.at[3, there], links.near))
        if h == 0:
            entering.pop(0)()
    attend(2)
    last.append(links.go(mix.at[2], turned.at[links.shard], links.far))
    entering.pop(0)()
    entering.pop(0)()
    for copy in on:
        copy.wait()
    flush.go(hid_b, hidden_out)
    attend(3)
    last.append(links.go(mix.at[3], turned.at[links.shard], links.across))
    flush.go(soft_ref, soft_out)
    entering.pop(0)()
    entering.pop(0)()
    for copy in last:
        copy.wait()
    width = mix.shape[2]
    total = one_ref[...] + vector_row(pack, 11)
    for t in range(turned.shape[0]):
        total = total + dot_rows(turned[t], w_out[t * width : (t + 1) * width])
    two_ref[...] = total
    w_mine[...] = w_out[pl.ds(pl.multiple_of(links.shard * width, 16), width), :]
    while entering:
        entering.pop(0)()
    flush.settle()


def front(
    rows_in, gains, own_biases, taps, lengths, b_in, base, pos_proj, qkv_proj, ffn_in, ffn_out, out_proj, conv_in,
    conv_out, heads, ident,
):
    ns = lax.axis_size("shard")
    rows, features = rows_in.shape
    hidden = ffn_in.shape[2]
    width = features // ns
    low, full = jnp.bfloat16, jnp.float32
    shape, vmem = jax.ShapeDtypeStruct, pltpu.VMEM
    narrow = shape((ns, rows, width), low)
    dma = pltpu.SemaphoreType.DMA
    return pl.pallas_call(
        functools.partial(front_body, heads, width // heads),
        out_shape=[
            shape((rows, features), full), shape((rows, features), full),
            shape((ns, 32, width), low),
            shape((2 * rows, features), low), shape((2 * rows, width), low),
            narrow, narrow, narrow, narrow, narrow,
            shape((conv_in.shape[0], ns * conv_in.shape[1]), low),
            shape((width, features), low),
            shape((features, features), low),
            shape((4, rows, features), low), shape((4, rows, hidden), low), shape((4, rows, hidden), low),
            shape((hidden, features), low),
            shape((ns, rows, features), low),
            shape((ns, rows, heads * rows), full),
        ],
        in_specs=[VMEM_SPEC] * 6 + [pl.BlockSpec(memory_space=pltpu.SMEM)] + [HBM_SPEC] * 7,
        out_specs=[VMEM_SPEC] * 13 + [HBM_SPEC] * 6,
        scratch_shapes=[
            vmem((4, rows, features), low), vmem((4, rows, hidden), low), vmem((4, rows, hidden), low),
            vmem((hidden, features), low), vmem((features, hidden), low), vmem((features, features), low),
            vmem(pos_proj.shape, low), vmem(qkv_proj.shape, low),
            vmem((ns, rows, features), low), vmem((ns, rows, heads * rows), full), vmem((ns, rows, width), low),
        ]
        + sums_scratch(rows, features)
        + link_scratch(80, 4)
        + [dma((3,)), dma((6,)), vmem((32, width), low)],
        compiler_params=pltpu.CompilerParams(
            collective_id=ident, has_side_effects=True, vmem_limit_bytes=60 << 20
        ),
        name="front",
    )(
        rows_in, gains, own_biases, taps, b_in, base, lengths, pos_proj, qkv_proj, ffn_in, ffn_out, out_proj,
        conv_in, conv_out,
    )


def middle_body(
    nb, early, rows_ref, pack, b_ref, w_rows_hbm, cotangent_hbm, ffn_in,
    result, out_ref, gw_in, gw_out, sums_ref, early_a, early_b,
    hid, act, slope, grad, inner, w_in, cotangent, stream, w_rows, *refs,
):
    first, second, refs = refs[:5], refs[5:10], refs[10:]
    send_sem, recv_sem, ride_send, ride_recv, load_sem = refs
    batch = lax.axis_index("batch")
    links = Links(send_sem, recv_sem)
    loads = Loads(load_sem, [(ffn_in.at[1], w_in), (cotangent_hbm, cotangent), (w_rows_hbm, w_rows)])
    orders = ride_orders(nb)
    links.greet([links.near, links.far] + [{"batch": flip_bits(batch, 1 << k)} for k in range(2)])
    rows, features = rows_ref.shape
    half = rows // 2
    gain, shift = vector_row(pack, 4), vector_row(pack, 19)

    def fill(h):
        at = slice(h * half, (h + 1) * half)
        hid[0, at] = b16(norm_rows(rows_ref[at], gain, shift))

    up, down = ffn_up(hid, act, slope, w_in, b_ref, 1), ffn_down(act, w_rows)

    def work(block, emit):
        loads.need(0)
        up(block)
        loads.need(2)
        down(block, emit)

    sums = gather_work_scatter(links, hid, fill, work, first)
    last_gain, last_shift, out_bias = vector_row(pack, 5), vector_row(pack, 21), vector_row(pack, 20)
    live = f32(pack[links.shard, 27:28, 0:1])
    mask = f32(f32(lax.broadcasted_iota(jnp.int32, (rows, 1), 0)) < live)
    loads.need(1)
    ends = []

    def turn_back(h):
        at = slice(h * half, (h + 1) * half)
        scaled, inverse = norm_parts(rows_ref[at] + 0.5 * (sums.arrive(h) + out_bias))
        result[at] = (scaled * last_gain + last_shift) * mask[at]
        given = cotangent[at] * mask[at]
        slide = norm_slope(given, scaled, inverse, last_gain)
        stream[at] = slide
        grad[0, at] = b16(0.5 * slide)
        ends.append((column_sum(given * scaled), column_sum(given)))

    back = gather_work_scatter(
        links, grad, turn_back, ffn_inward(grad, inner, slope, w_in, w_rows), second
    )
    pieces = 4
    riders = [
        Rider(batch, ride_send, ride_recv, at * early).halve_pieces(
            (gw_in, gw_out)[at], (early_a, early_b)[at], orders[at][0], pieces, gw_in.shape[0] // 2
        )
        for at in range(2)
    ]
    weight_out(act, grad, gw_out)
    for p in range(early):
        riders[1][0](p)
    weight_in(hid, inner, gw_in, sums_ref)
    for p in range(early):
        riders[0][0](p)
    sums_ref[0:3, :] = jnp.zeros((3, features), jnp.float32)
    sums_ref[2:3, :] = column_sum(f32(grad[0]))
    sums_ref[4:5, :] = ends[0][0] + ends[1][0]
    sums_ref[5:6, :] = ends[0][1] + ends[1][1]
    sums_ref[6:8, :] = jnp.zeros((2, features), jnp.float32)
    for h in range(2):
        at = slice(h * half, (h + 1) * half)
        scaled, inverse = norm_parts(rows_ref[at])
        given = back.arrive(h)
        out_ref[at] = stream[at] + norm_slope(given, scaled, inverse, gain)
        sums_ref[0:1, :] += column_sum(given * scaled)
        sums_ref[1:2, :] += column_sum(given)
    for _, settle, _ in riders:
        settle()


EARLY = 1


def middle(rows_in, pack, b_in, w_rows, cotangent, ffn_in, ident):
    rows, features = rows_in.shape
    hidden = ffn_in.shape[2]
    nb = lax.axis_size("batch")
    low, full = jnp.bfloat16, jnp.float32
    shape, vmem = jax.ShapeDtypeStruct, pltpu.VMEM
    dma = pltpu.SemaphoreType.DMA
    piece = features // 8
    return pl.pallas_call(
        functools.partial(middle_body, nb, EARLY),
        out_shape=[
            shape((rows, features), full), shape((rows, features), full),
            shape((features, hidden), low), shape((hidden, features), low), shape((8, features), full),
            shape((EARLY * piece, hidden), low), shape((EARLY * piece, features), low),
        ],
        in_specs=[VMEM_SPEC] * 3 + [HBM_SPEC] * 3,
        out_specs=[VMEM_SPEC] * 7,
        scratch_shapes=[
            vmem((4, rows, features), low), vmem((4, rows, hidden), low), vmem((4, rows, hidden), low),
            vmem((4, rows, features), low), vmem((4, rows, hidden), low), vmem((features, hidden), low),
            vmem((rows, features), full), vmem((rows, features), full), vmem((hidden, features), low),
        ]
        + sums_scratch(rows, features)
        + sums_scratch(rows, features)
        + [dma((20,)), dma((20,)), dma((2 * EARLY,)), dma((2 * EARLY,)), dma((3,))],
        compiler_params=pltpu.CompilerParams(
            collective_id=ident, has_side_effects=True, vmem_limit_bytes=60 << 20
        ),
        name="middle",
    )(rows_in, pack, b_in, w_rows, cotangent, ffn_in)


def pack_rows(ref, at, row):
    for i in range(row.shape[1] // 128):
        ref[at + i : at + i + 1, :] = row[:, i * 128 : (i + 1) * 128]


def unpack_rows(value, at, lanes):
    return jnp.concatenate([value[at + i : at + i + 1, :] for i in range(lanes)], 1)


def everywhere(links, nb, source, mid, land_s, land_b, result, small, sems):
    s, b = links.shard, lax.axis_index("batch")
    ns = land_s.shape[0]
    ss, rs, sb, rb = sems
    first = exchange("shard", s, ns, source, land_s, ss, rs)
    for copy in first:
        copy.start()
    land_s[s] = source[...]
    for copy in first:
        copy.wait()
    mid[...] = sum_slots(land_s, ns)
    second = exchange("batch", b, nb, mid, land_b, sb, rb)
    for copy in second:
        copy.start()
    land_b[b] = mid[...]
    small()
    for copy in second:
        copy.wait()
    return sum_slots(land_b, nb)


def conv_body(
    nb, rows_ref, pack, w_in, w_out, ffn_out,
    out_ref, hid, open_ref, gate_ref, gated_ref, scaled_ref, act, slope, stats, w_rows,
    padded, source, mid, land_s, land_b, ss, rs, sb, rb, send_sem, recv_sem, local_sem,
):
    batch = lax.axis_index("batch")
    links = Links(send_sem, recv_sem)
    fetch = Fetch(links, batch, local_sem)
    rows, features = rows_ref.shape
    ns = land_s.shape[0]
    links.greet(
        [links.near, links.far, links.across]
        + [{"batch": lax.rem(batch + j, nb)} for j in range(1, nb)]
    )
    down = fetch.rows(ffn_out.at[1], w_rows, 1)
    down.pop(0)()
    live = f32(pack[links.shard, 27:28, 0:1])
    mask = f32(f32(lax.broadcasted_iota(jnp.int32, (rows, 1), 0)) < live)
    hid[...] = b16(norm_rows(rows_ref[...], vector_row(pack, 2), vector_row(pack, 14)))
    bias_v, bias_g = vector_row(pack, 15), vector_row(pack, 16)
    lead = 8
    tile = 512
    padded[0:lead, :] = jnp.zeros((lead, features), jnp.float32)
    padded[lead + rows :, :] = jnp.zeros((lead, features), jnp.float32)
    for n in range(features // tile):
        cols = slice(n * tile, (n + 1) * tile)
        left = dot_rows(hid[...], w_in[:, cols]) + bias_v[:, cols]
        right = dot_rows(hid[...], w_in[:, features + n * tile : features + (n + 1) * tile])
        gate = jax.nn.sigmoid(right + bias_g[:, cols])
        opened = gate * mask
        gated = left * opened
        open_ref[:, cols] = b16(opened)
        gate_ref[:, cols] = b16(gated * (1.0 - gate))
        gated_ref[:, cols] = b16(gated)
        padded[lead : lead + rows, cols] = gated
    taps = 5
    total = 0.0
    for k in range(taps):
        at = lead - (taps - 1) // 2 + k
        total = total + padded[at : at + rows, :] * vector_row(pack, 22 + k)
    live_total = total * mask
    lanes = features // 128
    pack_rows(source, 0, jnp.sum(live_total, axis=0, keepdims=True))
    pack_rows(source, lanes, jnp.sum(live_total * total, axis=0, keepdims=True))
    source[2 * lanes : 2 * lanes + 8, :] = jnp.broadcast_to(live, (8, 128))
    scaled_ref[...] = total
    down.pop(0)()
    down.pop(0)()
    sums = everywhere(links, nb, source, mid, land_s, land_b, None, lambda: None, (ss, rs, sb, rb))
    down.pop(0)()
    down.pop(0)()
    frames = sums[2 * lanes : 2 * lanes + 1, 0:1]
    mean = unpack_rows(sums, 0, lanes) / frames
    inverse = lax.rsqrt(unpack_rows(sums, lanes, lanes) / frames - mean * mean + epsilon)
    stats[0:1, :] = inverse
    stats[1:2, :] = jnp.broadcast_to(frames, (1, features))
    stats[2:8, :] = jnp.zeros((6, features), jnp.float32)
    scaled = (scaled_ref[...] - mean) * inverse
    scaled_ref[...] = scaled
    normed = scaled * vector_row(pack, 3) + vector_row(pack, 17)
    gate = jax.nn.sigmoid(normed)
    act[...] = b16(normed * gate)
    slope[...] = b16(gate * (1.0 + normed * (1.0 - gate)))
    out_ref[...] = rows_ref[...] + (dot_rows(act[...], w_out[...]) + vector_row(pack, 18))
    while down:
        down.pop(0)()


def conv_forward(rows_in, pack, w_in, w_out, ffn_out, ident):
    ns, nb = lax.axis_size("shard"), lax.axis_size("batch")
    rows, features = rows_in.shape
    shape = jax.ShapeDtypeStruct
    low, full = jnp.bfloat16, jnp.float32
    plain = shape((rows, features), low)
    small = (24, 128)
    return pl.pallas_call(
        functools.partial(conv_body, nb),
        out_shape=[
            shape((rows, features), full), plain, plain, plain, plain,
            shape((rows, features), full), plain, plain, shape((8, features), full),
            shape((ffn_out.shape[1] // ns, features), low),
        ],
        in_specs=[VMEM_SPEC] * 4 + [HBM_SPEC],
        out_specs=[VMEM_SPEC] * 10,
        scratch_shapes=[
            pltpu.VMEM((rows + 16, features), full),
            pltpu.VMEM(small, full), pltpu.VMEM(small, full),
            pltpu.VMEM((ns,) + small, full), pltpu.VMEM((nb,) + small, full),
            pltpu.SemaphoreType.DMA((ns,)), pltpu.SemaphoreType.DMA((ns,)),
            pltpu.SemaphoreType.DMA((nb,)), pltpu.SemaphoreType.DMA((nb,)),
        ]
        + link_scratch(32, 3),
        compiler_params=pltpu.CompilerParams(
            collective_id=ident, has_side_effects=True, vmem_limit_bytes=60 << 20
        ),
        name="conv_forward",
    )(rows_in, pack, w_in, w_out, ffn_out)


def conv_back_body(
    nb, stream_ref, rows_ref, pack, w_out, hid, open_ref, gate_ref, gated_ref, scaled_ref, act, slope, stats,
    early_a, early_b, w_in_hbm, ride_a, ride_b, out_ref, gw_out, gw_in, sums_ref, half_a, half_b,
    padded, normed, grad, inner, source, mid, land_s, land_b, ss, rs, sb, rb, send_sem, recv_sem,
    w_in, kept_a, kept_b, load_sem,
):
    batch = lax.axis_index("batch")
    links = Links(send_sem, recv_sem)
    kept = [
        row_view(ref, bit_of(batch, order[0]) * out.shape[0], out.shape[0])
        for ref, out, order in zip((ride_a, ride_b), (kept_a, kept_b), ride_orders(nb))
    ]
    loads = Loads(load_sem, [(w_in_hbm, w_in), (kept[0], kept_a), (kept[1], kept_b)])
    rows, features = rows_ref.shape
    links.greet(
        [links.near, links.far, links.across]
        + [{"batch": lax.rem(batch + j, nb)} for j in range(1, nb)]
    )
    orders = ride_orders(nb)
    pieces = 4
    ride = [
        Rider(batch, send_sem, recv_sem, at * pieces).halve_pieces(
            source_ref, landing, orders[at][0], pieces, landing.shape[0]
        )
        for at, (source_ref, landing) in enumerate(((ride_a, half_a), (ride_b, half_b)))
    ]
    for start, _, _ in ride:
        start(EARLY)
    lanes = features // 128
    lead, tile, taps = 8, 512, 5
    grad[...] = b16(stream_ref[...])
    gain = vector_row(pack, 3)
    sums_ref[...] = jnp.zeros_like(sums_ref)
    for n in range(features // tile):
        cols = slice(n * tile, (n + 1) * tile)
        value = dot_back(grad[...], w_out[cols, :]) * f32(slope[:, cols])
        normed[:, cols] = value
        for at, total in (
            (0, jnp.sum(value, axis=0, keepdims=True)),
            (lanes, jnp.sum(value * scaled_ref[:, cols], axis=0, keepdims=True)),
        ):
            for i in range(tile // 128):
                row = at + n * (tile // 128) + i
                source[row : row + 1, :] = total[:, i * 128 : (i + 1) * 128]

    def meanwhile():
        @tiles(features, 256)
        def _(cols):
            gw_out[cols, :] = b16(dot_over(act[:, cols], grad[...]))

        sums_ref[4:5, :] = jnp.sum(f32(grad[...]), axis=0, keepdims=True)

    sums = everywhere(links, nb, source, mid, land_s, land_b, None, meanwhile, (ss, rs, sb, rb))
    beta, gamma = unpack_rows(sums, 0, lanes), unpack_rows(sums, lanes, lanes)
    for p in range(EARLY + 1, pieces):
        for start, _, _ in ride:
            start(p)
    sums_ref[5:6, :] = gamma
    sums_ref[6:7, :] = beta
    inverse, frames = stats[0:1, :], stats[1:2, 0:1]
    live = f32(pack[links.shard, 27:28, 0:1])
    mask = f32(f32(lax.broadcasted_iota(jnp.int32, (rows, 1), 0)) < live)
    padded[0:lead, :] = jnp.zeros((lead, features), jnp.float32)
    padded[lead + rows :, :] = jnp.zeros((lead, features), jnp.float32)
    padded[lead : lead + rows, :] = inverse * (
        normed[...] * gain - mask * (gain * beta + scaled_ref[...] * (gain * gamma)) / frames
    )
    given = 0.0
    gated = f32(gated_ref[...])
    for k in range(taps):
        at = lead + (taps - 1) // 2 - k
        moved = padded[at : at + rows, :]
        given = given + moved * vector_row(pack, 22 + k)
        sums_ref[8 + k : 9 + k, :] = jnp.sum(moved * gated, axis=0, keepdims=True)
    left = b16(given * f32(open_ref[...]))
    right = b16(given * f32(gate_ref[...]))
    inner[:, 0:features] = left
    inner[:, features:] = right
    sums_ref[2:3, :] = jnp.sum(f32(left), axis=0, keepdims=True)
    sums_ref[3:4, :] = jnp.sum(f32(right), axis=0, keepdims=True)
    loads.need(0)
    total = dot_back(inner[...], w_in[...])
    scaled, inverse = norm_parts(rows_ref[...])
    out_ref[...] = stream_ref[...] + norm_slope(total, scaled, inverse, vector_row(pack, 2))
    sums_ref[0:1, :] = jnp.sum(total * scaled, axis=0, keepdims=True)
    sums_ref[1:2, :] = jnp.sum(total, axis=0, keepdims=True)

    @tiles(2 * features, 512)
    def _(cols):
        gw_in[:, cols] = b16(dot_over(hid[...], inner[:, cols]))

    loads.need(1, 2)
    for (_, settle, _), own, landing, early in zip(ride, (kept_a, kept_b), (half_a, half_b), (early_a, early_b)):
        settle()
        done = early.shape[0]
        landing[0:done] = b16(f32(own[0:done]) + f32(early[...]))
        landing[done:] = b16(f32(own[done:]) + f32(landing[done:]))


def conv_back(stream, rows_in, pack, w_in, w_out, saved, ridden, early, ident):
    ns, nb = lax.axis_size("shard"), lax.axis_size("batch")
    rows, features = rows_in.shape
    shape = jax.ShapeDtypeStruct
    low, full = jnp.bfloat16, jnp.float32
    small = (2 * features // 128, 128)
    return pl.pallas_call(
        functools.partial(conv_back_body, nb),
        out_shape=[
            shape((rows, features), full), shape((features, features), low),
            shape((features, 2 * features), low), shape((16, features), full),
        ]
        + [shape((r.shape[0] // 2, r.shape[1]), low) for r in ridden],
        in_specs=[VMEM_SPEC] * 14 + [HBM_SPEC] * 3,
        out_specs=[VMEM_SPEC] * 6,
        scratch_shapes=[
            pltpu.VMEM((rows + 16, features), full), pltpu.VMEM((rows, features), full),
            pltpu.VMEM((rows, features), low), pltpu.VMEM((rows, 2 * features), low),
            pltpu.VMEM(small, full), pltpu.VMEM(small, full),
            pltpu.VMEM((ns,) + small, full), pltpu.VMEM((nb,) + small, full),
            pltpu.SemaphoreType.DMA((ns,)), pltpu.SemaphoreType.DMA((ns,)),
            pltpu.SemaphoreType.DMA((nb,)), pltpu.SemaphoreType.DMA((nb,)),
        ]
        + link_scratch(8, 1)[:2]
        + [pltpu.VMEM(w_in.shape, low)]
        + [pltpu.VMEM((r.shape[0] // 2, r.shape[1]), low) for r in ridden]
        + [pltpu.SemaphoreType.DMA((3,))],
        compiler_params=pltpu.CompilerParams(
            collective_id=ident, has_side_effects=True, vmem_limit_bytes=60 << 20
        ),
        name="conv_back",
    )(stream, rows_in, pack, w_out, *saved, *early, w_in, *ridden)


def rear_body(
    heads, size, nb, stream_ref, rows_ref, pack, w_mine, ride_a, ride_b,
    hid_b_hbm, with_u_hbm, with_v_hbm, key_hbm, value_hbm, soft_hbm, mix_hbm, table_hbm, proj_hbm, w_qkv_hbm,
    start_hbm, hid_hbm, act_hbm, slope_hbm, w_rows_hbm, ffn_in,
    out_ref, gw_q, gw_k, gw_x, gw_pos, gw_mix, mix_sums, own_sums, gw_in, gw_out, sums_ref, out_a, out_b,
    grad, dq, dk, dx, dp, stream, grad_b, inner, start, hid, act, slope, w_rows, w_in,
    hid_b, with_u, with_v, key, value, soft_ref, mix, table, proj, w_qkv, *refs,
):
    first, second, refs = refs[:5], refs[5:10], refs[10:]
    send_sem, recv_sem, ride_send, ride_recv, load_sem, *between = refs
    links = Links(send_sem, recv_sem)
    batch = lax.axis_index("batch")
    loads = Loads(
        load_sem,
        [
            (soft_hbm, soft_ref), (value_hbm, value), (key_hbm, key), (with_u_hbm, with_u), (with_v_hbm, with_v),
            (proj_hbm, proj), (w_qkv_hbm, w_qkv), (hid_b_hbm, hid_b), (mix_hbm, mix), (table_hbm, table),
            (slope_hbm, slope), (w_rows_hbm, w_rows), (ffn_in.at[0], w_in), (act_hbm, act), (hid_hbm, hid),
            (start_hbm, start),
        ],
    )
    orders = ride_orders(nb)
    steps = len(orders[0]) - 1
    scale = 1.0 / math.sqrt(size)
    rows, features = rows_ref.shape
    half = rows // 2
    links.greet([links.near, links.far] + [{"batch": flip_bits(batch, 1 << k)} for k in orders[0]])
    inward, outward = [], []
    count = 2 * steps - 1
    for at, (begin, end) in enumerate(((ride_a, out_a), (ride_b, out_b))):
        middle_refs = between[at * count : (at + 1) * count]
        down_refs = [begin, *middle_refs[:steps]]
        up_refs = [*middle_refs[steps - 1 :], end]
        rider = Rider(batch, ride_send, ride_recv, at * 2 * steps)
        inward.append(rider.chain(down_refs, orders[at][1:], rider.halve))
        rider = Rider(batch, ride_send, ride_recv, at * 2 * steps + steps)
        outward.append(rider.chain(up_refs, orders[at][:0:-1], rider.double))

    def tick(chains):
        for chain in chains:
            if chain:
                chain.pop(0)()

    tick(inward)
    grad[0] = b16(stream_ref[...])
    out = [
        links.go(grad.at[0, pl.ds(h * half, half)], grad.at[2, pl.ds(h * half, half)], links.far)
        for h in range(2)
    ]
    near = links.go(grad.at[0], grad.at[1], links.near)
    at_row = lax.broadcasted_iota(jnp.int32, (rows, rows), 0)
    at_col = lax.broadcasted_iota(jnp.int32, (rows, rows), 1)
    flip = b16(f32(at_row + at_col == rows - 1))
    keys = f32(at_col)
    own_sums[...] = jnp.zeros_like(own_sums)

    def work(slot, emit):
        mixed = b16(dot_back(grad[slot], w_mine[...]))
        live = f32(pack[flip_bits(links.shard, slot), 27:28, 0:1])
        for h in range(heads):
            cols = slice(h * size, (h + 1) * size)
            soft = soft_ref[slot, :, h * rows : (h + 1) * rows]
            given = mixed[:, cols]
            grad_soft = dot_back(given, value[slot, :, cols])
            dx[slot, :, cols] = b16(dot_over(b16(soft), given))
            grad_scores = soft * (grad_soft - jnp.sum(grad_soft * soft, axis=-1, keepdims=True))
            raw = b16(jnp.where(keys < live, grad_scores, 0.0) * scale)
            grad_u = dot_rows(raw, key[slot, :, cols])
            dk[slot, :, cols] = b16(dot_over(raw, with_u[slot, :, cols]))
            turned = dot_rows(flip, raw)
            wide = jnp.concatenate([turned, jnp.zeros_like(turned)], 1)
            wide = b16(pltpu.roll(wide, 0, 1, stride=1, stride_axis=0))
            grad_v = dot_rows(wide, proj[:, cols])
            v_turned = b16(dot_rows(flip, with_v[slot, :, cols]))
            dp[slot, :, cols] = b16(dot_over(wide, v_turned))
            own_sums[2:3, cols] += column_sum(grad_u)
            own_sums[3:4, cols] += column_sum(grad_v)
            high = b16(grad_v)
            rest = b16(grad_v - f32(high))
            dq[slot, :, cols] = b16(grad_u + (dot_rows(flip, high) + dot_rows(flip, rest)))
        own_sums[0:1, :] += column_sum(f32(dq[slot]))
        own_sums[1:2, :] += column_sum(f32(dx[slot]))

        @tiles(features, 512)
        def _(cols):
            emit(
                cols,
                dot_back(dq[slot], w_qkv[0, cols, :])
                + dot_back(dk[slot], w_qkv[1, cols, :])
                + dot_back(dx[slot], w_qkv[2, cols, :]),
            )

    sums = Sums(links, first)
    loads.need(*range(7))
    work(0, sums.keep)
    near.wait()
    work(1, sums.give)
    sums.send_near()
    tick(inward)
    on = []
    for h in range(2):
        out[h].wait()
        there = pl.ds(h * half, half)
        on.append(links.go(grad.at[2, there], grad.at[3, there], links.near))
    for copy in on:
        copy.wait()
    work(3, sums.give_far)
    for h in range(2):
        sums.send_back(h)
    work(2, sums.keep_far)
    for h in range(2):
        sums.send_cross(h)
    loads.need(7, 8, 9)
    for ref, target in ((dq, gw_q), (dk, gw_k), (dx, gw_x)):
        right = flat(ref)

        @tiles(features, 256)
        def _(cols, target=target, right=right):
            target[cols, :] = b16(dot_over(flat_columns(hid_b, cols, 256), right))

    @tiles(features, 256)
    def _(cols):
        total = dot_over(table[:, cols], dp[0])
        for slot in range(1, 4):
            total = total + dot_over(table[:, cols], dp[slot])
        gw_pos[cols, :] = b16(total)

    gw_mix[...] = b16(dot_over(flat(mix), flat(grad)))
    mix_sums[...] = jnp.zeros_like(mix_sums)
    mix_sums[2:3, :] = column_sum(f32(grad[0]))
    gain = vector_row(pack, 1)

    def fill(h):
        at = slice(h * half, (h + 1) * half)
        given = sums.arrive(h)
        scaled, inverse = norm_parts(rows_ref[at])
        slide = stream_ref[at] + norm_slope(given, scaled, inverse, gain)
        stream[at] = slide
        grad_b[0, at] = b16(0.5 * slide)
        mix_sums[0:1, :] += column_sum(given * scaled)
        mix_sums[1:2, :] += column_sum(given)

    step = ffn_inward(grad_b, inner, slope, w_in, w_rows)

    def back_work(block, emit):
        loads.need(10, 11, 12)
        if block == 1:
            for chain in inward:
                while chain:
                    chain.pop(0)()
            tick(outward)
        step(block, emit)

    back = gather_work_scatter(links, grad_b, fill, back_work, second)
    loads.need(13, 14, 15)
    weight_out(act, grad_b, gw_out)
    tick(outward)
    weight_in(hid, inner, gw_in, sums_ref)
    sums_ref[0:3, :] = jnp.zeros((3, features), jnp.float32)
    sums_ref[2:3, :] = column_sum(f32(grad_b[0]))
    sums_ref[4:8, :] = jnp.zeros((4, features), jnp.float32)
    gain = vector_row(pack, 0)
    for h in range(2):
        at = slice(h * half, (h + 1) * half)
        scaled, inverse = norm_parts(start[at])
        given = back.arrive(h)
        out_ref[at] = stream[at] + norm_slope(given, scaled, inverse, gain)
        sums_ref[0:1, :] += column_sum(given * scaled)
        sums_ref[1:2, :] += column_sum(given)
    for chain in outward:
        while chain:
            chain.pop(0)()


def rear(stream, rows_one, pack, saved_mix, table, proj, w_qkv, w_mine, ridden, rows_in, saved, w_rows, ffn_in, heads, ident):
    rows, features = rows_one.shape
    hidden = ffn_in.shape[2]
    width = proj.shape[1]
    nb = lax.axis_size("batch")
    steps = nb.bit_length() - 2
    low, full = jnp.bfloat16, jnp.float32
    shape, vmem = jax.ShapeDtypeStruct, pltpu.VMEM
    dma = pltpu.SemaphoreType.DMA
    narrow = vmem((4, rows, width), low)
    between = []
    for r in ridden:
        sizes = [r.shape[0] >> k for k in range(1, steps + 1)]
        between += [vmem((size, r.shape[1]), low) for size in sizes + sizes[-2::-1]]
    return pl.pallas_call(
        functools.partial(rear_body, heads, width // heads, nb),
        out_shape=[
            shape((rows, features), full),
            shape((features, width), low), shape((features, width), low), shape((features, width), low),
            shape((features, width), low),
            shape((width, features), low), shape((8, features), full), shape((8, width), full),
            shape((features, hidden), low), shape((hidden, features), low), shape((8, features), full),
        ]
        + [shape(r.shape, low) for r in ridden],
        in_specs=[VMEM_SPEC] * 6 + [HBM_SPEC] * 16,
        out_specs=[VMEM_SPEC] * 13,
        scratch_shapes=[
            vmem((4, rows, features), low), narrow, narrow, narrow, vmem((4, 2 * rows, width), low),
            vmem((rows, features), full), vmem((4, rows, features), low), vmem((4, rows, hidden), low),
            vmem((rows, features), full), vmem((4, rows, features), low), vmem((4, rows, hidden), low),
            vmem((4, rows, hidden), low), vmem((hidden, features), low), vmem((features, hidden), low),
        ]
        + [vmem(a.shape, a.dtype) for a in (*saved_mix, table, proj, w_qkv)]
        + sums_scratch(rows, features)
        + sums_scratch(rows, features)
        + [dma((24,)), dma((24,)), dma((4 * steps,)), dma((4 * steps,)), dma((16,))]
        + between,
        compiler_params=pltpu.CompilerParams(
            collective_id=ident, has_side_effects=True, vmem_limit_bytes=62 << 20
        ),
        name="rear",
    )(
        stream, rows_one, pack, w_mine, *ridden, *saved_mix, table, proj, w_qkv, rows_in, *saved, w_rows, ffn_in
    )


def body(
    tokens, cotangent, lengths, ffn_in, ffn_out, ffn_bias, qkv_proj, pos_proj, out_proj,
    conv_in, conv_out, depthwise, norm_gains, biases,
):
    _, length, features = tokens.shape
    ns, nb = lax.axis_size("shard"), lax.axis_size("batch")
    width = features // ns
    heads = HEADS // ns
    rows_in = tokens[0]

    rates = jnp.exp(
        jnp.arange(features // 2, dtype=jnp.float32) * (-2.0 * math.log(10000.0) / features)
    )
    turns = jnp.concatenate(
        [
            length - 1.0 - jnp.arange(16, dtype=jnp.float32),
            -16.0 * jnp.arange(2 * length // 16, dtype=jnp.float32),
        ]
    )
    angles = turns[:, None] * rates[None, :]
    base = jnp.concatenate([jnp.sin(angles), jnp.cos(angles)], 1)
    (
        rows_one, rows_two, pack, table, proj, with_u, with_v, key, value, mix, wc_in, w_mine, wc_out,
        *saved_one, w_rows_one, hidden_mix, soft,
    ) = front(
        rows_in, norm_gains, biases, depthwise, lengths, ffn_bias, base, pos_proj, qkv_proj, ffn_in, ffn_out, out_proj, conv_in, conv_out,
        heads, 5,
    )
    saved_mix = (hidden_mix, with_u, with_v, key, value, soft, mix)
    rows_three, *saved_conv, w_rows_two = conv_forward(
        rows_two, pack, wc_in, wc_out, ffn_out, 10
    )
    result, stream, two_in, two_out, two_sums, *early = middle(
        rows_three, pack, ffn_bias, w_rows_two, cotangent[0], ffn_in, 6
    )

    stream, grad_conv_out, grad_conv_in, conv_sums, *ridden = conv_back(
        stream, rows_two, pack, wc_in, wc_out, saved_conv, (two_in, two_out), early, 11
    )
    stream, grad_q, grad_k, grad_x, grad_pos, grad_out, mix_sums, own_sums, one_in, one_out, one_sums, *ridden = rear(
        stream, rows_one, pack, saved_mix, table, proj, qkv_proj, w_mine, ridden, rows_in, saved_one, w_rows_one,
        ffn_in, heads, 12
    )
    tall, deep = one_in.shape
    piece = max(128, 8 * nb)
    *sums, out_gains, out_biases, out_taps, out_hidden = tail_sum(
        [grad_out, one_out, one_in, grad_q, grad_k, grad_x, grad_pos, grad_conv_in, grad_conv_out],
        ridden,
        [one_sums, mix_sums, two_sums, conv_sums, own_sums],
        [("turn", 4, None), ("turn", 1, 0), ("plain", 0, 0)]
        + [("plain", 2, at) for at in range(3)]
        + [("plain", 3, None), ("gather", 5, None), ("gather", 6, None)],
        [
            (2, tall, deep), (2, ns * deep, width), (3, tall, width), (tall, width), (tall, width),
            (tall, 2 * width), (tall, width),
        ],
        ["near", "line"],
        [width, piece, piece] + [min(tall, 4 * piece)] * 4 + [2 * piece, min(tall, 4 * piece)],
        deep,
        4,
    )
    *sums, result, stream, out_gains, out_biases, out_taps, out_hidden = widen(
        sums, [result, stream, out_gains, out_biases, out_taps, out_hidden]
    )
    return (
        result[None],
        stream[None],
        sums[0],
        sums[1],
        out_hidden,
        sums[2],
        sums[3],
        sums[4],
        sums[5],
        sums[6],
        out_taps,
        out_gains,
        out_biases,
    )


def solution(mesh):
    rows = P(("batch", "shard"), None, None)
    cube, flat = P(None, None, "shard"), P(None, "shard")
    return jax.shard_map(
        body,
        mesh=mesh,
        in_specs=(rows, rows, P(("batch", "shard")), cube, cube, flat, cube)
        + (flat,) * 7,
        out_specs=(rows, rows, cube, cube, flat, cube) + (flat,) * 7,
        check_vma=False,
    )
```

```python
import functools
import math

import jax
import jax.numpy as jnp
from jax import lax
from jax.experimental import pallas as pl
from jax.experimental.pallas import tpu as pltpu
from jax.sharding import PartitionSpec as P

HEADS = 8
MESH = pl.DeviceIdType.MESH
VMEM_SPEC = pl.BlockSpec(memory_space=pltpu.VMEM)
HBM_SPEC = pl.BlockSpec(memory_space=pltpu.HBM)
epsilon = 1e-05


def f32(a):
    return a.astype(jnp.float32)


def b16(a):
    return a.astype(jnp.bfloat16)


def norm_rows(values_in, gain_row, bias_row):
    row_mean = jnp.mean(values_in, axis=-1, keepdims=True)
    centered = values_in - row_mean
    spread = jnp.mean(centered * centered, axis=-1, keepdims=True)
    return centered * lax.rsqrt(spread + epsilon) * gain_row + bias_row


def dot_rows(a, b):
    return jnp.dot(a, b, preferred_element_type=jnp.float32)


def dot_back(a, b):
    return lax.dot_general(a, b, (((1,), (1,)), ((), ())), preferred_element_type=jnp.float32)


def dot_over(a, b):
    return lax.dot_general(a, b, (((0,), (0,)), ((), ())), preferred_element_type=jnp.float32)


def exchange(axis, index, count, source, landing, send_sem, recv_sem):
    copies = []
    for j in range(1, count):
        peer = lax.rem(index + j, count)
        copies.append(
            pltpu.make_async_remote_copy(
                src_ref=source,
                dst_ref=landing.at[index],
                send_sem=send_sem.at[j],
                recv_sem=recv_sem.at[j],
                device_id={axis: peer},
                device_id_type=MESH,
            )
        )
    return copies


def sum_slots(ref, count):
    total = ref[0]
    for j in range(1, count):
        total = total + ref[j]
    return total


class Loads:
    def __init__(self, sem, pairs):
        self.open = []
        for at, (src, dst) in enumerate(pairs):
            copy = pltpu.make_async_copy(src, dst, sem.at[at])
            copy.start()
            self.open.append(copy)

    def need(self, *which):
        for at in which:
            if self.open[at] is not None:
                self.open[at].wait()
                self.open[at] = None


class Flush:
    def __init__(self, sem):
        self.sem, self.open = sem, []

    def go(self, src, dst):
        copy = pltpu.make_async_copy(src, dst, self.sem.at[len(self.open)])
        copy.start()
        self.open.append(copy)

    def settle(self):
        for copy in self.open:
            copy.wait()


class Chunk:
    def __init__(self, at, source, row, rows, columns, first, count):
        self.at, self.source, self.row, self.rows, self.columns = at, source, row, rows, columns
        extra = [(1 << k, k) for k in range(3, count.bit_length() - 1)]
        line = (6, 1)
        if first == "near":
            self.pre, self.post = [(1, 0)], [line] + extra
        else:
            self.pre, self.post = [], [line, (1, 0)] + extra
        size, self.landings = rows, []
        for _ in self.pre:
            size //= 2
            self.landings.append((size, columns))
        self.landings.append((size, columns))
        for _ in self.post:
            size //= 2
            self.landings.append((size, columns))
        self.steps = len(self.landings)


def bit_of(value, k):
    return lax.rem(lax.div(value, 1 << k), 2)


def flip_bits(value, mask):
    out = value
    k = 0
    while (1 << k) <= mask:
        if mask & (1 << k):
            out = out + (1 - 2 * bit_of(value, k)) * (1 << k)
        k += 1
    return out


class Mover:
    def __init__(self, chunk, batch, source, base, held, landings, sems, finish, early):
        self.c, self.b = chunk, batch
        self.source, self.base, self.held, self.landings, self.sems = source, base, held, landings, sems
        lo, hi = bit_of(batch, 1), bit_of(batch, 2)
        self.inner = lo != hi
        self.ended = lo == hi
        self.finish, self.early = finish, early
        self.build()

    def copy(self, at, src, dst, mask):
        send, recv = self.sems
        return pltpu.make_async_remote_copy(
            src_ref=src,
            dst_ref=dst,
            send_sem=send.at[self.c.at, at],
            recv_sem=recv.at[self.c.at, at],
            device_id={"batch": flip_bits(self.b, mask)},
            device_id_type=MESH,
        )

    def build(self):
        c = self.c
        held = self.held
        here, base = self.source, self.base
        off, size, step = 0, c.rows, 0
        plan, trail = [], []
        sequence = [("all",) + p for p in c.pre] + [("fold", 2, None)]
        sequence += [("inner",) + p for p in c.post]
        for kind, mask, sel in sequence:
            landing = self.landings[step]
            if kind == "fold":
                own = row_view(here, base, size)
                cp = self.copy(step, own, landing, mask)
            else:
                size //= 2
                mine = bit_of(self.b, sel)
                cp = self.copy(step, row_view(here, base + (1 - mine) * size, size), landing, mask)
                own = row_view(here, base + mine * size, size)
                off = off + mine * size
            trail.append((kind, mask, off, size))
            step += 1
            out = landing if step < len(sequence) else held(off, size)
            plan.append((kind, cp, (own, landing, out)))
            here, base = landing, 0
        for kind, mask, off, size in reversed(trail):
            cp = self.copy(step, held(off, size), held(off, size), mask)
            plan.append(("unfold" if kind == "fold" else kind, cp, None))
            step += 1
        self.plan = plan
        self.depth = len(plan) + len(self.early)

    def begin(self, k):
        kind, cp, _ = self.plan[k]
        if kind == "all":
            cp.start()
        elif kind == "fold":
            pl.when(self.ended)(cp.start)
        else:
            pl.when(self.inner)(cp.start)

    def end(self, k):
        kind, cp, add = self.plan[k]

        def gather():
            if add is not None:
                own, landing, out = add
                out[...] = b16(f32(own[...]) + f32(landing[...]))

        if kind == "all":
            cp.wait()
            gather()
        elif kind in ("fold", "unfold"):
            sender, taker = (
                (self.ended, self.inner) if kind == "fold" else (self.inner, self.ended)
            )
            pl.when(sender)(cp.wait_send)

            @pl.when(taker)
            def _():
                cp.wait_recv()
                gather()
        else:

            @pl.when(self.inner)
            def _():
                cp.wait()
                gather()

    def advance(self, k):
        if k < len(self.early):
            self.early[k]()
            return
        k -= len(self.early)
        if k > 0:
            self.end(k - 1)
        elif self.early:
            self.settle_early()
        if k < len(self.plan):
            self.begin(k)
        else:
            self.finish(self.c)


def row_view(ref, start, size):
    start = start if isinstance(start, int) else pl.multiple_of(start, 16 if size % 16 == 0 else 8)
    return ref.at[pl.ds(start, size)]


def column_block(index, columns):
    return pl.ds(pl.multiple_of(index * columns, 128), columns)


class Rider:
    def __init__(self, batch, send, recv, first):
        self.b, self.send, self.recv, self.at = batch, send, recv, first

    def go(self, src, dst, bit):
        copy = pltpu.make_async_remote_copy(
            src_ref=src, dst_ref=dst, send_sem=self.send.at[self.at], recv_sem=self.recv.at[self.at],
            device_id={"batch": flip_bits(self.b, 1 << bit)}, device_id_type=MESH,
        )
        self.at += 1
        copy.start()
        return copy

    def halve_pieces(self, source, landing, bit, pieces, half):
        size = half // pieces
        mine = bit_of(self.b, bit)
        copies = []

        def start(p):
            copies.append(
                self.go(
                    row_view(source, (1 - mine) * half + p * size, size), row_view(landing, p * size, size), bit
                )
            )

        def settle():
            for copy in copies:
                copy.wait()

        return start, settle, row_view(source, mine * half, half)

    def halve(self, source, landing, bit):
        half = landing.shape[0]
        mine = bit_of(self.b, bit)
        copy = self.go(row_view(source, (1 - mine) * half, half), landing, bit)

        def end():
            copy.wait()
            own = row_view(source, mine * half, half)
            landing[...] = b16(f32(own[...]) + f32(landing[...]))

        return end

    def double(self, source, target, bit):
        half = source.shape[0]
        there = row_view(target, bit_of(self.b, bit) * half, half)
        copy = self.go(source, there, bit)
        there[...] = source[...]
        return copy.wait

    def chain(self, refs, bits, move):
        ends, stages = [], []
        for i, bit in enumerate(bits):

            def stage(i=i, bit=bit):
                if ends:
                    ends.pop()()
                ends.append(move(refs[i], refs[i + 1], bit))

            stages.append(stage)
        stages.append(lambda: ends.pop()())
        return stages


def ride_orders(count):
    bits = list(range(count.bit_length() - 1))
    return bits, [1, 0] + bits[2:]


def tail_body(specs, chunks, ns, nb, n_in, n_out, *refs):
    (one_sums, mix_sums, two_sums, conv_sums, own_sums), refs = refs[:5], refs[5:]
    given, refs = refs[: n_in + 2], refs[n_in + 2 :]
    outs_hbm, refs = refs[:n_out], refs[n_out:]
    (o_gains, o_biases, o_taps, o_hidden), refs = refs[:4], refs[4:]
    send, recv, turn_send, turn_recv, pre_send, pre_recv, ride_send, ride_recv = refs[:8]
    ss, rs, sb, rb, wide, land_s, mid, land_b, ride_fin, load_sem = refs[8:18]
    shard, batch = lax.axis_index("shard"), lax.axis_index("batch")
    flush = Flush(refs[18])
    outs = refs[19 : 19 + n_out]
    rest = list(refs[19 + n_out :])
    pairs, ins, blocks = [], [], {}
    for i, ref in enumerate(given):
        if i < n_in and specs["arrays"][i][0] == "gather":
            pair = []
            for index in (shard, flip_bits(shard, 2)):
                held_block = rest.pop(0)
                pairs.append((ref.at[:, column_block(index, held_block.shape[1])], held_block))
                pair.append(held_block)
            blocks[i] = (pair, (len(pairs) - 2, len(pairs) - 1))
            ins.append(ref)
        else:
            held_ref = rest.pop(0)
            pairs.append((ref, held_ref))
            blocks[i] = (None, (len(pairs) - 1,))
            ins.append(held_ref)
    loads = Loads(load_sem, pairs)
    ins, ridden = ins[:n_in], ins[n_in:]
    shard, batch = lax.axis_index("shard"), lax.axis_index("batch")
    barrier = pltpu.get_barrier_semaphore()
    greeted = [{"batch": lax.rem(batch + j, nb)} for j in range(1, nb)]
    greeted += [{"shard": flip_bits(shard, m)} for m in range(1, ns)]
    for device in greeted:
        pl.semaphore_signal(barrier, inc=1, device_id=device, device_id_type=MESH)
    width = own_sums.shape[1]
    for t in range(ns):
        cols = slice(t * width, (t + 1) * width)
        wide[t, 0:3, :] = one_sums[0:3, cols]
        wide[t, 3:6, :] = mix_sums[0:3, cols]
        wide[t, 6:9, :] = two_sums[0:3, cols]
        wide[t, 9:14, :] = conv_sums[0:5, cols]
        wide[t, 14:19, :] = conv_sums[8:13, cols]
        wide[t, 19:21, :] = two_sums[4:6, cols]
        wide[t, 21:24, :] = jnp.zeros((3, width), jnp.float32)
    pl.semaphore_wait(barrier, len(greeted))

    vector_copies = []
    for j in range(1, ns):
        peer = lax.rem(shard + j, ns)
        copy = pltpu.make_async_remote_copy(
            src_ref=wide.at[peer], dst_ref=land_s.at[shard], send_sem=ss.at[j], recv_sem=rs.at[j],
            device_id={"shard": peer}, device_id_type=MESH,
        )
        copy.start()
        vector_copies.append(copy)
    land_s[shard] = wide[shard]

    def vectors_on():
        for copy in vector_copies:
            copy.wait()
        mid[0:24, :] = sum_slots(land_s, ns)
        mid[24:28, :] = own_sums[0:4, :]
        per = one_sums.shape[1] // width
        for t in range(per):
            cols = slice(t * width, (t + 1) * width)
            mid[28 + t : 29 + t, :] = one_sums[3:4, cols]
            mid[28 + per + t : 29 + per + t, :] = two_sums[3:4, cols]
        mid[28 + 2 * per :, :] = jnp.zeros((mid.shape[0] - 28 - 2 * per, width), jnp.float32)
        vector_copies[:] = exchange("batch", batch, nb, mid, land_b, sb, rb)
        for copy in vector_copies:
            copy.start()
        land_b[batch] = mid[...]

    def vectors_out():
        for copy in vector_copies:
            copy.wait()
        vec = sum_slots(land_b, nb)
        row = lambda k: vec[k : k + 1]
        mine = conv_sums[5:7, column_block(shard, width)]
        gains = [row(0), row(3), row(9), mine[0:1], row(6), row(19)]
        order = [1, 2, 4, 24, 25, 5, 26, 27, 10, 11, 12, None, 13, 7, 8, 20]
        for k, value in enumerate(gains):
            o_gains[k : k + 1, :] = value
        for k, at in enumerate(order):
            o_biases[k : k + 1, :] = mine[1:2] if at is None else row(at)
        o_taps[...] = vec[14:19]
        per = o_hidden.shape[1] // width
        for k in range(2):
            for t in range(per):
                at = 28 + k * per + t
                o_hidden[k : k + 1, t * width : (t + 1) * width] = row(at)

    late = []

    def leave(out, lead, start, rows):
        src, dst = outs[out], outs_hbm[out]
        if lead is not None:
            src, dst = src.at[lead], dst.at[lead]
        flush.go(src.at[pl.ds(start, rows)], dst.at[pl.ds(start, rows)])

    def turn(c_at, total, row, rows, out, lead):
        target = outs[out] if lead is None else outs[out].at[lead]
        columns = target.shape[1]
        height = target.shape[0] // ns
        there = row_view(target, shard * height + row, rows)
        copies = []
        for j in range(1, ns):
            peer = flip_bits(shard, j)
            copy = pltpu.make_async_remote_copy(
                src_ref=total.at[:, column_block(peer, columns)],
                dst_ref=there,
                send_sem=turn_send.at[c_at, j],
                recv_sem=turn_recv.at[c_at, j],
                device_id={"shard": peer},
                device_id_type=MESH,
            )
            copy.start()
            copies.append(copy)
        there[...] = total[:, column_block(shard, columns)]

        def after():
            for copy in copies:
                copy.wait()
            for t in range(ns):
                leave(out, lead, t * height + row, rows)

        late.append(after)

    rides = []
    orders = ride_orders(nb)
    plain_target = outs[0].at[1]
    rider_a = Rider(batch, ride_send, ride_recv, 0)
    rider_b = Rider(batch, ride_send, ride_recv, 1)
    loads.need(*blocks[n_in][1], *blocks[n_in + 1][1])
    end_a = rider_a.double(ridden[0], plain_target, orders[0][0])
    end_b = rider_b.double(ridden[1], ride_fin, orders[1][0])

    movers = []
    for c in chunks:
        kind, out, lead = specs["arrays"][c.source]
        source, base, early, settle = ins[c.source], c.row, [], None
        if kind == "gather":
            near_land, far_land = rest.pop(0), rest.pop(0)
            whole, columns, rows = ins[c.source], c.columns, pl.ds(c.row, c.rows)
            own_block, far_block = blocks[c.source][0]
            state = {}

            def pre(at, src, dst, mask, c=c):
                copy = pltpu.make_async_remote_copy(
                    src_ref=src, dst_ref=dst, send_sem=pre_send.at[c.at, at], recv_sem=pre_recv.at[c.at, at],
                    device_id={"shard": flip_bits(shard, mask)}, device_id_type=MESH,
                )
                copy.start()
                return copy

            def first(near_land=near_land, whole=whole, columns=columns, rows=rows, state=state, pre=pre):
                state["n"] = [
                    pre(i, whole.at[rows, column_block(flip_bits(shard, m), columns)], near_land.at[i], 1)
                    for i, m in enumerate((1, 3))
                ]

            def second(
                near_land=near_land, far_land=far_land, far_block=far_block, rows=rows, state=state, pre=pre,
            ):
                for copy in state["n"]:
                    copy.wait()
                near_land[1] = b16(f32(near_land[1]) + f32(far_block[rows]))
                state["f"] = pre(2, near_land.at[1], far_land, 2)

            def settle(
                near_land=near_land, far_land=far_land, own_block=own_block, rows=rows, state=state,
            ):
                state["f"].wait()
                far_land[...] = b16(
                    f32(far_land[...]) + f32(near_land[0]) + f32(own_block[rows])
                )

            early = [first, second]
            source, base = far_land, 0
        if kind == "turn":
            total = rest.pop(0)
            held = lambda off, size, total=total: row_view(total, off, size)

            def finish(c, total=total, out=out, lead=lead):
                turn(c.at, total, c.row, c.rows, out, lead)
        else:
            target = outs[out] if lead is None else outs[out].at[lead]
            held = lambda off, size, target=target, c=c: row_view(target, c.row + off, size)

            def finish(c, out=out, lead=lead):
                leave(out, lead, c.row, c.rows)
        landings = [rest.pop(0) for _ in range(c.steps)]
        m = Mover(c, batch, source, base, held, landings, (send, recv), finish, early)
        m.settle_early = settle
        movers.append(m)
    starts, lag = [], specs["lag"]
    for i, m in enumerate(movers):
        starts.append(max(0, i // lag - len(m.early)))
    rounds = max(s + m.depth + 1 for s, m in zip(starts, movers))
    for r in range(rounds):
        ready, late[:] = late[:], []
        if r == 1:
            vectors_on()
        if r == 2:
            end_b()
            turn(len(chunks), ride_fin, 0, ride_fin.shape[0], 1, 1)
        if r == 3:
            vectors_out()
            end_a()
            leave(0, 1, 0, outs[0].shape[1])
        for s, m in zip(starts, movers):
            if 0 <= r - s <= m.depth:
                loads.need(*blocks[m.c.source][1])
                m.advance(r - s)
        for after in ready:
            after()
    for after in late:
        after()
    flush.settle()


def tail_sum(arrays, ridden, sums, kinds, outputs, firsts, chunk_rows, hidden, ident):
    ns, nb = lax.axis_size("shard"), lax.axis_size("batch")
    low, full = jnp.bfloat16, jnp.float32
    chunks = []
    for i, a in enumerate(arrays):
        step = chunk_rows[i]
        columns = a.shape[1] // ns if kinds[i][0] == "gather" else a.shape[1]
        for row in range(0, a.shape[0], step):
            chunks.append(Chunk(len(chunks), i, row, step, columns, firsts[len(chunks) % len(firsts)], nb))
    depth = max(2 * c.steps for c in chunks)
    specs = dict(arrays=kinds, lag=2)
    width = sums[-1].shape[1]
    per = hidden // width
    small = -(-(28 + 2 * per) // 8) * 8
    dma = pltpu.SemaphoreType.DMA
    n = len(chunks)
    scratch = [
        dma((n, depth)), dma((n, depth)), dma((n + 1, ns)), dma((n + 1, ns)), dma((n, 3)), dma((n, 3)),
        dma((2,)), dma((2,)), dma((ns,)), dma((ns,)), dma((nb,)), dma((nb,)),
        pltpu.VMEM((ns, 24, width), full), pltpu.VMEM((ns, 24, width), full),
        pltpu.VMEM((small, width), full), pltpu.VMEM((nb, small, width), full),
        pltpu.VMEM((2 * ridden[1].shape[0], ridden[1].shape[1]), low),
        dma((2 * len(arrays) + 2,)),
        dma(((ns + 1) * (n + 1) + 1,)),
    ]
    scratch += [pltpu.VMEM(o, low) for o in outputs]
    for i, a in enumerate(list(arrays) + list(ridden)):
        if i < len(arrays) and kinds[i][0] == "gather":
            scratch += [pltpu.VMEM((a.shape[0], a.shape[1] // ns), low)] * 2
        else:
            scratch.append(pltpu.VMEM(a.shape, low))
    for c in chunks:
        if kinds[c.source][0] == "gather":
            scratch += [pltpu.VMEM((2, c.rows, c.columns), low), pltpu.VMEM((c.rows, c.columns), low)]
        if kinds[c.source][0] == "turn":
            scratch.append(pltpu.VMEM((c.rows, c.columns), low))
        scratch += [pltpu.VMEM(shape, low) for shape in c.landings]
    shape = jax.ShapeDtypeStruct
    shapes = [shape(s, low) for s in outputs]
    shapes += [shape((6, width), full), shape((16, width), full), shape((5, width), full), shape((2, hidden), full)]
    operands = list(sums) + list(arrays) + list(ridden)
    return pl.pallas_call(
        functools.partial(tail_body, specs, chunks, ns, nb, len(arrays), len(outputs)),
        out_shape=shapes,
        in_specs=[VMEM_SPEC] * len(sums) + [HBM_SPEC] * (len(arrays) + 2),
        out_specs=[HBM_SPEC] * len(outputs) + [VMEM_SPEC] * 4,
        scratch_shapes=scratch,
        compiler_params=pltpu.CompilerParams(
            collective_id=ident, has_side_effects=True, vmem_limit_bytes=60 << 20
        ),
        name="tail_sum",
    )(*operands)


def widen_body(count, others, slots, *refs):
    n = count + others
    ins, outs = refs[:n], refs[n : 2 * n]
    stages, in_sem, out_sem, pass_sem = refs[2 * n : -3], refs[-3], refs[-2], refs[-1]
    passed = []
    for at in range(others):
        passed.append(pltpu.make_async_copy(ins[count + at], outs[count + at], pass_sem.at[at]))
        passed[-1].start()
    half = len(stages) // 2
    items, used = [], {}
    for src, dst in zip(ins[:count], outs[:count]):
        for lead in range(src.shape[0]) if len(src.shape) == 3 else [None]:
            source = src if lead is None else src.at[lead]
            target = dst if lead is None else dst.at[lead]
            rows, columns = source.shape
            kind = [k.shape[2] for k in stages[:half]].index(columns)
            size = stages[kind].shape[1]
            for row in range(0, rows, size):
                slot = used.get(kind, 0) % slots
                used[kind] = used.get(kind, 0) + 1
                items.append((source.at[pl.ds(row, size)], target.at[pl.ds(row, size)], kind, slot))
    items.sort(key=lambda item: item[2])
    loads, stores = {}, {}

    def load(i):
        if i < len(items):
            source, _, kind, slot = items[i]
            loads[i] = pltpu.make_async_copy(source, stages[kind].at[slot], in_sem.at[kind, slot])
            loads[i].start()

    ahead = slots - 1
    for i in range(ahead):
        load(i)
    for i, (_, target, kind, slot) in enumerate(items):
        loads[i].wait()
        if (kind, slot) in stores:
            stores.pop((kind, slot)).wait()
        narrow, wide = stages[kind].at[slot], stages[half + kind].at[slot]

        @pl.loop(0, narrow.shape[0] // 64)
        def _(k, narrow=narrow, wide=wide):
            part = pl.ds(pl.multiple_of(k * 64, 64), 64)
            wide[part] = f32(narrow[part])

        stores[kind, slot] = pltpu.make_async_copy(wide, target, out_sem.at[kind, slot])
        stores[kind, slot].start()
        load(i + ahead)
    for copy in list(stores.values()) + passed:
        copy.wait()


def widen(arrays, others):
    columns = sorted({a.shape[-1] for a in arrays})
    slots = 6
    least = lambda c: min([a.shape[-2] for a in arrays if a.shape[-1] == c] + [(256 * 1024) // c])
    stages = [pltpu.VMEM((slots, least(c), c), d) for d in (jnp.bfloat16, jnp.float32) for c in columns]
    dma = pltpu.SemaphoreType.DMA
    return pl.pallas_call(
        functools.partial(widen_body, len(arrays), len(others), slots),
        out_shape=[jax.ShapeDtypeStruct(a.shape, jnp.float32) for a in (*arrays, *others)],
        in_specs=[HBM_SPEC] * len(arrays) + [VMEM_SPEC] * len(others),
        out_specs=[HBM_SPEC] * (len(arrays) + len(others)),
        scratch_shapes=stages + [dma((len(columns), slots)), dma((len(columns), slots)), dma((len(others),))],
        compiler_params=pltpu.CompilerParams(vmem_limit_bytes=60 << 20),
        name="widen",
    )(*arrays, *others)


class Links:
    def __init__(self, send, recv):
        self.send, self.recv, self.count = send, recv, 0
        s = lax.axis_index("shard")
        self.shard = s
        self.near = {"shard": flip_bits(s, 1)}
        self.far = {"shard": flip_bits(s, 2)}
        self.across = {"shard": flip_bits(s, 3)}

    def greet(self, devices):
        barrier = pltpu.get_barrier_semaphore()
        for device in devices:
            pl.semaphore_signal(barrier, inc=1, device_id=device, device_id_type=MESH)
        pl.semaphore_wait(barrier, len(devices))

    def go(self, src, dst, device):
        at = self.count
        self.count += 1
        copy = pltpu.make_async_remote_copy(
            src_ref=src, dst_ref=dst, send_sem=self.send.at[at], recv_sem=self.recv.at[at],
            device_id=device, device_id_type=MESH,
        )
        copy.start()
        return copy


def sums_scratch(rows, columns):
    half = rows // 2
    return [
        pltpu.VMEM((2, rows, columns), jnp.float32),
        pltpu.VMEM((4, half, columns), jnp.bfloat16),
        pltpu.VMEM((4, half, columns), jnp.bfloat16),
        pltpu.VMEM((2, half, columns), jnp.bfloat16),
        pltpu.VMEM((2, half, columns), jnp.bfloat16),
    ]


class Sums:
    def __init__(self, links, refs):
        self.links = links
        self.part, self.send, self.land, self.cross, self.land_cross = refs
        self.half = self.send.shape[1]
        self.near, self.crossing, self.backs = None, [], []

    def rows(self, h):
        return slice(h * self.half, (h + 1) * self.half)

    def keep(self, cols, value):
        self.part[0, :, cols] = value

    def keep_far(self, cols, value):
        self.part[1, :, cols] = value

    def give(self, cols, value):
        self.send[0, :, cols] = b16(value[: self.half])
        self.send[1, :, cols] = b16(value[self.half :])

    def give_far(self, cols, value):
        self.send[2, :, cols] = b16(value[: self.half])
        self.send[3, :, cols] = b16(value[self.half :])

    def split(self, h):
        def emit(cols, value):
            self.part[1, self.rows(h), cols] = value[: self.half]
            self.send[2 + h, :, cols] = b16(value[self.half :])

        return emit

    def send_near(self):
        both = pl.ds(0, 2)
        self.near = self.links.go(self.send.at[both], self.land.at[both], self.links.near)

    def send_back(self, h):
        self.backs.append(self.links.go(self.send.at[2 + h], self.land.at[2 + h], self.links.near))

    def send_cross(self, h):
        self.backs[h].wait()
        self.cross[h] = b16(self.part[1, self.rows(h)] + f32(self.land[2 + h]))
        self.crossing.append(self.links.go(self.cross.at[h], self.land_cross.at[h], self.links.far))

    def arrive(self, h):
        if self.near is not None:
            self.near.wait()
            self.near = None
        self.crossing[h].wait()
        return self.part[0, self.rows(h)] + f32(self.land[h]) + f32(self.land_cross[h])


def gather_work_scatter(links, x, fill, work, refs):
    sums = Sums(links, refs)
    half = x.shape[1] // 2
    out = []
    for h in range(2):
        fill(h)
        out.append(links.go(x.at[0, pl.ds(h * half, half)], x.at[2 + h, pl.ds(0, half)], links.far))
    near = links.go(x.at[0], x.at[1], links.near)
    work(0, sums.keep)
    near.wait()
    work(1, sums.give)
    sums.send_near()
    for h in range(2):
        out[h].wait()
        on = links.go(x.at[2 + h, pl.ds(0, half)], x.at[2 + h, pl.ds(half, half)], links.near)
        on.wait()
        work(2 + h, sums.split(h))
        sums.send_back(h)
        sums.send_cross(h)
    return sums


def tiles(total, size):
    def over(body):
        pl.loop(0, total // size)(
            lambda n: body(pl.ds(pl.multiple_of(n * size, size), size))
        )

    return over


def norm_parts(rows):
    row_mean = jnp.mean(rows, axis=-1, keepdims=True)
    centered = rows - row_mean
    inverse = lax.rsqrt(jnp.mean(centered * centered, axis=-1, keepdims=True) + epsilon)
    return centered * inverse, inverse


def norm_slope(grad, scaled, inverse, gain):
    inner = grad * gain
    return inverse * (
        inner
        - jnp.mean(inner, axis=-1, keepdims=True)
        - scaled * jnp.mean(inner * scaled, axis=-1, keepdims=True)
    )


def column_sum(value):
    return jnp.sum(value, axis=0, keepdims=True)


def ffn_up(hid, act, slope, w_in, b_ref, which):
    def run(block):
        @tiles(w_in.shape[1], 512)
        def _(cols):
            pre = dot_rows(hid[block], w_in[:, cols]) + f32(b_ref[which : which + 1, cols])
            gate = jax.nn.sigmoid(pre)
            act[block, :, cols] = b16(pre * gate)
            slope[block, :, cols] = b16(gate * (1.0 + pre * (1.0 - gate)))

    return run


def ffn_down(act, w_rows):
    def run(block, emit):
        @tiles(w_rows.shape[1], 512)
        def _(cols):
            emit(cols, dot_rows(act[block], w_rows[:, cols]))

    return run


def ffn_inward(grad, inner, slope, w_in, w_rows):
    def run(block, emit):
        @tiles(w_in.shape[1], 512)
        def _(cols):
            wide = dot_back(grad[block], w_rows[cols, :])
            inner[block, :, cols] = b16(wide * f32(slope[block, :, cols]))

        @tiles(w_in.shape[0], 512)
        def _(cols):
            emit(cols, dot_back(inner[block], w_in[cols, :]))

    return run


def flat(ref):
    return ref[...].reshape(ref.shape[0] * ref.shape[1], ref.shape[2])


def flat_columns(ref, cols, size):
    return ref[:, :, cols].reshape(ref.shape[0] * ref.shape[1], size)


def weight_out(act, grad, gw_out):
    @tiles(act.shape[2], 256)
    def _(cols):
        gw_out[cols, :] = b16(dot_over(flat_columns(act, cols, 256), flat(grad)))


def weight_in(hid, inner, gw_in, sums_ref):
    @tiles(inner.shape[2], 256)
    def _(cols):
        right = flat_columns(inner, cols, 256)
        gw_in[:, cols] = b16(dot_over(flat(hid), right))
        sums_ref[3:4, cols] = column_sum(f32(right))


class Fetch:
    def __init__(self, links, batch, local_sem):
        self.links, self.local_sem = links, local_sem
        self.quarter = bit_of(batch, 0) + 2 * bit_of(batch, 1)
        self.peers = [{"batch": flip_bits(batch, 1)}, {"batch": flip_bits(batch, 2)}]

    def flow(self, source_rows, target, blocks, rows):
        links, size, held = self.links, rows // 8, {}
        span = lambda q, p: pl.ds(pl.multiple_of(q * (2 * size) + p * size, 16), size)
        mine = self.quarter
        own = blocks[0]

        def first():
            for p in range(2):
                for t, device, _ in blocks[1:]:
                    held["y", p, t] = links.go(
                        source_rows(t, mine * (2 * size) + p * size, size),
                        target.at[span(mine, p), own],
                        device,
                    )

        def pass_on(p, q, t, block, way):
            there = target.at[span(q, p), block]
            return links.go(there, there, self.peers[way])

        def second(p):
            def run():
                for t, _, block in blocks[1:]:
                    held["y", p, t].wait()
                    held["a", p, t] = pass_on(p, mine, t, block, p)

            return run

        def third(p):
            def run():
                other = flip_bits(mine, 1 << p)
                for t, _, block in blocks[1:]:
                    held["a", p, t].wait()
                    held["b", p, t] = pass_on(p, mine, t, block, 1 - p)
                    held["c", p, t] = pass_on(p, other, t, block, 1 - p)

            return run

        def last():
            for p in range(2):
                for t, _, _ in blocks[1:]:
                    held["b", p, t].wait()
                    held["c", p, t].wait()

        return [first, second(0), second(1), third(0), third(1), last]

    def columns(self, source, target, at):
        links, (rows, columns) = self.links, source.shape
        far = flip_bits(links.shard, 2)
        own = column_block(links.shard, columns)
        far_block = column_block(far, columns)
        row = lambda t, start, size: source.at[pl.ds(pl.multiple_of(start, 16), size)]
        stages = self.flow(row, target, [own, (2, links.far, far_block)], rows)
        held = {}

        def first():
            stages[0]()
            held["own"] = pltpu.make_async_copy(source, target.at[:, own], self.local_sem.at[at])
            held["own"].start()
            held["near"] = links.go(source, target.at[:, own], links.near)

        def pass_near():
            stages[-1]()
            held["on"] = links.go(target.at[:, far_block], target.at[:, far_block], links.near)

        def finish():
            held["on"].wait()
            held["near"].wait()
            held["own"].wait()

        return [first] + stages[1:-1] + [pass_near, finish]

    def rows(self, source, target, at):
        links, rows = self.links, target.shape[0]
        columns = source.shape[1]
        index = [flip_bits(links.shard, m) for m in range(4)]
        own = column_block(links.shard, columns)
        row = lambda m, start, size: source.at[pl.ds(pl.multiple_of(index[m] * rows + start, 16), size)]
        blocks = [own] + [
            (m, device, column_block(index[m], columns)) for m, device in ((2, links.far), (3, links.across))
        ]
        stages = self.flow(row, target, blocks, rows)
        held = {}

        def first():
            stages[0]()
            held["own"] = pltpu.make_async_copy(row(0, 0, rows), target.at[:, own], self.local_sem.at[at])
            held["own"].start()
            held["near"] = links.go(row(1, 0, rows), target.at[:, own], links.near)

        def last():
            stages[-1]()
            held["near"].wait()
            held["own"].wait()

        return [first] + stages[1:-1] + [last]


def vector_row(pack, row):
    return f32(jnp.concatenate([pack[t, row : row + 1, :] for t in range(pack.shape[0])], 1))

def link_scratch(count, local):
    return [
        pltpu.SemaphoreType.DMA((count,)),
        pltpu.SemaphoreType.DMA((count,)),
        pltpu.SemaphoreType.DMA((local,)),
    ]


def front_body(
    heads, size,
    rows_ref, gains_ref, own_ref, taps_ref, b_ref, base_ref, length_ref,
    pos_hbm, qkv_hbm, ffn_in, ffn_out, out_proj, conv_in, conv_out,
    one_ref, two_ref, pack, table, proj, with_u, with_v, key, value, mix, wc_in, w_mine, wc_out, w_rows_two,
    hid_out, act_out, slope_out, w_rows_out, hidden_out, soft_out,
    hid, act, slope, w_rows, w_in, w_out, pos_ref, w_qkv, hid_b, soft_ref, turned,
    part, send, land, cross, land_cross, send_sem, recv_sem, local_sem, load_sem, flush_sem, pack_in,
):
    batch = lax.axis_index("batch")
    links = Links(send_sem, recv_sem)
    fetch = Fetch(links, batch, local_sem)
    flush = Flush(flush_sem)
    pack_in[0:6, :] = gains_ref[...]
    pack_in[6:22, :] = own_ref[...]
    pack_in[22:27, :] = taps_ref[...]
    pack_in[27:32, :] = b16(jnp.full((5, pack_in.shape[1]), length_ref[0], jnp.int32).astype(jnp.float32))
    loads = Loads(load_sem, [(ffn_in.at[0], w_in), (pos_hbm, pos_ref), (qkv_hbm, w_qkv)])
    links.greet([links.near, links.far, links.across] + fetch.peers)
    small = [
        links.go(pack_in, pack.at[links.shard], device)
        for device in (links.far, links.across, links.near)
    ]
    down = fetch.rows(ffn_out.at[0], w_rows, 0)
    down.pop(0)()
    pack[links.shard] = pack_in[...]
    for copy in small:
        copy.wait()
    rows, features = rows_ref.shape
    hid[0] = b16(norm_rows(rows_ref[...], vector_row(pack, 0), vector_row(pack, 6)))
    half = rows // 2
    out = [
        links.go(hid.at[0, pl.ds(h * half, half)], hid.at[2 + h, pl.ds(0, half)], links.far)
        for h in range(2)
    ]
    near = links.go(hid.at[0], hid.at[1], links.near)
    up = ffn_up(hid, act, slope, w_in, b_ref, 0)
    loads.need(0)
    up(0)
    down.pop(0)()
    down.pop(0)()
    near.wait()
    up(1)
    lanes = features // 2

    @pl.loop(0, table.shape[0] // 16)
    def _(i):
        at = pl.ds(pl.multiple_of(i * 16, 16), 16)
        s_a, c_a = base_ref[pl.ds(16 + i, 1), 0:lanes], base_ref[pl.ds(16 + i, 1), lanes:]
        s_b, c_b = base_ref[0:16, 0:lanes], base_ref[0:16, lanes:]
        table[at, 0:lanes] = b16(s_a * c_b + c_a * s_b)
        table[at, lanes:] = b16(c_a * c_b - s_a * s_b)

    loads.need(1)
    proj[...] = b16(dot_rows(table[...], pos_ref[...]))
    down.pop(0)()
    down.pop(0)()
    other = fetch.columns(out_proj, w_out, 1)
    leaving = fetch.columns(conv_in, wc_in, 3)
    second = fetch.rows(ffn_out.at[1], w_rows_two, 4)
    for h in range(2):
        out[h].wait()
        on = links.go(hid.at[2 + h, pl.ds(0, half)], hid.at[2 + h, pl.ds(half, half)], links.near)
        on.wait()
        if h == 1:
            other.pop(0)()
        up(2 + h)
    leaving.pop(0)()
    for pair in ((hid, hid_out), (act, act_out), (slope, slope_out)):
        flush.go(*pair)
    while down:
        down.pop(0)()
    flush.go(w_rows, w_rows_out)
    sums = Sums(links, (part, send, land, cross, land_cross))
    work = ffn_down(act, w_rows)
    for h in range(2):
        work(2 + h, sums.split(h))
        sums.send_back(h)
    for h in range(2):
        sums.send_cross(h)
    second.pop(0)()
    work(1, sums.give)
    sums.send_near()
    work(0, sums.keep)
    for _ in range(4):
        other.pop(0)()
        leaving.pop(0)()

    out_bias, gain, shift = vector_row(pack, 7), vector_row(pack, 1), vector_row(pack, 8)
    out = []
    for h in range(2):
        at = slice(h * half, (h + 1) * half)
        one = rows_ref[at] + 0.5 * (sums.arrive(h) + out_bias)
        one_ref[at] = one
        hid_b[0, at] = b16(norm_rows(one, gain, shift))
        there = pl.ds(h * half, half)
        out.append(links.go(hid_b.at[0, there], hid_b.at[2, there], links.far))
    near = links.go(hid_b.at[0], hid_b.at[1], links.near)
    while other:
        other.pop(0)()
        leaving.pop(0)()
    entering = fetch.columns(conv_out, wc_out, 2)
    own = f32(own_ref[...])
    keys = f32(lax.broadcasted_iota(jnp.int32, (rows, rows), 1))
    scale = 1.0 / math.sqrt(size)
    loads.need(2)

    def attend(slot):
        hidden = hid_b[slot]
        query = dot_rows(hidden, w_qkv[0]) + own[3:4]
        with_u[slot] = b16(query + own[6:7])
        with_v[slot] = b16(query + own[7:8])
        key[slot] = b16(dot_rows(hidden, w_qkv[1]))
        value[slot] = b16(dot_rows(hidden, w_qkv[2]) + own[4:5])
        live = f32(pack[flip_bits(links.shard, slot), 27:28, 0:1])
        for h in range(heads):
            cols = slice(h * size, (h + 1) * size)
            wide = dot_back(with_v[slot, :, cols], proj[:, cols])
            moved = pltpu.roll(wide, rows + 1, 1, stride=1, stride_axis=0)[:, :rows]
            raw = dot_back(with_u[slot, :, cols], key[slot, :, cols]) + moved
            scores = jnp.where(keys < live, raw * scale, -1e30)
            grown = jnp.exp(scores - jnp.max(scores, axis=-1, keepdims=True))
            soft = grown / jnp.sum(grown, axis=-1, keepdims=True)
            soft_ref[slot, :, h * rows : (h + 1) * rows] = soft
            mix[slot, :, cols] = b16(dot_rows(b16(soft), value[slot, :, cols]))

    last = []
    attend(0)
    turned[links.shard] = mix[0]
    near.wait()
    second.pop(0)()
    second.pop(0)()
    attend(1)
    second.pop(0)()
    second.pop(0)()
    last.append(links.go(mix.at[1], turned.at[links.shard], links.near))
    on = []
    for h in range(2):
        out[h].wait()
        there = pl.ds(h * half, half)
        on.append(links.go(hid_b.at[2, there], hid_b.at[3, there], links.near))
        if h == 0:
            entering.pop(0)()
    attend(2)
    last.append(links.go(mix.at[2], turned.at[links.shard], links.far))
    entering.pop(0)()
    entering.pop(0)()
    for copy in on:
        copy.wait()
    flush.go(hid_b, hidden_out)
    attend(3)
    last.append(links.go(mix.at[3], turned.at[links.shard], links.across))
    flush.go(soft_ref, soft_out)
    entering.pop(0)()
    entering.pop(0)()
    for copy in last:
        copy.wait()
    width = mix.shape[2]
    total = one_ref[...] + vector_row(pack, 11)
    for t in range(turned.shape[0]):
        total = total + dot_rows(turned[t], w_out[t * width : (t + 1) * width])
    two_ref[...] = total
    w_mine[...] = w_out[pl.ds(pl.multiple_of(links.shard * width, 16), width), :]
    while entering:
        entering.pop(0)()
    while second:
        second.pop(0)()
    flush.settle()


def front(
    rows_in, gains, own_biases, taps, lengths, b_in, base, pos_proj, qkv_proj, ffn_in, ffn_out, out_proj, conv_in,
    conv_out, heads, ident,
):
    ns = lax.axis_size("shard")
    rows, features = rows_in.shape
    hidden = ffn_in.shape[2]
    width = features // ns
    low, full = jnp.bfloat16, jnp.float32
    shape, vmem = jax.ShapeDtypeStruct, pltpu.VMEM
    narrow = shape((ns, rows, width), low)
    dma = pltpu.SemaphoreType.DMA
    return pl.pallas_call(
        functools.partial(front_body, heads, width // heads),
        out_shape=[
            shape((rows, features), full), shape((rows, features), full),
            shape((ns, 32, width), low),
            shape((2 * rows, features), low), shape((2 * rows, width), low),
            narrow, narrow, narrow, narrow, narrow,
            shape((conv_in.shape[0], ns * conv_in.shape[1]), low),
            shape((width, features), low),
            shape((features, features), low),
            shape((hidden, features), low),
            shape((4, rows, features), low), shape((4, rows, hidden), low), shape((4, rows, hidden), low),
            shape((hidden, features), low),
            shape((ns, rows, features), low),
            shape((ns, rows, heads * rows), full),
        ],
        in_specs=[VMEM_SPEC] * 6 + [pl.BlockSpec(memory_space=pltpu.SMEM)] + [HBM_SPEC] * 7,
        out_specs=[VMEM_SPEC] * 14 + [HBM_SPEC] * 6,
        scratch_shapes=[
            vmem((4, rows, features), low), vmem((4, rows, hidden), low), vmem((4, rows, hidden), low),
            vmem((hidden, features), low), vmem((features, hidden), low), vmem((features, features), low),
            vmem(pos_proj.shape, low), vmem(qkv_proj.shape, low),
            vmem((ns, rows, features), low), vmem((ns, rows, heads * rows), full), vmem((ns, rows, width), low),
        ]
        + sums_scratch(rows, features)
        + link_scratch(100, 5)
        + [dma((3,)), dma((6,)), vmem((32, width), low)],
        compiler_params=pltpu.CompilerParams(
            collective_id=ident, has_side_effects=True, vmem_limit_bytes=60 << 20
        ),
        name="front",
    )(
        rows_in, gains, own_biases, taps, b_in, base, lengths, pos_proj, qkv_proj, ffn_in, ffn_out, out_proj,
        conv_in, conv_out,
    )


def middle_body(
    nb, early, rows_ref, pack, b_ref, w_rows_hbm, cotangent_hbm, ffn_in,
    result, out_ref, gw_in, gw_out, sums_ref, early_a, early_b,
    hid, act, slope, grad, inner, w_in, cotangent, stream, w_rows, *refs,
):
    first, second, refs = refs[:5], refs[5:10], refs[10:]
    send_sem, recv_sem, ride_send, ride_recv, load_sem = refs
    batch = lax.axis_index("batch")
    links = Links(send_sem, recv_sem)
    loads = Loads(load_sem, [(ffn_in.at[1], w_in), (cotangent_hbm, cotangent), (w_rows_hbm, w_rows)])
    orders = ride_orders(nb)
    links.greet([links.near, links.far] + [{"batch": flip_bits(batch, 1 << k)} for k in range(2)])
    rows, features = rows_ref.shape
    half = rows // 2
    gain, shift = vector_row(pack, 4), vector_row(pack, 19)

    def fill(h):
        at = slice(h * half, (h + 1) * half)
        hid[0, at] = b16(norm_rows(rows_ref[at], gain, shift))

    up, down = ffn_up(hid, act, slope, w_in, b_ref, 1), ffn_down(act, w_rows)

    def work(block, emit):
        loads.need(0)
        up(block)
        loads.need(2)
        down(block, emit)

    sums = gather_work_scatter(links, hid, fill, work, first)
    last_gain, last_shift, out_bias = vector_row(pack, 5), vector_row(pack, 21), vector_row(pack, 20)
    live = f32(pack[links.shard, 27:28, 0:1])
    mask = f32(f32(lax.broadcasted_iota(jnp.int32, (rows, 1), 0)) < live)
    loads.need(1)
    ends = []

    def turn_back(h):
        at = slice(h * half, (h + 1) * half)
        scaled, inverse = norm_parts(rows_ref[at] + 0.5 * (sums.arrive(h) + out_bias))
        result[at] = (scaled * last_gain + last_shift) * mask[at]
        given = cotangent[at] * mask[at]
        slide = norm_slope(given, scaled, inverse, last_gain)
        stream[at] = slide
        grad[0, at] = b16(0.5 * slide)
        ends.append((column_sum(given * scaled), column_sum(given)))

    back = gather_work_scatter(
        links, grad, turn_back, ffn_inward(grad, inner, slope, w_in, w_rows), second
    )
    pieces = 4
    riders = [
        Rider(batch, ride_send, ride_recv, at * early).halve_pieces(
            (gw_in, gw_out)[at], (early_a, early_b)[at], orders[at][0], pieces, gw_in.shape[0] // 2
        )
        for at in range(2)
    ]
    weight_out(act, grad, gw_out)
    for p in range(early):
        riders[1][0](p)
    weight_in(hid, inner, gw_in, sums_ref)
    for p in range(early):
        riders[0][0](p)
    sums_ref[0:3, :] = jnp.zeros((3, features), jnp.float32)
    sums_ref[2:3, :] = column_sum(f32(grad[0]))
    sums_ref[4:5, :] = ends[0][0] + ends[1][0]
    sums_ref[5:6, :] = ends[0][1] + ends[1][1]
    sums_ref[6:8, :] = jnp.zeros((2, features), jnp.float32)
    for h in range(2):
        at = slice(h * half, (h + 1) * half)
        scaled, inverse = norm_parts(rows_ref[at])
        given = back.arrive(h)
        out_ref[at] = stream[at] + norm_slope(given, scaled, inverse, gain)
        sums_ref[0:1, :] += column_sum(given * scaled)
        sums_ref[1:2, :] += column_sum(given)
    for _, settle, _ in riders:
        settle()


EARLY = 1


def middle(rows_in, pack, b_in, w_rows, cotangent, ffn_in, ident):
    rows, features = rows_in.shape
    hidden = ffn_in.shape[2]
    nb = lax.axis_size("batch")
    low, full = jnp.bfloat16, jnp.float32
    shape, vmem = jax.ShapeDtypeStruct, pltpu.VMEM
    dma = pltpu.SemaphoreType.DMA
    piece = features // 8
    return pl.pallas_call(
        functools.partial(middle_body, nb, EARLY),
        out_shape=[
            shape((rows, features), full), shape((rows, features), full),
            shape((features, hidden), low), shape((hidden, features), low), shape((8, features), full),
            shape((EARLY * piece, hidden), low), shape((EARLY * piece, features), low),
        ],
        in_specs=[VMEM_SPEC] * 3 + [HBM_SPEC] * 3,
        out_specs=[VMEM_SPEC] * 7,
        scratch_shapes=[
            vmem((4, rows, features), low), vmem((4, rows, hidden), low), vmem((4, rows, hidden), low),
            vmem((4, rows, features), low), vmem((4, rows, hidden), low), vmem((features, hidden), low),
            vmem((rows, features), full), vmem((rows, features), full), vmem((hidden, features), low),
        ]
        + sums_scratch(rows, features)
        + sums_scratch(rows, features)
        + [dma((20,)), dma((20,)), dma((2 * EARLY,)), dma((2 * EARLY,)), dma((3,))],
        compiler_params=pltpu.CompilerParams(
            collective_id=ident, has_side_effects=True, vmem_limit_bytes=60 << 20
        ),
        name="middle",
    )(rows_in, pack, b_in, w_rows, cotangent, ffn_in)


def pack_rows(ref, at, row):
    for i in range(row.shape[1] // 128):
        ref[at + i : at + i + 1, :] = row[:, i * 128 : (i + 1) * 128]


def unpack_rows(value, at, lanes):
    return jnp.concatenate([value[at + i : at + i + 1, :] for i in range(lanes)], 1)


def everywhere(links, nb, source, mid, land_s, land_b, result, small, sems):
    s, b = links.shard, lax.axis_index("batch")
    ns = land_s.shape[0]
    ss, rs, sb, rb = sems
    first = exchange("shard", s, ns, source, land_s, ss, rs)
    for copy in first:
        copy.start()
    land_s[s] = source[...]
    for copy in first:
        copy.wait()
    mid[...] = sum_slots(land_s, ns)
    second = exchange("batch", b, nb, mid, land_b, sb, rb)
    for copy in second:
        copy.start()
    land_b[b] = mid[...]
    small()
    for copy in second:
        copy.wait()
    return sum_slots(land_b, nb)


def conv_body(
    nb, rows_ref, pack, w_in_hbm, w_out_hbm,
    out_ref, hid, open_ref, gate_ref, gated_ref, scaled_ref, act, slope, stats,
    padded, source, mid, land_s, land_b, ss, rs, sb, rb, send_sem, recv_sem, local_sem, w_in, w_out, load_sem,
):
    batch = lax.axis_index("batch")
    links = Links(send_sem, recv_sem)
    loads = Loads(load_sem, [(w_in_hbm, w_in), (w_out_hbm, w_out)])
    rows, features = rows_ref.shape
    ns = land_s.shape[0]
    links.greet(
        [links.near, links.far, links.across]
        + [{"batch": lax.rem(batch + j, nb)} for j in range(1, nb)]
    )
    live = f32(pack[links.shard, 27:28, 0:1])
    mask = f32(f32(lax.broadcasted_iota(jnp.int32, (rows, 1), 0)) < live)
    hid[...] = b16(norm_rows(rows_ref[...], vector_row(pack, 2), vector_row(pack, 14)))
    bias_v, bias_g = vector_row(pack, 15), vector_row(pack, 16)
    loads.need(0)
    lead = 8
    tile = 512
    padded[0:lead, :] = jnp.zeros((lead, features), jnp.float32)
    padded[lead + rows :, :] = jnp.zeros((lead, features), jnp.float32)
    for n in range(features // tile):
        cols = slice(n * tile, (n + 1) * tile)
        left = dot_rows(hid[...], w_in[:, cols]) + bias_v[:, cols]
        right = dot_rows(hid[...], w_in[:, features + n * tile : features + (n + 1) * tile])
        gate = jax.nn.sigmoid(right + bias_g[:, cols])
        opened = gate * mask
        gated = left * opened
        open_ref[:, cols] = b16(opened)
        gate_ref[:, cols] = b16(gated * (1.0 - gate))
        gated_ref[:, cols] = b16(gated)
        padded[lead : lead + rows, cols] = gated
    taps = 5
    total = 0.0
    for k in range(taps):
        at = lead - (taps - 1) // 2 + k
        total = total + padded[at : at + rows, :] * vector_row(pack, 22 + k)
    live_total = total * mask
    lanes = features // 128
    pack_rows(source, 0, jnp.sum(live_total, axis=0, keepdims=True))
    pack_rows(source, lanes, jnp.sum(live_total * total, axis=0, keepdims=True))
    source[2 * lanes : 2 * lanes + 8, :] = jnp.broadcast_to(live, (8, 128))
    scaled_ref[...] = total
    sums = everywhere(links, nb, source, mid, land_s, land_b, None, lambda: None, (ss, rs, sb, rb))
    frames = sums[2 * lanes : 2 * lanes + 1, 0:1]
    mean = unpack_rows(sums, 0, lanes) / frames
    inverse = lax.rsqrt(unpack_rows(sums, lanes, lanes) / frames - mean * mean + epsilon)
    stats[0:1, :] = inverse
    stats[1:2, :] = jnp.broadcast_to(frames, (1, features))
    stats[2:8, :] = jnp.zeros((6, features), jnp.float32)
    scaled = (scaled_ref[...] - mean) * inverse
    scaled_ref[...] = scaled
    normed = scaled * vector_row(pack, 3) + vector_row(pack, 17)
    gate = jax.nn.sigmoid(normed)
    act[...] = b16(normed * gate)
    slope[...] = b16(gate * (1.0 + normed * (1.0 - gate)))
    loads.need(1)
    out_ref[...] = rows_ref[...] + (dot_rows(act[...], w_out[...]) + vector_row(pack, 18))


def conv_forward(rows_in, pack, w_in, w_out, ident):
    ns, nb = lax.axis_size("shard"), lax.axis_size("batch")
    rows, features = rows_in.shape
    shape = jax.ShapeDtypeStruct
    low, full = jnp.bfloat16, jnp.float32
    plain = shape((rows, features), low)
    small = (24, 128)
    return pl.pallas_call(
        functools.partial(conv_body, nb),
        out_shape=[
            shape((rows, features), full), plain, plain, plain, plain,
            shape((rows, features), full), plain, plain, shape((8, features), full),
        ],
        in_specs=[VMEM_SPEC] * 2 + [HBM_SPEC] * 2,
        out_specs=[VMEM_SPEC] * 9,
        scratch_shapes=[
            pltpu.VMEM((rows + 16, features), full),
            pltpu.VMEM(small, full), pltpu.VMEM(small, full),
            pltpu.VMEM((ns,) + small, full), pltpu.VMEM((nb,) + small, full),
            pltpu.SemaphoreType.DMA((ns,)), pltpu.SemaphoreType.DMA((ns,)),
            pltpu.SemaphoreType.DMA((nb,)), pltpu.SemaphoreType.DMA((nb,)),
        ]
        + link_scratch(2, 1)
        + [pltpu.VMEM(w_in.shape, low), pltpu.VMEM(w_out.shape, low), pltpu.SemaphoreType.DMA((2,))],
        compiler_params=pltpu.CompilerParams(
            collective_id=ident, has_side_effects=True, vmem_limit_bytes=60 << 20
        ),
        name="conv_forward",
    )(rows_in, pack, w_in, w_out)


def conv_back_body(
    nb, stream_ref, rows_ref, pack, w_out, hid, open_ref, gate_ref, gated_ref, scaled_ref, act, slope, stats,
    early_a, early_b, w_in_hbm, ride_a, ride_b, out_ref, gw_out, gw_in, sums_ref, half_a, half_b,
    padded, normed, grad, inner, source, mid, land_s, land_b, ss, rs, sb, rb, send_sem, recv_sem,
    w_in, kept_a, kept_b, load_sem,
):
    batch = lax.axis_index("batch")
    links = Links(send_sem, recv_sem)
    kept = [
        row_view(ref, bit_of(batch, order[0]) * out.shape[0], out.shape[0])
        for ref, out, order in zip((ride_a, ride_b), (kept_a, kept_b), ride_orders(nb))
    ]
    loads = Loads(load_sem, [(w_in_hbm, w_in), (kept[0], kept_a), (kept[1], kept_b)])
    rows, features = rows_ref.shape
    links.greet(
        [links.near, links.far, links.across]
        + [{"batch": lax.rem(batch + j, nb)} for j in range(1, nb)]
    )
    orders = ride_orders(nb)
    pieces = 4
    ride = [
        Rider(batch, send_sem, recv_sem, at * pieces).halve_pieces(
            source_ref, landing, orders[at][0], pieces, landing.shape[0]
        )
        for at, (source_ref, landing) in enumerate(((ride_a, half_a), (ride_b, half_b)))
    ]
    for start, _, _ in ride:
        start(EARLY)
    lanes = features // 128
    lead, tile, taps = 8, 512, 5
    grad[...] = b16(stream_ref[...])
    gain = vector_row(pack, 3)
    sums_ref[...] = jnp.zeros_like(sums_ref)
    for n in range(features // tile):
        cols = slice(n * tile, (n + 1) * tile)
        value = dot_back(grad[...], w_out[cols, :]) * f32(slope[:, cols])
        normed[:, cols] = value
        for at, total in (
            (0, jnp.sum(value, axis=0, keepdims=True)),
            (lanes, jnp.sum(value * scaled_ref[:, cols], axis=0, keepdims=True)),
        ):
            for i in range(tile // 128):
                row = at + n * (tile // 128) + i
                source[row : row + 1, :] = total[:, i * 128 : (i + 1) * 128]

    def meanwhile():
        @tiles(features, 256)
        def _(cols):
            gw_out[cols, :] = b16(dot_over(act[:, cols], grad[...]))

        sums_ref[4:5, :] = jnp.sum(f32(grad[...]), axis=0, keepdims=True)

    sums = everywhere(links, nb, source, mid, land_s, land_b, None, meanwhile, (ss, rs, sb, rb))
    beta, gamma = unpack_rows(sums, 0, lanes), unpack_rows(sums, lanes, lanes)
    for p in range(EARLY + 1, pieces):
        for start, _, _ in ride:
            start(p)
    sums_ref[5:6, :] = gamma
    sums_ref[6:7, :] = beta
    inverse, frames = stats[0:1, :], stats[1:2, 0:1]
    live = f32(pack[links.shard, 27:28, 0:1])
    mask = f32(f32(lax.broadcasted_iota(jnp.int32, (rows, 1), 0)) < live)
    padded[0:lead, :] = jnp.zeros((lead, features), jnp.float32)
    padded[lead + rows :, :] = jnp.zeros((lead, features), jnp.float32)
    padded[lead : lead + rows, :] = inverse * (
        normed[...] * gain - mask * (gain * beta + scaled_ref[...] * (gain * gamma)) / frames
    )
    given = 0.0
    gated = f32(gated_ref[...])
    for k in range(taps):
        at = lead + (taps - 1) // 2 - k
        moved = padded[at : at + rows, :]
        given = given + moved * vector_row(pack, 22 + k)
        sums_ref[8 + k : 9 + k, :] = jnp.sum(moved * gated, axis=0, keepdims=True)
    left = b16(given * f32(open_ref[...]))
    right = b16(given * f32(gate_ref[...]))
    inner[:, 0:features] = left
    inner[:, features:] = right
    sums_ref[2:3, :] = jnp.sum(f32(left), axis=0, keepdims=True)
    sums_ref[3:4, :] = jnp.sum(f32(right), axis=0, keepdims=True)
    loads.need(0)
    total = dot_back(inner[...], w_in[...])
    scaled, inverse = norm_parts(rows_ref[...])
    out_ref[...] = stream_ref[...] + norm_slope(total, scaled, inverse, vector_row(pack, 2))
    sums_ref[0:1, :] = jnp.sum(total * scaled, axis=0, keepdims=True)
    sums_ref[1:2, :] = jnp.sum(total, axis=0, keepdims=True)

    @tiles(2 * features, 512)
    def _(cols):
        gw_in[:, cols] = b16(dot_over(hid[...], inner[:, cols]))

    loads.need(1, 2)
    for (_, settle, _), own, landing, early in zip(ride, (kept_a, kept_b), (half_a, half_b), (early_a, early_b)):
        settle()
        done = early.shape[0]
        landing[0:done] = b16(f32(own[0:done]) + f32(early[...]))
        landing[done:] = b16(f32(own[done:]) + f32(landing[done:]))


def conv_back(stream, rows_in, pack, w_in, w_out, saved, ridden, early, ident):
    ns, nb = lax.axis_size("shard"), lax.axis_size("batch")
    rows, features = rows_in.shape
    shape = jax.ShapeDtypeStruct
    low, full = jnp.bfloat16, jnp.float32
    small = (2 * features // 128, 128)
    return pl.pallas_call(
        functools.partial(conv_back_body, nb),
        out_shape=[
            shape((rows, features), full), shape((features, features), low),
            shape((features, 2 * features), low), shape((16, features), full),
        ]
        + [shape((r.shape[0] // 2, r.shape[1]), low) for r in ridden],
        in_specs=[VMEM_SPEC] * 14 + [HBM_SPEC] * 3,
        out_specs=[VMEM_SPEC] * 6,
        scratch_shapes=[
            pltpu.VMEM((rows + 16, features), full), pltpu.VMEM((rows, features), full),
            pltpu.VMEM((rows, features), low), pltpu.VMEM((rows, 2 * features), low),
            pltpu.VMEM(small, full), pltpu.VMEM(small, full),
            pltpu.VMEM((ns,) + small, full), pltpu.VMEM((nb,) + small, full),
            pltpu.SemaphoreType.DMA((ns,)), pltpu.SemaphoreType.DMA((ns,)),
            pltpu.SemaphoreType.DMA((nb,)), pltpu.SemaphoreType.DMA((nb,)),
        ]
        + link_scratch(8, 1)[:2]
        + [pltpu.VMEM(w_in.shape, low)]
        + [pltpu.VMEM((r.shape[0] // 2, r.shape[1]), low) for r in ridden]
        + [pltpu.SemaphoreType.DMA((3,))],
        compiler_params=pltpu.CompilerParams(
            collective_id=ident, has_side_effects=True, vmem_limit_bytes=60 << 20
        ),
        name="conv_back",
    )(stream, rows_in, pack, w_out, *saved, *early, w_in, *ridden)


def rear_body(
    heads, size, nb, stream_ref, rows_ref, pack, w_mine, ride_a, ride_b,
    hid_b_hbm, with_u_hbm, with_v_hbm, key_hbm, value_hbm, soft_hbm, mix_hbm, table_hbm, proj_hbm, w_qkv_hbm,
    start_hbm, hid_hbm, act_hbm, slope_hbm, w_rows_hbm, ffn_in,
    out_ref, gw_q, gw_k, gw_x, gw_pos, gw_mix, mix_sums, own_sums, gw_in, gw_out, sums_ref, out_a, out_b,
    grad, dq, dk, dx, dp, stream, grad_b, inner, start, hid, act, slope, w_rows, w_in,
    hid_b, with_u, with_v, key, value, soft_ref, mix, table, proj, w_qkv, *refs,
):
    first, second, refs = refs[:5], refs[5:10], refs[10:]
    send_sem, recv_sem, ride_send, ride_recv, load_sem, *between = refs
    links = Links(send_sem, recv_sem)
    batch = lax.axis_index("batch")
    loads = Loads(
        load_sem,
        [
            (soft_hbm, soft_ref), (value_hbm, value), (key_hbm, key), (with_u_hbm, with_u), (with_v_hbm, with_v),
            (proj_hbm, proj), (w_qkv_hbm, w_qkv), (hid_b_hbm, hid_b), (mix_hbm, mix), (table_hbm, table),
            (slope_hbm, slope), (w_rows_hbm, w_rows), (ffn_in.at[0], w_in), (act_hbm, act), (hid_hbm, hid),
            (start_hbm, start),
        ],
    )
    orders = ride_orders(nb)
    steps = len(orders[0]) - 1
    scale = 1.0 / math.sqrt(size)
    rows, features = rows_ref.shape
    half = rows // 2
    links.greet([links.near, links.far] + [{"batch": flip_bits(batch, 1 << k)} for k in orders[0]])
    inward, outward = [], []
    count = 2 * steps - 1
    for at, (begin, end) in enumerate(((ride_a, out_a), (ride_b, out_b))):
        middle_refs = between[at * count : (at + 1) * count]
        down_refs = [begin, *middle_refs[:steps]]
        up_refs = [*middle_refs[steps - 1 :], end]
        rider = Rider(batch, ride_send, ride_recv, at * 2 * steps)
        inward.append(rider.chain(down_refs, orders[at][1:], rider.halve))
        rider = Rider(batch, ride_send, ride_recv, at * 2 * steps + steps)
        outward.append(rider.chain(up_refs, orders[at][:0:-1], rider.double))

    def tick(chains):
        for chain in chains:
            if chain:
                chain.pop(0)()

    tick(inward)
    grad[0] = b16(stream_ref[...])
    out = [
        links.go(grad.at[0, pl.ds(h * half, half)], grad.at[2, pl.ds(h * half, half)], links.far)
        for h in range(2)
    ]
    near = links.go(grad.at[0], grad.at[1], links.near)
    at_row = lax.broadcasted_iota(jnp.int32, (rows, rows), 0)
    at_col = lax.broadcasted_iota(jnp.int32, (rows, rows), 1)
    flip = b16(f32(at_row + at_col == rows - 1))
    keys = f32(at_col)
    own_sums[...] = jnp.zeros_like(own_sums)

    def work(slot, emit):
        mixed = b16(dot_back(grad[slot], w_mine[...]))
        live = f32(pack[flip_bits(links.shard, slot), 27:28, 0:1])
        for h in range(heads):
            cols = slice(h * size, (h + 1) * size)
            soft = soft_ref[slot, :, h * rows : (h + 1) * rows]
            given = mixed[:, cols]
            grad_soft = dot_back(given, value[slot, :, cols])
            dx[slot, :, cols] = b16(dot_over(b16(soft), given))
            grad_scores = soft * (grad_soft - jnp.sum(grad_soft * soft, axis=-1, keepdims=True))
            raw = b16(jnp.where(keys < live, grad_scores, 0.0) * scale)
            grad_u = dot_rows(raw, key[slot, :, cols])
            dk[slot, :, cols] = b16(dot_over(raw, with_u[slot, :, cols]))
            turned = dot_rows(flip, raw)
            wide = jnp.concatenate([turned, jnp.zeros_like(turned)], 1)
            wide = b16(pltpu.roll(wide, 0, 1, stride=1, stride_axis=0))
            grad_v = dot_rows(wide, proj[:, cols])
            v_turned = b16(dot_rows(flip, with_v[slot, :, cols]))
            dp[slot, :, cols] = b16(dot_over(wide, v_turned))
            own_sums[2:3, cols] += column_sum(grad_u)
            own_sums[3:4, cols] += column_sum(grad_v)
            high = b16(grad_v)
            rest = b16(grad_v - f32(high))
            dq[slot, :, cols] = b16(grad_u + (dot_rows(flip, high) + dot_rows(flip, rest)))
        own_sums[0:1, :] += column_sum(f32(dq[slot]))
        own_sums[1:2, :] += column_sum(f32(dx[slot]))

        @tiles(features, 512)
        def _(cols):
            emit(
                cols,
                dot_back(dq[slot], w_qkv[0, cols, :])
                + dot_back(dk[slot], w_qkv[1, cols, :])
                + dot_back(dx[slot], w_qkv[2, cols, :]),
            )

    sums = Sums(links, first)
    loads.need(*range(7))
    work(0, sums.keep)
    near.wait()
    work(1, sums.give)
    sums.send_near()
    tick(inward)
    on = []
    for h in range(2):
        out[h].wait()
        there = pl.ds(h * half, half)
        on.append(links.go(grad.at[2, there], grad.at[3, there], links.near))
    for copy in on:
        copy.wait()
    work(3, sums.give_far)
    for h in range(2):
        sums.send_back(h)
    work(2, sums.keep_far)
    for h in range(2):
        sums.send_cross(h)
    loads.need(7, 8, 9)
    for ref, target in ((dq, gw_q), (dk, gw_k), (dx, gw_x)):
        right = flat(ref)

        @tiles(features, 256)
        def _(cols, target=target, right=right):
            target[cols, :] = b16(dot_over(flat_columns(hid_b, cols, 256), right))

    @tiles(features, 256)
    def _(cols):
        total = dot_over(table[:, cols], dp[0])
        for slot in range(1, 4):
            total = total + dot_over(table[:, cols], dp[slot])
        gw_pos[cols, :] = b16(total)

    gw_mix[...] = b16(dot_over(flat(mix), flat(grad)))
    mix_sums[...] = jnp.zeros_like(mix_sums)
    mix_sums[2:3, :] = column_sum(f32(grad[0]))
    gain = vector_row(pack, 1)

    def fill(h):
        at = slice(h * half, (h + 1) * half)
        given = sums.arrive(h)
        scaled, inverse = norm_parts(rows_ref[at])
        slide = stream_ref[at] + norm_slope(given, scaled, inverse, gain)
        stream[at] = slide
        grad_b[0, at] = b16(0.5 * slide)
        mix_sums[0:1, :] += column_sum(given * scaled)
        mix_sums[1:2, :] += column_sum(given)

    step = ffn_inward(grad_b, inner, slope, w_in, w_rows)

    def back_work(block, emit):
        loads.need(10, 11, 12)
        if block == 1:
            for chain in inward:
                while chain:
                    chain.pop(0)()
            tick(outward)
        step(block, emit)

    back = gather_work_scatter(links, grad_b, fill, back_work, second)
    loads.need(13, 14, 15)
    weight_out(act, grad_b, gw_out)
    tick(outward)
    weight_in(hid, inner, gw_in, sums_ref)
    sums_ref[0:3, :] = jnp.zeros((3, features), jnp.float32)
    sums_ref[2:3, :] = column_sum(f32(grad_b[0]))
    sums_ref[4:8, :] = jnp.zeros((4, features), jnp.float32)
    gain = vector_row(pack, 0)
    for h in range(2):
        at = slice(h * half, (h + 1) * half)
        scaled, inverse = norm_parts(start[at])
        given = back.arrive(h)
        out_ref[at] = stream[at] + norm_slope(given, scaled, inverse, gain)
        sums_ref[0:1, :] += column_sum(given * scaled)
        sums_ref[1:2, :] += column_sum(given)
    for chain in outward:
        while chain:
            chain.pop(0)()


def rear(stream, rows_one, pack, saved_mix, table, proj, w_qkv, w_mine, ridden, rows_in, saved, w_rows, ffn_in, heads, ident):
    rows, features = rows_one.shape
    hidden = ffn_in.shape[2]
    width = proj.shape[1]
    nb = lax.axis_size("batch")
    steps = nb.bit_length() - 2
    low, full = jnp.bfloat16, jnp.float32
    shape, vmem = jax.ShapeDtypeStruct, pltpu.VMEM
    dma = pltpu.SemaphoreType.DMA
    narrow = vmem((4, rows, width), low)
    between = []
    for r in ridden:
        sizes = [r.shape[0] >> k for k in range(1, steps + 1)]
        between += [vmem((size, r.shape[1]), low) for size in sizes + sizes[-2::-1]]
    return pl.pallas_call(
        functools.partial(rear_body, heads, width // heads, nb),
        out_shape=[
            shape((rows, features), full),
            shape((features, width), low), shape((features, width), low), shape((features, width), low),
            shape((features, width), low),
            shape((width, features), low), shape((8, features), full), shape((8, width), full),
            shape((features, hidden), low), shape((hidden, features), low), shape((8, features), full),
        ]
        + [shape(r.shape, low) for r in ridden],
        in_specs=[VMEM_SPEC] * 6 + [HBM_SPEC] * 16,
        out_specs=[VMEM_SPEC] * 13,
        scratch_shapes=[
            vmem((4, rows, features), low), narrow, narrow, narrow, vmem((4, 2 * rows, width), low),
            vmem((rows, features), full), vmem((4, rows, features), low), vmem((4, rows, hidden), low),
            vmem((rows, features), full), vmem((4, rows, features), low), vmem((4, rows, hidden), low),
            vmem((4, rows, hidden), low), vmem((hidden, features), low), vmem((features, hidden), low),
        ]
        + [vmem(a.shape, a.dtype) for a in (*saved_mix, table, proj, w_qkv)]
        + sums_scratch(rows, features)
        + sums_scratch(rows, features)
        + [dma((24,)), dma((24,)), dma((4 * steps,)), dma((4 * steps,)), dma((16,))]
        + between,
        compiler_params=pltpu.CompilerParams(
            collective_id=ident, has_side_effects=True, vmem_limit_bytes=62 << 20
        ),
        name="rear",
    )(
        stream, rows_one, pack, w_mine, *ridden, *saved_mix, table, proj, w_qkv, rows_in, *saved, w_rows, ffn_in
    )


def body(
    tokens, cotangent, lengths, ffn_in, ffn_out, ffn_bias, qkv_proj, pos_proj, out_proj,
    conv_in, conv_out, depthwise, norm_gains, biases,
):
    _, length, features = tokens.shape
    ns, nb = lax.axis_size("shard"), lax.axis_size("batch")
    width = features // ns
    heads = HEADS // ns
    rows_in = tokens[0]

    rates = jnp.exp(
        jnp.arange(features // 2, dtype=jnp.float32) * (-2.0 * math.log(10000.0) / features)
    )
    turns = jnp.concatenate(
        [
            length - 1.0 - jnp.arange(16, dtype=jnp.float32),
            -16.0 * jnp.arange(2 * length // 16, dtype=jnp.float32),
        ]
    )
    angles = turns[:, None] * rates[None, :]
    base = jnp.concatenate([jnp.sin(angles), jnp.cos(angles)], 1)
    (
        rows_one, rows_two, pack, table, proj, with_u, with_v, key, value, mix, wc_in, w_mine, wc_out,
        w_rows_two, *saved_one, w_rows_one, hidden_mix, soft,
    ) = front(
        rows_in, norm_gains, biases, depthwise, lengths, ffn_bias, base, pos_proj, qkv_proj, ffn_in, ffn_out, out_proj, conv_in, conv_out,
        heads, 5,
    )
    saved_mix = (hidden_mix, with_u, with_v, key, value, soft, mix)
    rows_three, *saved_conv = conv_forward(
        rows_two, pack, wc_in, wc_out, 10
    )
    result, stream, two_in, two_out, two_sums, *early = middle(
        rows_three, pack, ffn_bias, w_rows_two, cotangent[0], ffn_in, 6
    )

    stream, grad_conv_out, grad_conv_in, conv_sums, *ridden = conv_back(
        stream, rows_two, pack, wc_in, wc_out, saved_conv, (two_in, two_out), early, 11
    )
    stream, grad_q, grad_k, grad_x, grad_pos, grad_out, mix_sums, own_sums, one_in, one_out, one_sums, *ridden = rear(
        stream, rows_one, pack, saved_mix, table, proj, qkv_proj, w_mine, ridden, rows_in, saved_one, w_rows_one,
        ffn_in, heads, 12
    )
    tall, deep = one_in.shape
    piece = max(128, 8 * nb)
    *sums, out_gains, out_biases, out_taps, out_hidden = tail_sum(
        [grad_out, one_out, one_in, grad_q, grad_k, grad_x, grad_pos, grad_conv_in, grad_conv_out],
        ridden,
        [one_sums, mix_sums, two_sums, conv_sums, own_sums],
        [("turn", 4, None), ("turn", 1, 0), ("plain", 0, 0)]
        + [("plain", 2, at) for at in range(3)]
        + [("plain", 3, None), ("gather", 5, None), ("gather", 6, None)],
        [
            (2, tall, deep), (2, ns * deep, width), (3, tall, width), (tall, width), (tall, width),
            (tall, 2 * width), (tall, width),
        ],
        ["near", "line"],
        [width, piece, piece] + [min(tall, 4 * piece)] * 4 + [2 * piece, min(tall, 4 * piece)],
        deep,
        4,
    )
    *sums, result, stream, out_gains, out_biases, out_taps, out_hidden = widen(
        sums, [result, stream, out_gains, out_biases, out_taps, out_hidden]
    )
    return (
        result[None],
        stream[None],
        sums[0],
        sums[1],
        out_hidden,
        sums[2],
        sums[3],
        sums[4],
        sums[5],
        sums[6],
        out_taps,
        out_gains,
        out_biases,
    )


def solution(mesh):
    rows = P(("batch", "shard"), None, None)
    cube, flat = P(None, None, "shard"), P(None, "shard")
    return jax.shard_map(
        body,
        mesh=mesh,
        in_specs=(rows, rows, P(("batch", "shard")), cube, cube, flat, cube)
        + (flat,) * 7,
        out_specs=(rows, rows, cube, cube, flat, cube) + (flat,) * 7,
        check_vma=False,
    )
```

```python
import functools
import math

import jax
import jax.numpy as jnp
from jax import lax
from jax.experimental import pallas as pl
from jax.experimental.pallas import tpu as pltpu
from jax.sharding import PartitionSpec as P

HEADS = 8
MESH = pl.DeviceIdType.MESH
VMEM_SPEC = pl.BlockSpec(memory_space=pltpu.VMEM)
HBM_SPEC = pl.BlockSpec(memory_space=pltpu.HBM)
epsilon = 1e-05


def f32(a):
    return a.astype(jnp.float32)


def b16(a):
    return a.astype(jnp.bfloat16)


def norm_rows(values_in, gain_row, bias_row):
    row_mean = jnp.mean(values_in, axis=-1, keepdims=True)
    centered = values_in - row_mean
    spread = jnp.mean(centered * centered, axis=-1, keepdims=True)
    return centered * lax.rsqrt(spread + epsilon) * gain_row + bias_row


def dot_rows(a, b):
    return jnp.dot(a, b, preferred_element_type=jnp.float32)


def dot_back(a, b):
    return lax.dot_general(a, b, (((1,), (1,)), ((), ())), preferred_element_type=jnp.float32)


def dot_over(a, b):
    return lax.dot_general(a, b, (((0,), (0,)), ((), ())), preferred_element_type=jnp.float32)


def exchange(axis, index, count, source, landing, send_sem, recv_sem):
    copies = []
    for j in range(1, count):
        peer = lax.rem(index + j, count)
        copies.append(
            pltpu.make_async_remote_copy(
                src_ref=source,
                dst_ref=landing.at[index],
                send_sem=send_sem.at[j],
                recv_sem=recv_sem.at[j],
                device_id={axis: peer},
                device_id_type=MESH,
            )
        )
    return copies


def sum_slots(ref, count):
    total = ref[0]
    for j in range(1, count):
        total = total + ref[j]
    return total


class Loads:
    def __init__(self, sem, pairs):
        self.open = []
        for at, (src, dst) in enumerate(pairs):
            copy = pltpu.make_async_copy(src, dst, sem.at[at])
            copy.start()
            self.open.append(copy)

    def need(self, *which):
        for at in which:
            if self.open[at] is not None:
                self.open[at].wait()
                self.open[at] = None


class Flush:
    def __init__(self, sem):
        self.sem, self.open = sem, []

    def go(self, src, dst):
        copy = pltpu.make_async_copy(src, dst, self.sem.at[len(self.open)])
        copy.start()
        self.open.append(copy)

    def settle(self):
        for copy in self.open:
            copy.wait()


class Chunk:
    def __init__(self, at, source, row, rows, columns, first, count):
        self.at, self.source, self.row, self.rows, self.columns = at, source, row, rows, columns
        extra = [(1 << k, k) for k in range(3, count.bit_length() - 1)]
        line = (6, 1)
        self.halved = first == "half"
        if first == "near":
            self.pre, self.post = [(1, 0)], [line] + extra
        elif self.halved:
            self.pre, self.post = [], [line] + extra
        else:
            self.pre, self.post = [], [line, (1, 0)] + extra
        size, self.landings = rows, []
        for _ in self.pre:
            size //= 2
            self.landings.append((size, columns))
        self.landings.append((size, columns))
        for _ in self.post:
            size //= 2
            self.landings.append((size, columns))
        self.steps = len(self.landings)


def bit_of(value, k):
    return lax.rem(lax.div(value, 1 << k), 2)


def flip_bits(value, mask):
    out = value
    k = 0
    while (1 << k) <= mask:
        if mask & (1 << k):
            out = out + (1 - 2 * bit_of(value, k)) * (1 << k)
        k += 1
    return out


class Mover:
    def __init__(self, chunk, batch, source, base, held, landings, sems, finish, early):
        self.c, self.b = chunk, batch
        self.source, self.base, self.held, self.landings, self.sems = source, base, held, landings, sems
        lo, hi = bit_of(batch, 1), bit_of(batch, 2)
        self.inner = lo != hi
        self.ended = lo == hi
        self.finish, self.early = finish, early
        self.build()

    def copy(self, at, src, dst, mask):
        send, recv = self.sems
        return pltpu.make_async_remote_copy(
            src_ref=src,
            dst_ref=dst,
            send_sem=send.at[self.c.at, at],
            recv_sem=recv.at[self.c.at, at],
            device_id={"batch": flip_bits(self.b, mask)},
            device_id_type=MESH,
        )

    def build(self):
        c = self.c
        held = self.held
        here, base = self.source, self.base
        off, size, step = 0, c.rows, 0
        plan, trail = [], []
        if c.halved:
            trail.append(("all", 1, off, size))
        sequence = [("all",) + p for p in c.pre] + [("fold", 2, None)]
        sequence += [("inner",) + p for p in c.post]
        for kind, mask, sel in sequence:
            landing = self.landings[step]
            if kind == "fold":
                own = row_view(here, base, size)
                cp = self.copy(step, own, landing, mask)
            else:
                size //= 2
                mine = bit_of(self.b, sel)
                cp = self.copy(step, row_view(here, base + (1 - mine) * size, size), landing, mask)
                own = row_view(here, base + mine * size, size)
                off = off + mine * size
            trail.append((kind, mask, off, size))
            step += 1
            out = landing if step < len(sequence) else held(off, size)
            plan.append((kind, cp, (own, landing, out)))
            here, base = landing, 0
        for kind, mask, off, size in reversed(trail):
            cp = self.copy(step, held(off, size), held(off, size), mask)
            plan.append(("unfold" if kind == "fold" else kind, cp, None))
            step += 1
        self.plan = plan
        self.depth = len(plan) + len(self.early)

    def begin(self, k):
        kind, cp, _ = self.plan[k]
        if kind == "all":
            cp.start()
        elif kind == "fold":
            pl.when(self.ended)(cp.start)
        else:
            pl.when(self.inner)(cp.start)

    def end(self, k):
        kind, cp, add = self.plan[k]

        def gather():
            if add is not None:
                own, landing, out = add
                out[...] = b16(f32(own[...]) + f32(landing[...]))

        if kind == "all":
            cp.wait()
            gather()
        elif kind in ("fold", "unfold"):
            sender, taker = (
                (self.ended, self.inner) if kind == "fold" else (self.inner, self.ended)
            )
            pl.when(sender)(cp.wait_send)

            @pl.when(taker)
            def _():
                cp.wait_recv()
                gather()
        else:

            @pl.when(self.inner)
            def _():
                cp.wait()
                gather()

    def advance(self, k):
        if k < len(self.early):
            self.early[k]()
            return
        k -= len(self.early)
        if k > 0:
            self.end(k - 1)
        elif self.early:
            self.settle_early()
        if k < len(self.plan):
            self.begin(k)
        else:
            self.finish(self.c)


def row_view(ref, start, size):
    start = start if isinstance(start, int) else pl.multiple_of(start, 16 if size % 16 == 0 else 8)
    return ref.at[pl.ds(start, size)]


def column_block(index, columns):
    return pl.ds(pl.multiple_of(index * columns, 128), columns)


class Rider:
    def __init__(self, batch, send, recv, first):
        self.b, self.send, self.recv, self.at = batch, send, recv, first

    def go(self, src, dst, bit):
        copy = pltpu.make_async_remote_copy(
            src_ref=src, dst_ref=dst, send_sem=self.send.at[self.at], recv_sem=self.recv.at[self.at],
            device_id={"batch": flip_bits(self.b, 1 << bit)}, device_id_type=MESH,
        )
        self.at += 1
        copy.start()
        return copy

    def halve_pieces(self, source, landing, bit, pieces, half):
        size = half // pieces
        mine = bit_of(self.b, bit)
        copies = []

        def start(p):
            copies.append(
                self.go(
                    row_view(source, (1 - mine) * half + p * size, size), row_view(landing, p * size, size), bit
                )
            )

        def settle():
            for copy in copies:
                copy.wait()

        return start, settle, row_view(source, mine * half, half)

    def halve(self, source, landing, bit):
        half = landing.shape[0]
        mine = bit_of(self.b, bit)
        copy = self.go(row_view(source, (1 - mine) * half, half), landing, bit)

        def end():
            copy.wait()
            own = row_view(source, mine * half, half)
            landing[...] = b16(f32(own[...]) + f32(landing[...]))

        return end

    def double(self, source, target, bit):
        half = source.shape[0]
        there = row_view(target, bit_of(self.b, bit) * half, half)
        copy = self.go(source, there, bit)
        there[...] = source[...]
        return copy.wait

    def chain(self, refs, bits, move):
        ends, stages = [], []
        for i, bit in enumerate(bits):

            def stage(i=i, bit=bit):
                if ends:
                    ends.pop()()
                ends.append(move(refs[i], refs[i + 1], bit))

            stages.append(stage)
        stages.append(lambda: ends.pop()())
        return stages


def ride_orders(count):
    bits = list(range(count.bit_length() - 1))
    return bits, [1, 0] + bits[2:]


def tail_body(specs, chunks, ns, nb, n_in, n_out, *refs):
    (one_sums, mix_sums, two_sums, conv_sums, own_sums), refs = refs[:5], refs[5:]
    given, refs = refs[: n_in + 2], refs[n_in + 2 :]
    outs_hbm, refs = refs[:n_out], refs[n_out:]
    (o_gains, o_biases, o_taps, o_hidden), refs = refs[:4], refs[4:]
    send, recv, turn_send, turn_recv, pre_send, pre_recv, ride_send, ride_recv = refs[:8]
    ss, rs, sb, rb, wide, land_s, mid, land_b, ride_fin, load_sem = refs[8:18]
    shard, batch = lax.axis_index("shard"), lax.axis_index("batch")
    flush = Flush(refs[18])
    outs = refs[19 : 19 + n_out]
    rest = list(refs[19 + n_out :])
    pairs, ins, blocks = [], [], {}
    for i, ref in enumerate(given):
        if i < n_in and specs["arrays"][i][0] == "gather":
            pair = []
            for index in (shard, flip_bits(shard, 2)):
                held_block = rest.pop(0)
                pairs.append((ref.at[:, column_block(index, held_block.shape[1])], held_block))
                pair.append(held_block)
            blocks[i] = (pair, (len(pairs) - 2, len(pairs) - 1))
            ins.append(ref)
        else:
            held_ref = rest.pop(0)
            pairs.append((ref, held_ref))
            blocks[i] = (None, (len(pairs) - 1,))
            ins.append(held_ref)
    loads = Loads(load_sem, pairs)
    ins, ridden = ins[:n_in], ins[n_in:]
    shard, batch = lax.axis_index("shard"), lax.axis_index("batch")
    barrier = pltpu.get_barrier_semaphore()
    greeted = [{"batch": lax.rem(batch + j, nb)} for j in range(1, nb)]
    greeted += [{"shard": flip_bits(shard, m)} for m in range(1, ns)]
    for device in greeted:
        pl.semaphore_signal(barrier, inc=1, device_id=device, device_id_type=MESH)
    width = own_sums.shape[1]
    for t in range(ns):
        cols = slice(t * width, (t + 1) * width)
        wide[t, 0:3, :] = one_sums[0:3, cols]
        wide[t, 3:6, :] = mix_sums[0:3, cols]
        wide[t, 6:9, :] = two_sums[0:3, cols]
        wide[t, 9:14, :] = conv_sums[0:5, cols]
        wide[t, 14:19, :] = conv_sums[8:13, cols]
        wide[t, 19:21, :] = two_sums[4:6, cols]
        wide[t, 21:24, :] = jnp.zeros((3, width), jnp.float32)
    pl.semaphore_wait(barrier, len(greeted))

    vector_copies = []
    for j in range(1, ns):
        peer = lax.rem(shard + j, ns)
        copy = pltpu.make_async_remote_copy(
            src_ref=wide.at[peer], dst_ref=land_s.at[shard], send_sem=ss.at[j], recv_sem=rs.at[j],
            device_id={"shard": peer}, device_id_type=MESH,
        )
        copy.start()
        vector_copies.append(copy)
    land_s[shard] = wide[shard]

    def vectors_on():
        for copy in vector_copies:
            copy.wait()
        mid[0:24, :] = sum_slots(land_s, ns)
        mid[24:28, :] = own_sums[0:4, :]
        per = one_sums.shape[1] // width
        for t in range(per):
            cols = slice(t * width, (t + 1) * width)
            mid[28 + t : 29 + t, :] = one_sums[3:4, cols]
            mid[28 + per + t : 29 + per + t, :] = two_sums[3:4, cols]
        mid[28 + 2 * per :, :] = jnp.zeros((mid.shape[0] - 28 - 2 * per, width), jnp.float32)
        vector_copies[:] = exchange("batch", batch, nb, mid, land_b, sb, rb)
        for copy in vector_copies:
            copy.start()
        land_b[batch] = mid[...]

    def vectors_out():
        for copy in vector_copies:
            copy.wait()
        vec = sum_slots(land_b, nb)
        row = lambda k: vec[k : k + 1]
        mine = conv_sums[5:7, column_block(shard, width)]
        gains = [row(0), row(3), row(9), mine[0:1], row(6), row(19)]
        order = [1, 2, 4, 24, 25, 5, 26, 27, 10, 11, 12, None, 13, 7, 8, 20]
        for k, value in enumerate(gains):
            o_gains[k : k + 1, :] = value
        for k, at in enumerate(order):
            o_biases[k : k + 1, :] = mine[1:2] if at is None else row(at)
        o_taps[...] = vec[14:19]
        per = o_hidden.shape[1] // width
        for k in range(2):
            for t in range(per):
                at = 28 + k * per + t
                o_hidden[k : k + 1, t * width : (t + 1) * width] = row(at)

    late = []

    def leave(out, lead, start, rows):
        src, dst = outs[out], outs_hbm[out]
        if lead is not None:
            src, dst = src.at[lead], dst.at[lead]
        flush.go(src.at[pl.ds(start, rows)], dst.at[pl.ds(start, rows)])

    def turn(c_at, total, row, rows, out, lead):
        target = outs[out] if lead is None else outs[out].at[lead]
        columns = target.shape[1]
        height = target.shape[0] // ns
        there = row_view(target, shard * height + row, rows)
        copies = []
        for j in range(1, ns):
            peer = flip_bits(shard, j)
            copy = pltpu.make_async_remote_copy(
                src_ref=total.at[:, column_block(peer, columns)],
                dst_ref=there,
                send_sem=turn_send.at[c_at, j],
                recv_sem=turn_recv.at[c_at, j],
                device_id={"shard": peer},
                device_id_type=MESH,
            )
            copy.start()
            copies.append(copy)
        there[...] = total[:, column_block(shard, columns)]

        def after():
            for copy in copies:
                copy.wait()
            for t in range(ns):
                leave(out, lead, t * height + row, rows)

        late.append(after)

    rides = []
    orders = ride_orders(nb)
    plain_target = outs[0].at[1]
    rider_a = Rider(batch, ride_send, ride_recv, 0)
    rider_b = Rider(batch, ride_send, ride_recv, 1)
    loads.need(*blocks[n_in][1], *blocks[n_in + 1][1])
    end_a = rider_a.double(ridden[0], plain_target, orders[0][0])
    end_b = rider_b.double(ridden[1], ride_fin, orders[1][0])

    movers = []
    for c in chunks:
        kind, out, lead = specs["arrays"][c.source]
        source, base, early, settle = ins[c.source], c.row, [], None
        if kind == "gather":
            near_land, far_land = rest.pop(0), rest.pop(0)
            whole, columns, rows = ins[c.source], c.columns, pl.ds(c.row, c.rows)
            own_block, far_block = blocks[c.source][0]
            state = {}

            def pre(at, src, dst, mask, c=c):
                copy = pltpu.make_async_remote_copy(
                    src_ref=src, dst_ref=dst, send_sem=pre_send.at[c.at, at], recv_sem=pre_recv.at[c.at, at],
                    device_id={"shard": flip_bits(shard, mask)}, device_id_type=MESH,
                )
                copy.start()
                return copy

            def first(near_land=near_land, whole=whole, columns=columns, rows=rows, state=state, pre=pre):
                state["n"] = [
                    pre(i, whole.at[rows, column_block(flip_bits(shard, m), columns)], near_land.at[i], 1)
                    for i, m in enumerate((1, 3))
                ]

            def second(
                near_land=near_land, far_land=far_land, far_block=far_block, rows=rows, state=state, pre=pre,
            ):
                for copy in state["n"]:
                    copy.wait()
                near_land[1] = b16(f32(near_land[1]) + f32(far_block[rows]))
                state["f"] = pre(2, near_land.at[1], far_land, 2)

            def settle(
                near_land=near_land, far_land=far_land, own_block=own_block, rows=rows, state=state,
            ):
                state["f"].wait()
                far_land[...] = b16(
                    f32(far_land[...]) + f32(near_land[0]) + f32(own_block[rows])
                )

            early = [first, second]
            source, base = far_land, 0
        if kind == "turn":
            total = rest.pop(0)
            held = lambda off, size, total=total: row_view(total, off, size)

            def finish(c, total=total, out=out, lead=lead):
                turn(c.at, total, c.row, c.rows, out, lead)
        else:
            target = outs[out] if lead is None else outs[out].at[lead]
            held = lambda off, size, target=target, c=c: row_view(target, c.row + off, size)

            def finish(c, out=out, lead=lead):
                leave(out, lead, c.row, c.rows)

            if c.halved:
                apart = outs[out].shape[-2] // 2
                mine = bit_of(batch, 0) * apart
                held = lambda off, size, target=target, c=c, mine=mine: row_view(target, mine + c.row + off, size)

                def finish(c, out=out, lead=lead, apart=apart):
                    leave(out, lead, c.row, c.rows)
                    leave(out, lead, apart + c.row, c.rows)
        landings = [rest.pop(0) for _ in range(c.steps)]
        m = Mover(c, batch, source, base, held, landings, (send, recv), finish, early)
        m.settle_early = settle
        movers.append(m)
    starts, lag = [], specs["lag"]
    for i, m in enumerate(movers):
        starts.append(max(0, i // lag - len(m.early)))
    rounds = max(s + m.depth + 1 for s, m in zip(starts, movers))
    for r in range(rounds):
        ready, late[:] = late[:], []
        if r == 1:
            vectors_on()
        if r == 2:
            end_b()
            turn(len(chunks), ride_fin, 0, ride_fin.shape[0], 1, 1)
        if r == 3:
            vectors_out()
            end_a()
            leave(0, 1, 0, outs[0].shape[1])
        for s, m in zip(starts, movers):
            if 0 <= r - s <= m.depth:
                loads.need(*blocks[m.c.source][1])
                m.advance(r - s)
        for after in ready:
            after()
    for after in late:
        after()
    flush.settle()


def tail_sum(arrays, ridden, sums, kinds, outputs, firsts, chunk_rows, hidden, ident):
    ns, nb = lax.axis_size("shard"), lax.axis_size("batch")
    low, full = jnp.bfloat16, jnp.float32
    chunks = []
    for i, a in enumerate(arrays):
        step = chunk_rows[i]
        columns = a.shape[1] // ns if kinds[i][0] == "gather" else a.shape[1]
        for row in range(0, a.shape[0], step):
            first = "half" if kinds[i][0] == "half" else firsts[len(chunks) % len(firsts)]
            chunks.append(Chunk(len(chunks), i, row, step, columns, first, nb))
    depth = max(2 * c.steps + c.halved for c in chunks)
    specs = dict(arrays=kinds, lag=2)
    width = sums[-1].shape[1]
    per = hidden // width
    small = -(-(28 + 2 * per) // 8) * 8
    dma = pltpu.SemaphoreType.DMA
    n = len(chunks)
    scratch = [
        dma((n, depth)), dma((n, depth)), dma((n + 1, ns)), dma((n + 1, ns)), dma((n, 3)), dma((n, 3)),
        dma((2,)), dma((2,)), dma((ns,)), dma((ns,)), dma((nb,)), dma((nb,)),
        pltpu.VMEM((ns, 24, width), full), pltpu.VMEM((ns, 24, width), full),
        pltpu.VMEM((small, width), full), pltpu.VMEM((nb, small, width), full),
        pltpu.VMEM((2 * ridden[1].shape[0], ridden[1].shape[1]), low),
        dma((2 * len(arrays) + 2,)),
        dma(((ns + 1) * (n + 1) + 1,)),
    ]
    scratch += [pltpu.VMEM(o, low) for o in outputs]
    for i, a in enumerate(list(arrays) + list(ridden)):
        if i < len(arrays) and kinds[i][0] == "gather":
            scratch += [pltpu.VMEM((a.shape[0], a.shape[1] // ns), low)] * 2
        else:
            scratch.append(pltpu.VMEM(a.shape, low))
    for c in chunks:
        if kinds[c.source][0] == "gather":
            scratch += [pltpu.VMEM((2, c.rows, c.columns), low), pltpu.VMEM((c.rows, c.columns), low)]
        if kinds[c.source][0] == "turn":
            scratch.append(pltpu.VMEM((c.rows, c.columns), low))
        scratch += [pltpu.VMEM(shape, low) for shape in c.landings]
    shape = jax.ShapeDtypeStruct
    shapes = [shape(s, low) for s in outputs]
    shapes += [shape((6, width), full), shape((16, width), full), shape((5, width), full), shape((2, hidden), full)]
    operands = list(sums) + list(arrays) + list(ridden)
    return pl.pallas_call(
        functools.partial(tail_body, specs, chunks, ns, nb, len(arrays), len(outputs)),
        out_shape=shapes,
        in_specs=[VMEM_SPEC] * len(sums) + [HBM_SPEC] * (len(arrays) + 2),
        out_specs=[HBM_SPEC] * len(outputs) + [VMEM_SPEC] * 4,
        scratch_shapes=scratch,
        compiler_params=pltpu.CompilerParams(
            collective_id=ident, has_side_effects=True, vmem_limit_bytes=60 << 20
        ),
        name="tail_sum",
    )(*operands)


def widen_body(count, others, slots, *refs):
    n = count + others
    ins, outs = refs[:n], refs[n : 2 * n]
    stages, in_sem, out_sem, pass_sem = refs[2 * n : -3], refs[-3], refs[-2], refs[-1]
    passed = []
    for at in range(others):
        passed.append(pltpu.make_async_copy(ins[count + at], outs[count + at], pass_sem.at[at]))
        passed[-1].start()
    half = len(stages) // 2
    items, used = [], {}
    for src, dst in zip(ins[:count], outs[:count]):
        for lead in range(src.shape[0]) if len(src.shape) == 3 else [None]:
            source = src if lead is None else src.at[lead]
            target = dst if lead is None else dst.at[lead]
            rows, columns = source.shape
            kind = [k.shape[2] for k in stages[:half]].index(columns)
            size = stages[kind].shape[1]
            for row in range(0, rows, size):
                slot = used.get(kind, 0) % slots
                used[kind] = used.get(kind, 0) + 1
                items.append((source.at[pl.ds(row, size)], target.at[pl.ds(row, size)], kind, slot))
    items.sort(key=lambda item: item[2])
    loads, stores = {}, {}

    def load(i):
        if i < len(items):
            source, _, kind, slot = items[i]
            loads[i] = pltpu.make_async_copy(source, stages[kind].at[slot], in_sem.at[kind, slot])
            loads[i].start()

    ahead = slots - 1
    for i in range(ahead):
        load(i)
    for i, (_, target, kind, slot) in enumerate(items):
        loads[i].wait()
        if (kind, slot) in stores:
            stores.pop((kind, slot)).wait()
        narrow, wide = stages[kind].at[slot], stages[half + kind].at[slot]

        @pl.loop(0, narrow.shape[0] // 64)
        def _(k, narrow=narrow, wide=wide):
            part = pl.ds(pl.multiple_of(k * 64, 64), 64)
            wide[part] = f32(narrow[part])

        stores[kind, slot] = pltpu.make_async_copy(wide, target, out_sem.at[kind, slot])
        stores[kind, slot].start()
        load(i + ahead)
    for copy in list(stores.values()) + passed:
        copy.wait()


def widen(arrays, others):
    columns = sorted({a.shape[-1] for a in arrays})
    slots = 6
    least = lambda c: min([a.shape[-2] for a in arrays if a.shape[-1] == c] + [(256 * 1024) // c])
    stages = [pltpu.VMEM((slots, least(c), c), d) for d in (jnp.bfloat16, jnp.float32) for c in columns]
    dma = pltpu.SemaphoreType.DMA
    return pl.pallas_call(
        functools.partial(widen_body, len(arrays), len(others), slots),
        out_shape=[jax.ShapeDtypeStruct(a.shape, jnp.float32) for a in (*arrays, *others)],
        in_specs=[HBM_SPEC] * len(arrays) + [VMEM_SPEC] * len(others),
        out_specs=[HBM_SPEC] * (len(arrays) + len(others)),
        scratch_shapes=stages + [dma((len(columns), slots)), dma((len(columns), slots)), dma((len(others),))],
        compiler_params=pltpu.CompilerParams(vmem_limit_bytes=60 << 20),
        name="widen",
    )(*arrays, *others)


class Links:
    def __init__(self, send, recv):
        self.send, self.recv, self.count = send, recv, 0
        s = lax.axis_index("shard")
        self.shard = s
        self.near = {"shard": flip_bits(s, 1)}
        self.far = {"shard": flip_bits(s, 2)}
        self.across = {"shard": flip_bits(s, 3)}

    def greet(self, devices):
        barrier = pltpu.get_barrier_semaphore()
        for device in devices:
            pl.semaphore_signal(barrier, inc=1, device_id=device, device_id_type=MESH)
        pl.semaphore_wait(barrier, len(devices))

    def go(self, src, dst, device):
        at = self.count
        self.count += 1
        copy = pltpu.make_async_remote_copy(
            src_ref=src, dst_ref=dst, send_sem=self.send.at[at], recv_sem=self.recv.at[at],
            device_id=device, device_id_type=MESH,
        )
        copy.start()
        return copy


def sums_scratch(rows, columns):
    half = rows // 2
    return [
        pltpu.VMEM((2, rows, columns), jnp.float32),
        pltpu.VMEM((4, half, columns), jnp.bfloat16),
        pltpu.VMEM((4, half, columns), jnp.bfloat16),
        pltpu.VMEM((2, half, columns), jnp.bfloat16),
        pltpu.VMEM((2, half, columns), jnp.bfloat16),
    ]


class Sums:
    def __init__(self, links, refs):
        self.links = links
        self.part, self.send, self.land, self.cross, self.land_cross = refs
        self.half = self.send.shape[1]
        self.near, self.crossing, self.backs = None, [], []

    def rows(self, h):
        return slice(h * self.half, (h + 1) * self.half)

    def keep(self, cols, value):
        self.part[0, :, cols] = value

    def keep_far(self, cols, value):
        self.part[1, :, cols] = value

    def give(self, cols, value):
        self.send[0, :, cols] = b16(value[: self.half])
        self.send[1, :, cols] = b16(value[self.half :])

    def give_far(self, cols, value):
        self.send[2, :, cols] = b16(value[: self.half])
        self.send[3, :, cols] = b16(value[self.half :])

    def split(self, h):
        def emit(cols, value):
            self.part[1, self.rows(h), cols] = value[: self.half]
            self.send[2 + h, :, cols] = b16(value[self.half :])

        return emit

    def send_near(self):
        both = pl.ds(0, 2)
        self.near = self.links.go(self.send.at[both], self.land.at[both], self.links.near)

    def send_back(self, h):
        self.backs.append(self.links.go(self.send.at[2 + h], self.land.at[2 + h], self.links.near))

    def send_cross(self, h):
        self.backs[h].wait()
        self.cross[h] = b16(self.part[1, self.rows(h)] + f32(self.land[2 + h]))
        self.crossing.append(self.links.go(self.cross.at[h], self.land_cross.at[h], self.links.far))

    def arrive(self, h):
        if self.near is not None:
            self.near.wait()
            self.near = None
        self.crossing[h].wait()
        return self.part[0, self.rows(h)] + f32(self.land[h]) + f32(self.land_cross[h])


def gather_work_scatter(links, x, fill, work, refs):
    sums = Sums(links, refs)
    half = x.shape[1] // 2
    out = []
    for h in range(2):
        fill(h)
        out.append(links.go(x.at[0, pl.ds(h * half, half)], x.at[2 + h, pl.ds(0, half)], links.far))
    near = links.go(x.at[0], x.at[1], links.near)
    work(0, sums.keep)
    near.wait()
    work(1, sums.give)
    sums.send_near()
    for h in range(2):
        out[h].wait()
        on = links.go(x.at[2 + h, pl.ds(0, half)], x.at[2 + h, pl.ds(half, half)], links.near)
        on.wait()
        work(2 + h, sums.split(h))
        sums.send_back(h)
        sums.send_cross(h)
    return sums


def tiles(total, size):
    def over(body):
        pl.loop(0, total // size)(
            lambda n: body(pl.ds(pl.multiple_of(n * size, size), size))
        )

    return over


def norm_parts(rows):
    row_mean = jnp.mean(rows, axis=-1, keepdims=True)
    centered = rows - row_mean
    inverse = lax.rsqrt(jnp.mean(centered * centered, axis=-1, keepdims=True) + epsilon)
    return centered * inverse, inverse


def norm_slope(grad, scaled, inverse, gain):
    inner = grad * gain
    return inverse * (
        inner
        - jnp.mean(inner, axis=-1, keepdims=True)
        - scaled * jnp.mean(inner * scaled, axis=-1, keepdims=True)
    )


def column_sum(value):
    return jnp.sum(value, axis=0, keepdims=True)


def ffn_up(hid, act, slope, w_in, b_ref, which):
    def run(block):
        @tiles(w_in.shape[1], 512)
        def _(cols):
            pre = dot_rows(hid[block], w_in[:, cols]) + f32(b_ref[which : which + 1, cols])
            gate = jax.nn.sigmoid(pre)
            act[block, :, cols] = b16(pre * gate)
            slope[block, :, cols] = b16(gate * (1.0 + pre * (1.0 - gate)))

    return run


def ffn_down(act, w_rows):
    def run(block, emit):
        @tiles(w_rows.shape[1], 512)
        def _(cols):
            emit(cols, dot_rows(act[block], w_rows[:, cols]))

    return run


def ffn_inward(grad, inner, slope, w_in, w_rows):
    def run(block, emit):
        @tiles(w_in.shape[1], 512)
        def _(cols):
            wide = dot_back(grad[block], w_rows[cols, :])
            inner[block, :, cols] = b16(wide * f32(slope[block, :, cols]))

        @tiles(w_in.shape[0], 512)
        def _(cols):
            emit(cols, dot_back(inner[block], w_in[cols, :]))

    return run


def flat(ref):
    return ref[...].reshape(ref.shape[0] * ref.shape[1], ref.shape[2])


def flat_columns(ref, cols, size):
    return ref[:, :, cols].reshape(ref.shape[0] * ref.shape[1], size)


def weight_out(act, grad, gw_out):
    @tiles(act.shape[2], 256)
    def _(cols):
        gw_out[cols, :] = b16(dot_over(flat_columns(act, cols, 256), flat(grad)))


def weight_in(hid, inner, gw_in, sums_ref):
    @tiles(inner.shape[2], 256)
    def _(cols):
        right = flat_columns(inner, cols, 256)
        gw_in[:, cols] = b16(dot_over(flat(hid), right))
        sums_ref[3:4, cols] = column_sum(f32(right))


class Fetch:
    def __init__(self, links, batch, local_sem):
        self.links, self.local_sem = links, local_sem
        self.quarter = bit_of(batch, 0) + 2 * bit_of(batch, 1)
        self.peers = [{"batch": flip_bits(batch, 1)}, {"batch": flip_bits(batch, 2)}]

    def flow(self, source_rows, target, blocks, rows):
        links, size, held = self.links, rows // 8, {}
        span = lambda q, p: pl.ds(pl.multiple_of(q * (2 * size) + p * size, 16), size)
        mine = self.quarter
        own = blocks[0]

        def first():
            for p in range(2):
                for t, device, _ in blocks[1:]:
                    held["y", p, t] = links.go(
                        source_rows(t, mine * (2 * size) + p * size, size),
                        target.at[span(mine, p), own],
                        device,
                    )

        def pass_on(p, q, t, block, way):
            there = target.at[span(q, p), block]
            return links.go(there, there, self.peers[way])

        def second(p):
            def run():
                for t, _, block in blocks[1:]:
                    held["y", p, t].wait()
                    held["a", p, t] = pass_on(p, mine, t, block, p)

            return run

        def third(p):
            def run():
                other = flip_bits(mine, 1 << p)
                for t, _, block in blocks[1:]:
                    held["a", p, t].wait()
                    held["b", p, t] = pass_on(p, mine, t, block, 1 - p)
                    held["c", p, t] = pass_on(p, other, t, block, 1 - p)

            return run

        def last():
            for p in range(2):
                for t, _, _ in blocks[1:]:
                    held["b", p, t].wait()
                    held["c", p, t].wait()

        return [first, second(0), second(1), third(0), third(1), last]

    def columns(self, source, target, at):
        links, (rows, columns) = self.links, source.shape
        far = flip_bits(links.shard, 2)
        own = column_block(links.shard, columns)
        far_block = column_block(far, columns)
        row = lambda t, start, size: source.at[pl.ds(pl.multiple_of(start, 16), size)]
        stages = self.flow(row, target, [own, (2, links.far, far_block)], rows)
        held = {}

        def first():
            stages[0]()
            held["own"] = pltpu.make_async_copy(source, target.at[:, own], self.local_sem.at[at])
            held["own"].start()
            held["near"] = links.go(source, target.at[:, own], links.near)

        def pass_near():
            stages[-1]()
            held["on"] = links.go(target.at[:, far_block], target.at[:, far_block], links.near)

        def finish():
            held["on"].wait()
            held["near"].wait()
            held["own"].wait()

        return [first] + stages[1:-1] + [pass_near, finish]

    def rows(self, source, target, at):
        links, rows = self.links, target.shape[0]
        columns = source.shape[1]
        index = [flip_bits(links.shard, m) for m in range(4)]
        own = column_block(links.shard, columns)
        row = lambda m, start, size: source.at[pl.ds(pl.multiple_of(index[m] * rows + start, 16), size)]
        blocks = [own] + [
            (m, device, column_block(index[m], columns)) for m, device in ((2, links.far), (3, links.across))
        ]
        stages = self.flow(row, target, blocks, rows)
        held = {}

        def first():
            stages[0]()
            held["own"] = pltpu.make_async_copy(row(0, 0, rows), target.at[:, own], self.local_sem.at[at])
            held["own"].start()
            held["near"] = links.go(row(1, 0, rows), target.at[:, own], links.near)

        def last():
            stages[-1]()
            held["near"].wait()
            held["own"].wait()

        return [first] + stages[1:-1] + [last]


def vector_row(pack, row):
    return f32(jnp.concatenate([pack[t, row : row + 1, :] for t in range(pack.shape[0])], 1))

def link_scratch(count, local):
    return [
        pltpu.SemaphoreType.DMA((count,)),
        pltpu.SemaphoreType.DMA((count,)),
        pltpu.SemaphoreType.DMA((local,)),
    ]


def front_body(
    heads, size,
    rows_ref, gains_ref, own_ref, taps_ref, b_ref, base_ref, length_ref,
    pos_hbm, qkv_hbm, ffn_in, ffn_out, out_proj, conv_in, conv_out,
    one_ref, two_ref, pack, table, proj, with_u, with_v, key, value, mix, wc_in, w_mine, wc_out, w_rows_two,
    hid_out, act_out, slope_out, w_rows_out, hidden_out, soft_out,
    hid, act, slope, w_rows, w_in, w_out, pos_ref, w_qkv, hid_b, soft_ref, turned,
    part, send, land, cross, land_cross, send_sem, recv_sem, local_sem, load_sem, flush_sem, pack_in,
):
    batch = lax.axis_index("batch")
    links = Links(send_sem, recv_sem)
    fetch = Fetch(links, batch, local_sem)
    flush = Flush(flush_sem)
    pack_in[0:6, :] = gains_ref[...]
    pack_in[6:22, :] = own_ref[...]
    pack_in[22:27, :] = taps_ref[...]
    pack_in[27:32, :] = b16(jnp.full((5, pack_in.shape[1]), length_ref[0], jnp.int32).astype(jnp.float32))
    loads = Loads(load_sem, [(ffn_in.at[0], w_in), (pos_hbm, pos_ref), (qkv_hbm, w_qkv)])
    links.greet([links.near, links.far, links.across] + fetch.peers)
    small = [
        links.go(pack_in, pack.at[links.shard], device)
        for device in (links.far, links.across, links.near)
    ]
    down = fetch.rows(ffn_out.at[0], w_rows, 0)
    down.pop(0)()
    pack[links.shard] = pack_in[...]
    for copy in small:
        copy.wait()
    rows, features = rows_ref.shape
    hid[0] = b16(norm_rows(rows_ref[...], vector_row(pack, 0), vector_row(pack, 6)))
    half = rows // 2
    out = [
        links.go(hid.at[0, pl.ds(h * half, half)], hid.at[2 + h, pl.ds(0, half)], links.far)
        for h in range(2)
    ]
    near = links.go(hid.at[0], hid.at[1], links.near)
    up = ffn_up(hid, act, slope, w_in, b_ref, 0)
    loads.need(0)
    up(0)
    down.pop(0)()
    down.pop(0)()
    near.wait()
    up(1)
    lanes = features // 2

    @pl.loop(0, table.shape[0] // 16)
    def _(i):
        at = pl.ds(pl.multiple_of(i * 16, 16), 16)
        s_a, c_a = base_ref[pl.ds(16 + i, 1), 0:lanes], base_ref[pl.ds(16 + i, 1), lanes:]
        s_b, c_b = base_ref[0:16, 0:lanes], base_ref[0:16, lanes:]
        table[at, 0:lanes] = b16(s_a * c_b + c_a * s_b)
        table[at, lanes:] = b16(c_a * c_b - s_a * s_b)

    loads.need(1)
    proj[...] = b16(dot_rows(table[...], pos_ref[...]))
    down.pop(0)()
    down.pop(0)()
    other = fetch.columns(out_proj, w_out, 1)
    leaving = fetch.columns(conv_in, wc_in, 3)
    second = fetch.rows(ffn_out.at[1], w_rows_two, 4)
    for h in range(2):
        out[h].wait()
        on = links.go(hid.at[2 + h, pl.ds(0, half)], hid.at[2 + h, pl.ds(half, half)], links.near)
        on.wait()
        if h == 1:
            other.pop(0)()
        up(2 + h)
    leaving.pop(0)()
    for pair in ((hid, hid_out), (act, act_out), (slope, slope_out)):
        flush.go(*pair)
    while down:
        down.pop(0)()
    flush.go(w_rows, w_rows_out)
    sums = Sums(links, (part, send, land, cross, land_cross))
    work = ffn_down(act, w_rows)
    for h in range(2):
        work(2 + h, sums.split(h))
        sums.send_back(h)
    for h in range(2):
        sums.send_cross(h)
    second.pop(0)()
    work(1, sums.give)
    sums.send_near()
    work(0, sums.keep)
    for _ in range(4):
        other.pop(0)()
        leaving.pop(0)()

    out_bias, gain, shift = vector_row(pack, 7), vector_row(pack, 1), vector_row(pack, 8)
    out = []
    for h in range(2):
        at = slice(h * half, (h + 1) * half)
        one = rows_ref[at] + 0.5 * (sums.arrive(h) + out_bias)
        one_ref[at] = one
        hid_b[0, at] = b16(norm_rows(one, gain, shift))
        there = pl.ds(h * half, half)
        out.append(links.go(hid_b.at[0, there], hid_b.at[2, there], links.far))
    near = links.go(hid_b.at[0], hid_b.at[1], links.near)
    while other:
        other.pop(0)()
        leaving.pop(0)()
    entering = fetch.columns(conv_out, wc_out, 2)
    own = f32(own_ref[...])
    keys = f32(lax.broadcasted_iota(jnp.int32, (rows, rows), 1))
    scale = 1.0 / math.sqrt(size)
    loads.need(2)

    def attend(slot):
        hidden = hid_b[slot]
        query = dot_rows(hidden, w_qkv[0]) + own[3:4]
        with_u[slot] = b16(query + own[6:7])
        with_v[slot] = b16(query + own[7:8])
        key[slot] = b16(dot_rows(hidden, w_qkv[1]))
        value[slot] = b16(dot_rows(hidden, w_qkv[2]) + own[4:5])
        live = f32(pack[flip_bits(links.shard, slot), 27:28, 0:1])
        for h in range(heads):
            cols = slice(h * size, (h + 1) * size)
            wide = dot_back(with_v[slot, :, cols], proj[:, cols])
            moved = pltpu.roll(wide, rows + 1, 1, stride=1, stride_axis=0)[:, :rows]
            raw = dot_back(with_u[slot, :, cols], key[slot, :, cols]) + moved
            scores = jnp.where(keys < live, raw * scale, -1e30)
            grown = jnp.exp(scores - jnp.max(scores, axis=-1, keepdims=True))
            soft = grown / jnp.sum(grown, axis=-1, keepdims=True)
            soft_ref[slot, :, h * rows : (h + 1) * rows] = soft
            mix[slot, :, cols] = b16(dot_rows(b16(soft), value[slot, :, cols]))

    last = []
    attend(0)
    turned[links.shard] = mix[0]
    near.wait()
    second.pop(0)()
    second.pop(0)()
    attend(1)
    second.pop(0)()
    second.pop(0)()
    last.append(links.go(mix.at[1], turned.at[links.shard], links.near))
    on = []
    for h in range(2):
        out[h].wait()
        there = pl.ds(h * half, half)
        on.append(links.go(hid_b.at[2, there], hid_b.at[3, there], links.near))
        if h == 0:
            entering.pop(0)()
    attend(2)
    last.append(links.go(mix.at[2], turned.at[links.shard], links.far))
    entering.pop(0)()
    entering.pop(0)()
    for copy in on:
        copy.wait()
    flush.go(hid_b, hidden_out)
    attend(3)
    last.append(links.go(mix.at[3], turned.at[links.shard], links.across))
    flush.go(soft_ref, soft_out)
    entering.pop(0)()
    entering.pop(0)()
    for copy in last:
        copy.wait()
    width = mix.shape[2]
    total = one_ref[...] + vector_row(pack, 11)
    for t in range(turned.shape[0]):
        total = total + dot_rows(turned[t], w_out[t * width : (t + 1) * width])
    two_ref[...] = total
    w_mine[...] = w_out[pl.ds(pl.multiple_of(links.shard * width, 16), width), :]
    while entering:
        entering.pop(0)()
    while second:
        second.pop(0)()
    flush.settle()


def front(
    rows_in, gains, own_biases, taps, lengths, b_in, base, pos_proj, qkv_proj, ffn_in, ffn_out, out_proj, conv_in,
    conv_out, heads, ident,
):
    ns = lax.axis_size("shard")
    rows, features = rows_in.shape
    hidden = ffn_in.shape[2]
    width = features // ns
    low, full = jnp.bfloat16, jnp.float32
    shape, vmem = jax.ShapeDtypeStruct, pltpu.VMEM
    narrow = shape((ns, rows, width), low)
    dma = pltpu.SemaphoreType.DMA
    return pl.pallas_call(
        functools.partial(front_body, heads, width // heads),
        out_shape=[
            shape((rows, features), full), shape((rows, features), full),
            shape((ns, 32, width), low),
            shape((2 * rows, features), low), shape((2 * rows, width), low),
            narrow, narrow, narrow, narrow, narrow,
            shape((conv_in.shape[0], ns * conv_in.shape[1]), low),
            shape((width, features), low),
            shape((features, features), low),
            shape((hidden, features), low),
            shape((4, rows, features), low), shape((4, rows, hidden), low), shape((4, rows, hidden), low),
            shape((hidden, features), low),
            shape((ns, rows, features), low),
            shape((ns, rows, heads * rows), full),
        ],
        in_specs=[VMEM_SPEC] * 6 + [pl.BlockSpec(memory_space=pltpu.SMEM)] + [HBM_SPEC] * 7,
        out_specs=[VMEM_SPEC] * 14 + [HBM_SPEC] * 6,
        scratch_shapes=[
            vmem((4, rows, features), low), vmem((4, rows, hidden), low), vmem((4, rows, hidden), low),
            vmem((hidden, features), low), vmem((features, hidden), low), vmem((features, features), low),
            vmem(pos_proj.shape, low), vmem(qkv_proj.shape, low),
            vmem((ns, rows, features), low), vmem((ns, rows, heads * rows), full), vmem((ns, rows, width), low),
        ]
        + sums_scratch(rows, features)
        + link_scratch(100, 5)
        + [dma((3,)), dma((6,)), vmem((32, width), low)],
        compiler_params=pltpu.CompilerParams(
            collective_id=ident, has_side_effects=True, vmem_limit_bytes=60 << 20
        ),
        name="front",
    )(
        rows_in, gains, own_biases, taps, b_in, base, lengths, pos_proj, qkv_proj, ffn_in, ffn_out, out_proj,
        conv_in, conv_out,
    )


def pack_rows(ref, at, row):
    for i in range(row.shape[1] // 128):
        ref[at + i : at + i + 1, :] = row[:, i * 128 : (i + 1) * 128]


def unpack_rows(value, at, lanes):
    return jnp.concatenate([value[at + i : at + i + 1, :] for i in range(lanes)], 1)


def everywhere(links, nb, source, mid, land_s, land_b, result, small, sems):
    s, b = links.shard, lax.axis_index("batch")
    ns = land_s.shape[0]
    ss, rs, sb, rb = sems
    first = exchange("shard", s, ns, source, land_s, ss, rs)
    for copy in first:
        copy.start()
    land_s[s] = source[...]
    for copy in first:
        copy.wait()
    mid[...] = sum_slots(land_s, ns)
    second = exchange("batch", b, nb, mid, land_b, sb, rb)
    for copy in second:
        copy.start()
    land_b[b] = mid[...]
    small()
    for copy in second:
        copy.wait()
    return sum_slots(land_b, nb)


def conv_part(
    links, nb, loads, rows_ref, pack, w_in, w_out,
    out_ref, hid, open_ref, gate_ref, gated_ref, scaled_ref, act, slope, stats,
    padded, source, mid, land_s, land_b, sems,
):
    rows, features = rows_ref.shape
    live = f32(pack[links.shard, 27:28, 0:1])
    mask = f32(f32(lax.broadcasted_iota(jnp.int32, (rows, 1), 0)) < live)
    hid[...] = b16(norm_rows(rows_ref[...], vector_row(pack, 2), vector_row(pack, 14)))
    bias_v, bias_g = vector_row(pack, 15), vector_row(pack, 16)
    loads.need(0)
    lead = 8
    tile = 512
    padded[0:lead, :] = jnp.zeros((lead, features), jnp.float32)
    padded[lead + rows :, :] = jnp.zeros((lead, features), jnp.float32)
    for n in range(features // tile):
        cols = slice(n * tile, (n + 1) * tile)
        left = dot_rows(hid[...], w_in[:, cols]) + bias_v[:, cols]
        right = dot_rows(hid[...], w_in[:, features + n * tile : features + (n + 1) * tile])
        gate = jax.nn.sigmoid(right + bias_g[:, cols])
        opened = gate * mask
        gated = left * opened
        open_ref[:, cols] = b16(opened)
        gate_ref[:, cols] = b16(gated * (1.0 - gate))
        gated_ref[:, cols] = b16(gated)
        padded[lead : lead + rows, cols] = gated
    taps = 5
    total = 0.0
    for k in range(taps):
        at = lead - (taps - 1) // 2 + k
        total = total + padded[at : at + rows, :] * vector_row(pack, 22 + k)
    live_total = total * mask
    lanes = features // 128
    pack_rows(source, 0, jnp.sum(live_total, axis=0, keepdims=True))
    pack_rows(source, lanes, jnp.sum(live_total * total, axis=0, keepdims=True))
    source[2 * lanes : 2 * lanes + 8, :] = jnp.broadcast_to(live, (8, 128))
    scaled_ref[...] = total
    sums = everywhere(links, nb, source, mid, land_s, land_b, None, lambda: None, sems)
    frames = sums[2 * lanes : 2 * lanes + 1, 0:1]
    mean = unpack_rows(sums, 0, lanes) / frames
    inverse = lax.rsqrt(unpack_rows(sums, lanes, lanes) / frames - mean * mean + epsilon)
    stats[0:1, :] = inverse
    stats[1:2, :] = jnp.broadcast_to(frames, (1, features))
    stats[2:8, :] = jnp.zeros((6, features), jnp.float32)
    scaled = (scaled_ref[...] - mean) * inverse
    scaled_ref[...] = scaled
    normed = scaled * vector_row(pack, 3) + vector_row(pack, 17)
    gate = jax.nn.sigmoid(normed)
    act[...] = b16(normed * gate)
    slope[...] = b16(gate * (1.0 + normed * (1.0 - gate)))
    loads.need(1)
    out_ref[...] = rows_ref[...] + (dot_rows(act[...], w_out[...]) + vector_row(pack, 18))


def middle_part(
    links, loads, riders, rows_ref, pack, b_ref, result, out_ref, gw_in, gw_out, sums_ref,
    hid, act, slope, grad, inner, w_in, w_rows, cotangent, stream, first, second,
):
    rows, features = rows_ref.shape
    half = rows // 2
    gain, shift = vector_row(pack, 4), vector_row(pack, 19)

    def fill(h):
        at = slice(h * half, (h + 1) * half)
        hid[0, at] = b16(norm_rows(rows_ref[at], gain, shift))

    up, down = ffn_up(hid, act, slope, w_in, b_ref, 1), ffn_down(act, w_rows)

    def work(block, emit):
        loads.need(2)
        up(block)
        loads.need(3)
        down(block, emit)

    sums = gather_work_scatter(links, hid, fill, work, first)
    last_gain, last_shift, out_bias = vector_row(pack, 5), vector_row(pack, 21), vector_row(pack, 20)
    live = f32(pack[links.shard, 27:28, 0:1])
    mask = f32(f32(lax.broadcasted_iota(jnp.int32, (rows, 1), 0)) < live)
    loads.need(4)
    ends = []

    def turn_back(h):
        at = slice(h * half, (h + 1) * half)
        scaled, inverse = norm_parts(rows_ref[at] + 0.5 * (sums.arrive(h) + out_bias))
        result[at] = (scaled * last_gain + last_shift) * mask[at]
        given = cotangent[at] * mask[at]
        slide = norm_slope(given, scaled, inverse, last_gain)
        stream[at] = slide
        grad[0, at] = b16(0.5 * slide)
        ends.append((column_sum(given * scaled), column_sum(given)))

    back = gather_work_scatter(
        links, grad, turn_back, ffn_inward(grad, inner, slope, w_in, w_rows), second
    )
    weight_out(act, grad, gw_out)
    for p in range(EARLY):
        riders[1][0](p)
    weight_in(hid, inner, gw_in, sums_ref)
    for p in range(EARLY):
        riders[0][0](p)
    sums_ref[0:3, :] = jnp.zeros((3, features), jnp.float32)
    sums_ref[2:3, :] = column_sum(f32(grad[0]))
    sums_ref[4:5, :] = ends[0][0] + ends[1][0]
    sums_ref[5:6, :] = ends[0][1] + ends[1][1]
    sums_ref[6:8, :] = jnp.zeros((2, features), jnp.float32)
    for h in range(2):
        at = slice(h * half, (h + 1) * half)
        scaled, inverse = norm_parts(rows_ref[at])
        given = back.arrive(h)
        out_ref[at] = stream[at] + norm_slope(given, scaled, inverse, gain)
        sums_ref[0:1, :] += column_sum(given * scaled)
        sums_ref[1:2, :] += column_sum(given)


def conv_back_part(
    links, nb, ride_on, stream_ref, rows_ref, pack, w_in, w_out,
    hid, open_ref, gate_ref, gated_ref, scaled_ref, act, slope, stats,
    out_ref, gw_out, gw_in, sums_ref,
    padded, normed, grad, inner, source, mid, land_s, land_b, sems,
):
    rows, features = rows_ref.shape
    lanes = features // 128
    lead, tile, taps = 8, 512, 5
    grad[...] = b16(stream_ref[...])
    gain = vector_row(pack, 3)
    sums_ref[...] = jnp.zeros_like(sums_ref)
    for n in range(features // tile):
        cols = slice(n * tile, (n + 1) * tile)
        value = dot_back(grad[...], w_out[cols, :]) * f32(slope[:, cols])
        normed[:, cols] = value
        for at, total in (
            (0, jnp.sum(value, axis=0, keepdims=True)),
            (lanes, jnp.sum(value * scaled_ref[:, cols], axis=0, keepdims=True)),
        ):
            for i in range(tile // 128):
                row = at + n * (tile // 128) + i
                source[row : row + 1, :] = total[:, i * 128 : (i + 1) * 128]

    def meanwhile():
        @tiles(features, 256)
        def _(cols):
            gw_out[cols, :] = b16(dot_over(act[:, cols], grad[...]))

        sums_ref[4:5, :] = jnp.sum(f32(grad[...]), axis=0, keepdims=True)

    sums = everywhere(links, nb, source, mid, land_s, land_b, None, meanwhile, sems)
    beta, gamma = unpack_rows(sums, 0, lanes), unpack_rows(sums, lanes, lanes)
    ride_on()
    sums_ref[5:6, :] = gamma
    sums_ref[6:7, :] = beta
    inverse, frames = stats[0:1, :], stats[1:2, 0:1]
    live = f32(pack[links.shard, 27:28, 0:1])
    mask = f32(f32(lax.broadcasted_iota(jnp.int32, (rows, 1), 0)) < live)
    padded[0:lead, :] = jnp.zeros((lead, features), jnp.float32)
    padded[lead + rows :, :] = jnp.zeros((lead, features), jnp.float32)
    padded[lead : lead + rows, :] = inverse * (
        normed[...] * gain - mask * (gain * beta + scaled_ref[...] * (gain * gamma)) / frames
    )
    given = 0.0
    gated = f32(gated_ref[...])
    for k in range(taps):
        at = lead + (taps - 1) // 2 - k
        moved = padded[at : at + rows, :]
        given = given + moved * vector_row(pack, 22 + k)
        sums_ref[8 + k : 9 + k, :] = jnp.sum(moved * gated, axis=0, keepdims=True)
    left = b16(given * f32(open_ref[...]))
    right = b16(given * f32(gate_ref[...]))
    inner[:, 0:features] = left
    inner[:, features:] = right
    sums_ref[2:3, :] = jnp.sum(f32(left), axis=0, keepdims=True)
    sums_ref[3:4, :] = jnp.sum(f32(right), axis=0, keepdims=True)
    total = dot_back(inner[...], w_in[...])
    scaled, inverse = norm_parts(rows_ref[...])
    out_ref[...] = stream_ref[...] + norm_slope(total, scaled, inverse, vector_row(pack, 2))
    sums_ref[0:1, :] = jnp.sum(total * scaled, axis=0, keepdims=True)
    sums_ref[1:2, :] = jnp.sum(total, axis=0, keepdims=True)

    @tiles(2 * features, 512)
    def _(cols):
        gw_in[:, cols] = b16(dot_over(hid[...], inner[:, cols]))


def centre_body(nb, *refs):
    rows_ref, pack, b_ref, cw_in_hbm, cw_out_hbm, w_rows_hbm, cotangent_hbm, ffn_in, *refs = refs
    result, out_ref, gwc_out, gwc_in, two_sums, conv_sums, half_a, half_b, *refs = refs
    cw_in, cw_out, w_in, w_rows, cotangent, *refs = refs
    three, hid_c, open_ref, gate_ref, gated_ref, scaled_ref, act_c, slope_c, stats, padded, *refs = refs
    hid, act, slope, grad, inner, gw_in, gw_out, stream, between, normed, grad_c, inner_c, *refs = refs
    sums_a, sums_b, (first, second) = refs[:5], refs[5:10], (refs[10:18], refs[18:26])
    send_sem, recv_sem, ride_send, ride_recv, load_sem = refs[26:]
    batch = lax.axis_index("batch")
    links = Links(send_sem, recv_sem)
    loads = Loads(
        load_sem,
        [
            (cw_in_hbm, cw_in), (cw_out_hbm, cw_out), (ffn_in.at[1], w_in), (w_rows_hbm, w_rows),
            (cotangent_hbm, cotangent),
        ],
    )
    links.greet(
        [links.near, links.far, links.across]
        + [{"batch": lax.rem(batch + j, nb)} for j in range(1, nb)]
    )
    saved = (hid_c, open_ref, gate_ref, gated_ref, scaled_ref, act_c, slope_c, stats)
    conv_part(links, nb, loads, rows_ref, pack, cw_in, cw_out, three, *saved, padded, *first[:4], first[4:])
    orders = ride_orders(nb)
    pieces = 4
    riders = [
        Rider(batch, ride_send, ride_recv, at * pieces).halve_pieces(
            source, landing, orders[at][0], pieces, landing.shape[0]
        )
        for at, (source, landing) in enumerate(((gw_in, half_a), (gw_out, half_b)))
    ]
    middle_part(
        links, loads, riders, three, pack, b_ref, result, between, gw_in, gw_out, two_sums,
        hid, act, slope, grad, inner, w_in, w_rows, cotangent, stream, sums_a, sums_b,
    )
    for start, _, _ in riders:
        start(EARLY)

    def ride_on():
        for p in range(EARLY + 1, pieces):
            for start, _, _ in riders:
                start(p)

    conv_back_part(
        links, nb, ride_on, between, rows_ref, pack, cw_in, cw_out, *saved, out_ref, gwc_out, gwc_in, conv_sums,
        padded, normed, grad_c, inner_c, *second[:4], second[4:],
    )
    for (_, settle, own), landing in zip(riders, (half_a, half_b)):
        settle()
        landing[...] = b16(f32(own[...]) + f32(landing[...]))


EARLY = 1


def centre(rows_in, pack, b_in, wc_in, wc_out, w_rows, cotangent, ffn_in, ident):
    ns, nb = lax.axis_size("shard"), lax.axis_size("batch")
    rows, features = rows_in.shape
    hidden = ffn_in.shape[2]
    low, full = jnp.bfloat16, jnp.float32
    shape, vmem, dma = jax.ShapeDtypeStruct, pltpu.VMEM, pltpu.SemaphoreType.DMA
    wide, plain = vmem((4, rows, features), low), vmem((rows, features), low)
    tall = vmem((4, rows, hidden), low)
    whole = vmem((rows, features), full)
    lanes = features // 128

    def exchange_scratch(count):
        small = (count, 128)
        return [
            vmem(small, full), vmem(small, full), vmem((ns,) + small, full), vmem((nb,) + small, full),
            dma((ns,)), dma((ns,)), dma((nb,)), dma((nb,)),
        ]

    return pl.pallas_call(
        functools.partial(centre_body, nb),
        out_shape=[
            shape((rows, features), full), shape((rows, features), full),
            shape((features, features), low), shape((features, 2 * features), low),
            shape((8, features), full), shape((16, features), full),
            shape((features // 2, hidden), low), shape((hidden // 2, features), low),
        ],
        in_specs=[VMEM_SPEC] * 3 + [HBM_SPEC] * 5,
        out_specs=[VMEM_SPEC] * 8,
        scratch_shapes=[
            vmem(wc_in.shape, low), vmem(wc_out.shape, low), vmem((features, hidden), low),
            vmem((hidden, features), low), whole,
            whole, plain, plain, plain, plain, whole, plain, plain, vmem((8, features), full),
            vmem((rows + 16, features), full),
            wide, tall, tall, wide, tall, vmem((features, hidden), low), vmem((hidden, features), low),
            whole, whole, whole, plain, vmem((rows, 2 * features), low),
        ]
        + sums_scratch(rows, features)
        + sums_scratch(rows, features)
        + exchange_scratch(2 * lanes + 8)
        + exchange_scratch(2 * lanes)
        + [dma((20,)), dma((20,)), dma((8,)), dma((8,)), dma((5,))],
        compiler_params=pltpu.CompilerParams(
            collective_id=ident, has_side_effects=True, vmem_limit_bytes=62 << 20
        ),
        name="centre",
    )(rows_in, pack, b_in, wc_in, wc_out, w_rows, cotangent, ffn_in)


def rear_body(
    heads, size, nb, stream_ref, rows_ref, pack, w_mine, ride_a, ride_b,
    hid_b_hbm, with_u_hbm, with_v_hbm, key_hbm, value_hbm, soft_hbm, mix_hbm, table_hbm, proj_hbm, w_qkv_hbm,
    start_hbm, hid_hbm, act_hbm, slope_hbm, w_rows_hbm, ffn_in,
    out_ref, half_q, half_k, half_x, half_pos, gw_mix, mix_sums, own_sums, gw_in, gw_out, sums_ref, out_a, out_b,
    grad, dq, dk, dx, dp, stream, grad_b, inner, start, hid, act, slope, w_rows, w_in,
    hid_b, with_u, with_v, key, value, soft_ref, mix, table, proj, w_qkv, *refs,
):
    first, second, refs = refs[:5], refs[5:10], refs[10:]
    send_sem, recv_sem, ride_send, ride_recv, load_sem, gw_q, gw_k, gw_x, gw_pos, halve_send, halve_recv, *between = refs
    links = Links(send_sem, recv_sem)
    batch = lax.axis_index("batch")
    loads = Loads(
        load_sem,
        [
            (soft_hbm, soft_ref), (value_hbm, value), (key_hbm, key), (with_u_hbm, with_u), (with_v_hbm, with_v),
            (proj_hbm, proj), (w_qkv_hbm, w_qkv), (hid_b_hbm, hid_b), (mix_hbm, mix), (table_hbm, table),
            (slope_hbm, slope), (w_rows_hbm, w_rows), (ffn_in.at[0], w_in), (act_hbm, act), (hid_hbm, hid),
            (start_hbm, start),
        ],
    )
    orders = ride_orders(nb)
    steps = len(orders[0]) - 1
    scale = 1.0 / math.sqrt(size)
    rows, features = rows_ref.shape
    half = rows // 2
    links.greet([links.near, links.far] + [{"batch": flip_bits(batch, 1 << k)} for k in orders[0]])
    inward, outward = [], []
    count = 2 * steps - 1
    for at, (begin, end) in enumerate(((ride_a, out_a), (ride_b, out_b))):
        middle_refs = between[at * count : (at + 1) * count]
        down_refs = [begin, *middle_refs[:steps]]
        up_refs = [*middle_refs[steps - 1 :], end]
        rider = Rider(batch, ride_send, ride_recv, at * 2 * steps)
        inward.append(rider.chain(down_refs, orders[at][1:], rider.halve))
        rider = Rider(batch, ride_send, ride_recv, at * 2 * steps + steps)
        outward.append(rider.chain(up_refs, orders[at][:0:-1], rider.double))

    def tick(chains):
        for chain in chains:
            if chain:
                chain.pop(0)()

    tick(inward)
    grad[0] = b16(stream_ref[...])
    out = [
        links.go(grad.at[0, pl.ds(h * half, half)], grad.at[2, pl.ds(h * half, half)], links.far)
        for h in range(2)
    ]
    near = links.go(grad.at[0], grad.at[1], links.near)
    at_row = lax.broadcasted_iota(jnp.int32, (rows, rows), 0)
    at_col = lax.broadcasted_iota(jnp.int32, (rows, rows), 1)
    flip = b16(f32(at_row + at_col == rows - 1))
    keys = f32(at_col)
    own_sums[...] = jnp.zeros_like(own_sums)

    def work(slot, emit):
        mixed = b16(dot_back(grad[slot], w_mine[...]))
        live = f32(pack[flip_bits(links.shard, slot), 27:28, 0:1])
        for h in range(heads):
            cols = slice(h * size, (h + 1) * size)
            soft = soft_ref[slot, :, h * rows : (h + 1) * rows]
            given = mixed[:, cols]
            grad_soft = dot_back(given, value[slot, :, cols])
            dx[slot, :, cols] = b16(dot_over(b16(soft), given))
            grad_scores = soft * (grad_soft - jnp.sum(grad_soft * soft, axis=-1, keepdims=True))
            raw = b16(jnp.where(keys < live, grad_scores, 0.0) * scale)
            grad_u = dot_rows(raw, key[slot, :, cols])
            dk[slot, :, cols] = b16(dot_over(raw, with_u[slot, :, cols]))
            turned = dot_rows(flip, raw)
            wide = jnp.concatenate([turned, jnp.zeros_like(turned)], 1)
            wide = b16(pltpu.roll(wide, 0, 1, stride=1, stride_axis=0))
            grad_v = dot_rows(wide, proj[:, cols])
            v_turned = b16(dot_rows(flip, with_v[slot, :, cols]))
            dp[slot, :, cols] = b16(dot_over(wide, v_turned))
            own_sums[2:3, cols] += column_sum(grad_u)
            own_sums[3:4, cols] += column_sum(grad_v)
            high = b16(grad_v)
            rest = b16(grad_v - f32(high))
            dq[slot, :, cols] = b16(grad_u + (dot_rows(flip, high) + dot_rows(flip, rest)))
        own_sums[0:1, :] += column_sum(f32(dq[slot]))
        own_sums[1:2, :] += column_sum(f32(dx[slot]))

        @tiles(features, 512)
        def _(cols):
            emit(
                cols,
                dot_back(dq[slot], w_qkv[0, cols, :])
                + dot_back(dk[slot], w_qkv[1, cols, :])
                + dot_back(dx[slot], w_qkv[2, cols, :]),
            )

    sums = Sums(links, first)
    loads.need(*range(7))
    work(0, sums.keep)
    near.wait()
    work(1, sums.give)
    sums.send_near()
    tick(inward)
    on = []
    for h in range(2):
        out[h].wait()
        there = pl.ds(h * half, half)
        on.append(links.go(grad.at[2, there], grad.at[3, there], links.near))
    for copy in on:
        copy.wait()
    work(3, sums.give_far)
    for h in range(2):
        sums.send_back(h)
    work(2, sums.keep_far)
    for h in range(2):
        sums.send_cross(h)
    loads.need(7, 8, 9)
    for ref, target in ((dq, gw_q), (dk, gw_k), (dx, gw_x)):
        right = flat(ref)

        @tiles(features, 256)
        def _(cols, target=target, right=right):
            target[cols, :] = b16(dot_over(flat_columns(hid_b, cols, 256), right))

    @tiles(features, 256)
    def _(cols):
        total = dot_over(table[:, cols], dp[0])
        for slot in range(1, 4):
            total = total + dot_over(table[:, cols], dp[slot])
        gw_pos[cols, :] = b16(total)

    halver = Rider(batch, halve_send, halve_recv, 0)
    halvings = [
        halver.halve(source, landing, 0)
        for source, landing in ((gw_q, half_q), (gw_k, half_k), (gw_x, half_x), (gw_pos, half_pos))
    ]
    gw_mix[...] = b16(dot_over(flat(mix), flat(grad)))
    mix_sums[...] = jnp.zeros_like(mix_sums)
    mix_sums[2:3, :] = column_sum(f32(grad[0]))
    gain = vector_row(pack, 1)

    def fill(h):
        at = slice(h * half, (h + 1) * half)
        given = sums.arrive(h)
        scaled, inverse = norm_parts(rows_ref[at])
        slide = stream_ref[at] + norm_slope(given, scaled, inverse, gain)
        stream[at] = slide
        grad_b[0, at] = b16(0.5 * slide)
        mix_sums[0:1, :] += column_sum(given * scaled)
        mix_sums[1:2, :] += column_sum(given)

    step = ffn_inward(grad_b, inner, slope, w_in, w_rows)

    def back_work(block, emit):
        loads.need(10, 11, 12)
        if block == 1:
            for chain in inward:
                while chain:
                    chain.pop(0)()
            tick(outward)
        step(block, emit)

    back = gather_work_scatter(links, grad_b, fill, back_work, second)
    loads.need(13, 14, 15)
    weight_out(act, grad_b, gw_out)
    tick(outward)
    weight_in(hid, inner, gw_in, sums_ref)
    sums_ref[0:3, :] = jnp.zeros((3, features), jnp.float32)
    sums_ref[2:3, :] = column_sum(f32(grad_b[0]))
    sums_ref[4:8, :] = jnp.zeros((4, features), jnp.float32)
    gain = vector_row(pack, 0)
    for h in range(2):
        at = slice(h * half, (h + 1) * half)
        scaled, inverse = norm_parts(start[at])
        given = back.arrive(h)
        out_ref[at] = stream[at] + norm_slope(given, scaled, inverse, gain)
        sums_ref[0:1, :] += column_sum(given * scaled)
        sums_ref[1:2, :] += column_sum(given)
    for end in halvings:
        end()
    for chain in outward:
        while chain:
            chain.pop(0)()


def rear(stream, rows_one, pack, saved_mix, table, proj, w_qkv, w_mine, ridden, rows_in, saved, w_rows, ffn_in, heads, ident):
    rows, features = rows_one.shape
    hidden = ffn_in.shape[2]
    width = proj.shape[1]
    nb = lax.axis_size("batch")
    steps = nb.bit_length() - 2
    low, full = jnp.bfloat16, jnp.float32
    shape, vmem = jax.ShapeDtypeStruct, pltpu.VMEM
    dma = pltpu.SemaphoreType.DMA
    narrow = vmem((4, rows, width), low)
    between = []
    for r in ridden:
        sizes = [r.shape[0] >> k for k in range(1, steps + 1)]
        between += [vmem((size, r.shape[1]), low) for size in sizes + sizes[-2::-1]]
    return pl.pallas_call(
        functools.partial(rear_body, heads, width // heads, nb),
        out_shape=[
            shape((rows, features), full),
            shape((features // 2, width), low), shape((features // 2, width), low),
            shape((features // 2, width), low), shape((features // 2, width), low),
            shape((width, features), low), shape((8, features), full), shape((8, width), full),
            shape((features, hidden), low), shape((hidden, features), low), shape((8, features), full),
        ]
        + [shape(r.shape, low) for r in ridden],
        in_specs=[VMEM_SPEC] * 6 + [HBM_SPEC] * 16,
        out_specs=[VMEM_SPEC] * 13,
        scratch_shapes=[
            vmem((4, rows, features), low), narrow, narrow, narrow, vmem((4, 2 * rows, width), low),
            vmem((rows, features), full), vmem((4, rows, features), low), vmem((4, rows, hidden), low),
            vmem((rows, features), full), vmem((4, rows, features), low), vmem((4, rows, hidden), low),
            vmem((4, rows, hidden), low), vmem((hidden, features), low), vmem((features, hidden), low),
        ]
        + [vmem(a.shape, a.dtype) for a in (*saved_mix, table, proj, w_qkv)]
        + sums_scratch(rows, features)
        + sums_scratch(rows, features)
        + [dma((24,)), dma((24,)), dma((4 * steps,)), dma((4 * steps,)), dma((16,))]
        + [vmem((features, width), low)] * 4
        + [dma((4,)), dma((4,))]
        + between,
        compiler_params=pltpu.CompilerParams(
            collective_id=ident, has_side_effects=True, vmem_limit_bytes=62 << 20
        ),
        name="rear",
    )(
        stream, rows_one, pack, w_mine, *ridden, *saved_mix, table, proj, w_qkv, rows_in, *saved, w_rows, ffn_in
    )


def body(
    tokens, cotangent, lengths, ffn_in, ffn_out, ffn_bias, qkv_proj, pos_proj, out_proj,
    conv_in, conv_out, depthwise, norm_gains, biases,
):
    _, length, features = tokens.shape
    ns, nb = lax.axis_size("shard"), lax.axis_size("batch")
    width = features // ns
    heads = HEADS // ns
    rows_in = tokens[0]

    rates = jnp.exp(
        jnp.arange(features // 2, dtype=jnp.float32) * (-2.0 * math.log(10000.0) / features)
    )
    turns = jnp.concatenate(
        [
            length - 1.0 - jnp.arange(16, dtype=jnp.float32),
            -16.0 * jnp.arange(2 * length // 16, dtype=jnp.float32),
        ]
    )
    angles = turns[:, None] * rates[None, :]
    base = jnp.concatenate([jnp.sin(angles), jnp.cos(angles)], 1)
    (
        rows_one, rows_two, pack, table, proj, with_u, with_v, key, value, mix, wc_in, w_mine, wc_out,
        w_rows_two, *saved_one, w_rows_one, hidden_mix, soft,
    ) = front(
        rows_in, norm_gains, biases, depthwise, lengths, ffn_bias, base, pos_proj, qkv_proj, ffn_in, ffn_out, out_proj, conv_in, conv_out,
        heads, 5,
    )
    saved_mix = (hidden_mix, with_u, with_v, key, value, soft, mix)
    result, stream, grad_conv_out, grad_conv_in, two_sums, conv_sums, *ridden = centre(
        rows_two, pack, ffn_bias, wc_in, wc_out, w_rows_two, cotangent[0], ffn_in, 6
    )
    stream, grad_q, grad_k, grad_x, grad_pos, grad_out, mix_sums, own_sums, one_in, one_out, one_sums, *ridden = rear(
        stream, rows_one, pack, saved_mix, table, proj, qkv_proj, w_mine, ridden, rows_in, saved_one, w_rows_one,
        ffn_in, heads, 12
    )
    tall, deep = one_in.shape
    piece = max(128, 8 * nb)
    *sums, out_gains, out_biases, out_taps, out_hidden = tail_sum(
        [grad_out, one_out, one_in, grad_q, grad_k, grad_x, grad_pos, grad_conv_in, grad_conv_out],
        ridden,
        [one_sums, mix_sums, two_sums, conv_sums, own_sums],
        [("turn", 4, None), ("turn", 1, 0), ("plain", 0, 0)]
        + [("half", 2, at) for at in range(3)]
        + [("half", 3, None), ("gather", 5, None), ("gather", 6, None)],
        [
            (2, tall, deep), (2, ns * deep, width), (3, tall, width), (tall, width), (tall, width),
            (tall, 2 * width), (tall, width),
        ],
        ["near", "line"],
        [width, piece, piece] + [tall // 4] * 4 + [2 * piece, min(tall, 4 * piece)],
        deep,
        4,
    )
    *sums, result, stream, out_gains, out_biases, out_taps, out_hidden = widen(
        sums, [result, stream, out_gains, out_biases, out_taps, out_hidden]
    )
    return (
        result[None],
        stream[None],
        sums[0],
        sums[1],
        out_hidden,
        sums[2],
        sums[3],
        sums[4],
        sums[5],
        sums[6],
        out_taps,
        out_gains,
        out_biases,
    )


def solution(mesh):
    rows = P(("batch", "shard"), None, None)
    cube, flat = P(None, None, "shard"), P(None, "shard")
    return jax.shard_map(
        body,
        mesh=mesh,
        in_specs=(rows, rows, P(("batch", "shard")), cube, cube, flat, cube)
        + (flat,) * 7,
        out_specs=(rows, rows, cube, cube, flat, cube) + (flat,) * 7,
        check_vma=False,
    )
```

```python
import functools
import math

import jax
import jax.numpy as jnp
from jax import lax
from jax.experimental import pallas as pl
from jax.experimental.pallas import tpu as pltpu
from jax.sharding import PartitionSpec as P

HEADS = 8
MESH = pl.DeviceIdType.MESH
VMEM_SPEC = pl.BlockSpec(memory_space=pltpu.VMEM)
HBM_SPEC = pl.BlockSpec(memory_space=pltpu.HBM)
epsilon = 1e-05


def f32(a):
    return a.astype(jnp.float32)


def b16(a):
    return a.astype(jnp.bfloat16)


def norm_rows(values_in, gain_row, bias_row):
    row_mean = jnp.mean(values_in, axis=-1, keepdims=True)
    centered = values_in - row_mean
    spread = jnp.mean(centered * centered, axis=-1, keepdims=True)
    return centered * lax.rsqrt(spread + epsilon) * gain_row + bias_row


def dot_rows(a, b):
    return jnp.dot(a, b, preferred_element_type=jnp.float32)


def dot_back(a, b):
    return lax.dot_general(a, b, (((1,), (1,)), ((), ())), preferred_element_type=jnp.float32)


def dot_over(a, b):
    return lax.dot_general(a, b, (((0,), (0,)), ((), ())), preferred_element_type=jnp.float32)


def exchange(axis, index, count, source, landing, send_sem, recv_sem):
    copies = []
    for j in range(1, count):
        peer = lax.rem(index + j, count)
        copies.append(
            pltpu.make_async_remote_copy(
                src_ref=source,
                dst_ref=landing.at[index],
                send_sem=send_sem.at[j],
                recv_sem=recv_sem.at[j],
                device_id={axis: peer},
                device_id_type=MESH,
            )
        )
    return copies


def sum_slots(ref, count):
    total = ref[0]
    for j in range(1, count):
        total = total + ref[j]
    return total


class Loads:
    def __init__(self, sem, pairs):
        self.open = []
        for at, (src, dst) in enumerate(pairs):
            copy = pltpu.make_async_copy(src, dst, sem.at[at])
            copy.start()
            self.open.append(copy)

    def need(self, *which):
        for at in which:
            if self.open[at] is not None:
                self.open[at].wait()
                self.open[at] = None


class Flush:
    def __init__(self, sem):
        self.sem, self.open = sem, []

    def go(self, src, dst):
        copy = pltpu.make_async_copy(src, dst, self.sem.at[len(self.open)])
        copy.start()
        self.open.append(copy)

    def settle(self):
        for copy in self.open:
            copy.wait()


class Chunk:
    def __init__(self, at, source, row, rows, columns, first, count):
        self.at, self.source, self.row, self.rows, self.columns = at, source, row, rows, columns
        extra = [(1 << k, k) for k in range(3, count.bit_length() - 1)]
        line = (6, 1)
        self.halved = first == "half"
        if first == "near":
            self.pre, self.post = [(1, 0)], [line] + extra
        elif self.halved:
            self.pre, self.post = [], [line] + extra
        else:
            self.pre, self.post = [], [line, (1, 0)] + extra
        size, self.landings = rows, []
        for _ in self.pre:
            size //= 2
            self.landings.append((size, columns))
        self.landings.append((size, columns))
        for _ in self.post:
            size //= 2
            self.landings.append((size, columns))
        self.steps = len(self.landings)


def bit_of(value, k):
    return lax.rem(lax.div(value, 1 << k), 2)


def flip_bits(value, mask):
    out = value
    k = 0
    while (1 << k) <= mask:
        if mask & (1 << k):
            out = out + (1 - 2 * bit_of(value, k)) * (1 << k)
        k += 1
    return out


class Mover:
    def __init__(self, chunk, batch, source, base, held, landings, sems, finish, early):
        self.c, self.b = chunk, batch
        self.source, self.base, self.held, self.landings, self.sems = source, base, held, landings, sems
        lo, hi = bit_of(batch, 1), bit_of(batch, 2)
        self.inner = lo != hi
        self.ended = lo == hi
        self.finish, self.early = finish, early
        self.build()

    def copy(self, at, src, dst, mask):
        send, recv = self.sems
        return pltpu.make_async_remote_copy(
            src_ref=src,
            dst_ref=dst,
            send_sem=send.at[self.c.at, at],
            recv_sem=recv.at[self.c.at, at],
            device_id={"batch": flip_bits(self.b, mask)},
            device_id_type=MESH,
        )

    def build(self):
        c = self.c
        held = self.held
        here, base = self.source, self.base
        off, size, step = 0, c.rows, 0
        plan, trail = [], []
        if c.halved:
            trail.append(("all", 1, off, size))
        sequence = [("all",) + p for p in c.pre] + [("fold", 2, None)]
        sequence += [("inner",) + p for p in c.post]
        for kind, mask, sel in sequence:
            landing = self.landings[step]
            if kind == "fold":
                own = row_view(here, base, size)
                cp = self.copy(step, own, landing, mask)
            else:
                size //= 2
                mine = bit_of(self.b, sel)
                cp = self.copy(step, row_view(here, base + (1 - mine) * size, size), landing, mask)
                own = row_view(here, base + mine * size, size)
                off = off + mine * size
            trail.append((kind, mask, off, size))
            step += 1
            out = landing if step < len(sequence) else held(off, size)
            plan.append((kind, cp, (own, landing, out)))
            here, base = landing, 0
        for kind, mask, off, size in reversed(trail):
            cp = self.copy(step, held(off, size), held(off, size), mask)
            plan.append(("unfold" if kind == "fold" else kind, cp, None))
            step += 1
        self.plan = plan
        self.depth = len(plan) + len(self.early)

    def begin(self, k):
        kind, cp, _ = self.plan[k]
        if kind == "all":
            cp.start()
        elif kind == "fold":
            pl.when(self.ended)(cp.start)
        else:
            pl.when(self.inner)(cp.start)

    def end(self, k):
        kind, cp, add = self.plan[k]

        def gather():
            if add is not None:
                own, landing, out = add
                out[...] = b16(f32(own[...]) + f32(landing[...]))

        if kind == "all":
            cp.wait()
            gather()
        elif kind in ("fold", "unfold"):
            sender, taker = (
                (self.ended, self.inner) if kind == "fold" else (self.inner, self.ended)
            )
            pl.when(sender)(cp.wait_send)

            @pl.when(taker)
            def _():
                cp.wait_recv()
                gather()
        else:

            @pl.when(self.inner)
            def _():
                cp.wait()
                gather()

    def advance(self, k):
        if k < len(self.early):
            self.early[k]()
            return
        k -= len(self.early)
        if k > 0:
            self.end(k - 1)
        elif self.early:
            self.settle_early()
        if k < len(self.plan):
            self.begin(k)
        else:
            self.finish(self.c)


def row_view(ref, start, size):
    start = start if isinstance(start, int) else pl.multiple_of(start, 16 if size % 16 == 0 else 8)
    return ref.at[pl.ds(start, size)]


def column_block(index, columns):
    return pl.ds(pl.multiple_of(index * columns, 128), columns)


class Rider:
    def __init__(self, batch, send, recv, first):
        self.b, self.send, self.recv, self.at = batch, send, recv, first

    def go(self, src, dst, bit):
        copy = pltpu.make_async_remote_copy(
            src_ref=src, dst_ref=dst, send_sem=self.send.at[self.at], recv_sem=self.recv.at[self.at],
            device_id={"batch": flip_bits(self.b, 1 << bit)}, device_id_type=MESH,
        )
        self.at += 1
        copy.start()
        return copy

    def halve_pieces(self, source, landing, bit, pieces, half):
        size = half // pieces
        mine = bit_of(self.b, bit)
        copies = []

        def start(p):
            copies.append(
                self.go(
                    row_view(source, (1 - mine) * half + p * size, size), row_view(landing, p * size, size), bit
                )
            )

        def settle():
            for copy in copies:
                copy.wait()

        return start, settle, row_view(source, mine * half, half)

    def halve(self, source, landing, bit):
        half = landing.shape[0]
        mine = bit_of(self.b, bit)
        copy = self.go(row_view(source, (1 - mine) * half, half), landing, bit)

        def end():
            copy.wait()
            own = row_view(source, mine * half, half)
            landing[...] = b16(f32(own[...]) + f32(landing[...]))

        return end

    def double(self, source, target, bit):
        half = source.shape[0]
        there = row_view(target, bit_of(self.b, bit) * half, half)
        copy = self.go(source, there, bit)
        there[...] = source[...]
        return copy.wait

    def chain(self, refs, bits, move):
        ends, stages = [], []
        for i, bit in enumerate(bits):

            def stage(i=i, bit=bit):
                if ends:
                    ends.pop()()
                ends.append(move(refs[i], refs[i + 1], bit))

            stages.append(stage)
        stages.append(lambda: ends.pop()())
        return stages


def ride_orders(count):
    bits = list(range(count.bit_length() - 1))
    return bits, [1, 0] + bits[2:]


def tail_body(specs, chunks, ns, nb, n_in, n_out, *refs):
    (one_sums, mix_sums, two_sums, conv_sums, own_sums), refs = refs[:5], refs[5:]
    given, refs = refs[: n_in + 2], refs[n_in + 2 :]
    outs_hbm, refs = refs[:n_out], refs[n_out:]
    (o_gains, o_biases, o_taps, o_hidden), refs = refs[:4], refs[4:]
    send, recv, turn_send, turn_recv, pre_send, pre_recv, ride_send, ride_recv = refs[:8]
    ss, rs, sb, rb, wide, land_s, mid, land_b, ride_fin, load_sem = refs[8:18]
    shard, batch = lax.axis_index("shard"), lax.axis_index("batch")
    flush = Flush(refs[18])
    outs = refs[19 : 19 + n_out]
    rest = list(refs[19 + n_out :])
    pairs, ins, blocks = [], [], {}
    for i, ref in enumerate(given):
        if i < n_in and specs["arrays"][i][0] == "gather":
            pair = []
            for index in (shard, flip_bits(shard, 2)):
                held_block = rest.pop(0)
                pairs.append((ref.at[:, column_block(index, held_block.shape[1])], held_block))
                pair.append(held_block)
            blocks[i] = (pair, (len(pairs) - 2, len(pairs) - 1))
            ins.append(ref)
        else:
            held_ref = rest.pop(0)
            pairs.append((ref, held_ref))
            blocks[i] = (None, (len(pairs) - 1,))
            ins.append(held_ref)
    loads = Loads(load_sem, pairs)
    ins, ridden = ins[:n_in], ins[n_in:]
    shard, batch = lax.axis_index("shard"), lax.axis_index("batch")
    barrier = pltpu.get_barrier_semaphore()
    greeted = [{"batch": lax.rem(batch + j, nb)} for j in range(1, nb)]
    greeted += [{"shard": flip_bits(shard, m)} for m in range(1, ns)]
    for device in greeted:
        pl.semaphore_signal(barrier, inc=1, device_id=device, device_id_type=MESH)
    width = own_sums.shape[1]
    for t in range(ns):
        cols = slice(t * width, (t + 1) * width)
        wide[t, 0:3, :] = one_sums[0:3, cols]
        wide[t, 3:6, :] = mix_sums[0:3, cols]
        wide[t, 6:9, :] = two_sums[0:3, cols]
        wide[t, 9:14, :] = conv_sums[0:5, cols]
        wide[t, 14:19, :] = conv_sums[8:13, cols]
        wide[t, 19:21, :] = two_sums[4:6, cols]
        wide[t, 21:24, :] = jnp.zeros((3, width), jnp.float32)
    pl.semaphore_wait(barrier, len(greeted))

    vector_copies = []
    for j in range(1, ns):
        peer = lax.rem(shard + j, ns)
        copy = pltpu.make_async_remote_copy(
            src_ref=wide.at[peer], dst_ref=land_s.at[shard], send_sem=ss.at[j], recv_sem=rs.at[j],
            device_id={"shard": peer}, device_id_type=MESH,
        )
        copy.start()
        vector_copies.append(copy)
    land_s[shard] = wide[shard]

    def vectors_on():
        for copy in vector_copies:
            copy.wait()
        mid[0:24, :] = sum_slots(land_s, ns)
        mid[24:28, :] = own_sums[0:4, :]
        per = one_sums.shape[1] // width
        for t in range(per):
            cols = slice(t * width, (t + 1) * width)
            mid[28 + t : 29 + t, :] = one_sums[3:4, cols]
            mid[28 + per + t : 29 + per + t, :] = two_sums[3:4, cols]
        mid[28 + 2 * per :, :] = jnp.zeros((mid.shape[0] - 28 - 2 * per, width), jnp.float32)
        vector_copies[:] = exchange("batch", batch, nb, mid, land_b, sb, rb)
        for copy in vector_copies:
            copy.start()
        land_b[batch] = mid[...]

    def vectors_out():
        for copy in vector_copies:
            copy.wait()
        vec = sum_slots(land_b, nb)
        row = lambda k: vec[k : k + 1]
        mine = conv_sums[5:7, column_block(shard, width)]
        gains = [row(0), row(3), row(9), mine[0:1], row(6), row(19)]
        order = [1, 2, 4, 24, 25, 5, 26, 27, 10, 11, 12, None, 13, 7, 8, 20]
        for k, value in enumerate(gains):
            o_gains[k : k + 1, :] = value
        for k, at in enumerate(order):
            o_biases[k : k + 1, :] = mine[1:2] if at is None else row(at)
        o_taps[...] = vec[14:19]
        per = o_hidden.shape[1] // width
        for k in range(2):
            for t in range(per):
                at = 28 + k * per + t
                o_hidden[k : k + 1, t * width : (t + 1) * width] = row(at)

    late = []

    def leave(out, lead, start, rows):
        src, dst = outs[out], outs_hbm[out]
        if lead is not None:
            src, dst = src.at[lead], dst.at[lead]
        flush.go(src.at[pl.ds(start, rows)], dst.at[pl.ds(start, rows)])

    def turn(c_at, total, row, rows, out, lead):
        target = outs[out] if lead is None else outs[out].at[lead]
        columns = target.shape[1]
        height = target.shape[0] // ns
        there = row_view(target, shard * height + row, rows)
        copies = []
        for j in range(1, ns):
            peer = flip_bits(shard, j)
            copy = pltpu.make_async_remote_copy(
                src_ref=total.at[:, column_block(peer, columns)],
                dst_ref=there,
                send_sem=turn_send.at[c_at, j],
                recv_sem=turn_recv.at[c_at, j],
                device_id={"shard": peer},
                device_id_type=MESH,
            )
            copy.start()
            copies.append(copy)
        there[...] = total[:, column_block(shard, columns)]

        def after():
            for copy in copies:
                copy.wait()
            for t in range(ns):
                leave(out, lead, t * height + row, rows)

        late.append(after)

    rides = []
    orders = ride_orders(nb)
    plain_target = outs[0].at[1]
    rider_a = Rider(batch, ride_send, ride_recv, 0)
    rider_b = Rider(batch, ride_send, ride_recv, 1)
    loads.need(*blocks[n_in][1], *blocks[n_in + 1][1])
    end_a = rider_a.double(ridden[0], plain_target, orders[0][0])
    end_b = rider_b.double(ridden[1], ride_fin, orders[1][0])

    movers = []
    for c in chunks:
        kind, out, lead = specs["arrays"][c.source]
        source, base, early, settle = ins[c.source], c.row, [], None
        if kind == "gather":
            near_land, far_land = rest.pop(0), rest.pop(0)
            whole, columns, rows = ins[c.source], c.columns, pl.ds(c.row, c.rows)
            own_block, far_block = blocks[c.source][0]
            state = {}

            def pre(at, src, dst, mask, c=c):
                copy = pltpu.make_async_remote_copy(
                    src_ref=src, dst_ref=dst, send_sem=pre_send.at[c.at, at], recv_sem=pre_recv.at[c.at, at],
                    device_id={"shard": flip_bits(shard, mask)}, device_id_type=MESH,
                )
                copy.start()
                return copy

            def first(near_land=near_land, whole=whole, columns=columns, rows=rows, state=state, pre=pre):
                state["n"] = [
                    pre(i, whole.at[rows, column_block(flip_bits(shard, m), columns)], near_land.at[i], 1)
                    for i, m in enumerate((1, 3))
                ]

            def second(
                near_land=near_land, far_land=far_land, far_block=far_block, rows=rows, state=state, pre=pre,
            ):
                for copy in state["n"]:
                    copy.wait()
                near_land[1] = b16(f32(near_land[1]) + f32(far_block[rows]))
                state["f"] = pre(2, near_land.at[1], far_land, 2)

            def settle(
                near_land=near_land, far_land=far_land, own_block=own_block, rows=rows, state=state,
            ):
                state["f"].wait()
                far_land[...] = b16(
                    f32(far_land[...]) + f32(near_land[0]) + f32(own_block[rows])
                )

            early = [first, second]
            source, base = far_land, 0
        if kind == "turn":
            total = rest.pop(0)
            held = lambda off, size, total=total: row_view(total, off, size)

            def finish(c, total=total, out=out, lead=lead):
                turn(c.at, total, c.row, c.rows, out, lead)
        else:
            target = outs[out] if lead is None else outs[out].at[lead]
            held = lambda off, size, target=target, c=c: row_view(target, c.row + off, size)

            def finish(c, out=out, lead=lead):
                leave(out, lead, c.row, c.rows)

            if c.halved:
                apart = outs[out].shape[-2] // 2
                mine = bit_of(batch, 0) * apart
                held = lambda off, size, target=target, c=c, mine=mine: row_view(target, mine + c.row + off, size)

                def finish(c, out=out, lead=lead, apart=apart):
                    leave(out, lead, c.row, c.rows)
                    leave(out, lead, apart + c.row, c.rows)
        landings = [rest.pop(0) for _ in range(c.steps)]
        m = Mover(c, batch, source, base, held, landings, (send, recv), finish, early)
        m.settle_early = settle
        movers.append(m)
    starts, lag = [], specs["lag"]
    for i, m in enumerate(movers):
        starts.append(max(0, i // lag - len(m.early)))
    rounds = max(s + m.depth + 1 for s, m in zip(starts, movers))
    for r in range(rounds):
        ready, late[:] = late[:], []
        if r == 1:
            vectors_on()
        if r == 1:
            end_b()
            turn(len(chunks), ride_fin, 0, ride_fin.shape[0], 1, 1)
        if r == 3:
            vectors_out()
        if r == 1:
            end_a()
            leave(0, 1, 0, outs[0].shape[1])
        for s, m in zip(starts, movers):
            if 0 <= r - s <= m.depth:
                loads.need(*blocks[m.c.source][1])
                m.advance(r - s)
        for after in ready:
            after()
    for after in late:
        after()
    flush.settle()


def tail_sum(arrays, ridden, sums, kinds, outputs, firsts, chunk_rows, hidden, ident):
    ns, nb = lax.axis_size("shard"), lax.axis_size("batch")
    low, full = jnp.bfloat16, jnp.float32
    chunks = []
    for i, a in enumerate(arrays):
        step = chunk_rows[i]
        columns = a.shape[1] // ns if kinds[i][0] == "gather" else a.shape[1]
        for row in range(0, a.shape[0], step):
            first = "half" if kinds[i][0] == "half" else firsts[len(chunks) % len(firsts)]
            chunks.append(Chunk(len(chunks), i, row, step, columns, first, nb))
    depth = max(2 * c.steps + c.halved for c in chunks)
    specs = dict(arrays=kinds, lag=2)
    width = sums[-1].shape[1]
    per = hidden // width
    small = -(-(28 + 2 * per) // 8) * 8
    dma = pltpu.SemaphoreType.DMA
    n = len(chunks)
    scratch = [
        dma((n, depth)), dma((n, depth)), dma((n + 1, ns)), dma((n + 1, ns)), dma((n, 3)), dma((n, 3)),
        dma((2,)), dma((2,)), dma((ns,)), dma((ns,)), dma((nb,)), dma((nb,)),
        pltpu.VMEM((ns, 24, width), full), pltpu.VMEM((ns, 24, width), full),
        pltpu.VMEM((small, width), full), pltpu.VMEM((nb, small, width), full),
        pltpu.VMEM((2 * ridden[1].shape[0], ridden[1].shape[1]), low),
        dma((2 * len(arrays) + 2,)),
        dma(((ns + 1) * (n + 1) + 1,)),
    ]
    scratch += [pltpu.VMEM(o, low) for o in outputs]
    for i, a in enumerate(list(arrays) + list(ridden)):
        if i < len(arrays) and kinds[i][0] == "gather":
            scratch += [pltpu.VMEM((a.shape[0], a.shape[1] // ns), low)] * 2
        else:
            scratch.append(pltpu.VMEM(a.shape, low))
    for c in chunks:
        if kinds[c.source][0] == "gather":
            scratch += [pltpu.VMEM((2, c.rows, c.columns), low), pltpu.VMEM((c.rows, c.columns), low)]
        if kinds[c.source][0] == "turn":
            scratch.append(pltpu.VMEM((c.rows, c.columns), low))
        scratch += [pltpu.VMEM(shape, low) for shape in c.landings]
    shape = jax.ShapeDtypeStruct
    shapes = [shape(s, low) for s in outputs]
    shapes += [shape((6, width), full), shape((16, width), full), shape((5, width), full), shape((2, hidden), full)]
    operands = list(sums) + list(arrays) + list(ridden)
    return pl.pallas_call(
        functools.partial(tail_body, specs, chunks, ns, nb, len(arrays), len(outputs)),
        out_shape=shapes,
        in_specs=[VMEM_SPEC] * len(sums) + [HBM_SPEC] * (len(arrays) + 2),
        out_specs=[HBM_SPEC] * len(outputs) + [VMEM_SPEC] * 4,
        scratch_shapes=scratch,
        compiler_params=pltpu.CompilerParams(
            collective_id=ident, has_side_effects=True, vmem_limit_bytes=60 << 20
        ),
        name="tail_sum",
    )(*operands)


def widen_body(count, others, slots, *refs):
    n = count + others
    ins, outs = refs[:n], refs[n : 2 * n]
    stages, in_sem, out_sem, pass_sem = refs[2 * n : -3], refs[-3], refs[-2], refs[-1]
    passed = []
    for at in range(others):
        passed.append(pltpu.make_async_copy(ins[count + at], outs[count + at], pass_sem.at[at]))
        passed[-1].start()
    half = len(stages) // 2
    items, used = [], {}
    for src, dst in zip(ins[:count], outs[:count]):
        for lead in range(src.shape[0]) if len(src.shape) == 3 else [None]:
            source = src if lead is None else src.at[lead]
            target = dst if lead is None else dst.at[lead]
            rows, columns = source.shape
            kind = [k.shape[2] for k in stages[:half]].index(columns)
            size = stages[kind].shape[1]
            for row in range(0, rows, size):
                slot = used.get(kind, 0) % slots
                used[kind] = used.get(kind, 0) + 1
                items.append((source.at[pl.ds(row, size)], target.at[pl.ds(row, size)], kind, slot))
    items.sort(key=lambda item: item[2])
    loads, stores = {}, {}

    def load(i):
        if i < len(items):
            source, _, kind, slot = items[i]
            loads[i] = pltpu.make_async_copy(source, stages[kind].at[slot], in_sem.at[kind, slot])
            loads[i].start()

    ahead = slots - 1
    for i in range(ahead):
        load(i)
    for i, (_, target, kind, slot) in enumerate(items):
        loads[i].wait()
        if (kind, slot) in stores:
            stores.pop((kind, slot)).wait()
        narrow, wide = stages[kind].at[slot], stages[half + kind].at[slot]

        @pl.loop(0, narrow.shape[0] // 64)
        def _(k, narrow=narrow, wide=wide):
            part = pl.ds(pl.multiple_of(k * 64, 64), 64)
            wide[part] = f32(narrow[part])

        stores[kind, slot] = pltpu.make_async_copy(wide, target, out_sem.at[kind, slot])
        stores[kind, slot].start()
        load(i + ahead)
    for copy in list(stores.values()) + passed:
        copy.wait()


def widen(arrays, others):
    columns = sorted({a.shape[-1] for a in arrays})
    slots = 6
    least = lambda c: min([a.shape[-2] for a in arrays if a.shape[-1] == c] + [(256 * 1024) // c])
    stages = [pltpu.VMEM((slots, least(c), c), d) for d in (jnp.bfloat16, jnp.float32) for c in columns]
    dma = pltpu.SemaphoreType.DMA
    return pl.pallas_call(
        functools.partial(widen_body, len(arrays), len(others), slots),
        out_shape=[jax.ShapeDtypeStruct(a.shape, jnp.float32) for a in (*arrays, *others)],
        in_specs=[HBM_SPEC] * len(arrays) + [VMEM_SPEC] * len(others),
        out_specs=[HBM_SPEC] * (len(arrays) + len(others)),
        scratch_shapes=stages + [dma((len(columns), slots)), dma((len(columns), slots)), dma((len(others),))],
        compiler_params=pltpu.CompilerParams(vmem_limit_bytes=60 << 20),
        name="widen",
    )(*arrays, *others)


class Links:
    def __init__(self, send, recv):
        self.send, self.recv, self.count = send, recv, 0
        s = lax.axis_index("shard")
        self.shard = s
        self.near = {"shard": flip_bits(s, 1)}
        self.far = {"shard": flip_bits(s, 2)}
        self.across = {"shard": flip_bits(s, 3)}

    def greet(self, devices):
        barrier = pltpu.get_barrier_semaphore()
        for device in devices:
            pl.semaphore_signal(barrier, inc=1, device_id=device, device_id_type=MESH)
        pl.semaphore_wait(barrier, len(devices))

    def go(self, src, dst, device):
        at = self.count
        self.count += 1
        copy = pltpu.make_async_remote_copy(
            src_ref=src, dst_ref=dst, send_sem=self.send.at[at], recv_sem=self.recv.at[at],
            device_id=device, device_id_type=MESH,
        )
        copy.start()
        return copy


def sums_scratch(rows, columns):
    half = rows // 2
    return [
        pltpu.VMEM((2, rows, columns), jnp.float32),
        pltpu.VMEM((4, half, columns), jnp.bfloat16),
        pltpu.VMEM((4, half, columns), jnp.bfloat16),
        pltpu.VMEM((2, half, columns), jnp.bfloat16),
        pltpu.VMEM((2, half, columns), jnp.bfloat16),
    ]


class Sums:
    def __init__(self, links, refs):
        self.links = links
        self.part, self.send, self.land, self.cross, self.land_cross = refs
        self.half = self.send.shape[1]
        self.near, self.crossing, self.backs = None, [], []

    def rows(self, h):
        return slice(h * self.half, (h + 1) * self.half)

    def keep(self, cols, value):
        self.part[0, :, cols] = value

    def keep_far(self, cols, value):
        self.part[1, :, cols] = value

    def give(self, cols, value):
        self.send[0, :, cols] = b16(value[: self.half])
        self.send[1, :, cols] = b16(value[self.half :])

    def give_far(self, cols, value):
        self.send[2, :, cols] = b16(value[: self.half])
        self.send[3, :, cols] = b16(value[self.half :])

    def split(self, h):
        def emit(cols, value):
            self.part[1, self.rows(h), cols] = value[: self.half]
            self.send[2 + h, :, cols] = b16(value[self.half :])

        return emit

    def send_near(self):
        both = pl.ds(0, 2)
        self.near = self.links.go(self.send.at[both], self.land.at[both], self.links.near)

    def send_back(self, h):
        self.backs.append(self.links.go(self.send.at[2 + h], self.land.at[2 + h], self.links.near))

    def send_cross(self, h):
        self.backs[h].wait()
        self.cross[h] = b16(self.part[1, self.rows(h)] + f32(self.land[2 + h]))
        self.crossing.append(self.links.go(self.cross.at[h], self.land_cross.at[h], self.links.far))

    def arrive(self, h):
        if self.near is not None:
            self.near.wait()
            self.near = None
        self.crossing[h].wait()
        return self.part[0, self.rows(h)] + f32(self.land[h]) + f32(self.land_cross[h])


def gather_work_scatter(links, x, fill, work, refs):
    sums = Sums(links, refs)
    half = x.shape[1] // 2
    out = []
    for h in range(2):
        fill(h)
        out.append(links.go(x.at[0, pl.ds(h * half, half)], x.at[2 + h, pl.ds(0, half)], links.far))
    near = links.go(x.at[0], x.at[1], links.near)
    work(0, sums.keep)
    near.wait()
    work(1, sums.give)
    sums.send_near()
    for h in range(2):
        out[h].wait()
        on = links.go(x.at[2 + h, pl.ds(0, half)], x.at[2 + h, pl.ds(half, half)], links.near)
        on.wait()
        work(2 + h, sums.split(h))
        sums.send_back(h)
        sums.send_cross(h)
    return sums


def tiles(total, size):
    def over(body):
        pl.loop(0, total // size)(
            lambda n: body(pl.ds(pl.multiple_of(n * size, size), size))
        )

    return over


def norm_parts(rows):
    row_mean = jnp.mean(rows, axis=-1, keepdims=True)
    centered = rows - row_mean
    inverse = lax.rsqrt(jnp.mean(centered * centered, axis=-1, keepdims=True) + epsilon)
    return centered * inverse, inverse


def norm_slope(grad, scaled, inverse, gain):
    inner = grad * gain
    return inverse * (
        inner
        - jnp.mean(inner, axis=-1, keepdims=True)
        - scaled * jnp.mean(inner * scaled, axis=-1, keepdims=True)
    )


def column_sum(value):
    return jnp.sum(value, axis=0, keepdims=True)


def ffn_up(hid, act, slope, w_in, b_ref, which):
    def run(block):
        @tiles(w_in.shape[1], 512)
        def _(cols):
            pre = dot_rows(hid[block], w_in[:, cols]) + f32(b_ref[which : which + 1, cols])
            gate = jax.nn.sigmoid(pre)
            act[block, :, cols] = b16(pre * gate)
            slope[block, :, cols] = b16(gate * (1.0 + pre * (1.0 - gate)))

    return run


def ffn_down(act, w_rows):
    def run(block, emit):
        @tiles(w_rows.shape[1], 512)
        def _(cols):
            emit(cols, dot_rows(act[block], w_rows[:, cols]))

    return run


def ffn_inward(grad, inner, slope, w_in, w_rows):
    def run(block, emit):
        @tiles(w_in.shape[1], 512)
        def _(cols):
            wide = dot_back(grad[block], w_rows[cols, :])
            inner[block, :, cols] = b16(wide * f32(slope[block, :, cols]))

        @tiles(w_in.shape[0], 512)
        def _(cols):
            emit(cols, dot_back(inner[block], w_in[cols, :]))

    return run


def flat(ref):
    return ref[...].reshape(ref.shape[0] * ref.shape[1], ref.shape[2])


def flat_columns(ref, cols, size):
    return ref[:, :, cols].reshape(ref.shape[0] * ref.shape[1], size)


def weight_out(act, grad, gw_out):
    @tiles(act.shape[2], 256)
    def _(cols):
        gw_out[cols, :] = b16(dot_over(flat_columns(act, cols, 256), flat(grad)))


def weight_in(hid, inner, gw_in, sums_ref):
    @tiles(inner.shape[2], 256)
    def _(cols):
        right = flat_columns(inner, cols, 256)
        gw_in[:, cols] = b16(dot_over(flat(hid), right))
        sums_ref[3:4, cols] = column_sum(f32(right))


class Fetch:
    def __init__(self, links, batch, local_sem):
        self.links, self.local_sem = links, local_sem
        self.quarter = bit_of(batch, 0) + 2 * bit_of(batch, 1)
        self.peers = [{"batch": flip_bits(batch, 1)}, {"batch": flip_bits(batch, 2)}]

    def flow(self, source_rows, target, blocks, rows):
        links, size, held = self.links, rows // 8, {}
        span = lambda q, p: pl.ds(pl.multiple_of(q * (2 * size) + p * size, 16), size)
        mine = self.quarter
        own = blocks[0]

        def first():
            for p in range(2):
                for t, device, _ in blocks[1:]:
                    held["y", p, t] = links.go(
                        source_rows(t, mine * (2 * size) + p * size, size),
                        target.at[span(mine, p), own],
                        device,
                    )

        def pass_on(p, q, t, block, way):
            there = target.at[span(q, p), block]
            return links.go(there, there, self.peers[way])

        def second(p):
            def run():
                for t, _, block in blocks[1:]:
                    held["y", p, t].wait()
                    held["a", p, t] = pass_on(p, mine, t, block, p)

            return run

        def third(p):
            def run():
                other = flip_bits(mine, 1 << p)
                for t, _, block in blocks[1:]:
                    held["a", p, t].wait()
                    held["b", p, t] = pass_on(p, mine, t, block, 1 - p)
                    held["c", p, t] = pass_on(p, other, t, block, 1 - p)

            return run

        def last():
            for p in range(2):
                for t, _, _ in blocks[1:]:
                    held["b", p, t].wait()
                    held["c", p, t].wait()

        return [first, second(0), second(1), third(0), third(1), last]

    def columns(self, source, target, at):
        links, (rows, columns) = self.links, source.shape
        far = flip_bits(links.shard, 2)
        own = column_block(links.shard, columns)
        far_block = column_block(far, columns)
        row = lambda t, start, size: source.at[pl.ds(pl.multiple_of(start, 16), size)]
        stages = self.flow(row, target, [own, (2, links.far, far_block)], rows)
        held = {}

        def first():
            stages[0]()
            held["own"] = pltpu.make_async_copy(source, target.at[:, own], self.local_sem.at[at])
            held["own"].start()
            held["near"] = links.go(source, target.at[:, own], links.near)

        def pass_near():
            stages[-1]()
            held["on"] = links.go(target.at[:, far_block], target.at[:, far_block], links.near)

        def finish():
            held["on"].wait()
            held["near"].wait()
            held["own"].wait()

        return [first] + stages[1:-1] + [pass_near, finish]

    def rows(self, source, target, at):
        links, rows = self.links, target.shape[0]
        columns = source.shape[1]
        index = [flip_bits(links.shard, m) for m in range(4)]
        own = column_block(links.shard, columns)
        row = lambda m, start, size: source.at[pl.ds(pl.multiple_of(index[m] * rows + start, 16), size)]
        blocks = [own] + [
            (m, device, column_block(index[m], columns)) for m, device in ((2, links.far), (3, links.across))
        ]
        stages = self.flow(row, target, blocks, rows)
        held = {}

        def first():
            stages[0]()
            held["own"] = pltpu.make_async_copy(row(0, 0, rows), target.at[:, own], self.local_sem.at[at])
            held["own"].start()
            held["near"] = links.go(row(1, 0, rows), target.at[:, own], links.near)

        def last():
            stages[-1]()
            held["near"].wait()
            held["own"].wait()

        return [first] + stages[1:-1] + [last]


def vector_row(pack, row):
    return f32(jnp.concatenate([pack[t, row : row + 1, :] for t in range(pack.shape[0])], 1))

def link_scratch(count, local):
    return [
        pltpu.SemaphoreType.DMA((count,)),
        pltpu.SemaphoreType.DMA((count,)),
        pltpu.SemaphoreType.DMA((local,)),
    ]


def front_body(
    heads, size,
    rows_ref, gains_ref, own_ref, taps_ref, b_ref, base_ref, length_ref,
    pos_hbm, qkv_hbm, ffn_in, ffn_out, out_proj, conv_in, conv_out,
    one_ref, two_ref, pack, table, proj, with_u, with_v, key, value, mix, wc_in, w_mine, wc_out, w_rows_two,
    hid_out, act_out, slope_out, w_rows_out, hidden_out, soft_out,
    hid, act, slope, w_rows, w_in, w_out, pos_ref, w_qkv, hid_b, soft_ref, turned,
    part, send, land, cross, land_cross, send_sem, recv_sem, local_sem, load_sem, flush_sem, pack_in,
):
    batch = lax.axis_index("batch")
    links = Links(send_sem, recv_sem)
    fetch = Fetch(links, batch, local_sem)
    flush = Flush(flush_sem)
    pack_in[0:6, :] = gains_ref[...]
    pack_in[6:22, :] = own_ref[...]
    pack_in[22:27, :] = taps_ref[...]
    pack_in[27:32, :] = b16(jnp.full((5, pack_in.shape[1]), length_ref[0], jnp.int32).astype(jnp.float32))
    loads = Loads(load_sem, [(ffn_in.at[0], w_in), (pos_hbm, pos_ref), (qkv_hbm, w_qkv)])
    links.greet([links.near, links.far, links.across] + fetch.peers)
    small = [
        links.go(pack_in, pack.at[links.shard], device)
        for device in (links.far, links.across, links.near)
    ]
    down = fetch.rows(ffn_out.at[0], w_rows, 0)
    down.pop(0)()
    pack[links.shard] = pack_in[...]
    for copy in small:
        copy.wait()
    rows, features = rows_ref.shape
    hid[0] = b16(norm_rows(rows_ref[...], vector_row(pack, 0), vector_row(pack, 6)))
    half = rows // 2
    out = [
        links.go(hid.at[0, pl.ds(h * half, half)], hid.at[2 + h, pl.ds(0, half)], links.far)
        for h in range(2)
    ]
    near = links.go(hid.at[0], hid.at[1], links.near)
    up = ffn_up(hid, act, slope, w_in, b_ref, 0)
    loads.need(0)
    up(0)
    down.pop(0)()
    down.pop(0)()
    near.wait()
    up(1)
    lanes = features // 2

    @pl.loop(0, table.shape[0] // 16)
    def _(i):
        at = pl.ds(pl.multiple_of(i * 16, 16), 16)
        s_a, c_a = base_ref[pl.ds(16 + i, 1), 0:lanes], base_ref[pl.ds(16 + i, 1), lanes:]
        s_b, c_b = base_ref[0:16, 0:lanes], base_ref[0:16, lanes:]
        table[at, 0:lanes] = b16(s_a * c_b + c_a * s_b)
        table[at, lanes:] = b16(c_a * c_b - s_a * s_b)

    loads.need(1)
    proj[...] = b16(dot_rows(table[...], pos_ref[...]))
    down.pop(0)()
    down.pop(0)()
    other = fetch.columns(out_proj, w_out, 1)
    leaving = fetch.columns(conv_in, wc_in, 3)
    second = fetch.rows(ffn_out.at[1], w_rows_two, 4)
    for h in range(2):
        out[h].wait()
        on = links.go(hid.at[2 + h, pl.ds(0, half)], hid.at[2 + h, pl.ds(half, half)], links.near)
        on.wait()
        if h == 1:
            other.pop(0)()
        up(2 + h)
    leaving.pop(0)()
    for pair in ((hid, hid_out), (act, act_out), (slope, slope_out)):
        flush.go(*pair)
    while down:
        down.pop(0)()
    flush.go(w_rows, w_rows_out)
    sums = Sums(links, (part, send, land, cross, land_cross))
    work = ffn_down(act, w_rows)
    for h in range(2):
        work(2 + h, sums.split(h))
        sums.send_back(h)
    for h in range(2):
        sums.send_cross(h)
    second.pop(0)()
    work(1, sums.give)
    sums.send_near()
    work(0, sums.keep)
    for _ in range(4):
        other.pop(0)()
        leaving.pop(0)()

    out_bias, gain, shift = vector_row(pack, 7), vector_row(pack, 1), vector_row(pack, 8)
    out = []
    for h in range(2):
        at = slice(h * half, (h + 1) * half)
        one = rows_ref[at] + 0.5 * (sums.arrive(h) + out_bias)
        one_ref[at] = one
        hid_b[0, at] = b16(norm_rows(one, gain, shift))
        there = pl.ds(h * half, half)
        out.append(links.go(hid_b.at[0, there], hid_b.at[2, there], links.far))
    near = links.go(hid_b.at[0], hid_b.at[1], links.near)
    while other:
        other.pop(0)()
        leaving.pop(0)()
    entering = fetch.columns(conv_out, wc_out, 2)
    own = f32(own_ref[...])
    keys = f32(lax.broadcasted_iota(jnp.int32, (rows, rows), 1))
    scale = 1.0 / math.sqrt(size)
    loads.need(2)

    def attend(slot):
        hidden = hid_b[slot]
        query = dot_rows(hidden, w_qkv[0]) + own[3:4]
        with_u[slot] = b16(query + own[6:7])
        with_v[slot] = b16(query + own[7:8])
        key[slot] = b16(dot_rows(hidden, w_qkv[1]))
        value[slot] = b16(dot_rows(hidden, w_qkv[2]) + own[4:5])
        live = f32(pack[flip_bits(links.shard, slot), 27:28, 0:1])
        for h in range(heads):
            cols = slice(h * size, (h + 1) * size)
            wide = dot_back(with_v[slot, :, cols], proj[:, cols])
            moved = pltpu.roll(wide, rows + 1, 1, stride=1, stride_axis=0)[:, :rows]
            raw = dot_back(with_u[slot, :, cols], key[slot, :, cols]) + moved
            scores = jnp.where(keys < live, raw * scale, -1e30)
            grown = jnp.exp(scores - jnp.max(scores, axis=-1, keepdims=True))
            soft = grown / jnp.sum(grown, axis=-1, keepdims=True)
            soft_ref[slot, :, h * rows : (h + 1) * rows] = soft
            mix[slot, :, cols] = b16(dot_rows(b16(soft), value[slot, :, cols]))

    last = []
    attend(0)
    turned[links.shard] = mix[0]
    near.wait()
    second.pop(0)()
    second.pop(0)()
    attend(1)
    second.pop(0)()
    second.pop(0)()
    last.append(links.go(mix.at[1], turned.at[links.shard], links.near))
    on = []
    for h in range(2):
        out[h].wait()
        there = pl.ds(h * half, half)
        on.append(links.go(hid_b.at[2, there], hid_b.at[3, there], links.near))
        if h == 0:
            entering.pop(0)()
    attend(2)
    last.append(links.go(mix.at[2], turned.at[links.shard], links.far))
    entering.pop(0)()
    entering.pop(0)()
    for copy in on:
        copy.wait()
    flush.go(hid_b, hidden_out)
    attend(3)
    last.append(links.go(mix.at[3], turned.at[links.shard], links.across))
    flush.go(soft_ref, soft_out)
    entering.pop(0)()
    entering.pop(0)()
    for copy in last:
        copy.wait()
    width = mix.shape[2]
    total = one_ref[...] + vector_row(pack, 11)
    for t in range(turned.shape[0]):
        total = total + dot_rows(turned[t], w_out[t * width : (t + 1) * width])
    two_ref[...] = total
    w_mine[...] = w_out[pl.ds(pl.multiple_of(links.shard * width, 16), width), :]
    while entering:
        entering.pop(0)()
    while second:
        second.pop(0)()
    flush.settle()


def front(
    rows_in, gains, own_biases, taps, lengths, b_in, base, pos_proj, qkv_proj, ffn_in, ffn_out, out_proj, conv_in,
    conv_out, heads, ident,
):
    ns = lax.axis_size("shard")
    rows, features = rows_in.shape
    hidden = ffn_in.shape[2]
    width = features // ns
    low, full = jnp.bfloat16, jnp.float32
    shape, vmem = jax.ShapeDtypeStruct, pltpu.VMEM
    narrow = shape((ns, rows, width), low)
    dma = pltpu.SemaphoreType.DMA
    return pl.pallas_call(
        functools.partial(front_body, heads, width // heads),
        out_shape=[
            shape((rows, features), full), shape((rows, features), full),
            shape((ns, 32, width), low),
            shape((2 * rows, features), low), shape((2 * rows, width), low),
            narrow, narrow, narrow, narrow, narrow,
            shape((conv_in.shape[0], ns * conv_in.shape[1]), low),
            shape((width, features), low),
            shape((features, features), low),
            shape((hidden, features), low),
            shape((4, rows, features), low), shape((4, rows, hidden), low), shape((4, rows, hidden), low),
            shape((hidden, features), low),
            shape((ns, rows, features), low),
            shape((ns, rows, heads * rows), full),
        ],
        in_specs=[VMEM_SPEC] * 6 + [pl.BlockSpec(memory_space=pltpu.SMEM)] + [HBM_SPEC] * 7,
        out_specs=[VMEM_SPEC] * 14 + [HBM_SPEC] * 6,
        scratch_shapes=[
            vmem((4, rows, features), low), vmem((4, rows, hidden), low), vmem((4, rows, hidden), low),
            vmem((hidden, features), low), vmem((features, hidden), low), vmem((features, features), low),
            vmem(pos_proj.shape, low), vmem(qkv_proj.shape, low),
            vmem((ns, rows, features), low), vmem((ns, rows, heads * rows), full), vmem((ns, rows, width), low),
        ]
        + sums_scratch(rows, features)
        + link_scratch(100, 5)
        + [dma((3,)), dma((6,)), vmem((32, width), low)],
        compiler_params=pltpu.CompilerParams(
            collective_id=ident, has_side_effects=True, vmem_limit_bytes=60 << 20
        ),
        name="front",
    )(
        rows_in, gains, own_biases, taps, b_in, base, lengths, pos_proj, qkv_proj, ffn_in, ffn_out, out_proj,
        conv_in, conv_out,
    )


def pack_rows(ref, at, row):
    for i in range(row.shape[1] // 128):
        ref[at + i : at + i + 1, :] = row[:, i * 128 : (i + 1) * 128]


def unpack_rows(value, at, lanes):
    return jnp.concatenate([value[at + i : at + i + 1, :] for i in range(lanes)], 1)


def everywhere(links, nb, source, mid, land_s, land_b, result, small, sems):
    s, b = links.shard, lax.axis_index("batch")
    ns = land_s.shape[0]
    ss, rs, sb, rb = sems
    first = exchange("shard", s, ns, source, land_s, ss, rs)
    for copy in first:
        copy.start()
    land_s[s] = source[...]
    for copy in first:
        copy.wait()
    mid[...] = sum_slots(land_s, ns)
    second = exchange("batch", b, nb, mid, land_b, sb, rb)
    for copy in second:
        copy.start()
    land_b[b] = mid[...]
    small()
    for copy in second:
        copy.wait()
    return sum_slots(land_b, nb)


def conv_part(
    links, nb, loads, rows_ref, pack, w_in, w_out,
    out_ref, hid, open_ref, gate_ref, gated_ref, scaled_ref, act, slope, stats,
    padded, source, mid, land_s, land_b, sems,
):
    rows, features = rows_ref.shape
    live = f32(pack[links.shard, 27:28, 0:1])
    mask = f32(f32(lax.broadcasted_iota(jnp.int32, (rows, 1), 0)) < live)
    hid[...] = b16(norm_rows(rows_ref[...], vector_row(pack, 2), vector_row(pack, 14)))
    bias_v, bias_g = vector_row(pack, 15), vector_row(pack, 16)
    loads.need(0)
    lead = 8
    tile = 512
    padded[0:lead, :] = jnp.zeros((lead, features), jnp.float32)
    padded[lead + rows :, :] = jnp.zeros((lead, features), jnp.float32)
    for n in range(features // tile):
        cols = slice(n * tile, (n + 1) * tile)
        left = dot_rows(hid[...], w_in[:, cols]) + bias_v[:, cols]
        right = dot_rows(hid[...], w_in[:, features + n * tile : features + (n + 1) * tile])
        gate = jax.nn.sigmoid(right + bias_g[:, cols])
        opened = gate * mask
        gated = left * opened
        open_ref[:, cols] = b16(opened)
        gate_ref[:, cols] = b16(gated * (1.0 - gate))
        gated_ref[:, cols] = b16(gated)
        padded[lead : lead + rows, cols] = gated
    taps = 5
    total = 0.0
    for k in range(taps):
        at = lead - (taps - 1) // 2 + k
        total = total + padded[at : at + rows, :] * vector_row(pack, 22 + k)
    live_total = total * mask
    lanes = features // 128
    pack_rows(source, 0, jnp.sum(live_total, axis=0, keepdims=True))
    pack_rows(source, lanes, jnp.sum(live_total * total, axis=0, keepdims=True))
    source[2 * lanes : 2 * lanes + 8, :] = jnp.broadcast_to(live, (8, 128))
    scaled_ref[...] = total
    sums = everywhere(links, nb, source, mid, land_s, land_b, None, lambda: None, sems)
    frames = sums[2 * lanes : 2 * lanes + 1, 0:1]
    mean = unpack_rows(sums, 0, lanes) / frames
    inverse = lax.rsqrt(unpack_rows(sums, lanes, lanes) / frames - mean * mean + epsilon)
    stats[0:1, :] = inverse
    stats[1:2, :] = jnp.broadcast_to(frames, (1, features))
    stats[2:8, :] = jnp.zeros((6, features), jnp.float32)
    scaled = (scaled_ref[...] - mean) * inverse
    scaled_ref[...] = scaled
    normed = scaled * vector_row(pack, 3) + vector_row(pack, 17)
    gate = jax.nn.sigmoid(normed)
    act[...] = b16(normed * gate)
    slope[...] = b16(gate * (1.0 + normed * (1.0 - gate)))
    loads.need(1)
    out_ref[...] = rows_ref[...] + (dot_rows(act[...], w_out[...]) + vector_row(pack, 18))


def middle_part(
    links, loads, riders, rows_ref, pack, b_ref, result, out_ref, gw_in, gw_out, sums_ref,
    hid, act, slope, grad, inner, w_in, w_rows, cotangent, stream, first, second,
):
    rows, features = rows_ref.shape
    half = rows // 2
    gain, shift = vector_row(pack, 4), vector_row(pack, 19)

    def fill(h):
        at = slice(h * half, (h + 1) * half)
        hid[0, at] = b16(norm_rows(rows_ref[at], gain, shift))

    up, down = ffn_up(hid, act, slope, w_in, b_ref, 1), ffn_down(act, w_rows)

    def work(block, emit):
        loads.need(2)
        up(block)
        loads.need(3)
        down(block, emit)

    sums = gather_work_scatter(links, hid, fill, work, first)
    last_gain, last_shift, out_bias = vector_row(pack, 5), vector_row(pack, 21), vector_row(pack, 20)
    live = f32(pack[links.shard, 27:28, 0:1])
    mask = f32(f32(lax.broadcasted_iota(jnp.int32, (rows, 1), 0)) < live)
    loads.need(4)
    ends = []

    def turn_back(h):
        at = slice(h * half, (h + 1) * half)
        scaled, inverse = norm_parts(rows_ref[at] + 0.5 * (sums.arrive(h) + out_bias))
        result[at] = (scaled * last_gain + last_shift) * mask[at]
        given = cotangent[at] * mask[at]
        slide = norm_slope(given, scaled, inverse, last_gain)
        stream[at] = slide
        grad[0, at] = b16(0.5 * slide)
        ends.append((column_sum(given * scaled), column_sum(given)))

    back = gather_work_scatter(
        links, grad, turn_back, ffn_inward(grad, inner, slope, w_in, w_rows), second
    )
    weight_out(act, grad, gw_out)
    for p in range(EARLY):
        riders[1][0](p)
    weight_in(hid, inner, gw_in, sums_ref)
    for p in range(EARLY):
        riders[0][0](p)
    sums_ref[0:3, :] = jnp.zeros((3, features), jnp.float32)
    sums_ref[2:3, :] = column_sum(f32(grad[0]))
    sums_ref[4:5, :] = ends[0][0] + ends[1][0]
    sums_ref[5:6, :] = ends[0][1] + ends[1][1]
    sums_ref[6:8, :] = jnp.zeros((2, features), jnp.float32)
    for h in range(2):
        at = slice(h * half, (h + 1) * half)
        scaled, inverse = norm_parts(rows_ref[at])
        given = back.arrive(h)
        out_ref[at] = stream[at] + norm_slope(given, scaled, inverse, gain)
        sums_ref[0:1, :] += column_sum(given * scaled)
        sums_ref[1:2, :] += column_sum(given)


def conv_back_part(
    links, nb, ride_on, stream_ref, rows_ref, pack, w_in, w_out,
    hid, open_ref, gate_ref, gated_ref, scaled_ref, act, slope, stats,
    out_ref, gw_out, gw_in, sums_ref,
    padded, normed, grad, inner, source, mid, land_s, land_b, sems,
):
    rows, features = rows_ref.shape
    lanes = features // 128
    lead, tile, taps = 8, 512, 5
    grad[...] = b16(stream_ref[...])
    gain = vector_row(pack, 3)
    sums_ref[...] = jnp.zeros_like(sums_ref)
    for n in range(features // tile):
        cols = slice(n * tile, (n + 1) * tile)
        value = dot_back(grad[...], w_out[cols, :]) * f32(slope[:, cols])
        normed[:, cols] = value
        for at, total in (
            (0, jnp.sum(value, axis=0, keepdims=True)),
            (lanes, jnp.sum(value * scaled_ref[:, cols], axis=0, keepdims=True)),
        ):
            for i in range(tile // 128):
                row = at + n * (tile // 128) + i
                source[row : row + 1, :] = total[:, i * 128 : (i + 1) * 128]

    def meanwhile():
        @tiles(features, 256)
        def _(cols):
            gw_out[cols, :] = b16(dot_over(act[:, cols], grad[...]))

        sums_ref[4:5, :] = jnp.sum(f32(grad[...]), axis=0, keepdims=True)

    sums = everywhere(links, nb, source, mid, land_s, land_b, None, meanwhile, sems)
    beta, gamma = unpack_rows(sums, 0, lanes), unpack_rows(sums, lanes, lanes)
    ride_on()
    sums_ref[5:6, :] = gamma
    sums_ref[6:7, :] = beta
    inverse, frames = stats[0:1, :], stats[1:2, 0:1]
    live = f32(pack[links.shard, 27:28, 0:1])
    mask = f32(f32(lax.broadcasted_iota(jnp.int32, (rows, 1), 0)) < live)
    padded[0:lead, :] = jnp.zeros((lead, features), jnp.float32)
    padded[lead + rows :, :] = jnp.zeros((lead, features), jnp.float32)
    padded[lead : lead + rows, :] = inverse * (
        normed[...] * gain - mask * (gain * beta + scaled_ref[...] * (gain * gamma)) / frames
    )
    given = 0.0
    gated = f32(gated_ref[...])
    for k in range(taps):
        at = lead + (taps - 1) // 2 - k
        moved = padded[at : at + rows, :]
        given = given + moved * vector_row(pack, 22 + k)
        sums_ref[8 + k : 9 + k, :] = jnp.sum(moved * gated, axis=0, keepdims=True)
    left = b16(given * f32(open_ref[...]))
    right = b16(given * f32(gate_ref[...]))
    inner[:, 0:features] = left
    inner[:, features:] = right
    sums_ref[2:3, :] = jnp.sum(f32(left), axis=0, keepdims=True)
    sums_ref[3:4, :] = jnp.sum(f32(right), axis=0, keepdims=True)
    total = dot_back(inner[...], w_in[...])
    scaled, inverse = norm_parts(rows_ref[...])
    out_ref[...] = stream_ref[...] + norm_slope(total, scaled, inverse, vector_row(pack, 2))
    sums_ref[0:1, :] = jnp.sum(total * scaled, axis=0, keepdims=True)
    sums_ref[1:2, :] = jnp.sum(total, axis=0, keepdims=True)

    @tiles(2 * features, 512)
    def _(cols):
        gw_in[:, cols] = b16(dot_over(hid[...], inner[:, cols]))


def centre_body(nb, *refs):
    rows_ref, pack, b_ref, cw_in_hbm, cw_out_hbm, w_rows_hbm, cotangent_hbm, ffn_in, *refs = refs
    result, out_ref, gwc_out, gwc_in, two_sums, conv_sums, half_a, half_b, *refs = refs
    cw_in, cw_out, w_in, w_rows, cotangent, *refs = refs
    three, hid_c, open_ref, gate_ref, gated_ref, scaled_ref, act_c, slope_c, stats, padded, *refs = refs
    hid, act, slope, grad, inner, gw_in, gw_out, stream, between, normed, grad_c, inner_c, *refs = refs
    sums_a, sums_b, (first, second) = refs[:5], refs[5:10], (refs[10:18], refs[18:26])
    send_sem, recv_sem, ride_send, ride_recv, load_sem = refs[26:]
    batch = lax.axis_index("batch")
    links = Links(send_sem, recv_sem)
    loads = Loads(
        load_sem,
        [
            (cw_in_hbm, cw_in), (cw_out_hbm, cw_out), (ffn_in.at[1], w_in), (w_rows_hbm, w_rows),
            (cotangent_hbm, cotangent),
        ],
    )
    links.greet(
        [links.near, links.far, links.across]
        + [{"batch": lax.rem(batch + j, nb)} for j in range(1, nb)]
    )
    saved = (hid_c, open_ref, gate_ref, gated_ref, scaled_ref, act_c, slope_c, stats)
    conv_part(links, nb, loads, rows_ref, pack, cw_in, cw_out, three, *saved, padded, *first[:4], first[4:])
    orders = ride_orders(nb)
    pieces = 4
    riders = [
        Rider(batch, ride_send, ride_recv, at * pieces).halve_pieces(
            source, landing, orders[at][0], pieces, landing.shape[0]
        )
        for at, (source, landing) in enumerate(((gw_in, half_a), (gw_out, half_b)))
    ]
    middle_part(
        links, loads, riders, three, pack, b_ref, result, between, gw_in, gw_out, two_sums,
        hid, act, slope, grad, inner, w_in, w_rows, cotangent, stream, sums_a, sums_b,
    )
    for start, _, _ in riders:
        start(EARLY)

    def ride_on():
        for p in range(EARLY + 1, pieces):
            for start, _, _ in riders:
                start(p)

    conv_back_part(
        links, nb, ride_on, between, rows_ref, pack, cw_in, cw_out, *saved, out_ref, gwc_out, gwc_in, conv_sums,
        padded, normed, grad_c, inner_c, *second[:4], second[4:],
    )
    for (_, settle, own), landing in zip(riders, (half_a, half_b)):
        settle()
        landing[...] = b16(f32(own[...]) + f32(landing[...]))


EARLY = 1


def centre(rows_in, pack, b_in, wc_in, wc_out, w_rows, cotangent, ffn_in, ident):
    ns, nb = lax.axis_size("shard"), lax.axis_size("batch")
    rows, features = rows_in.shape
    hidden = ffn_in.shape[2]
    low, full = jnp.bfloat16, jnp.float32
    shape, vmem, dma = jax.ShapeDtypeStruct, pltpu.VMEM, pltpu.SemaphoreType.DMA
    wide, plain = vmem((4, rows, features), low), vmem((rows, features), low)
    tall = vmem((4, rows, hidden), low)
    whole = vmem((rows, features), full)
    lanes = features // 128

    def exchange_scratch(count):
        small = (count, 128)
        return [
            vmem(small, full), vmem(small, full), vmem((ns,) + small, full), vmem((nb,) + small, full),
            dma((ns,)), dma((ns,)), dma((nb,)), dma((nb,)),
        ]

    return pl.pallas_call(
        functools.partial(centre_body, nb),
        out_shape=[
            shape((rows, features), full), shape((rows, features), full),
            shape((features, features), low), shape((features, 2 * features), low),
            shape((8, features), full), shape((16, features), full),
            shape((features // 2, hidden), low), shape((hidden // 2, features), low),
        ],
        in_specs=[VMEM_SPEC] * 3 + [HBM_SPEC] * 5,
        out_specs=[VMEM_SPEC] * 8,
        scratch_shapes=[
            vmem(wc_in.shape, low), vmem(wc_out.shape, low), vmem((features, hidden), low),
            vmem((hidden, features), low), whole,
            whole, plain, plain, plain, plain, whole, plain, plain, vmem((8, features), full),
            vmem((rows + 16, features), full),
            wide, tall, tall, wide, tall, vmem((features, hidden), low), vmem((hidden, features), low),
            whole, whole, whole, plain, vmem((rows, 2 * features), low),
        ]
        + sums_scratch(rows, features)
        + sums_scratch(rows, features)
        + exchange_scratch(2 * lanes + 8)
        + exchange_scratch(2 * lanes)
        + [dma((20,)), dma((20,)), dma((8,)), dma((8,)), dma((5,))],
        compiler_params=pltpu.CompilerParams(
            collective_id=ident, has_side_effects=True, vmem_limit_bytes=62 << 20
        ),
        name="centre",
    )(rows_in, pack, b_in, wc_in, wc_out, w_rows, cotangent, ffn_in)


def rear_body(
    heads, size, nb, stream_ref, rows_ref, pack, w_mine, ride_a, ride_b,
    hid_b_hbm, with_u_hbm, with_v_hbm, key_hbm, value_hbm, soft_hbm, mix_hbm, table_hbm, proj_hbm, w_qkv_hbm,
    start_hbm, hid_hbm, act_hbm, slope_hbm, w_rows_hbm, ffn_in,
    out_ref, half_q, half_k, half_x, half_pos, gw_mix, mix_sums, own_sums, gw_in, gw_out, sums_ref, out_a, out_b,
    grad, dq, dk, dx, dp, stream, grad_b, inner, start, hid, act, slope, w_rows, w_in,
    hid_b, with_u, with_v, key, value, soft_ref, mix, table, proj, w_qkv, *refs,
):
    first, second, refs = refs[:5], refs[5:10], refs[10:]
    send_sem, recv_sem, ride_send, ride_recv, load_sem, gw_q, gw_k, gw_x, gw_pos, halve_send, halve_recv, *between = refs
    links = Links(send_sem, recv_sem)
    batch = lax.axis_index("batch")
    loads = Loads(
        load_sem,
        [
            (soft_hbm, soft_ref), (value_hbm, value), (key_hbm, key), (with_u_hbm, with_u), (with_v_hbm, with_v),
            (proj_hbm, proj), (w_qkv_hbm, w_qkv), (hid_b_hbm, hid_b), (mix_hbm, mix), (table_hbm, table),
            (slope_hbm, slope), (w_rows_hbm, w_rows), (ffn_in.at[0], w_in), (act_hbm, act), (hid_hbm, hid),
            (start_hbm, start),
        ],
    )
    orders = ride_orders(nb)
    steps = len(orders[0]) - 1
    scale = 1.0 / math.sqrt(size)
    rows, features = rows_ref.shape
    half = rows // 2
    links.greet([links.near, links.far] + [{"batch": flip_bits(batch, 1 << k)} for k in orders[0]])
    inward, outward = [], []
    count = 2 * steps - 1
    for at, (begin, end) in enumerate(((ride_a, out_a), (ride_b, out_b))):
        middle_refs = between[at * count : (at + 1) * count]
        down_refs = [begin, *middle_refs[:steps]]
        up_refs = [*middle_refs[steps - 1 :], end]
        rider = Rider(batch, ride_send, ride_recv, at * 2 * steps)
        inward.append(rider.chain(down_refs, orders[at][1:], rider.halve))
        rider = Rider(batch, ride_send, ride_recv, at * 2 * steps + steps)
        outward.append(rider.chain(up_refs, orders[at][:0:-1], rider.double))

    def tick(chains):
        for chain in chains:
            if chain:
                chain.pop(0)()

    tick(inward)
    grad[0] = b16(stream_ref[...])
    out = [
        links.go(grad.at[0, pl.ds(h * half, half)], grad.at[2, pl.ds(h * half, half)], links.far)
        for h in range(2)
    ]
    near = links.go(grad.at[0], grad.at[1], links.near)
    at_row = lax.broadcasted_iota(jnp.int32, (rows, rows), 0)
    at_col = lax.broadcasted_iota(jnp.int32, (rows, rows), 1)
    flip = b16(f32(at_row + at_col == rows - 1))
    keys = f32(at_col)
    own_sums[...] = jnp.zeros_like(own_sums)

    def work(slot, emit):
        mixed = b16(dot_back(grad[slot], w_mine[...]))
        live = f32(pack[flip_bits(links.shard, slot), 27:28, 0:1])
        for h in range(heads):
            cols = slice(h * size, (h + 1) * size)
            soft = soft_ref[slot, :, h * rows : (h + 1) * rows]
            given = mixed[:, cols]
            grad_soft = dot_back(given, value[slot, :, cols])
            dx[slot, :, cols] = b16(dot_over(b16(soft), given))
            grad_scores = soft * (grad_soft - jnp.sum(grad_soft * soft, axis=-1, keepdims=True))
            raw = b16(jnp.where(keys < live, grad_scores, 0.0) * scale)
            grad_u = dot_rows(raw, key[slot, :, cols])
            dk[slot, :, cols] = b16(dot_over(raw, with_u[slot, :, cols]))
            turned = dot_rows(flip, raw)
            wide = jnp.concatenate([turned, jnp.zeros_like(turned)], 1)
            wide = b16(pltpu.roll(wide, 0, 1, stride=1, stride_axis=0))
            grad_v = dot_rows(wide, proj[:, cols])
            v_turned = b16(dot_rows(flip, with_v[slot, :, cols]))
            dp[slot, :, cols] = b16(dot_over(wide, v_turned))
            own_sums[2:3, cols] += column_sum(grad_u)
            own_sums[3:4, cols] += column_sum(grad_v)
            high = b16(grad_v)
            rest = b16(grad_v - f32(high))
            dq[slot, :, cols] = b16(grad_u + (dot_rows(flip, high) + dot_rows(flip, rest)))
        own_sums[0:1, :] += column_sum(f32(dq[slot]))
        own_sums[1:2, :] += column_sum(f32(dx[slot]))

        @tiles(features, 512)
        def _(cols):
            emit(
                cols,
                dot_back(dq[slot], w_qkv[0, cols, :])
                + dot_back(dk[slot], w_qkv[1, cols, :])
                + dot_back(dx[slot], w_qkv[2, cols, :]),
            )

    sums = Sums(links, first)
    loads.need(*range(7))
    work(0, sums.keep)
    near.wait()
    work(1, sums.give)
    sums.send_near()
    on = []
    for h in range(2):
        out[h].wait()
        there = pl.ds(h * half, half)
        on.append(links.go(grad.at[2, there], grad.at[3, there], links.near))
    tick(inward)
    for copy in on:
        copy.wait()
    work(3, sums.give_far)
    for h in range(2):
        sums.send_back(h)
    work(2, sums.keep_far)
    for h in range(2):
        sums.send_cross(h)
    loads.need(7, 8, 9)
    for ref, target in ((dq, gw_q), (dk, gw_k), (dx, gw_x)):
        right = flat(ref)

        @tiles(features, 256)
        def _(cols, target=target, right=right):
            target[cols, :] = b16(dot_over(flat_columns(hid_b, cols, 256), right))

    @tiles(features, 256)
    def _(cols):
        total = dot_over(table[:, cols], dp[0])
        for slot in range(1, 4):
            total = total + dot_over(table[:, cols], dp[slot])
        gw_pos[cols, :] = b16(total)

    halver = Rider(batch, halve_send, halve_recv, 0)
    halvings = [
        halver.halve(source, landing, 0)
        for source, landing in ((gw_q, half_q), (gw_k, half_k), (gw_x, half_x), (gw_pos, half_pos))
    ]
    gw_mix[...] = b16(dot_over(flat(mix), flat(grad)))
    mix_sums[...] = jnp.zeros_like(mix_sums)
    mix_sums[2:3, :] = column_sum(f32(grad[0]))
    gain = vector_row(pack, 1)

    def fill(h):
        at = slice(h * half, (h + 1) * half)
        given = sums.arrive(h)
        scaled, inverse = norm_parts(rows_ref[at])
        slide = stream_ref[at] + norm_slope(given, scaled, inverse, gain)
        stream[at] = slide
        grad_b[0, at] = b16(0.5 * slide)
        mix_sums[0:1, :] += column_sum(given * scaled)
        mix_sums[1:2, :] += column_sum(given)

    step = ffn_inward(grad_b, inner, slope, w_in, w_rows)

    def back_work(block, emit):
        loads.need(10, 11, 12)
        if block == 1:
            for chain in inward:
                while chain:
                    chain.pop(0)()
            tick(outward)
        step(block, emit)

    back = gather_work_scatter(links, grad_b, fill, back_work, second)
    loads.need(13, 14, 15)
    weight_out(act, grad_b, gw_out)
    tick(outward)
    weight_in(hid, inner, gw_in, sums_ref)
    sums_ref[0:3, :] = jnp.zeros((3, features), jnp.float32)
    sums_ref[2:3, :] = column_sum(f32(grad_b[0]))
    sums_ref[4:8, :] = jnp.zeros((4, features), jnp.float32)
    gain = vector_row(pack, 0)
    for h in range(2):
        at = slice(h * half, (h + 1) * half)
        scaled, inverse = norm_parts(start[at])
        given = back.arrive(h)
        out_ref[at] = stream[at] + norm_slope(given, scaled, inverse, gain)
        sums_ref[0:1, :] += column_sum(given * scaled)
        sums_ref[1:2, :] += column_sum(given)
    for end in halvings:
        end()
    for chain in outward:
        while chain:
            chain.pop(0)()


def rear(stream, rows_one, pack, saved_mix, table, proj, w_qkv, w_mine, ridden, rows_in, saved, w_rows, ffn_in, heads, ident):
    rows, features = rows_one.shape
    hidden = ffn_in.shape[2]
    width = proj.shape[1]
    nb = lax.axis_size("batch")
    steps = nb.bit_length() - 2
    low, full = jnp.bfloat16, jnp.float32
    shape, vmem = jax.ShapeDtypeStruct, pltpu.VMEM
    dma = pltpu.SemaphoreType.DMA
    narrow = vmem((4, rows, width), low)
    between = []
    for r in ridden:
        sizes = [r.shape[0] >> k for k in range(1, steps + 1)]
        between += [vmem((size, r.shape[1]), low) for size in sizes + sizes[-2::-1]]
    return pl.pallas_call(
        functools.partial(rear_body, heads, width // heads, nb),
        out_shape=[
            shape((rows, features), full),
            shape((features // 2, width), low), shape((features // 2, width), low),
            shape((features // 2, width), low), shape((features // 2, width), low),
            shape((width, features), low), shape((8, features), full), shape((8, width), full),
            shape((features, hidden), low), shape((hidden, features), low), shape((8, features), full),
        ]
        + [shape(r.shape, low) for r in ridden],
        in_specs=[VMEM_SPEC] * 6 + [HBM_SPEC] * 16,
        out_specs=[VMEM_SPEC] * 13,
        scratch_shapes=[
            vmem((4, rows, features), low), narrow, narrow, narrow, vmem((4, 2 * rows, width), low),
            vmem((rows, features), full), vmem((4, rows, features), low), vmem((4, rows, hidden), low),
            vmem((rows, features), full), vmem((4, rows, features), low), vmem((4, rows, hidden), low),
            vmem((4, rows, hidden), low), vmem((hidden, features), low), vmem((features, hidden), low),
        ]
        + [vmem(a.shape, a.dtype) for a in (*saved_mix, table, proj, w_qkv)]
        + sums_scratch(rows, features)
        + sums_scratch(rows, features)
        + [dma((24,)), dma((24,)), dma((4 * steps,)), dma((4 * steps,)), dma((16,))]
        + [vmem((features, width), low)] * 4
        + [dma((4,)), dma((4,))]
        + between,
        compiler_params=pltpu.CompilerParams(
            collective_id=ident, has_side_effects=True, vmem_limit_bytes=62 << 20
        ),
        name="rear",
    )(
        stream, rows_one, pack, w_mine, *ridden, *saved_mix, table, proj, w_qkv, rows_in, *saved, w_rows, ffn_in
    )


def body(
    tokens, cotangent, lengths, ffn_in, ffn_out, ffn_bias, qkv_proj, pos_proj, out_proj,
    conv_in, conv_out, depthwise, norm_gains, biases,
):
    _, length, features = tokens.shape
    ns, nb = lax.axis_size("shard"), lax.axis_size("batch")
    width = features // ns
    heads = HEADS // ns
    rows_in = tokens[0]

    rates = jnp.exp(
        jnp.arange(features // 2, dtype=jnp.float32) * (-2.0 * math.log(10000.0) / features)
    )
    turns = jnp.concatenate(
        [
            length - 1.0 - jnp.arange(16, dtype=jnp.float32),
            -16.0 * jnp.arange(2 * length // 16, dtype=jnp.float32),
        ]
    )
    angles = turns[:, None] * rates[None, :]
    base = jnp.concatenate([jnp.sin(angles), jnp.cos(angles)], 1)
    (
        rows_one, rows_two, pack, table, proj, with_u, with_v, key, value, mix, wc_in, w_mine, wc_out,
        w_rows_two, *saved_one, w_rows_one, hidden_mix, soft,
    ) = front(
        rows_in, norm_gains, biases, depthwise, lengths, ffn_bias, base, pos_proj, qkv_proj, ffn_in, ffn_out, out_proj, conv_in, conv_out,
        heads, 5,
    )
    saved_mix = (hidden_mix, with_u, with_v, key, value, soft, mix)
    result, stream, grad_conv_out, grad_conv_in, two_sums, conv_sums, *ridden = centre(
        rows_two, pack, ffn_bias, wc_in, wc_out, w_rows_two, cotangent[0], ffn_in, 6
    )
    stream, grad_q, grad_k, grad_x, grad_pos, grad_out, mix_sums, own_sums, one_in, one_out, one_sums, *ridden = rear(
        stream, rows_one, pack, saved_mix, table, proj, qkv_proj, w_mine, ridden, rows_in, saved_one, w_rows_one,
        ffn_in, heads, 12
    )
    tall, deep = one_in.shape
    piece = max(128, 8 * nb)
    *sums, out_gains, out_biases, out_taps, out_hidden = tail_sum(
        [grad_out, one_out, one_in, grad_q, grad_k, grad_x, grad_pos, grad_conv_in, grad_conv_out],
        ridden,
        [one_sums, mix_sums, two_sums, conv_sums, own_sums],
        [("turn", 4, None), ("turn", 1, 0), ("plain", 0, 0)]
        + [("half", 2, at) for at in range(3)]
        + [("half", 3, None), ("gather", 5, None), ("gather", 6, None)],
        [
            (2, tall, deep), (2, ns * deep, width), (3, tall, width), (tall, width), (tall, width),
            (tall, 2 * width), (tall, width),
        ],
        ["near", "line"],
        [width, piece, piece] + [tall // 4] * 4 + [2 * piece, min(tall, 4 * piece)],
        deep,
        4,
    )
    *sums, result, stream, out_gains, out_biases, out_taps, out_hidden = widen(
        sums, [result, stream, out_gains, out_biases, out_taps, out_hidden]
    )
    return (
        result[None],
        stream[None],
        sums[0],
        sums[1],
        out_hidden,
        sums[2],
        sums[3],
        sums[4],
        sums[5],
        sums[6],
        out_taps,
        out_gains,
        out_biases,
    )


def solution(mesh):
    rows = P(("batch", "shard"), None, None)
    cube, flat = P(None, None, "shard"), P(None, "shard")
    return jax.shard_map(
        body,
        mesh=mesh,
        in_specs=(rows, rows, P(("batch", "shard")), cube, cube, flat, cube)
        + (flat,) * 7,
        out_specs=(rows, rows, cube, cube, flat, cube) + (flat,) * 7,
        check_vma=False,
    )
```
